512 devices in a mesh: rows: 32 (over y_lo, z), filt: 16 (over y_hi, x, core).
Axes of the slice: x: 4, y: 4 (y_hi: 2, y_lo: 2; y = y_hi * 2 + y_lo), z: 16, core: 2. Of those that a mesh axis runs over, the one named last changes fastest.
Arguments:
- features: bfloat16 [512, 32, 512], P('filt', 'rows'), may hold values from -6 to 6
- first_weight: bfloat16 [512, 3, 3, 512], P('filt'), may hold values from -0.09375 to 0.09375
- second_weight: bfloat16 [512, 3, 3, 512], P('filt'), may hold values from -0.09375 to 0.09375
- out_grad: bfloat16 [512, 32, 512], P('filt', 'rows'), may hold values from -0.046875 to 0.046875
Outputs:
- block_out: bfloat16 [512, 32, 512], P('filt', 'rows')
- first_grad: float32 [512, 3, 3, 512], P('filt')
- second_grad: float32 [512, 3, 3, 512], P('filt')
The draws below stay inside these ranges and needn't reach their ends.
All inputs are finite; a program needn't handle non-finite values.
Results may differ from the reference program's by a relative error of at most 0.024.
The reference program's roundings to bfloat16 on the way (of `hidden`, `grad_second` and `grad_first`) count: a program that leaves them out, or rounds other values in their place, can miss the bound.
Values may be sent and summed in bfloat16 or wider, within the bound.
A program may use at most 64 MiB of HBM per device.

```python
import jax
import jax.numpy as jnp

C = 512
W = 512
ROWS_DEV = 1
H = 32
N_ROWS = 32


def levels(own_key, dims, cuts, smallest, top_value):
    def one(axis_at, parts):
        steps = jax.random.uniform(jax.random.fold_in(jax.random.fold_in(own_key, 6), axis_at), (parts,), jnp.float32, smallest / len(cuts), top_value / len(cuts))
        return jnp.repeat(jnp.exp(steps), dims[axis_at] // parts).reshape((-1,) + (1,) * (len(dims) - axis_at - 1))

    level = one(*cuts[0])
    for cut in cuts[1:]:
        level = level * one(*cut)
    return level


def centred(key, shape, deviation, reach, cuts=(), dtype=jnp.bfloat16):
    entries = deviation * jax.random.normal(key, shape, jnp.float32)
    if cuts:
        entries = entries * levels(key, shape, cuts, -0.22, 0.18)
    return jnp.clip(entries, -reach, reach).astype(dtype)


def setup_inputs(seed: int = 0) -> dict:
    arg_keys = jax.random.split(jax.random.key(seed), 5)
    return {
        "features": centred(arg_keys[0], (C, H, W), 1.0, 6.0, ((0, 16), (1, 32))),
        "first_weight": centred(arg_keys[1], (C, 3, 3, C), (9 * C) ** -0.5, 0.09375, ((0, 16),)),
        "second_weight": centred(arg_keys[2], (C, 3, 3, C), (9 * C) ** -0.5, 0.09375, ((0, 16),)),
        "out_grad": centred(arg_keys[3], (C, H, W), (1.0 / (ROWS_DEV * N_ROWS * W) ** 0.5), 0.046875, ((0, 16), (1, 32))),
    }


def shift_cols(value, offset):
    if offset == 0:
        return value
    if offset > 0:
        return jnp.pad(value[..., offset:], ((0, 0), (0, 0), (0, offset)))
    return jnp.pad(value[..., :offset], ((0, 0), (0, 0), (-offset, 0)))


def conv_forward(weight, padded, count):
    total = jnp.zeros((weight.shape[0], count, padded.shape[2]), jnp.float32)
    for a in range(3):
        for b in range(3):
            part = jnp.einsum("oi,ihw->ohw", weight[:, a, b, :].astype(jnp.float32), padded[:, a:a + count, :].astype(jnp.float32))
            total = total + shift_cols(part, b - 1)
    return total


def conv_backward(weight, padded, count):
    total = jnp.zeros((weight.shape[3], count, padded.shape[2]), jnp.float32)
    for a in range(3):
        for b in range(3):
            part = jnp.einsum("oi,ohw->ihw", weight[:, a, b, :].astype(jnp.float32), padded[:, 2 - a:2 - a + count, :].astype(jnp.float32))
            total = total + shift_cols(part, 1 - b)
    return total


def weight_terms(grad, padded, count):
    rows_out = []
    for a in range(3):
        cols_out = []
        for b in range(3):
            moved = shift_cols(grad, 1 - b)
            cols_out.append(jnp.einsum("ohw,ihw->oi", moved.astype(jnp.float32), padded[:, a:a + count, :].astype(jnp.float32)))
        rows_out.append(jnp.stack(cols_out, axis=1))
    return jnp.stack(rows_out, axis=1)


def pad_rows(value):
    return jnp.pad(value, ((0, 0), (1, 1), (0, 0)))


def reference(features, first_weight, second_weight, out_grad):
    count = features.shape[1]
    padded_in = pad_rows(features)
    pre_first = conv_forward(first_weight, padded_in, count)
    hidden = jnp.maximum(pre_first, 0.0).astype(jnp.bfloat16)
    padded_hidden = pad_rows(hidden)
    pre_second = conv_forward(second_weight, padded_hidden, count) + features.astype(jnp.float32)
    block_out = jnp.maximum(pre_second, 0.0).astype(jnp.bfloat16)
    grad_second = jnp.where(pre_second > 0, out_grad.astype(jnp.float32), 0.0).astype(jnp.bfloat16)
    hidden_grad = conv_backward(second_weight, pad_rows(grad_second), count)
    grad_first = jnp.where(pre_first > 0, hidden_grad, 0.0).astype(jnp.bfloat16)
    second_grad = weight_terms(grad_second, padded_hidden, count)
    first_grad = weight_terms(grad_first, padded_in, count)
    return block_out, first_grad, second_grad
```

```python
import jax
import jax.numpy as jnp
from jax import lax
from jax.sharding import PartitionSpec as P


def shift_cols(value, offset):
    if offset == 0:
        return value
    pad = [(0, 0)] * (value.ndim - 1)
    if offset > 0:
        return jnp.pad(value[..., offset:], pad + [(0, offset)])
    return jnp.pad(value[..., :offset], pad + [(-offset, 0)])


def from_prev(value):
    count = lax.axis_size("rows")
    return lax.ppermute(value, "rows", [(i, i + 1) for i in range(count - 1)])


def from_next(value):
    count = lax.axis_size("rows")
    return lax.ppermute(value, "rows", [(i + 1, i) for i in range(count - 1)])


def conv_row(weight, row):
    o = weight.shape[0]
    flat = weight.reshape(o, 9, weight.shape[3])
    parts = jnp.einsum("oki,iw->kow", flat, row, preferred_element_type=jnp.float32)
    return [sum(shift_cols(parts[a * 3 + b], b - 1) for b in range(3)) for a in range(3)]


def conv_forward(weight, row):
    p0, p1, p2 = conv_row(weight, row)
    return p1 + from_prev(p0) + from_next(p2)


def grad_rows(grad):
    return jnp.stack([from_next(grad), grad, from_prev(grad)])


def weight_terms(rows3, full_row):
    cols = []
    for b in range(3):
        moved = shift_cols(rows3, 1 - b)
        cols.append(jnp.einsum("aow,iw->oai", moved, full_row, preferred_element_type=jnp.float32))
    return jnp.stack(cols, axis=2)


def hidden_terms(weight, rows3):
    total = None
    for b in range(3):
        part = jnp.einsum("oai,aow->iw", weight[:, :, b, :], rows3, preferred_element_type=jnp.float32)
        part = shift_cols(part, 1 - b)
        total = part if total is None else total + part
    return total


def per_device(features, first_weight, second_weight, out_grad):
    feat = features[:, 0, :]
    og = out_grad[:, 0, :]
    x_row = lax.all_gather(feat, "filt", axis=0, tiled=True)
    pre_first = conv_forward(first_weight, x_row)
    hidden = jnp.maximum(pre_first, 0.0).astype(jnp.bfloat16)
    h_row = lax.all_gather(hidden, "filt", axis=0, tiled=True)
    pre_second = conv_forward(second_weight, h_row) + feat.astype(jnp.float32)
    block_out = jnp.maximum(pre_second, 0.0).astype(jnp.bfloat16)
    grad_second = jnp.where(pre_second > 0, og.astype(jnp.float32), 0.0).astype(jnp.bfloat16)
    gs3 = grad_rows(grad_second)
    terms = hidden_terms(second_weight, gs3)
    hidden_grad = lax.psum_scatter(terms, "filt", scatter_dimension=0, tiled=True)
    grad_first = jnp.where(pre_first > 0, hidden_grad, 0.0).astype(jnp.bfloat16)
    gf3 = grad_rows(grad_first)
    second_local = weight_terms(gs3, h_row)
    first_local = weight_terms(gf3, x_row)
    first_grad, second_grad = lax.psum((first_local, second_local), "rows")
    return (block_out[:, None, :], first_grad, second_grad)


def solution(mesh):
    in_specs = (
        P("filt", "rows", None),
        P("filt", None, None, None),
        P("filt", None, None, None),
        P("filt", "rows", None),
    )
    out_specs = (P("filt", "rows", None), P("filt", None, None, None), P("filt", None, None, None))
    return jax.shard_map(
        per_device, mesh=mesh, in_specs=in_specs, out_specs=out_specs, check_vma=False
    )
```

```python
import functools

import jax
import jax.numpy as jnp
from jax import lax
from jax.experimental import pallas as pl
from jax.experimental.pallas import tpu as pltpu
from jax.sharding import PartitionSpec as P

MESH = pl.DeviceIdType.MESH


def peer_id(axis, j):
    if axis == "rows":
        return (j, lax.axis_index("filt"))
    return (lax.axis_index("rows"), j)


def exchange_kernel(axis, n, mode, *refs):
    me = lax.axis_index(axis)

    def each_peer(body):
        def step(k, carry):
            body(lax.rem(me + k, n), lax.rem(me + n - k, n))
            return carry

        lax.fori_loop(1, n, step, 0)

    barrier = pltpu.get_barrier_semaphore()

    def greet(j, s):
        pl.semaphore_signal(barrier, 1, device_id=peer_id(axis, j), device_id_type=MESH)

    each_peer(greet)
    pl.semaphore_wait(barrier, n - 1)

    def gather(src, out_ref, send, recv):
        def copy(j, s):
            return pltpu.make_async_remote_copy(
                src, out_ref.at[me], send.at[j], recv.at[me], device_id=peer_id(axis, j), device_id_type=MESH
            )

        def incoming(j, s):
            return pltpu.make_async_remote_copy(
                src, out_ref.at[s], send.at[s], recv.at[s], device_id=peer_id(axis, s), device_id_type=MESH
            )

        each_peer(lambda j, s: copy(j, s).start())
        return copy, incoming

    def reduce(x_ref, buf, send, recv):
        def copy(j, s):
            return pltpu.make_async_remote_copy(
                x_ref.at[j], buf.at[me], send.at[j], recv.at[me], device_id=peer_id(axis, j), device_id_type=MESH
            )

        def incoming(j, s):
            return pltpu.make_async_remote_copy(
                x_ref.at[s], buf.at[s], send.at[s], recv.at[s], device_id=peer_id(axis, s), device_id_type=MESH
            )

        each_peer(lambda j, s: copy(j, s).start())
        each_peer(lambda j, s: incoming(j, s).wait_recv())
        acc = x_ref[me].astype(jnp.float32)

        def add(k, acc):
            return acc + buf[lax.rem(me + k, n)].astype(jnp.float32)

        acc = lax.fori_loop(1, n, add, acc)
        each_peer(lambda j, s: copy(j, s).wait_send())
        return acc

    if mode == "ag":
        x_ref, out_ref, send, recv = refs
        copy, incoming = gather(x_ref, out_ref, send, recv)
        out_ref[me] = x_ref[...]
        each_peer(lambda j, s: incoming(j, s).wait_recv())
        each_peer(lambda j, s: copy(j, s).wait_send())
    elif mode == "rs":
        x_ref, out_ref, buf, send, recv = refs
        out_ref[...] = reduce(x_ref, buf, send, recv).astype(out_ref.dtype)
    else:
        x_ref, out_ref, buf, send, recv, send2, recv2 = refs
        out_ref[me] = reduce(x_ref, buf, send, recv).astype(out_ref.dtype)
        copy, incoming = gather(out_ref.at[me], out_ref, send2, recv2)
        each_peer(lambda j, s: incoming(j, s).wait_recv())
        each_peer(lambda j, s: copy(j, s).wait_send())


def exchange(x, axis, mode, collective_id, out_dtype=None):
    n = lax.axis_size(axis)
    out_dtype = out_dtype or x.dtype
    sems = [pltpu.SemaphoreType.DMA((n,)), pltpu.SemaphoreType.DMA((n,))]
    if mode == "ag":
        out_shape = (n,) + x.shape
        scratch = sems
    elif mode == "rs":
        out_shape = x.shape[1:]
        scratch = [pltpu.VMEM(x.shape, x.dtype)] + sems
    else:
        out_shape = x.shape
        scratch = [pltpu.VMEM(x.shape, x.dtype)] + sems + sems
    return pl.pallas_call(
        functools.partial(exchange_kernel, axis, n, mode),
        out_shape=jax.ShapeDtypeStruct(out_shape, out_dtype),
        in_specs=[pl.BlockSpec(memory_space=pltpu.VMEM)],
        out_specs=pl.BlockSpec(memory_space=pltpu.VMEM),
        scratch_shapes=scratch,
        compiler_params=pltpu.CompilerParams(collective_id=collective_id, has_side_effects=True),
    )(x)


def shift_cols(value, offset):
    if offset == 0:
        return value
    pad = [(0, 0)] * (value.ndim - 1)
    if offset > 0:
        return jnp.pad(value[..., offset:], pad + [(0, offset)])
    return jnp.pad(value[..., :offset], pad + [(-offset, 0)])


def from_prev(value):
    count = lax.axis_size("rows")
    return lax.ppermute(value, "rows", [(i, i + 1) for i in range(count - 1)])


def from_next(value):
    count = lax.axis_size("rows")
    return lax.ppermute(value, "rows", [(i + 1, i) for i in range(count - 1)])


def conv_row(weight, row):
    o = weight.shape[0]
    flat = weight.reshape(o, 9, weight.shape[3])
    parts = jnp.einsum("oki,iw->kow", flat, row, preferred_element_type=jnp.float32)
    return [sum(shift_cols(parts[a * 3 + b], b - 1) for b in range(3)) for a in range(3)]


def conv_forward(weight, row):
    p0, p1, p2 = conv_row(weight, row)
    return p1 + from_prev(p0) + from_next(p2)


def grad_rows(grad):
    return jnp.stack([from_next(grad), grad, from_prev(grad)])


def weight_terms(rows3, full_row):
    cols = []
    for b in range(3):
        moved = shift_cols(rows3, 1 - b)
        cols.append(jnp.einsum("aow,iw->oai", moved, full_row, preferred_element_type=jnp.float32))
    return jnp.stack(cols, axis=2)


def hidden_terms(weight, rows3):
    total = None
    for b in range(3):
        part = jnp.einsum("oai,aow->iw", weight[:, :, b, :], rows3, preferred_element_type=jnp.float32)
        part = shift_cols(part, 1 - b)
        total = part if total is None else total + part
    return total


def per_device(features, first_weight, second_weight, out_grad):
    feat = features[:, 0, :]
    og = out_grad[:, 0, :]
    x_row = lax.all_gather(feat, "filt", axis=0, tiled=True)
    pre_first = conv_forward(first_weight, x_row)
    hidden = jnp.maximum(pre_first, 0.0).astype(jnp.bfloat16)
    h_row = lax.all_gather(hidden, "filt", axis=0, tiled=True)
    pre_second = conv_forward(second_weight, h_row) + feat.astype(jnp.float32)
    block_out = jnp.maximum(pre_second, 0.0).astype(jnp.bfloat16)
    grad_second = jnp.where(pre_second > 0, og.astype(jnp.float32), 0.0).astype(jnp.bfloat16)
    gs3 = grad_rows(grad_second)
    terms = hidden_terms(second_weight, gs3)
    hidden_grad = lax.psum_scatter(terms, "filt", scatter_dimension=0, tiled=True)
    grad_first = jnp.where(pre_first > 0, hidden_grad, 0.0).astype(jnp.bfloat16)
    gf3 = grad_rows(grad_first)
    second_local = weight_terms(gs3, h_row)
    first_local = weight_terms(gf3, x_row)
    both = jnp.stack([first_local, second_local])
    n_rows = lax.axis_size("rows")
    summed = exchange(both.reshape(n_rows, -1, 128), "rows", "ar", 0)
    first_grad, second_grad = summed.reshape(both.shape)
    return (block_out[:, None, :], first_grad, second_grad)


def solution(mesh):
    in_specs = (
        P("filt", "rows", None),
        P("filt", None, None, None),
        P("filt", None, None, None),
        P("filt", "rows", None),
    )
    out_specs = (P("filt", "rows", None), P("filt", None, None, None), P("filt", None, None, None))
    return jax.shard_map(
        per_device, mesh=mesh, in_specs=in_specs, out_specs=out_specs, check_vma=False
    )
```

```python
import functools

import jax
import jax.numpy as jnp
from jax import lax
from jax.experimental import pallas as pl
from jax.experimental.pallas import tpu as pltpu
from jax.sharding import PartitionSpec as P

MESH = pl.DeviceIdType.MESH


def peer_id(axis, j):
    if axis == "rows":
        return (j, lax.axis_index("filt"))
    return (lax.axis_index("rows"), j)


def exchange_kernel(axis, n, mode, *refs):
    me = lax.axis_index(axis)

    def each_peer(body):
        def step(k, carry):
            body(lax.rem(me + k, n), lax.rem(me + n - k, n))
            return carry

        lax.fori_loop(1, n, step, 0)

    barrier = pltpu.get_barrier_semaphore()

    def greet(j, s):
        pl.semaphore_signal(barrier, 1, device_id=peer_id(axis, j), device_id_type=MESH)

    each_peer(greet)
    pl.semaphore_wait(barrier, n - 1)

    def gather(src, out_ref, send, recv):
        def copy(j, s):
            return pltpu.make_async_remote_copy(
                src, out_ref.at[me], send.at[j], recv.at[me], device_id=peer_id(axis, j), device_id_type=MESH
            )

        def incoming(j, s):
            return pltpu.make_async_remote_copy(
                src, out_ref.at[s], send.at[s], recv.at[s], device_id=peer_id(axis, s), device_id_type=MESH
            )

        each_peer(lambda j, s: copy(j, s).start())
        return copy, incoming

    def reduce(x_ref, buf, send, recv):
        def copy(j, s):
            return pltpu.make_async_remote_copy(
                x_ref.at[j], buf.at[me], send.at[j], recv.at[me], device_id=peer_id(axis, j), device_id_type=MESH
            )

        def incoming(j, s):
            return pltpu.make_async_remote_copy(
                x_ref.at[s], buf.at[s], send.at[s], recv.at[s], device_id=peer_id(axis, s), device_id_type=MESH
            )

        each_peer(lambda j, s: copy(j, s).start())
        each_peer(lambda j, s: incoming(j, s).wait_recv())
        acc = x_ref[me].astype(jnp.float32)

        def add(k, acc):
            return acc + buf[lax.rem(me + k, n)].astype(jnp.float32)

        acc = lax.fori_loop(1, n, add, acc)
        each_peer(lambda j, s: copy(j, s).wait_send())
        return acc

    if mode == "ag":
        x_ref, out_ref, send, recv = refs
        copy, incoming = gather(x_ref, out_ref, send, recv)
        out_ref[me] = x_ref[...]
        each_peer(lambda j, s: incoming(j, s).wait_recv())
        each_peer(lambda j, s: copy(j, s).wait_send())
    elif mode == "rs":
        x_ref, out_ref, buf, send, recv = refs
        out_ref[...] = reduce(x_ref, buf, send, recv).astype(out_ref.dtype)
    else:
        x_ref, out_ref, buf, send, recv, send2, recv2 = refs
        out_ref[me] = reduce(x_ref, buf, send, recv).astype(out_ref.dtype)
        copy, incoming = gather(out_ref.at[me], out_ref, send2, recv2)
        each_peer(lambda j, s: incoming(j, s).wait_recv())
        each_peer(lambda j, s: copy(j, s).wait_send())


def exchange(x, axis, mode, collective_id, out_dtype=None):
    n = lax.axis_size(axis)
    out_dtype = out_dtype or x.dtype
    sems = [pltpu.SemaphoreType.DMA((n,)), pltpu.SemaphoreType.DMA((n,))]
    if mode == "ag":
        out_shape = (n,) + x.shape
        scratch = sems
    elif mode == "rs":
        out_shape = x.shape[1:]
        scratch = [pltpu.VMEM(x.shape, x.dtype)] + sems
    else:
        out_shape = x.shape
        scratch = [pltpu.VMEM(x.shape, x.dtype)] + sems + sems
    return pl.pallas_call(
        functools.partial(exchange_kernel, axis, n, mode),
        out_shape=jax.ShapeDtypeStruct(out_shape, out_dtype),
        in_specs=[pl.BlockSpec(memory_space=pltpu.VMEM)],
        out_specs=pl.BlockSpec(memory_space=pltpu.VMEM),
        scratch_shapes=scratch,
        compiler_params=pltpu.CompilerParams(collective_id=collective_id, has_side_effects=True),
    )(x)


def shift_cols(value, offset):
    if offset == 0:
        return value
    pad = [(0, 0)] * (value.ndim - 1)
    if offset > 0:
        return jnp.pad(value[..., offset:], pad + [(0, offset)])
    return jnp.pad(value[..., :offset], pad + [(-offset, 0)])


def from_prev(value):
    count = lax.axis_size("rows")
    return lax.ppermute(value, "rows", [(i, i + 1) for i in range(count - 1)])


def from_next(value):
    count = lax.axis_size("rows")
    return lax.ppermute(value, "rows", [(i + 1, i) for i in range(count - 1)])


def conv_row(weight, row):
    o = weight.shape[0]
    flat = weight.reshape(o, 9, weight.shape[3])
    parts = jnp.einsum("oki,iw->kow", flat, row, preferred_element_type=jnp.float32)
    return [sum(shift_cols(parts[a * 3 + b], b - 1) for b in range(3)) for a in range(3)]


def conv_forward(weight, row):
    p0, p1, p2 = conv_row(weight, row)
    return p1 + from_prev(p0) + from_next(p2)


def grad_rows(grad):
    return jnp.stack([from_next(grad), grad, from_prev(grad)])


def weight_terms(rows3, full_row):
    cols = []
    for b in range(3):
        moved = shift_cols(rows3, 1 - b)
        cols.append(jnp.einsum("aow,iw->oai", moved, full_row, preferred_element_type=jnp.float32))
    return jnp.stack(cols, axis=2)


def hidden_terms(weight, rows3):
    total = None
    for b in range(3):
        part = jnp.einsum("oai,aow->iw", weight[:, :, b, :], rows3, preferred_element_type=jnp.float32)
        part = shift_cols(part, 1 - b)
        total = part if total is None else total + part
    return total


def per_device(features, first_weight, second_weight, out_grad):
    feat = features[:, 0, :]
    og = out_grad[:, 0, :]
    n_filt = lax.axis_size("filt")
    x_row = exchange(feat, "filt", "ag", 1).reshape(-1, feat.shape[1])
    pre_first = conv_forward(first_weight, x_row)
    hidden = jnp.maximum(pre_first, 0.0).astype(jnp.bfloat16)
    h_row = exchange(hidden, "filt", "ag", 2).reshape(-1, hidden.shape[1])
    pre_second = conv_forward(second_weight, h_row) + feat.astype(jnp.float32)
    block_out = jnp.maximum(pre_second, 0.0).astype(jnp.bfloat16)
    grad_second = jnp.where(pre_second > 0, og.astype(jnp.float32), 0.0).astype(jnp.bfloat16)
    gs3 = grad_rows(grad_second)
    terms = hidden_terms(second_weight, gs3)
    hidden_grad = exchange(terms.reshape(n_filt, -1, terms.shape[1]), "filt", "rs", 3)
    grad_first = jnp.where(pre_first > 0, hidden_grad, 0.0).astype(jnp.bfloat16)
    gf3 = grad_rows(grad_first)
    second_local = weight_terms(gs3, h_row)
    first_local = weight_terms(gf3, x_row)
    both = jnp.stack([first_local, second_local])
    n_rows = lax.axis_size("rows")
    summed = exchange(both.reshape(n_rows, -1, 128), "rows", "ar", 0)
    first_grad, second_grad = summed.reshape(both.shape)
    return (block_out[:, None, :], first_grad, second_grad)


def solution(mesh):
    in_specs = (
        P("filt", "rows", None),
        P("filt", None, None, None),
        P("filt", None, None, None),
        P("filt", "rows", None),
    )
    out_specs = (P("filt", "rows", None), P("filt", None, None, None), P("filt", None, None, None))
    return jax.shard_map(
        per_device, mesh=mesh, in_specs=in_specs, out_specs=out_specs, check_vma=False
    )
```

```python
import functools

import jax
import jax.numpy as jnp
from jax import lax
from jax.experimental import pallas as pl
from jax.experimental.pallas import tpu as pltpu
from jax.sharding import PartitionSpec as P

MESH = pl.DeviceIdType.MESH


def peer_id(axis, j):
    if axis == "rows":
        return (j, lax.axis_index("filt"))
    return (lax.axis_index("rows"), j)


def exchange_kernel(axis, n, mode, *refs):
    me = lax.axis_index(axis)

    def each_peer(body):
        def step(k, carry):
            body(lax.rem(me + k, n), lax.rem(me + n - k, n))
            return carry

        lax.fori_loop(1, n, step, 0)

    barrier = pltpu.get_barrier_semaphore()

    def greet(j, s):
        pl.semaphore_signal(barrier, 1, device_id=peer_id(axis, j), device_id_type=MESH)

    each_peer(greet)
    pl.semaphore_wait(barrier, n - 1)

    def gather(src, out_ref, send, recv):
        def copy(j, s):
            return pltpu.make_async_remote_copy(
                src, out_ref.at[me], send.at[j], recv.at[me], device_id=peer_id(axis, j), device_id_type=MESH
            )

        def incoming(j, s):
            return pltpu.make_async_remote_copy(
                src, out_ref.at[s], send.at[s], recv.at[s], device_id=peer_id(axis, s), device_id_type=MESH
            )

        each_peer(lambda j, s: copy(j, s).start())
        return copy, incoming

    def reduce(x_ref, buf, send, recv):
        def copy(j, s):
            return pltpu.make_async_remote_copy(
                x_ref.at[j], buf.at[me], send.at[j], recv.at[me], device_id=peer_id(axis, j), device_id_type=MESH
            )

        def incoming(j, s):
            return pltpu.make_async_remote_copy(
                x_ref.at[s], buf.at[s], send.at[s], recv.at[s], device_id=peer_id(axis, s), device_id_type=MESH
            )

        each_peer(lambda j, s: copy(j, s).start())
        each_peer(lambda j, s: incoming(j, s).wait_recv())
        acc = x_ref[me].astype(jnp.float32)

        def add(k, acc):
            return acc + buf[lax.rem(me + k, n)].astype(jnp.float32)

        acc = lax.fori_loop(1, n, add, acc)
        each_peer(lambda j, s: copy(j, s).wait_send())
        return acc

    if mode == "ag":
        x_ref, out_ref, send, recv = refs
        copy, incoming = gather(x_ref, out_ref, send, recv)
        out_ref[me] = x_ref[...]
        each_peer(lambda j, s: incoming(j, s).wait_recv())
        each_peer(lambda j, s: copy(j, s).wait_send())
    elif mode == "rs":
        x_ref, out_ref, buf, send, recv = refs
        out_ref[...] = reduce(x_ref, buf, send, recv).astype(out_ref.dtype)
    else:
        x_ref, out_ref, buf, send, recv, send2, recv2 = refs
        out_ref[me] = reduce(x_ref, buf, send, recv).astype(out_ref.dtype)
        copy, incoming = gather(out_ref.at[me], out_ref, send2, recv2)
        each_peer(lambda j, s: incoming(j, s).wait_recv())
        each_peer(lambda j, s: copy(j, s).wait_send())


def row_sum_kernel(n, x_ref, out_ref, half_buf, half_b, part_buf, sems):
    zn = n // 2
    me = lax.axis_index("rows")
    my_y, my_z = me // zn, lax.rem(me, zn)
    other = lax.rem(me + zn, n)
    mine, theirs = my_y * zn, (1 - my_y) * zn

    def dev(j):
        return (j, lax.axis_index("filt"))

    def each_z(body):
        def step(k, carry):
            body(lax.rem(my_z + k, zn), lax.rem(my_z + zn - k, zn))
            return carry

        lax.fori_loop(1, zn, step, 0)

    barrier = pltpu.get_barrier_semaphore()
    pl.semaphore_signal(barrier, 1, device_id=dev(other), device_id_type=MESH)
    each_z(lambda j, s: pl.semaphore_signal(barrier, 1, device_id=dev(mine + j), device_id_type=MESH))
    pl.semaphore_wait(barrier, zn)

    def rcopy(src, dst, send, recv, j):
        return pltpu.make_async_remote_copy(src, dst, send, recv, device_id=dev(j), device_id_type=MESH)

    swap = rcopy(x_ref.at[pl.ds(theirs, zn)], half_buf, sems.at[0, 0], sems.at[0, 1], other)
    swap.start()
    swap.wait_recv()

    def add_half(t, carry):
        half_b[t] = (x_ref[mine + t].astype(jnp.float32) + half_buf[t].astype(jnp.float32)).astype(half_b.dtype)
        return carry

    lax.fori_loop(0, zn, add_half, 0)
    swap.wait_send()

    def part_out(j, s):
        return rcopy(half_b.at[j], part_buf.at[my_z], sems.at[1, j], sems.at[2, my_z], mine + j)

    def part_in(j, s):
        return rcopy(half_b.at[s], part_buf.at[s], sems.at[1, s], sems.at[2, s], mine + s)

    each_z(lambda j, s: part_out(j, s).start())
    each_z(lambda j, s: part_in(j, s).wait_recv())
    acc = (x_ref[me].astype(jnp.float32) + half_buf[my_z].astype(jnp.float32))

    def add_part(k, acc):
        return acc + part_buf[lax.rem(my_z + k, zn)].astype(jnp.float32)

    acc = lax.fori_loop(1, zn, add_part, acc)
    out_ref[me] = acc.astype(out_ref.dtype)
    each_z(lambda j, s: part_out(j, s).wait_send())

    def sum_out(j, s):
        return rcopy(out_ref.at[me], out_ref.at[me], sems.at[3, j], sems.at[4, my_z], mine + j)

    def sum_in(j, s):
        return rcopy(out_ref.at[mine + s], out_ref.at[mine + s], sems.at[3, s], sems.at[4, s], mine + s)

    each_z(lambda j, s: sum_out(j, s).start())
    each_z(lambda j, s: sum_in(j, s).wait_recv())
    each_z(lambda j, s: sum_out(j, s).wait_send())
    back = rcopy(out_ref.at[pl.ds(mine, zn)], out_ref.at[pl.ds(mine, zn)], sems.at[5, 0], sems.at[5, 1], other)
    back.start()
    back.wait_recv()
    back.wait_send()


def row_sum(x, collective_id):
    n = x.shape[0]
    zn = n // 2
    blk = x.shape[1:]
    return pl.pallas_call(
        functools.partial(row_sum_kernel, n),
        out_shape=jax.ShapeDtypeStruct(x.shape, x.dtype),
        in_specs=[pl.BlockSpec(memory_space=pltpu.VMEM)],
        out_specs=pl.BlockSpec(memory_space=pltpu.VMEM),
        scratch_shapes=[
            pltpu.VMEM((zn,) + blk, x.dtype),
            pltpu.VMEM((zn,) + blk, x.dtype),
            pltpu.VMEM((zn,) + blk, x.dtype),
            pltpu.SemaphoreType.DMA((6, zn)),
        ],
        compiler_params=pltpu.CompilerParams(collective_id=collective_id, has_side_effects=True),
    )(x)


def exchange(x, axis, mode, collective_id, out_dtype=None):
    n = lax.axis_size(axis)
    out_dtype = out_dtype or x.dtype
    sems = [pltpu.SemaphoreType.DMA((n,)), pltpu.SemaphoreType.DMA((n,))]
    if mode == "ag":
        out_shape = (n,) + x.shape
        scratch = sems
    elif mode == "rs":
        out_shape = x.shape[1:]
        scratch = [pltpu.VMEM(x.shape, x.dtype)] + sems
    else:
        out_shape = x.shape
        scratch = [pltpu.VMEM(x.shape, x.dtype)] + sems + sems
    return pl.pallas_call(
        functools.partial(exchange_kernel, axis, n, mode),
        out_shape=jax.ShapeDtypeStruct(out_shape, out_dtype),
        in_specs=[pl.BlockSpec(memory_space=pltpu.VMEM)],
        out_specs=pl.BlockSpec(memory_space=pltpu.VMEM),
        scratch_shapes=scratch,
        compiler_params=pltpu.CompilerParams(collective_id=collective_id, has_side_effects=True),
    )(x)


def shift_cols(value, offset):
    if offset == 0:
        return value
    pad = [(0, 0)] * (value.ndim - 1)
    if offset > 0:
        return jnp.pad(value[..., offset:], pad + [(0, offset)])
    return jnp.pad(value[..., :offset], pad + [(-offset, 0)])


def from_prev(value):
    count = lax.axis_size("rows")
    return lax.ppermute(value, "rows", [(i, i + 1) for i in range(count - 1)])


def from_next(value):
    count = lax.axis_size("rows")
    return lax.ppermute(value, "rows", [(i + 1, i) for i in range(count - 1)])


def conv_row(weight, row):
    o = weight.shape[0]
    flat = weight.reshape(o, 9, weight.shape[3])
    parts = jnp.einsum("oki,iw->kow", flat, row, preferred_element_type=jnp.float32)
    return [sum(shift_cols(parts[a * 3 + b], b - 1) for b in range(3)) for a in range(3)]


def conv_forward(weight, row):
    p0, p1, p2 = conv_row(weight, row)
    return p1 + from_prev(p0) + from_next(p2)


def grad_rows(grad):
    return jnp.stack([from_next(grad), grad, from_prev(grad)])


def weight_terms(rows3, full_row):
    cols = []
    for b in range(3):
        moved = shift_cols(rows3, 1 - b)
        cols.append(jnp.einsum("aow,iw->oai", moved, full_row, preferred_element_type=jnp.float32))
    return jnp.stack(cols, axis=2)


def hidden_terms(weight, rows3):
    total = None
    for b in range(3):
        part = jnp.einsum("oai,aow->iw", weight[:, :, b, :], rows3, preferred_element_type=jnp.float32)
        part = shift_cols(part, 1 - b)
        total = part if total is None else total + part
    return total


def per_device(features, first_weight, second_weight, out_grad):
    feat = features[:, 0, :]
    og = out_grad[:, 0, :]
    n_filt = lax.axis_size("filt")
    x_row = exchange(feat, "filt", "ag", 1).reshape(-1, feat.shape[1])
    pre_first = conv_forward(first_weight, x_row)
    hidden = jnp.maximum(pre_first, 0.0).astype(jnp.bfloat16)
    h_row = exchange(hidden, "filt", "ag", 2).reshape(-1, hidden.shape[1])
    pre_second = conv_forward(second_weight, h_row) + feat.astype(jnp.float32)
    block_out = jnp.maximum(pre_second, 0.0).astype(jnp.bfloat16)
    grad_second = jnp.where(pre_second > 0, og.astype(jnp.float32), 0.0).astype(jnp.bfloat16)
    gs3 = grad_rows(grad_second)
    terms = hidden_terms(second_weight, gs3)
    hidden_grad = exchange(
        terms.astype(jnp.bfloat16).reshape(n_filt, -1, terms.shape[1]), "filt", "rs", 3, jnp.float32
    )
    grad_first = jnp.where(pre_first > 0, hidden_grad, 0.0).astype(jnp.bfloat16)
    gf3 = grad_rows(grad_first)
    second_local = weight_terms(gs3, h_row)
    first_local = weight_terms(gf3, x_row)
    both = jnp.stack([first_local, second_local])
    n_rows = lax.axis_size("rows")
    summed = row_sum(both.astype(jnp.bfloat16).reshape(n_rows, -1, 128), 0)
    first_grad, second_grad = summed.astype(jnp.float32).reshape(both.shape)
    return (block_out[:, None, :], first_grad, second_grad)


def solution(mesh):
    in_specs = (
        P("filt", "rows", None),
        P("filt", None, None, None),
        P("filt", None, None, None),
        P("filt", "rows", None),
    )
    out_specs = (P("filt", "rows", None), P("filt", None, None, None), P("filt", None, None, None))
    return jax.shard_map(
        per_device, mesh=mesh, in_specs=in_specs, out_specs=out_specs, check_vma=False
    )
```

```python
import functools

import jax
import jax.numpy as jnp
from jax import lax
from jax.experimental import pallas as pl
from jax.experimental.pallas import tpu as pltpu
from jax.sharding import PartitionSpec as P

MESH = pl.DeviceIdType.MESH


def peer_id(axis, j):
    if axis == "rows":
        return (j, lax.axis_index("filt"))
    return (lax.axis_index("rows"), j)


def exchange_kernel(axis, n, mode, *refs):
    me = lax.axis_index(axis)

    def each_peer(body):
        def step(k, carry):
            body(lax.rem(me + k, n), lax.rem(me + n - k, n))
            return carry

        lax.fori_loop(1, n, step, 0)

    barrier = pltpu.get_barrier_semaphore()

    def greet(j, s):
        pl.semaphore_signal(barrier, 1, device_id=peer_id(axis, j), device_id_type=MESH)

    each_peer(greet)
    pl.semaphore_wait(barrier, n - 1)

    def gather(src, out_ref, send, recv):
        def copy(j, s):
            return pltpu.make_async_remote_copy(
                src, out_ref.at[me], send.at[j], recv.at[me], device_id=peer_id(axis, j), device_id_type=MESH
            )

        def incoming(j, s):
            return pltpu.make_async_remote_copy(
                src, out_ref.at[s], send.at[s], recv.at[s], device_id=peer_id(axis, s), device_id_type=MESH
            )

        each_peer(lambda j, s: copy(j, s).start())
        return copy, incoming

    def reduce(x_ref, buf, send, recv):
        def copy(j, s):
            return pltpu.make_async_remote_copy(
                x_ref.at[j], buf.at[me], send.at[j], recv.at[me], device_id=peer_id(axis, j), device_id_type=MESH
            )

        def incoming(j, s):
            return pltpu.make_async_remote_copy(
                x_ref.at[s], buf.at[s], send.at[s], recv.at[s], device_id=peer_id(axis, s), device_id_type=MESH
            )

        each_peer(lambda j, s: copy(j, s).start())
        each_peer(lambda j, s: incoming(j, s).wait_recv())
        acc = x_ref[me].astype(jnp.float32)

        def add(k, acc):
            return acc + buf[lax.rem(me + k, n)].astype(jnp.float32)

        acc = lax.fori_loop(1, n, add, acc)
        each_peer(lambda j, s: copy(j, s).wait_send())
        return acc

    if mode == "ag":
        x_ref, out_ref, send, recv = refs
        copy, incoming = gather(x_ref, out_ref, send, recv)
        out_ref[me] = x_ref[...]
        each_peer(lambda j, s: incoming(j, s).wait_recv())
        each_peer(lambda j, s: copy(j, s).wait_send())
    elif mode == "rs":
        x_ref, out_ref, buf, send, recv = refs
        out_ref[...] = reduce(x_ref, buf, send, recv).astype(out_ref.dtype)
    else:
        x_ref, out_ref, buf, send, recv, send2, recv2 = refs
        out_ref[me] = reduce(x_ref, buf, send, recv).astype(out_ref.dtype)
        copy, incoming = gather(out_ref.at[me], out_ref, send2, recv2)
        each_peer(lambda j, s: incoming(j, s).wait_recv())
        each_peer(lambda j, s: copy(j, s).wait_send())


def row_sum_kernel(n, x_ref, out_ref, half_buf, half_b, part_buf, sems):
    zn = n // 2
    me = lax.axis_index("rows")
    my_y, my_z = me // zn, lax.rem(me, zn)
    other = lax.rem(me + zn, n)
    mine, theirs = my_y * zn, (1 - my_y) * zn

    def dev(j):
        return (j, lax.axis_index("filt"))

    def each_z(body):
        def step(k, carry):
            body(lax.rem(my_z + k, zn), lax.rem(my_z + zn - k, zn))
            return carry

        lax.fori_loop(1, zn, step, 0)

    barrier = pltpu.get_barrier_semaphore()
    pl.semaphore_signal(barrier, 1, device_id=dev(other), device_id_type=MESH)
    each_z(lambda j, s: pl.semaphore_signal(barrier, 1, device_id=dev(mine + j), device_id_type=MESH))
    pl.semaphore_wait(barrier, zn)

    def rcopy(src, dst, send, recv, j):
        return pltpu.make_async_remote_copy(src, dst, send, recv, device_id=dev(j), device_id_type=MESH)

    swap = rcopy(x_ref.at[pl.ds(theirs, zn)], half_buf, sems.at[0, 0], sems.at[0, 1], other)
    swap.start()
    swap.wait_recv()

    def add_half(t, carry):
        half_b[t] = (x_ref[mine + t].astype(jnp.float32) + half_buf[t].astype(jnp.float32)).astype(half_b.dtype)
        return carry

    lax.fori_loop(0, zn, add_half, 0)
    swap.wait_send()

    def part_out(j, s):
        return rcopy(half_b.at[j], part_buf.at[my_z], sems.at[1, j], sems.at[2, my_z], mine + j)

    def part_in(j, s):
        return rcopy(half_b.at[s], part_buf.at[s], sems.at[1, s], sems.at[2, s], mine + s)

    each_z(lambda j, s: part_out(j, s).start())
    each_z(lambda j, s: part_in(j, s).wait_recv())
    acc = (x_ref[me].astype(jnp.float32) + half_buf[my_z].astype(jnp.float32))

    def add_part(k, acc):
        return acc + part_buf[lax.rem(my_z + k, zn)].astype(jnp.float32)

    acc = lax.fori_loop(1, zn, add_part, acc)
    out_ref[me] = acc.astype(out_ref.dtype)
    each_z(lambda j, s: part_out(j, s).wait_send())

    def sum_out(j, s):
        return rcopy(out_ref.at[me], out_ref.at[me], sems.at[3, j], sems.at[4, my_z], mine + j)

    def sum_in(j, s):
        return rcopy(out_ref.at[mine + s], out_ref.at[mine + s], sems.at[3, s], sems.at[4, s], mine + s)

    each_z(lambda j, s: sum_out(j, s).start())
    each_z(lambda j, s: sum_in(j, s).wait_recv())
    each_z(lambda j, s: sum_out(j, s).wait_send())
    back = rcopy(out_ref.at[pl.ds(mine, zn)], out_ref.at[pl.ds(mine, zn)], sems.at[5, 0], sems.at[5, 1], other)
    back.start()
    back.wait_recv()
    back.wait_send()


def row_sum(x, collective_id):
    n = x.shape[0]
    zn = n // 2
    blk = x.shape[1:]
    return pl.pallas_call(
        functools.partial(row_sum_kernel, n),
        out_shape=jax.ShapeDtypeStruct(x.shape, x.dtype),
        in_specs=[pl.BlockSpec(memory_space=pltpu.VMEM)],
        out_specs=pl.BlockSpec(memory_space=pltpu.VMEM),
        scratch_shapes=[
            pltpu.VMEM((zn,) + blk, x.dtype),
            pltpu.VMEM((zn,) + blk, x.dtype),
            pltpu.VMEM((zn,) + blk, x.dtype),
            pltpu.SemaphoreType.DMA((6, zn)),
        ],
        compiler_params=pltpu.CompilerParams(collective_id=collective_id, has_side_effects=True),
    )(x)


def halo_kernel(n, down_ref, up_ref, from_prev, from_next, sems):
    me = lax.axis_index("rows")
    has_prev, has_next = me > 0, me < n - 1

    def dev(j):
        return (j, lax.axis_index("filt"))

    barrier = pltpu.get_barrier_semaphore()

    @pl.when(has_prev)
    def _():
        pl.semaphore_signal(barrier, 1, device_id=dev(me - 1), device_id_type=MESH)

    @pl.when(has_next)
    def _():
        pl.semaphore_signal(barrier, 1, device_id=dev(me + 1), device_id_type=MESH)

    pl.semaphore_wait(barrier, (me + n - 1) // n + (2 * n - 2 - me) // n)

    def down(j):
        return pltpu.make_async_remote_copy(down_ref, from_prev, sems.at[0], sems.at[1], device_id=dev(j), device_id_type=MESH)

    def up(j):
        return pltpu.make_async_remote_copy(up_ref, from_next, sems.at[2], sems.at[3], device_id=dev(j), device_id_type=MESH)

    @pl.when(has_next)
    def _():
        down(me + 1).start()

    @pl.when(has_prev)
    def _():
        up(me - 1).start()

    @pl.when(me == 0)
    def _():
        from_prev[...] = jnp.zeros(from_prev.shape, from_prev.dtype)

    @pl.when(me == n - 1)
    def _():
        from_next[...] = jnp.zeros(from_next.shape, from_next.dtype)

    @pl.when(has_prev)
    def _():
        down(me - 1).wait_recv()
        up(me - 1).wait_send()

    @pl.when(has_next)
    def _():
        up(me + 1).wait_recv()
        down(me + 1).wait_send()


def halo(down, up, collective_id):
    n = lax.axis_size("rows")
    spec = pl.BlockSpec(memory_space=pltpu.VMEM)
    shape = jax.ShapeDtypeStruct(down.shape, down.dtype)
    return pl.pallas_call(
        functools.partial(halo_kernel, n),
        out_shape=(shape, shape),
        in_specs=[spec, spec],
        out_specs=(spec, spec),
        scratch_shapes=[pltpu.SemaphoreType.DMA((4,))],
        compiler_params=pltpu.CompilerParams(collective_id=collective_id, has_side_effects=True),
    )(down, up)


def exchange(x, axis, mode, collective_id, out_dtype=None):
    n = lax.axis_size(axis)
    out_dtype = out_dtype or x.dtype
    sems = [pltpu.SemaphoreType.DMA((n,)), pltpu.SemaphoreType.DMA((n,))]
    if mode == "ag":
        out_shape = (n,) + x.shape
        scratch = sems
    elif mode == "rs":
        out_shape = x.shape[1:]
        scratch = [pltpu.VMEM(x.shape, x.dtype)] + sems
    else:
        out_shape = x.shape
        scratch = [pltpu.VMEM(x.shape, x.dtype)] + sems + sems
    return pl.pallas_call(
        functools.partial(exchange_kernel, axis, n, mode),
        out_shape=jax.ShapeDtypeStruct(out_shape, out_dtype),
        in_specs=[pl.BlockSpec(memory_space=pltpu.VMEM)],
        out_specs=pl.BlockSpec(memory_space=pltpu.VMEM),
        scratch_shapes=scratch,
        compiler_params=pltpu.CompilerParams(collective_id=collective_id, has_side_effects=True),
    )(x)


def shift_cols(value, offset):
    if offset == 0:
        return value
    pad = [(0, 0)] * (value.ndim - 1)
    if offset > 0:
        return jnp.pad(value[..., offset:], pad + [(0, offset)])
    return jnp.pad(value[..., :offset], pad + [(-offset, 0)])


def conv_row(weight, row):
    o = weight.shape[0]
    flat = weight.reshape(o, 9, weight.shape[3])
    parts = jnp.einsum("oki,iw->kow", flat, row, preferred_element_type=jnp.float32)
    return [sum(shift_cols(parts[a * 3 + b], b - 1) for b in range(3)) for a in range(3)]


def conv_forward(weight, row, collective_id):
    p0, p1, p2 = conv_row(weight, row)
    prev_p0, next_p2 = halo(p0, p2, collective_id)
    return p1 + prev_p0 + next_p2


def grad_rows(grad, collective_id):
    prev_g, next_g = halo(grad, grad, collective_id)
    return jnp.stack([next_g, grad, prev_g])


def weight_terms(rows3, full_row):
    cols = []
    for b in range(3):
        moved = shift_cols(rows3, 1 - b)
        cols.append(jnp.einsum("aow,iw->oai", moved, full_row, preferred_element_type=jnp.float32))
    return jnp.stack(cols, axis=2)


def hidden_terms(weight, rows3):
    total = None
    for b in range(3):
        part = jnp.einsum("oai,aow->iw", weight[:, :, b, :], rows3, preferred_element_type=jnp.float32)
        part = shift_cols(part, 1 - b)
        total = part if total is None else total + part
    return total


def per_device(features, first_weight, second_weight, out_grad):
    feat = features[:, 0, :]
    og = out_grad[:, 0, :]
    n_filt = lax.axis_size("filt")
    x_row = exchange(feat, "filt", "ag", 1).reshape(-1, feat.shape[1])
    pre_first = conv_forward(first_weight, x_row, 4)
    hidden = jnp.maximum(pre_first, 0.0).astype(jnp.bfloat16)
    h_row = exchange(hidden, "filt", "ag", 2).reshape(-1, hidden.shape[1])
    pre_second = conv_forward(second_weight, h_row, 5) + feat.astype(jnp.float32)
    block_out = jnp.maximum(pre_second, 0.0).astype(jnp.bfloat16)
    grad_second = jnp.where(pre_second > 0, og.astype(jnp.float32), 0.0).astype(jnp.bfloat16)
    gs3 = grad_rows(grad_second, 6)
    terms = hidden_terms(second_weight, gs3)
    hidden_grad = exchange(
        terms.astype(jnp.bfloat16).reshape(n_filt, -1, terms.shape[1]), "filt", "rs", 3, jnp.float32
    )
    grad_first = jnp.where(pre_first > 0, hidden_grad, 0.0).astype(jnp.bfloat16)
    gf3 = grad_rows(grad_first, 7)
    second_local = weight_terms(gs3, h_row)
    first_local = weight_terms(gf3, x_row)
    both = jnp.stack([first_local, second_local])
    n_rows = lax.axis_size("rows")
    summed = row_sum(both.astype(jnp.bfloat16).reshape(n_rows, -1, 128), 0)
    first_grad, second_grad = summed.astype(jnp.float32).reshape(both.shape)
    return (block_out[:, None, :], first_grad, second_grad)


def solution(mesh):
    in_specs = (
        P("filt", "rows", None),
        P("filt", None, None, None),
        P("filt", None, None, None),
        P("filt", "rows", None),
    )
    out_specs = (P("filt", "rows", None), P("filt", None, None, None), P("filt", None, None, None))
    return jax.shard_map(
        per_device, mesh=mesh, in_specs=in_specs, out_specs=out_specs, check_vma=False
    )
```

```python
import functools

import jax
import jax.numpy as jnp
from jax import lax
from jax.experimental import pallas as pl
from jax.experimental.pallas import tpu as pltpu
from jax.sharding import PartitionSpec as P

MESH = pl.DeviceIdType.MESH


def peer_id(axis, j):
    if axis == "rows":
        return (j, lax.axis_index("filt"))
    return (lax.axis_index("rows"), j)


def exchange_kernel(axis, n, mode, *refs):
    me = lax.axis_index(axis)

    def each_peer(body):
        def step(k, carry):
            body(lax.rem(me + k, n), lax.rem(me + n - k, n))
            return carry

        lax.fori_loop(1, n, step, 0)

    barrier = pltpu.get_barrier_semaphore()

    def greet(j, s):
        pl.semaphore_signal(barrier, 1, device_id=peer_id(axis, j), device_id_type=MESH)

    each_peer(greet)
    pl.semaphore_wait(barrier, n - 1)

    def gather(src, out_ref, send, recv):
        def copy(j, s):
            return pltpu.make_async_remote_copy(
                src, out_ref.at[me], send.at[j], recv.at[me], device_id=peer_id(axis, j), device_id_type=MESH
            )

        def incoming(j, s):
            return pltpu.make_async_remote_copy(
                src, out_ref.at[s], send.at[s], recv.at[s], device_id=peer_id(axis, s), device_id_type=MESH
            )

        each_peer(lambda j, s: copy(j, s).start())
        return copy, incoming

    def reduce(x_ref, buf, send, recv):
        def copy(j, s):
            return pltpu.make_async_remote_copy(
                x_ref.at[j], buf.at[me], send.at[j], recv.at[me], device_id=peer_id(axis, j), device_id_type=MESH
            )

        def incoming(j, s):
            return pltpu.make_async_remote_copy(
                x_ref.at[s], buf.at[s], send.at[s], recv.at[s], device_id=peer_id(axis, s), device_id_type=MESH
            )

        each_peer(lambda j, s: copy(j, s).start())
        each_peer(lambda j, s: incoming(j, s).wait_recv())
        acc = x_ref[me].astype(jnp.float32)

        def add(k, acc):
            return acc + buf[lax.rem(me + k, n)].astype(jnp.float32)

        acc = lax.fori_loop(1, n, add, acc)
        each_peer(lambda j, s: copy(j, s).wait_send())
        return acc

    if mode == "ag":
        x_ref, out_ref, send, recv = refs
        copy, incoming = gather(x_ref, out_ref, send, recv)
        out_ref[me] = x_ref[...]
        each_peer(lambda j, s: incoming(j, s).wait_recv())
        each_peer(lambda j, s: copy(j, s).wait_send())
    elif mode == "rs":
        x_ref, out_ref, buf, send, recv = refs
        out_ref[...] = reduce(x_ref, buf, send, recv).astype(out_ref.dtype)
    else:
        x_ref, out_ref, buf, send, recv, send2, recv2 = refs
        out_ref[me] = reduce(x_ref, buf, send, recv).astype(out_ref.dtype)
        copy, incoming = gather(out_ref.at[me], out_ref, send2, recv2)
        each_peer(lambda j, s: incoming(j, s).wait_recv())
        each_peer(lambda j, s: copy(j, s).wait_send())


def row_sum_kernel(n, x_ref, out_ref, half_buf, half_b, part_buf, sems):
    zn = n // 2
    me = lax.axis_index("rows")
    my_y, my_z = me // zn, lax.rem(me, zn)
    other = lax.rem(me + zn, n)
    mine, theirs = my_y * zn, (1 - my_y) * zn

    def dev(j):
        return (j, lax.axis_index("filt"))

    def each_z(body):
        def step(k, carry):
            body(lax.rem(my_z + k, zn), lax.rem(my_z + zn - k, zn))
            return carry

        lax.fori_loop(1, zn, step, 0)

    barrier = pltpu.get_barrier_semaphore()
    pl.semaphore_signal(barrier, 1, device_id=dev(other), device_id_type=MESH)
    each_z(lambda j, s: pl.semaphore_signal(barrier, 1, device_id=dev(mine + j), device_id_type=MESH))
    pl.semaphore_wait(barrier, zn)

    def rcopy(src, dst, send, recv, j):
        return pltpu.make_async_remote_copy(src, dst, send, recv, device_id=dev(j), device_id_type=MESH)

    swap = rcopy(x_ref.at[pl.ds(theirs, zn)], half_buf, sems.at[0, 0], sems.at[0, 1], other)
    swap.start()
    swap.wait_recv()

    def add_half(t, carry):
        half_b[t] = (x_ref[mine + t].astype(jnp.float32) + half_buf[t].astype(jnp.float32)).astype(half_b.dtype)
        return carry

    lax.fori_loop(0, zn, add_half, 0)
    swap.wait_send()

    def part_out(j, s):
        return rcopy(half_b.at[j], part_buf.at[my_z], sems.at[1, j], sems.at[2, my_z], mine + j)

    def part_in(j, s):
        return rcopy(half_b.at[s], part_buf.at[s], sems.at[1, s], sems.at[2, s], mine + s)

    each_z(lambda j, s: part_out(j, s).start())
    each_z(lambda j, s: part_in(j, s).wait_recv())
    acc = (x_ref[me].astype(jnp.float32) + half_buf[my_z].astype(jnp.float32))

    def add_part(k, acc):
        return acc + part_buf[lax.rem(my_z + k, zn)].astype(jnp.float32)

    acc = lax.fori_loop(1, zn, add_part, acc)
    out_ref[me] = acc.astype(out_ref.dtype)
    each_z(lambda j, s: part_out(j, s).wait_send())

    def sum_out(j, s):
        return rcopy(out_ref.at[me], out_ref.at[me], sems.at[3, j], sems.at[4, my_z], mine + j)

    def sum_in(j, s):
        return rcopy(out_ref.at[mine + s], out_ref.at[mine + s], sems.at[3, s], sems.at[4, s], mine + s)

    each_z(lambda j, s: sum_out(j, s).start())
    each_z(lambda j, s: sum_in(j, s).wait_recv())
    each_z(lambda j, s: sum_out(j, s).wait_send())
    back = rcopy(out_ref.at[pl.ds(mine, zn)], out_ref.at[pl.ds(mine, zn)], sems.at[5, 0], sems.at[5, 1], other)
    back.start()
    back.wait_recv()
    back.wait_send()


def row_sum(x, collective_id):
    n = x.shape[0]
    zn = n // 2
    blk = x.shape[1:]
    return pl.pallas_call(
        functools.partial(row_sum_kernel, n),
        out_shape=jax.ShapeDtypeStruct(x.shape, x.dtype),
        in_specs=[pl.BlockSpec(memory_space=pltpu.VMEM)],
        out_specs=pl.BlockSpec(memory_space=pltpu.VMEM),
        scratch_shapes=[
            pltpu.VMEM((zn,) + blk, x.dtype),
            pltpu.VMEM((zn,) + blk, x.dtype),
            pltpu.VMEM((zn,) + blk, x.dtype),
            pltpu.SemaphoreType.DMA((6, zn)),
        ],
        compiler_params=pltpu.CompilerParams(collective_id=collective_id, has_side_effects=True),
    )(x)


def row_dev(j):
    return (j, lax.axis_index("filt"))


def filt_dev(j):
    return (lax.axis_index("rows"), j)


def rcopy(src, dst, send, recv, dev):
    return pltpu.make_async_remote_copy(src, dst, send, recv, device_id=dev, device_id_type=MESH)


def each_filt_peer(body):
    nf = lax.axis_size("filt")
    me = lax.axis_index("filt")

    def step(k, carry):
        body(lax.rem(me + k, nf), lax.rem(me + nf - k, nf))
        return carry

    lax.fori_loop(1, nf, step, 0)


def enter(with_filt):
    nr = lax.axis_size("rows")
    me = lax.axis_index("rows")
    barrier = pltpu.get_barrier_semaphore()

    @pl.when(me > 0)
    def _():
        pl.semaphore_signal(barrier, 1, device_id=row_dev(me - 1), device_id_type=MESH)

    @pl.when(me < nr - 1)
    def _():
        pl.semaphore_signal(barrier, 1, device_id=row_dev(me + 1), device_id_type=MESH)

    count = (me + nr - 1) // nr + (2 * nr - 2 - me) // nr
    if with_filt:
        each_filt_peer(lambda j, s: pl.semaphore_signal(barrier, 1, device_id=filt_dev(j), device_id_type=MESH))
        count = count + lax.axis_size("filt") - 1
    pl.semaphore_wait(barrier, count)


class Halo:
    def __init__(self, down_src, up_src, from_prev, from_next, sems):
        self.nr = lax.axis_size("rows")
        self.me = lax.axis_index("rows")
        self.down = lambda j: rcopy(down_src, from_prev, sems.at[0], sems.at[1], row_dev(j))
        self.up = lambda j: rcopy(up_src, from_next, sems.at[2], sems.at[3], row_dev(j))
        me, nr = self.me, self.nr

        @pl.when(me < nr - 1)
        def _():
            self.down(me + 1).start()

        @pl.when(me > 0)
        def _():
            self.up(me - 1).start()

        @pl.when(me == 0)
        def _():
            from_prev[...] = jnp.zeros(from_prev.shape, from_prev.dtype)

        @pl.when(me == nr - 1)
        def _():
            from_next[...] = jnp.zeros(from_next.shape, from_next.dtype)

    def arrived(self):
        me, nr = self.me, self.nr

        @pl.when(me > 0)
        def _():
            self.down(me - 1).wait_recv()

        @pl.when(me < nr - 1)
        def _():
            self.up(me + 1).wait_recv()

    def sent(self):
        me, nr = self.me, self.nr

        @pl.when(me > 0)
        def _():
            self.up(me - 1).wait_send()

        @pl.when(me < nr - 1)
        def _():
            self.down(me + 1).wait_send()


def hidden_kernel(p0, p2, p1, pre_ref, h_ref, from_prev, from_next, hsems, fsend, frecv):
    mf = lax.axis_index("filt")
    enter(True)
    halo = Halo(p0, p2, from_prev, from_next, hsems)
    halo.arrived()
    pre = p1[...] + from_prev[...] + from_next[...]
    pre_ref[...] = pre
    h_ref[mf] = jnp.maximum(pre, 0.0).astype(h_ref.dtype)

    def out(j, s):
        return rcopy(h_ref.at[mf], h_ref.at[mf], fsend.at[j], frecv.at[mf], filt_dev(j))

    def inc(j, s):
        return rcopy(h_ref.at[s], h_ref.at[s], fsend.at[s], frecv.at[s], filt_dev(s))

    each_filt_peer(lambda j, s: out(j, s).start())
    each_filt_peer(lambda j, s: inc(j, s).wait_recv())
    each_filt_peer(lambda j, s: out(j, s).wait_send())
    halo.sent()


def output_kernel(p0, p2, p1, feat, og, out_ref, gs_ref, gprev, gnext, from_prev, from_next, sems1, sems2):
    enter(False)
    halo = Halo(p0, p2, from_prev, from_next, sems1)
    halo.arrived()
    pre = p1[...] + from_prev[...] + from_next[...] + feat[...].astype(jnp.float32)
    out_ref[...] = jnp.maximum(pre, 0.0).astype(out_ref.dtype)
    gs_ref[...] = jnp.where(pre > 0, og[...].astype(jnp.float32), 0.0).astype(gs_ref.dtype)
    halo2 = Halo(gs_ref, gs_ref, gprev, gnext, sems2)
    halo2.arrived()
    halo.sent()
    halo2.sent()


def first_grad_kernel(terms, pre_first, gf_ref, gprev, gnext, buf, fsend, frecv, hsems):
    nf = lax.axis_size("filt")
    mf = lax.axis_index("filt")
    enter(True)

    def out(j, s):
        return rcopy(terms.at[j], buf.at[mf], fsend.at[j], frecv.at[mf], filt_dev(j))

    def inc(j, s):
        return rcopy(terms.at[s], buf.at[s], fsend.at[s], frecv.at[s], filt_dev(s))

    each_filt_peer(lambda j, s: out(j, s).start())
    each_filt_peer(lambda j, s: inc(j, s).wait_recv())
    acc = terms[mf].astype(jnp.float32)

    def add(k, acc):
        return acc + buf[lax.rem(mf + k, nf)].astype(jnp.float32)

    acc = lax.fori_loop(1, nf, add, acc)
    gf_ref[...] = jnp.where(pre_first[...] > 0, acc, 0.0).astype(gf_ref.dtype)
    halo = Halo(gf_ref, gf_ref, gprev, gnext, hsems)
    halo.arrived()
    each_filt_peer(lambda j, s: out(j, s).wait_send())
    halo.sent()


def call(kernel, args, outs, scratch, collective_id):
    spec = pl.BlockSpec(memory_space=pltpu.VMEM)
    return pl.pallas_call(
        kernel,
        out_shape=tuple(jax.ShapeDtypeStruct(shape, dtype) for shape, dtype in outs),
        in_specs=[spec] * len(args),
        out_specs=tuple(spec for _ in outs),
        scratch_shapes=scratch,
        compiler_params=pltpu.CompilerParams(collective_id=collective_id, has_side_effects=True),
    )(*args)


def exchange(x, axis, mode, collective_id, out_dtype=None):
    n = lax.axis_size(axis)
    out_dtype = out_dtype or x.dtype
    sems = [pltpu.SemaphoreType.DMA((n,)), pltpu.SemaphoreType.DMA((n,))]
    if mode == "ag":
        out_shape = (n,) + x.shape
        scratch = sems
    elif mode == "rs":
        out_shape = x.shape[1:]
        scratch = [pltpu.VMEM(x.shape, x.dtype)] + sems
    else:
        out_shape = x.shape
        scratch = [pltpu.VMEM(x.shape, x.dtype)] + sems + sems
    return pl.pallas_call(
        functools.partial(exchange_kernel, axis, n, mode),
        out_shape=jax.ShapeDtypeStruct(out_shape, out_dtype),
        in_specs=[pl.BlockSpec(memory_space=pltpu.VMEM)],
        out_specs=pl.BlockSpec(memory_space=pltpu.VMEM),
        scratch_shapes=scratch,
        compiler_params=pltpu.CompilerParams(collective_id=collective_id, has_side_effects=True),
    )(x)


def shift_cols(value, offset):
    if offset == 0:
        return value
    pad = [(0, 0)] * (value.ndim - 1)
    if offset > 0:
        return jnp.pad(value[..., offset:], pad + [(0, offset)])
    return jnp.pad(value[..., :offset], pad + [(-offset, 0)])


def conv_row(weight, row):
    o = weight.shape[0]
    flat = weight.reshape(o, 9, weight.shape[3])
    parts = jnp.einsum("oki,iw->kow", flat, row, preferred_element_type=jnp.float32)
    return [sum(shift_cols(parts[a * 3 + b], b - 1) for b in range(3)) for a in range(3)]


def weight_terms(rows3, full_row):
    cols = []
    for b in range(3):
        moved = shift_cols(rows3, 1 - b)
        cols.append(jnp.einsum("aow,iw->oai", moved, full_row, preferred_element_type=jnp.float32))
    return jnp.stack(cols, axis=2)


def hidden_terms(weight, rows3):
    total = None
    for b in range(3):
        part = jnp.einsum("oai,aow->iw", weight[:, :, b, :], rows3, preferred_element_type=jnp.float32)
        part = shift_cols(part, 1 - b)
        total = part if total is None else total + part
    return total


def per_device(features, first_weight, second_weight, out_grad):
    feat = features[:, 0, :]
    og = out_grad[:, 0, :]
    n_filt = lax.axis_size("filt")
    blk = feat.shape
    f32, bf16 = jnp.float32, jnp.bfloat16
    x_row = exchange(feat, "filt", "ag", 1).reshape(-1, blk[1])
    p0, p1, p2 = conv_row(first_weight, x_row)
    pre_first, h_all = call(
        hidden_kernel,
        (p0, p2, p1),
        [(blk, f32), ((n_filt,) + blk, bf16)],
        [pltpu.VMEM(blk, f32), pltpu.VMEM(blk, f32), pltpu.SemaphoreType.DMA((4,)),
         pltpu.SemaphoreType.DMA((n_filt,)), pltpu.SemaphoreType.DMA((n_filt,))],
        2,
    )
    h_row = h_all.reshape(-1, blk[1])
    q0, q1, q2 = conv_row(second_weight, h_row)
    block_out, grad_second, gs_prev, gs_next = call(
        output_kernel,
        (q0, q2, q1, feat, og),
        [(blk, bf16)] * 4,
        [pltpu.VMEM(blk, f32), pltpu.VMEM(blk, f32), pltpu.SemaphoreType.DMA((4,)), pltpu.SemaphoreType.DMA((4,))],
        3,
    )
    gs3 = jnp.stack([gs_next, grad_second, gs_prev])
    terms = hidden_terms(second_weight, gs3).astype(bf16).reshape((n_filt,) + blk)
    grad_first, gf_prev, gf_next = call(
        first_grad_kernel,
        (terms, pre_first),
        [(blk, bf16)] * 3,
        [pltpu.VMEM((n_filt,) + blk, bf16), pltpu.SemaphoreType.DMA((n_filt,)),
         pltpu.SemaphoreType.DMA((n_filt,)), pltpu.SemaphoreType.DMA((4,))],
        4,
    )
    gf3 = jnp.stack([gf_next, grad_first, gf_prev])
    second_local = weight_terms(gs3, h_row)
    first_local = weight_terms(gf3, x_row)
    both = jnp.stack([first_local, second_local])
    n_rows = lax.axis_size("rows")
    summed = row_sum(both.astype(bf16).reshape(n_rows, -1, 128), 0)
    first_grad, second_grad = summed.astype(f32).reshape(both.shape)
    return (block_out[:, None, :], first_grad, second_grad)


def solution(mesh):
    in_specs = (
        P("filt", "rows", None),
        P("filt", None, None, None),
        P("filt", None, None, None),
        P("filt", "rows", None),
    )
    out_specs = (P("filt", "rows", None), P("filt", None, None, None), P("filt", None, None, None))
    return jax.shard_map(
        per_device, mesh=mesh, in_specs=in_specs, out_specs=out_specs, check_vma=False
    )
```

```python
import functools

import jax
import jax.numpy as jnp
from jax import lax
from jax.experimental import pallas as pl
from jax.experimental.pallas import tpu as pltpu
from jax.sharding import PartitionSpec as P

MESH = pl.DeviceIdType.MESH


def peer_id(axis, j):
    if axis == "rows":
        return (j, lax.axis_index("filt"))
    return (lax.axis_index("rows"), j)


def exchange_kernel(axis, n, mode, *refs):
    me = lax.axis_index(axis)

    def each_peer(body):
        def step(k, carry):
            body(lax.rem(me + k, n), lax.rem(me + n - k, n))
            return carry

        lax.fori_loop(1, n, step, 0)

    barrier = pltpu.get_barrier_semaphore()

    def greet(j, s):
        pl.semaphore_signal(barrier, 1, device_id=peer_id(axis, j), device_id_type=MESH)

    each_peer(greet)
    pl.semaphore_wait(barrier, n - 1)

    def gather(src, out_ref, send, recv):
        def copy(j, s):
            return pltpu.make_async_remote_copy(
                src, out_ref.at[me], send.at[j], recv.at[me], device_id=peer_id(axis, j), device_id_type=MESH
            )

        def incoming(j, s):
            return pltpu.make_async_remote_copy(
                src, out_ref.at[s], send.at[s], recv.at[s], device_id=peer_id(axis, s), device_id_type=MESH
            )

        each_peer(lambda j, s: copy(j, s).start())
        return copy, incoming

    def reduce(x_ref, buf, send, recv):
        def copy(j, s):
            return pltpu.make_async_remote_copy(
                x_ref.at[j], buf.at[me], send.at[j], recv.at[me], device_id=peer_id(axis, j), device_id_type=MESH
            )

        def incoming(j, s):
            return pltpu.make_async_remote_copy(
                x_ref.at[s], buf.at[s], send.at[s], recv.at[s], device_id=peer_id(axis, s), device_id_type=MESH
            )

        each_peer(lambda j, s: copy(j, s).start())
        each_peer(lambda j, s: incoming(j, s).wait_recv())
        acc = x_ref[me].astype(jnp.float32)

        def add(k, acc):
            return acc + buf[lax.rem(me + k, n)].astype(jnp.float32)

        acc = lax.fori_loop(1, n, add, acc)
        each_peer(lambda j, s: copy(j, s).wait_send())
        return acc

    if mode == "ag":
        x_ref, out_ref, send, recv = refs
        copy, incoming = gather(x_ref, out_ref, send, recv)
        out_ref[me] = x_ref[...]
        each_peer(lambda j, s: incoming(j, s).wait_recv())
        each_peer(lambda j, s: copy(j, s).wait_send())
    elif mode == "rs":
        x_ref, out_ref, buf, send, recv = refs
        out_ref[...] = reduce(x_ref, buf, send, recv).astype(out_ref.dtype)
    else:
        x_ref, out_ref, buf, send, recv, send2, recv2 = refs
        out_ref[me] = reduce(x_ref, buf, send, recv).astype(out_ref.dtype)
        copy, incoming = gather(out_ref.at[me], out_ref, send2, recv2)
        each_peer(lambda j, s: incoming(j, s).wait_recv())
        each_peer(lambda j, s: copy(j, s).wait_send())


def row_sum_peers(n, signal):
    zn = n // 2
    me = lax.axis_index("rows")
    my_z = lax.rem(me, zn)
    mine = (me // zn) * zn
    signal(lax.rem(me + zn, n))

    def step(k, carry):
        signal(mine + lax.rem(my_z + k, zn))
        return carry

    lax.fori_loop(1, zn, step, 0)
    return zn


def row_sum_kernel(n, x_ref, out_ref, half_buf, half_b, part_buf, sems):
    barrier = pltpu.get_barrier_semaphore()
    count = row_sum_peers(n, lambda j: pl.semaphore_signal(barrier, 1, device_id=(j, lax.axis_index("filt")), device_id_type=MESH))
    pl.semaphore_wait(barrier, count)
    row_sum_body(n, x_ref, out_ref, half_buf, half_b, part_buf, sems)


def row_sum_body(n, x_ref, out_ref, half_buf, half_b, part_buf, sems, between=None):
    zn = n // 2
    me = lax.axis_index("rows")
    my_y, my_z = me // zn, lax.rem(me, zn)
    other = lax.rem(me + zn, n)
    mine, theirs = my_y * zn, (1 - my_y) * zn

    def dev(j):
        return (j, lax.axis_index("filt"))

    def each_z(body):
        def step(k, carry):
            body(lax.rem(my_z + k, zn), lax.rem(my_z + zn - k, zn))
            return carry

        lax.fori_loop(1, zn, step, 0)

    def rcopy(src, dst, send, recv, j):
        return pltpu.make_async_remote_copy(src, dst, send, recv, device_id=dev(j), device_id_type=MESH)

    swap = rcopy(x_ref.at[pl.ds(theirs, zn)], half_buf, sems.at[0, 0], sems.at[0, 1], other)
    swap.start()
    if between is not None:
        between()
    swap.wait_recv()

    def add_half(t, carry):
        half_b[t] = (x_ref[mine + t].astype(jnp.float32) + half_buf[t].astype(jnp.float32)).astype(half_b.dtype)
        return carry

    lax.fori_loop(0, zn, add_half, 0)
    swap.wait_send()

    def part_out(j, s):
        return rcopy(half_b.at[j], part_buf.at[my_z], sems.at[1, j], sems.at[2, my_z], mine + j)

    def part_in(j, s):
        return rcopy(half_b.at[s], part_buf.at[s], sems.at[1, s], sems.at[2, s], mine + s)

    each_z(lambda j, s: part_out(j, s).start())
    each_z(lambda j, s: part_in(j, s).wait_recv())
    acc = (x_ref[me].astype(jnp.float32) + half_buf[my_z].astype(jnp.float32))

    def add_part(k, acc):
        return acc + part_buf[lax.rem(my_z + k, zn)].astype(jnp.float32)

    acc = lax.fori_loop(1, zn, add_part, acc)
    out_ref[me] = acc.astype(out_ref.dtype)
    each_z(lambda j, s: part_out(j, s).wait_send())

    def sum_out(j, s):
        return rcopy(out_ref.at[me], out_ref.at[me], sems.at[3, j], sems.at[4, my_z], mine + j)

    def sum_in(j, s):
        return rcopy(out_ref.at[mine + s], out_ref.at[mine + s], sems.at[3, s], sems.at[4, s], mine + s)

    each_z(lambda j, s: sum_out(j, s).start())
    each_z(lambda j, s: sum_in(j, s).wait_recv())
    each_z(lambda j, s: sum_out(j, s).wait_send())
    back = rcopy(out_ref.at[pl.ds(mine, zn)], out_ref.at[pl.ds(mine, zn)], sems.at[5, 0], sems.at[5, 1], other)
    back.start()
    back.wait_recv()
    back.wait_send()


def row_sum(x, collective_id):
    n = x.shape[0]
    zn = n // 2
    blk = x.shape[1:]
    return pl.pallas_call(
        functools.partial(row_sum_kernel, n),
        out_shape=jax.ShapeDtypeStruct(x.shape, x.dtype),
        in_specs=[pl.BlockSpec(memory_space=pltpu.VMEM)],
        out_specs=pl.BlockSpec(memory_space=pltpu.VMEM),
        scratch_shapes=[
            pltpu.VMEM((zn,) + blk, x.dtype),
            pltpu.VMEM((zn,) + blk, x.dtype),
            pltpu.VMEM((zn,) + blk, x.dtype),
            pltpu.SemaphoreType.DMA((6, zn)),
        ],
        compiler_params=pltpu.CompilerParams(collective_id=collective_id, has_side_effects=True),
    )(x)


def row_dev(j):
    return (j, lax.axis_index("filt"))


def filt_dev(j):
    return (lax.axis_index("rows"), j)


def rcopy(src, dst, send, recv, dev):
    return pltpu.make_async_remote_copy(src, dst, send, recv, device_id=dev, device_id_type=MESH)


def each_filt_peer(body):
    nf = lax.axis_size("filt")
    me = lax.axis_index("filt")

    def step(k, carry):
        body(lax.rem(me + k, nf), lax.rem(me + nf - k, nf))
        return carry

    lax.fori_loop(1, nf, step, 0)


def enter(with_filt, with_row_sum=False):
    nr = lax.axis_size("rows")
    me = lax.axis_index("rows")
    barrier = pltpu.get_barrier_semaphore()

    @pl.when(me > 0)
    def _():
        pl.semaphore_signal(barrier, 1, device_id=row_dev(me - 1), device_id_type=MESH)

    @pl.when(me < nr - 1)
    def _():
        pl.semaphore_signal(barrier, 1, device_id=row_dev(me + 1), device_id_type=MESH)

    count = (me + nr - 1) // nr + (2 * nr - 2 - me) // nr
    if with_filt:
        each_filt_peer(lambda j, s: pl.semaphore_signal(barrier, 1, device_id=filt_dev(j), device_id_type=MESH))
        count = count + lax.axis_size("filt") - 1
    if with_row_sum:
        count = count + row_sum_peers(
            nr, lambda j: pl.semaphore_signal(barrier, 1, device_id=row_dev(j), device_id_type=MESH)
        )
    pl.semaphore_wait(barrier, count)


class Halo:
    def __init__(self, down_src, up_src, from_prev, from_next, sems):
        self.nr = lax.axis_size("rows")
        self.me = lax.axis_index("rows")
        self.down = lambda j: rcopy(down_src, from_prev, sems.at[0], sems.at[1], row_dev(j))
        self.up = lambda j: rcopy(up_src, from_next, sems.at[2], sems.at[3], row_dev(j))
        me, nr = self.me, self.nr

        @pl.when(me < nr - 1)
        def _():
            self.down(me + 1).start()

        @pl.when(me > 0)
        def _():
            self.up(me - 1).start()

        @pl.when(me == 0)
        def _():
            from_prev[...] = jnp.zeros(from_prev.shape, from_prev.dtype)

        @pl.when(me == nr - 1)
        def _():
            from_next[...] = jnp.zeros(from_next.shape, from_next.dtype)

    def arrived(self):
        me, nr = self.me, self.nr

        @pl.when(me > 0)
        def _():
            self.down(me - 1).wait_recv()

        @pl.when(me < nr - 1)
        def _():
            self.up(me + 1).wait_recv()

    def sent(self):
        me, nr = self.me, self.nr

        @pl.when(me > 0)
        def _():
            self.up(me - 1).wait_send()

        @pl.when(me < nr - 1)
        def _():
            self.down(me + 1).wait_send()


def hidden_kernel(p0, p2, p1, pre_ref, h_ref, from_prev, from_next, hsems, fsend, frecv):
    mf = lax.axis_index("filt")
    enter(True)
    halo = Halo(p0, p2, from_prev, from_next, hsems)
    halo.arrived()
    pre = p1[...] + from_prev[...] + from_next[...]
    pre_ref[...] = pre
    h_ref[mf] = jnp.maximum(pre, 0.0).astype(h_ref.dtype)

    def out(j, s):
        return rcopy(h_ref.at[mf], h_ref.at[mf], fsend.at[j], frecv.at[mf], filt_dev(j))

    def inc(j, s):
        return rcopy(h_ref.at[s], h_ref.at[s], fsend.at[s], frecv.at[s], filt_dev(s))

    each_filt_peer(lambda j, s: out(j, s).start())
    each_filt_peer(lambda j, s: inc(j, s).wait_recv())
    each_filt_peer(lambda j, s: out(j, s).wait_send())
    halo.sent()


def output_kernel(p0, p2, p1, feat, og, out_ref, gs_ref, gprev, gnext, from_prev, from_next, sems1, sems2):
    enter(False)
    halo = Halo(p0, p2, from_prev, from_next, sems1)
    halo.arrived()
    pre = p1[...] + from_prev[...] + from_next[...] + feat[...].astype(jnp.float32)
    out_ref[...] = jnp.maximum(pre, 0.0).astype(out_ref.dtype)
    gs_ref[...] = jnp.where(pre > 0, og[...].astype(jnp.float32), 0.0).astype(gs_ref.dtype)
    halo2 = Halo(gs_ref, gs_ref, gprev, gnext, sems2)
    halo2.arrived()
    halo.sent()
    halo2.sent()


def first_grad_kernel(terms, pre_first, xs, gf_ref, gprev, gnext, s_out, buf, fsend, frecv, hsems, *row_sum_refs):
    nf = lax.axis_size("filt")
    mf = lax.axis_index("filt")
    enter(True, True)

    def out(j, s):
        return rcopy(terms.at[j], buf.at[mf], fsend.at[j], frecv.at[mf], filt_dev(j))

    def inc(j, s):
        return rcopy(terms.at[s], buf.at[s], fsend.at[s], frecv.at[s], filt_dev(s))

    each_filt_peer(lambda j, s: out(j, s).start())
    halos = []

    def reduce_filt():
        each_filt_peer(lambda j, s: inc(j, s).wait_recv())
        acc = terms[mf].astype(jnp.float32)

        def add(k, acc):
            return acc + buf[lax.rem(mf + k, nf)].astype(jnp.float32)

        acc = lax.fori_loop(1, nf, add, acc)
        gf_ref[...] = jnp.where(pre_first[...] > 0, acc, 0.0).astype(gf_ref.dtype)
        halos.append(Halo(gf_ref, gf_ref, gprev, gnext, hsems))

    row_sum_body(lax.axis_size("rows"), xs, s_out, *row_sum_refs, between=reduce_filt)
    halo = halos[0]
    halo.arrived()
    each_filt_peer(lambda j, s: out(j, s).wait_send())
    halo.sent()


def call(kernel, args, outs, scratch, collective_id):
    spec = pl.BlockSpec(memory_space=pltpu.VMEM)
    return pl.pallas_call(
        kernel,
        out_shape=tuple(jax.ShapeDtypeStruct(shape, dtype) for shape, dtype in outs),
        in_specs=[spec] * len(args),
        out_specs=tuple(spec for _ in outs),
        scratch_shapes=scratch,
        compiler_params=pltpu.CompilerParams(collective_id=collective_id, has_side_effects=True),
    )(*args)


def exchange(x, axis, mode, collective_id, out_dtype=None):
    n = lax.axis_size(axis)
    out_dtype = out_dtype or x.dtype
    sems = [pltpu.SemaphoreType.DMA((n,)), pltpu.SemaphoreType.DMA((n,))]
    if mode == "ag":
        out_shape = (n,) + x.shape
        scratch = sems
    elif mode == "rs":
        out_shape = x.shape[1:]
        scratch = [pltpu.VMEM(x.shape, x.dtype)] + sems
    else:
        out_shape = x.shape
        scratch = [pltpu.VMEM(x.shape, x.dtype)] + sems + sems
    return pl.pallas_call(
        functools.partial(exchange_kernel, axis, n, mode),
        out_shape=jax.ShapeDtypeStruct(out_shape, out_dtype),
        in_specs=[pl.BlockSpec(memory_space=pltpu.VMEM)],
        out_specs=pl.BlockSpec(memory_space=pltpu.VMEM),
        scratch_shapes=scratch,
        compiler_params=pltpu.CompilerParams(collective_id=collective_id, has_side_effects=True),
    )(x)


def shift_cols(value, offset):
    if offset == 0:
        return value
    pad = [(0, 0)] * (value.ndim - 1)
    if offset > 0:
        return jnp.pad(value[..., offset:], pad + [(0, offset)])
    return jnp.pad(value[..., :offset], pad + [(-offset, 0)])


def conv_row(weight, row):
    o = weight.shape[0]
    flat = weight.reshape(o, 9, weight.shape[3])
    parts = jnp.einsum("oki,iw->kow", flat, row, preferred_element_type=jnp.float32)
    return [sum(shift_cols(parts[a * 3 + b], b - 1) for b in range(3)) for a in range(3)]


def weight_terms(rows3, full_row):
    cols = []
    for b in range(3):
        moved = shift_cols(rows3, 1 - b)
        cols.append(jnp.einsum("aow,iw->oai", moved, full_row, preferred_element_type=jnp.float32))
    return jnp.stack(cols, axis=2)


def hidden_terms(weight, rows3):
    total = None
    for b in range(3):
        part = jnp.einsum("oai,aow->iw", weight[:, :, b, :], rows3, preferred_element_type=jnp.float32)
        part = shift_cols(part, 1 - b)
        total = part if total is None else total + part
    return total


def per_device(features, first_weight, second_weight, out_grad):
    feat = features[:, 0, :]
    og = out_grad[:, 0, :]
    n_filt = lax.axis_size("filt")
    blk = feat.shape
    f32, bf16 = jnp.float32, jnp.bfloat16
    x_row = exchange(feat, "filt", "ag", 1).reshape(-1, blk[1])
    p0, p1, p2 = conv_row(first_weight, x_row)
    pre_first, h_all = call(
        hidden_kernel,
        (p0, p2, p1),
        [(blk, f32), ((n_filt,) + blk, bf16)],
        [pltpu.VMEM(blk, f32), pltpu.VMEM(blk, f32), pltpu.SemaphoreType.DMA((4,)),
         pltpu.SemaphoreType.DMA((n_filt,)), pltpu.SemaphoreType.DMA((n_filt,))],
        2,
    )
    h_row = h_all.reshape(-1, blk[1])
    q0, q1, q2 = conv_row(second_weight, h_row)
    block_out, grad_second, gs_prev, gs_next = call(
        output_kernel,
        (q0, q2, q1, feat, og),
        [(blk, bf16)] * 4,
        [pltpu.VMEM(blk, f32), pltpu.VMEM(blk, f32), pltpu.SemaphoreType.DMA((4,)), pltpu.SemaphoreType.DMA((4,))],
        3,
    )
    gs3 = jnp.stack([gs_next, grad_second, gs_prev])
    terms = hidden_terms(second_weight, gs3).astype(bf16).reshape((n_filt,) + blk)
    n_rows = lax.axis_size("rows")
    second_local = weight_terms(gs3, h_row)
    xs = second_local.astype(bf16).reshape(n_rows, -1, 128)
    half = (n_rows // 2,) + xs.shape[1:]
    grad_first, gf_prev, gf_next, second_sum = call(
        first_grad_kernel,
        (terms, pre_first, xs),
        [(blk, bf16)] * 3 + [(xs.shape, bf16)],
        [pltpu.VMEM((n_filt,) + blk, bf16), pltpu.SemaphoreType.DMA((n_filt,)),
         pltpu.SemaphoreType.DMA((n_filt,)), pltpu.SemaphoreType.DMA((4,)),
         pltpu.VMEM(half, bf16), pltpu.VMEM(half, bf16), pltpu.VMEM(half, bf16), pltpu.SemaphoreType.DMA((6, half[0]))],
        4,
    )
    gf3 = jnp.stack([gf_next, grad_first, gf_prev])
    first_local = weight_terms(gf3, x_row)
    first_sum = row_sum(first_local.astype(bf16).reshape(n_rows, -1, 128), 0)
    first_grad = first_sum.astype(f32).reshape(first_local.shape)
    second_grad = second_sum.astype(f32).reshape(second_local.shape)
    return (block_out[:, None, :], first_grad, second_grad)


def solution(mesh):
    in_specs = (
        P("filt", "rows", None),
        P("filt", None, None, None),
        P("filt", None, None, None),
        P("filt", "rows", None),
    )
    out_specs = (P("filt", "rows", None), P("filt", None, None, None), P("filt", None, None, None))
    return jax.shard_map(
        per_device, mesh=mesh, in_specs=in_specs, out_specs=out_specs, check_vma=False
    )
```

```python
import functools

import jax
import jax.numpy as jnp
from jax import lax
from jax.experimental import pallas as pl
from jax.experimental.pallas import tpu as pltpu
from jax.sharding import PartitionSpec as P

MESH = pl.DeviceIdType.MESH


def peer_id(axis, j):
    if axis == "rows":
        return (j, lax.axis_index("filt"))
    return (lax.axis_index("rows"), j)


def exchange_kernel(axis, n, mode, *refs):
    me = lax.axis_index(axis)

    def each_peer(body):
        def step(k, carry):
            body(lax.rem(me + k, n), lax.rem(me + n - k, n))
            return carry

        lax.fori_loop(1, n, step, 0)

    barrier = pltpu.get_barrier_semaphore()

    def greet(j, s):
        pl.semaphore_signal(barrier, 1, device_id=peer_id(axis, j), device_id_type=MESH)

    each_peer(greet)
    pl.semaphore_wait(barrier, n - 1)

    def gather(src, out_ref, send, recv):
        def copy(j, s):
            return pltpu.make_async_remote_copy(
                src, out_ref.at[me], send.at[j], recv.at[me], device_id=peer_id(axis, j), device_id_type=MESH
            )

        def incoming(j, s):
            return pltpu.make_async_remote_copy(
                src, out_ref.at[s], send.at[s], recv.at[s], device_id=peer_id(axis, s), device_id_type=MESH
            )

        each_peer(lambda j, s: copy(j, s).start())
        return copy, incoming

    def reduce(x_ref, buf, send, recv):
        def copy(j, s):
            return pltpu.make_async_remote_copy(
                x_ref.at[j], buf.at[me], send.at[j], recv.at[me], device_id=peer_id(axis, j), device_id_type=MESH
            )

        def incoming(j, s):
            return pltpu.make_async_remote_copy(
                x_ref.at[s], buf.at[s], send.at[s], recv.at[s], device_id=peer_id(axis, s), device_id_type=MESH
            )

        each_peer(lambda j, s: copy(j, s).start())
        each_peer(lambda j, s: incoming(j, s).wait_recv())
        acc = x_ref[me].astype(jnp.float32)

        def add(k, acc):
            return acc + buf[lax.rem(me + k, n)].astype(jnp.float32)

        acc = lax.fori_loop(1, n, add, acc)
        each_peer(lambda j, s: copy(j, s).wait_send())
        return acc

    if mode == "ag":
        x_ref, out_ref, send, recv = refs
        copy, incoming = gather(x_ref, out_ref, send, recv)
        out_ref[me] = x_ref[...]
        each_peer(lambda j, s: incoming(j, s).wait_recv())
        each_peer(lambda j, s: copy(j, s).wait_send())
    elif mode == "rs":
        x_ref, out_ref, buf, send, recv = refs
        out_ref[...] = reduce(x_ref, buf, send, recv).astype(out_ref.dtype)
    else:
        x_ref, out_ref, buf, send, recv, send2, recv2 = refs
        out_ref[me] = reduce(x_ref, buf, send, recv).astype(out_ref.dtype)
        copy, incoming = gather(out_ref.at[me], out_ref, send2, recv2)
        each_peer(lambda j, s: incoming(j, s).wait_recv())
        each_peer(lambda j, s: copy(j, s).wait_send())


class RowSum:
    def __init__(self, n, x_ref, out_ref, half_buf, half_b, part_buf, sems):
        self.zn = zn = n // 2
        self.me = me = lax.axis_index("rows")
        my_y, self.my_z = me // zn, lax.rem(me, zn)
        self.other = lax.rem(me + zn, n)
        self.mine, self.theirs = my_y * zn, (1 - my_y) * zn
        self.x_ref, self.out_ref, self.half_buf, self.half_b, self.part_buf, self.sems = (
            x_ref, out_ref, half_buf, half_b, part_buf, sems)

    def rcopy(self, src, dst, send, recv, j):
        return pltpu.make_async_remote_copy(
            src, dst, send, recv, device_id=(j, lax.axis_index("filt")), device_id_type=MESH
        )

    def each_z(self, body):
        zn, my_z = self.zn, self.my_z

        def step(k, carry):
            body(lax.rem(my_z + k, zn), lax.rem(my_z + zn - k, zn))
            return carry

        lax.fori_loop(1, zn, step, 0)

    def swap(self):
        return self.rcopy(self.x_ref.at[pl.ds(self.theirs, self.zn)], self.half_buf, self.sems.at[0, 0],
                          self.sems.at[0, 1], self.other)

    def part_out(self, j, s):
        return self.rcopy(self.half_b.at[j], self.part_buf.at[self.my_z], self.sems.at[1, j],
                          self.sems.at[2, self.my_z], self.mine + j)

    def part_in(self, j, s):
        return self.rcopy(self.half_b.at[s], self.part_buf.at[s], self.sems.at[1, s], self.sems.at[2, s],
                          self.mine + s)

    def sum_out(self, j, s):
        me = self.me
        return self.rcopy(self.out_ref.at[me], self.out_ref.at[me], self.sems.at[3, j], self.sems.at[4, self.my_z],
                          self.mine + j)

    def sum_in(self, j, s):
        c = self.mine + s
        return self.rcopy(self.out_ref.at[c], self.out_ref.at[c], self.sems.at[3, s], self.sems.at[4, s], c)

    def back(self):
        half = pl.ds(self.mine, self.zn)
        return self.rcopy(self.out_ref.at[half], self.out_ref.at[half], self.sems.at[5, 0], self.sems.at[5, 1],
                          self.other)

    def s1_start(self):
        self.swap().start()

    def s1_finish(self):
        self.swap().wait_recv()
        x_ref, half_buf, half_b, mine = self.x_ref, self.half_buf, self.half_b, self.mine

        def add_half(t, carry):
            half_b[t] = (x_ref[mine + t].astype(jnp.float32) + half_buf[t].astype(jnp.float32)).astype(half_b.dtype)
            return carry

        lax.fori_loop(0, self.zn, add_half, 0)
        self.swap().wait_send()

    def s2_start(self):
        self.each_z(lambda j, s: self.part_out(j, s).start())

    def s2_finish(self):
        self.each_z(lambda j, s: self.part_in(j, s).wait_recv())
        zn, my_z, part_buf = self.zn, self.my_z, self.part_buf
        acc = self.x_ref[self.me].astype(jnp.float32) + self.half_buf[my_z].astype(jnp.float32)

        def add_part(k, acc):
            return acc + part_buf[lax.rem(my_z + k, zn)].astype(jnp.float32)

        acc = lax.fori_loop(1, zn, add_part, acc)
        self.out_ref[self.me] = acc.astype(self.out_ref.dtype)
        self.each_z(lambda j, s: self.part_out(j, s).wait_send())

    def s3_start(self):
        self.each_z(lambda j, s: self.sum_out(j, s).start())

    def s3_finish(self):
        self.each_z(lambda j, s: self.sum_in(j, s).wait_recv())
        self.each_z(lambda j, s: self.sum_out(j, s).wait_send())

    def s4_start(self):
        self.back().start()

    def s4_finish(self):
        self.back().wait_recv()
        self.back().wait_send()


def row_sum_kernel(n, xa, xb, oa, ob, *scratch):
    zn = n // 2
    me = lax.axis_index("rows")
    my_z = lax.rem(me, zn)
    mine = (me // zn) * zn

    def dev(j):
        return (j, lax.axis_index("filt"))

    barrier = pltpu.get_barrier_semaphore()
    pl.semaphore_signal(barrier, 1, device_id=dev(lax.rem(me + zn, n)), device_id_type=MESH)

    def greet(k, carry):
        pl.semaphore_signal(barrier, 1, device_id=dev(mine + lax.rem(my_z + k, zn)), device_id_type=MESH)
        return carry

    lax.fori_loop(1, zn, greet, 0)
    pl.semaphore_wait(barrier, zn)
    a = RowSum(n, xa, oa, *scratch[:4])
    b = RowSum(n, xb, ob, *scratch[4:])
    a.s1_start()
    a.s1_finish()
    a.s2_start()
    b.s1_start()
    b.s1_finish()
    b.s2_start()
    a.s2_finish()
    a.s3_start()
    b.s2_finish()
    b.s3_start()
    a.s3_finish()
    a.s4_start()
    b.s3_finish()
    b.s4_start()
    a.s4_finish()
    b.s4_finish()


def row_sum(xa, xb, collective_id):
    n = xa.shape[0]
    zn = n // 2
    spec = pl.BlockSpec(memory_space=pltpu.VMEM)
    scratch = []
    for x in (xa, xb):
        blk = (zn,) + x.shape[1:]
        scratch += [pltpu.VMEM(blk, x.dtype), pltpu.VMEM(blk, x.dtype), pltpu.VMEM(blk, x.dtype),
                    pltpu.SemaphoreType.DMA((6, zn))]
    return pl.pallas_call(
        functools.partial(row_sum_kernel, n),
        out_shape=(jax.ShapeDtypeStruct(xa.shape, xa.dtype), jax.ShapeDtypeStruct(xb.shape, xb.dtype)),
        in_specs=[spec, spec],
        out_specs=(spec, spec),
        scratch_shapes=scratch,
        compiler_params=pltpu.CompilerParams(collective_id=collective_id, has_side_effects=True),
    )(xa, xb)


def row_dev(j):
    return (j, lax.axis_index("filt"))


def filt_dev(j):
    return (lax.axis_index("rows"), j)


def rcopy(src, dst, send, recv, dev):
    return pltpu.make_async_remote_copy(src, dst, send, recv, device_id=dev, device_id_type=MESH)


def each_filt_peer(body):
    nf = lax.axis_size("filt")
    me = lax.axis_index("filt")

    def step(k, carry):
        body(lax.rem(me + k, nf), lax.rem(me + nf - k, nf))
        return carry

    lax.fori_loop(1, nf, step, 0)


def enter(with_filt):
    nr = lax.axis_size("rows")
    me = lax.axis_index("rows")
    barrier = pltpu.get_barrier_semaphore()

    @pl.when(me > 0)
    def _():
        pl.semaphore_signal(barrier, 1, device_id=row_dev(me - 1), device_id_type=MESH)

    @pl.when(me < nr - 1)
    def _():
        pl.semaphore_signal(barrier, 1, device_id=row_dev(me + 1), device_id_type=MESH)

    count = (me + nr - 1) // nr + (2 * nr - 2 - me) // nr
    if with_filt:
        each_filt_peer(lambda j, s: pl.semaphore_signal(barrier, 1, device_id=filt_dev(j), device_id_type=MESH))
        count = count + lax.axis_size("filt") - 1
    pl.semaphore_wait(barrier, count)


class Halo:
    def __init__(self, down_src, up_src, from_prev, from_next, sems):
        self.nr = lax.axis_size("rows")
        self.me = lax.axis_index("rows")
        self.down = lambda j: rcopy(down_src, from_prev, sems.at[0], sems.at[1], row_dev(j))
        self.up = lambda j: rcopy(up_src, from_next, sems.at[2], sems.at[3], row_dev(j))
        me, nr = self.me, self.nr

        @pl.when(me < nr - 1)
        def _():
            self.down(me + 1).start()

        @pl.when(me > 0)
        def _():
            self.up(me - 1).start()

        @pl.when(me == 0)
        def _():
            from_prev[...] = jnp.zeros(from_prev.shape, from_prev.dtype)

        @pl.when(me == nr - 1)
        def _():
            from_next[...] = jnp.zeros(from_next.shape, from_next.dtype)

    def arrived(self):
        me, nr = self.me, self.nr

        @pl.when(me > 0)
        def _():
            self.down(me - 1).wait_recv()

        @pl.when(me < nr - 1)
        def _():
            self.up(me + 1).wait_recv()

    def sent(self):
        me, nr = self.me, self.nr

        @pl.when(me > 0)
        def _():
            self.up(me - 1).wait_send()

        @pl.when(me < nr - 1)
        def _():
            self.down(me + 1).wait_send()


def hidden_kernel(p0, p2, p1, pre_ref, h_ref, from_prev, from_next, hsems, fsend, frecv):
    mf = lax.axis_index("filt")
    enter(True)
    halo = Halo(p0, p2, from_prev, from_next, hsems)
    halo.arrived()
    pre = p1[...] + from_prev[...] + from_next[...]
    pre_ref[...] = pre
    h_ref[mf] = jnp.maximum(pre, 0.0).astype(h_ref.dtype)

    def out(j, s):
        return rcopy(h_ref.at[mf], h_ref.at[mf], fsend.at[j], frecv.at[mf], filt_dev(j))

    def inc(j, s):
        return rcopy(h_ref.at[s], h_ref.at[s], fsend.at[s], frecv.at[s], filt_dev(s))

    each_filt_peer(lambda j, s: out(j, s).start())
    each_filt_peer(lambda j, s: inc(j, s).wait_recv())
    each_filt_peer(lambda j, s: out(j, s).wait_send())
    halo.sent()


def output_kernel(p0, p2, p1, feat, og, out_ref, gs_ref, gprev, gnext, from_prev, from_next, sems1, sems2):
    enter(False)
    halo = Halo(p0, p2, from_prev, from_next, sems1)
    halo.arrived()
    pre = p1[...] + from_prev[...] + from_next[...] + feat[...].astype(jnp.float32)
    out_ref[...] = jnp.maximum(pre, 0.0).astype(out_ref.dtype)
    gs_ref[...] = jnp.where(pre > 0, og[...].astype(jnp.float32), 0.0).astype(gs_ref.dtype)
    halo2 = Halo(gs_ref, gs_ref, gprev, gnext, sems2)
    halo2.arrived()
    halo.sent()
    halo2.sent()


def first_grad_kernel(terms, pre_first, gf_ref, gprev, gnext, buf, fsend, frecv, hsems):
    nf = lax.axis_size("filt")
    mf = lax.axis_index("filt")
    enter(True)

    def out(j, s):
        return rcopy(terms.at[j], buf.at[mf], fsend.at[j], frecv.at[mf], filt_dev(j))

    def inc(j, s):
        return rcopy(terms.at[s], buf.at[s], fsend.at[s], frecv.at[s], filt_dev(s))

    each_filt_peer(lambda j, s: out(j, s).start())
    each_filt_peer(lambda j, s: inc(j, s).wait_recv())
    acc = terms[mf].astype(jnp.float32)

    def add(k, acc):
        return acc + buf[lax.rem(mf + k, nf)].astype(jnp.float32)

    acc = lax.fori_loop(1, nf, add, acc)
    gf_ref[...] = jnp.where(pre_first[...] > 0, acc, 0.0).astype(gf_ref.dtype)
    halo = Halo(gf_ref, gf_ref, gprev, gnext, hsems)
    halo.arrived()
    each_filt_peer(lambda j, s: out(j, s).wait_send())
    halo.sent()


def call(kernel, args, outs, scratch, collective_id):
    spec = pl.BlockSpec(memory_space=pltpu.VMEM)
    return pl.pallas_call(
        kernel,
        out_shape=tuple(jax.ShapeDtypeStruct(shape, dtype) for shape, dtype in outs),
        in_specs=[spec] * len(args),
        out_specs=tuple(spec for _ in outs),
        scratch_shapes=scratch,
        compiler_params=pltpu.CompilerParams(collective_id=collective_id, has_side_effects=True),
    )(*args)


def exchange(x, axis, mode, collective_id, out_dtype=None):
    n = lax.axis_size(axis)
    out_dtype = out_dtype or x.dtype
    sems = [pltpu.SemaphoreType.DMA((n,)), pltpu.SemaphoreType.DMA((n,))]
    if mode == "ag":
        out_shape = (n,) + x.shape
        scratch = sems
    elif mode == "rs":
        out_shape = x.shape[1:]
        scratch = [pltpu.VMEM(x.shape, x.dtype)] + sems
    else:
        out_shape = x.shape
        scratch = [pltpu.VMEM(x.shape, x.dtype)] + sems + sems
    return pl.pallas_call(
        functools.partial(exchange_kernel, axis, n, mode),
        out_shape=jax.ShapeDtypeStruct(out_shape, out_dtype),
        in_specs=[pl.BlockSpec(memory_space=pltpu.VMEM)],
        out_specs=pl.BlockSpec(memory_space=pltpu.VMEM),
        scratch_shapes=scratch,
        compiler_params=pltpu.CompilerParams(collective_id=collective_id, has_side_effects=True),
    )(x)


def shift_cols(value, offset):
    if offset == 0:
        return value
    pad = [(0, 0)] * (value.ndim - 1)
    if offset > 0:
        return jnp.pad(value[..., offset:], pad + [(0, offset)])
    return jnp.pad(value[..., :offset], pad + [(-offset, 0)])


def conv_row(weight, row):
    o = weight.shape[0]
    flat = weight.reshape(o, 9, weight.shape[3])
    parts = jnp.einsum("oki,iw->kow", flat, row, preferred_element_type=jnp.float32)
    return [sum(shift_cols(parts[a * 3 + b], b - 1) for b in range(3)) for a in range(3)]


def weight_terms(rows3, full_row):
    cols = []
    for b in range(3):
        moved = shift_cols(rows3, 1 - b)
        cols.append(jnp.einsum("aow,iw->oai", moved, full_row, preferred_element_type=jnp.float32))
    return jnp.stack(cols, axis=2)


def hidden_terms(weight, rows3):
    total = None
    for b in range(3):
        part = jnp.einsum("oai,aow->iw", weight[:, :, b, :], rows3, preferred_element_type=jnp.float32)
        part = shift_cols(part, 1 - b)
        total = part if total is None else total + part
    return total


def per_device(features, first_weight, second_weight, out_grad):
    feat = features[:, 0, :]
    og = out_grad[:, 0, :]
    n_filt = lax.axis_size("filt")
    blk = feat.shape
    f32, bf16 = jnp.float32, jnp.bfloat16
    x_row = exchange(feat, "filt", "ag", 1).reshape(-1, blk[1])
    p0, p1, p2 = conv_row(first_weight, x_row)
    pre_first, h_all = call(
        hidden_kernel,
        (p0, p2, p1),
        [(blk, f32), ((n_filt,) + blk, bf16)],
        [pltpu.VMEM(blk, f32), pltpu.VMEM(blk, f32), pltpu.SemaphoreType.DMA((4,)),
         pltpu.SemaphoreType.DMA((n_filt,)), pltpu.SemaphoreType.DMA((n_filt,))],
        2,
    )
    h_row = h_all.reshape(-1, blk[1])
    q0, q1, q2 = conv_row(second_weight, h_row)
    block_out, grad_second, gs_prev, gs_next = call(
        output_kernel,
        (q0, q2, q1, feat, og),
        [(blk, bf16)] * 4,
        [pltpu.VMEM(blk, f32), pltpu.VMEM(blk, f32), pltpu.SemaphoreType.DMA((4,)), pltpu.SemaphoreType.DMA((4,))],
        3,
    )
    gs3 = jnp.stack([gs_next, grad_second, gs_prev])
    terms = hidden_terms(second_weight, gs3).astype(bf16).reshape((n_filt,) + blk)
    grad_first, gf_prev, gf_next = call(
        first_grad_kernel,
        (terms, pre_first),
        [(blk, bf16)] * 3,
        [pltpu.VMEM((n_filt,) + blk, bf16), pltpu.SemaphoreType.DMA((n_filt,)),
         pltpu.SemaphoreType.DMA((n_filt,)), pltpu.SemaphoreType.DMA((4,))],
        4,
    )
    gf3 = jnp.stack([gf_next, grad_first, gf_prev])
    second_local = weight_terms(gs3, h_row)
    first_local = weight_terms(gf3, x_row)
    n_rows = lax.axis_size("rows")
    summed_first, summed_second = row_sum(
        first_local.astype(bf16).reshape(n_rows, -1, 128), second_local.astype(bf16).reshape(n_rows, -1, 128), 0
    )
    first_grad = summed_first.astype(f32).reshape(first_local.shape)
    second_grad = summed_second.astype(f32).reshape(second_local.shape)
    return (block_out[:, None, :], first_grad, second_grad)


def solution(mesh):
    in_specs = (
        P("filt", "rows", None),
        P("filt", None, None, None),
        P("filt", None, None, None),
        P("filt", "rows", None),
    )
    out_specs = (P("filt", "rows", None), P("filt", None, None, None), P("filt", None, None, None))
    return jax.shard_map(
        per_device, mesh=mesh, in_specs=in_specs, out_specs=out_specs, check_vma=False
    )
```

```python
import functools

import jax
import jax.numpy as jnp
from jax import lax
from jax.experimental import pallas as pl
from jax.experimental.pallas import tpu as pltpu
from jax.sharding import PartitionSpec as P

MESH = pl.DeviceIdType.MESH


def peer_id(axis, j):
    if axis == "rows":
        return (j, lax.axis_index("filt"))
    return (lax.axis_index("rows"), j)


def exchange_kernel(axis, n, mode, *refs):
    me = lax.axis_index(axis)

    def each_peer(body):
        def step(k, carry):
            body(lax.rem(me + k, n), lax.rem(me + n - k, n))
            return carry

        lax.fori_loop(1, n, step, 0)

    barrier = pltpu.get_barrier_semaphore()

    def greet(j, s):
        pl.semaphore_signal(barrier, 1, device_id=peer_id(axis, j), device_id_type=MESH)

    each_peer(greet)
    pl.semaphore_wait(barrier, n - 1)

    def gather(src, out_ref, send, recv):
        def copy(j, s):
            return pltpu.make_async_remote_copy(
                src, out_ref.at[me], send.at[j], recv.at[me], device_id=peer_id(axis, j), device_id_type=MESH
            )

        def incoming(j, s):
            return pltpu.make_async_remote_copy(
                src, out_ref.at[s], send.at[s], recv.at[s], device_id=peer_id(axis, s), device_id_type=MESH
            )

        each_peer(lambda j, s: copy(j, s).start())
        return copy, incoming

    def reduce(x_ref, buf, send, recv):
        def copy(j, s):
            return pltpu.make_async_remote_copy(
                x_ref.at[j], buf.at[me], send.at[j], recv.at[me], device_id=peer_id(axis, j), device_id_type=MESH
            )

        def incoming(j, s):
            return pltpu.make_async_remote_copy(
                x_ref.at[s], buf.at[s], send.at[s], recv.at[s], device_id=peer_id(axis, s), device_id_type=MESH
            )

        each_peer(lambda j, s: copy(j, s).start())
        each_peer(lambda j, s: incoming(j, s).wait_recv())
        acc = x_ref[me].astype(jnp.float32)

        def add(k, acc):
            return acc + buf[lax.rem(me + k, n)].astype(jnp.float32)

        acc = lax.fori_loop(1, n, add, acc)
        each_peer(lambda j, s: copy(j, s).wait_send())
        return acc

    if mode == "ag":
        x_ref, out_ref, send, recv = refs
        copy, incoming = gather(x_ref, out_ref, send, recv)
        out_ref[me] = x_ref[...]
        each_peer(lambda j, s: incoming(j, s).wait_recv())
        each_peer(lambda j, s: copy(j, s).wait_send())
    elif mode == "rs":
        x_ref, out_ref, buf, send, recv = refs
        out_ref[...] = reduce(x_ref, buf, send, recv).astype(out_ref.dtype)
    else:
        x_ref, out_ref, buf, send, recv, send2, recv2 = refs
        out_ref[me] = reduce(x_ref, buf, send, recv).astype(out_ref.dtype)
        copy, incoming = gather(out_ref.at[me], out_ref, send2, recv2)
        each_peer(lambda j, s: incoming(j, s).wait_recv())
        each_peer(lambda j, s: copy(j, s).wait_send())


class RowSum:
    def __init__(self, n, x_ref, out_ref, half_buf, half_b, part_buf, sems):
        self.zn = zn = n // 2
        self.me = me = lax.axis_index("rows")
        my_y, self.my_z = me // zn, lax.rem(me, zn)
        self.other = lax.rem(me + zn, n)
        self.mine, self.theirs = my_y * zn, (1 - my_y) * zn
        self.x_ref, self.out_ref, self.half_buf, self.half_b, self.part_buf, self.sems = (
            x_ref, out_ref, half_buf, half_b, part_buf, sems)

    def rcopy(self, src, dst, send, recv, j):
        return pltpu.make_async_remote_copy(
            src, dst, send, recv, device_id=(j, lax.axis_index("filt")), device_id_type=MESH
        )

    def each_z(self, body):
        zn, my_z = self.zn, self.my_z

        def step(k, carry):
            body(lax.rem(my_z + k, zn), lax.rem(my_z + zn - k, zn))
            return carry

        lax.fori_loop(1, zn, step, 0)

    def swap(self):
        return self.rcopy(self.x_ref.at[pl.ds(self.theirs, self.zn)], self.half_buf, self.sems.at[0, 0],
                          self.sems.at[0, 1], self.other)

    def part_out(self, j, s):
        return self.rcopy(self.half_b.at[j], self.part_buf.at[self.my_z], self.sems.at[1, j],
                          self.sems.at[2, self.my_z], self.mine + j)

    def part_in(self, j, s):
        return self.rcopy(self.half_b.at[s], self.part_buf.at[s], self.sems.at[1, s], self.sems.at[2, s],
                          self.mine + s)

    def sum_out(self, j, s):
        me = self.me
        return self.rcopy(self.out_ref.at[me], self.out_ref.at[me], self.sems.at[3, j], self.sems.at[4, self.my_z],
                          self.mine + j)

    def sum_in(self, j, s):
        c = self.mine + s
        return self.rcopy(self.out_ref.at[c], self.out_ref.at[c], self.sems.at[3, s], self.sems.at[4, s], c)

    def back(self):
        half = pl.ds(self.mine, self.zn)
        return self.rcopy(self.out_ref.at[half], self.out_ref.at[half], self.sems.at[5, 0], self.sems.at[5, 1],
                          self.other)

    def s1_start(self):
        self.swap().start()

    def s1_finish(self):
        self.swap().wait_recv()
        x_ref, half_buf, half_b, mine = self.x_ref, self.half_buf, self.half_b, self.mine

        def add_half(t, carry):
            half_b[t] = (x_ref[mine + t].astype(jnp.float32) + half_buf[t].astype(jnp.float32)).astype(half_b.dtype)
            return carry

        lax.fori_loop(0, self.zn, add_half, 0)
        self.swap().wait_send()

    def s2_start(self):
        self.each_z(lambda j, s: self.part_out(j, s).start())

    def s2_finish(self):
        self.each_z(lambda j, s: self.part_in(j, s).wait_recv())
        zn, my_z, part_buf = self.zn, self.my_z, self.part_buf
        acc = self.x_ref[self.me].astype(jnp.float32) + self.half_buf[my_z].astype(jnp.float32)

        def add_part(k, acc):
            return acc + part_buf[lax.rem(my_z + k, zn)].astype(jnp.float32)

        acc = lax.fori_loop(1, zn, add_part, acc)
        self.out_ref[self.me] = acc.astype(self.out_ref.dtype)
        self.each_z(lambda j, s: self.part_out(j, s).wait_send())

    def s3_start(self):
        self.each_z(lambda j, s: self.sum_out(j, s).start())

    def s3_finish(self):
        self.each_z(lambda j, s: self.sum_in(j, s).wait_recv())
        self.each_z(lambda j, s: self.sum_out(j, s).wait_send())

    def s4_start(self):
        self.back().start()

    def s4_finish(self):
        self.back().wait_recv()
        self.back().wait_send()


def row_sum_kernel(n, xa, xb, oa, ob, *scratch):
    zn = n // 2
    me = lax.axis_index("rows")
    my_z = lax.rem(me, zn)
    mine = (me // zn) * zn

    def dev(j):
        return (j, lax.axis_index("filt"))

    barrier = pltpu.get_barrier_semaphore()
    pl.semaphore_signal(barrier, 1, device_id=dev(lax.rem(me + zn, n)), device_id_type=MESH)

    def greet(k, carry):
        pl.semaphore_signal(barrier, 1, device_id=dev(mine + lax.rem(my_z + k, zn)), device_id_type=MESH)
        return carry

    lax.fori_loop(1, zn, greet, 0)
    pl.semaphore_wait(barrier, zn)
    a = RowSum(n, xa, oa, *scratch[:4])
    b = RowSum(n, xb, ob, *scratch[4:])
    a.s1_start()
    a.s1_finish()
    a.s2_start()
    b.s1_start()
    b.s1_finish()
    b.s2_start()
    a.s2_finish()
    a.s3_start()
    b.s2_finish()
    b.s3_start()
    a.s3_finish()
    a.s4_start()
    b.s3_finish()
    b.s4_start()
    a.s4_finish()
    b.s4_finish()


def row_sum(xa, xb, collective_id):
    n = xa.shape[0]
    zn = n // 2
    spec = pl.BlockSpec(memory_space=pltpu.VMEM)
    scratch = []
    for x in (xa, xb):
        blk = (zn,) + x.shape[1:]
        scratch += [pltpu.VMEM(blk, x.dtype), pltpu.VMEM(blk, x.dtype), pltpu.VMEM(blk, x.dtype),
                    pltpu.SemaphoreType.DMA((6, zn))]
    return pl.pallas_call(
        functools.partial(row_sum_kernel, n),
        out_shape=(jax.ShapeDtypeStruct(xa.shape, xa.dtype), jax.ShapeDtypeStruct(xb.shape, xb.dtype)),
        in_specs=[spec, spec],
        out_specs=(spec, spec),
        scratch_shapes=scratch,
        compiler_params=pltpu.CompilerParams(collective_id=collective_id, has_side_effects=True),
    )(xa, xb)


def row_dev(j):
    return (j, lax.axis_index("filt"))


def filt_dev(j):
    return (lax.axis_index("rows"), j)


def rcopy(src, dst, send, recv, dev):
    return pltpu.make_async_remote_copy(src, dst, send, recv, device_id=dev, device_id_type=MESH)


def each_filt_peer(body):
    nf = lax.axis_size("filt")
    me = lax.axis_index("filt")

    def step(k, carry):
        body(lax.rem(me + k, nf), lax.rem(me + nf - k, nf))
        return carry

    lax.fori_loop(1, nf, step, 0)


def enter(with_filt):
    nr = lax.axis_size("rows")
    me = lax.axis_index("rows")
    barrier = pltpu.get_barrier_semaphore()

    @pl.when(me > 0)
    def _():
        pl.semaphore_signal(barrier, 1, device_id=row_dev(me - 1), device_id_type=MESH)

    @pl.when(me < nr - 1)
    def _():
        pl.semaphore_signal(barrier, 1, device_id=row_dev(me + 1), device_id_type=MESH)

    count = (me + nr - 1) // nr + (2 * nr - 2 - me) // nr
    if with_filt:
        each_filt_peer(lambda j, s: pl.semaphore_signal(barrier, 1, device_id=filt_dev(j), device_id_type=MESH))
        count = count + lax.axis_size("filt") - 1
    pl.semaphore_wait(barrier, count)


class Halo:
    def __init__(self, down_src, up_src, from_prev, from_next, sems):
        self.nr = lax.axis_size("rows")
        self.me = lax.axis_index("rows")
        self.down = lambda j: rcopy(down_src, from_prev, sems.at[0], sems.at[1], row_dev(j))
        self.up = lambda j: rcopy(up_src, from_next, sems.at[2], sems.at[3], row_dev(j))
        me, nr = self.me, self.nr

        @pl.when(me < nr - 1)
        def _():
            self.down(me + 1).start()

        @pl.when(me > 0)
        def _():
            self.up(me - 1).start()

        @pl.when(me == 0)
        def _():
            from_prev[...] = jnp.zeros(from_prev.shape, from_prev.dtype)

        @pl.when(me == nr - 1)
        def _():
            from_next[...] = jnp.zeros(from_next.shape, from_next.dtype)

    def arrived(self):
        me, nr = self.me, self.nr

        @pl.when(me > 0)
        def _():
            self.down(me - 1).wait_recv()

        @pl.when(me < nr - 1)
        def _():
            self.up(me + 1).wait_recv()

    def sent(self):
        me, nr = self.me, self.nr

        @pl.when(me > 0)
        def _():
            self.up(me - 1).wait_send()

        @pl.when(me < nr - 1)
        def _():
            self.down(me + 1).wait_send()


def hidden_kernel(p0, p2, p1, pre_ref, h_ref, from_prev, from_next, hsems, fsend, frecv):
    mf = lax.axis_index("filt")
    enter(True)
    halo = Halo(p0, p2, from_prev, from_next, hsems)
    halo.arrived()
    pre = p1[...] + from_prev[...] + from_next[...]
    pre_ref[...] = pre
    h_ref[mf] = jnp.maximum(pre, 0.0).astype(h_ref.dtype)

    def out(j, s):
        return rcopy(h_ref.at[mf], h_ref.at[mf], fsend.at[j], frecv.at[mf], filt_dev(j))

    def inc(j, s):
        return rcopy(h_ref.at[s], h_ref.at[s], fsend.at[s], frecv.at[s], filt_dev(s))

    each_filt_peer(lambda j, s: out(j, s).start())
    each_filt_peer(lambda j, s: inc(j, s).wait_recv())
    each_filt_peer(lambda j, s: out(j, s).wait_send())
    halo.sent()


def backward_kernel(q0, q2, q1, feat, og, w2t, pre_first, out_ref, gs_ref, gprev, gnext, gf_ref, fprev, fnext,
                    from_prev, from_next, tbuf, rbuf, fsend, frecv, sems1, sems2, sems3):
    nf = lax.axis_size("filt")
    mf = lax.axis_index("filt")
    enter(True)
    halo = Halo(q0, q2, from_prev, from_next, sems1)
    halo.arrived()
    pre = q1[...] + from_prev[...] + from_next[...] + feat[...].astype(jnp.float32)
    out_ref[...] = jnp.maximum(pre, 0.0).astype(out_ref.dtype)
    gs_ref[...] = jnp.where(pre > 0, og[...].astype(jnp.float32), 0.0).astype(gs_ref.dtype)
    halo2 = Halo(gs_ref, gs_ref, gprev, gnext, sems2)
    halo2.arrived()
    rows3 = jnp.concatenate([gnext[...], gs_ref[...], gprev[...]], axis=0)
    blk, width = tbuf.shape[1], tbuf.shape[2]
    col = lax.broadcasted_iota(jnp.int32, (blk, width), 1)

    def block(t, carry):
        rows = pl.ds(pl.multiple_of(t * blk, blk), blk)
        total = None
        for b in range(3):
            part = jnp.dot(w2t[b, rows, :], rows3, preferred_element_type=jnp.float32)
            if b == 0:
                part = jnp.where(col == width - 1, 0.0, pltpu.roll(part, width - 1, 1))
            elif b == 2:
                part = jnp.where(col == 0, 0.0, pltpu.roll(part, 1, 1))
            total = part if total is None else total + part
        tbuf[t] = total.astype(tbuf.dtype)
        return carry

    lax.fori_loop(0, nf, block, 0)

    def out(j, s):
        return rcopy(tbuf.at[j], rbuf.at[mf], fsend.at[j], frecv.at[mf], filt_dev(j))

    def inc(j, s):
        return rcopy(tbuf.at[s], rbuf.at[s], fsend.at[s], frecv.at[s], filt_dev(s))

    each_filt_peer(lambda j, s: out(j, s).start())
    each_filt_peer(lambda j, s: inc(j, s).wait_recv())
    acc = tbuf[mf].astype(jnp.float32)

    def add(k, acc):
        return acc + rbuf[lax.rem(mf + k, nf)].astype(jnp.float32)

    acc = lax.fori_loop(1, nf, add, acc)
    gf_ref[...] = jnp.where(pre_first[...] > 0, acc, 0.0).astype(gf_ref.dtype)
    halo3 = Halo(gf_ref, gf_ref, fprev, fnext, sems3)
    halo3.arrived()
    each_filt_peer(lambda j, s: out(j, s).wait_send())
    halo.sent()
    halo2.sent()
    halo3.sent()


def call(kernel, args, outs, scratch, collective_id):
    spec = pl.BlockSpec(memory_space=pltpu.VMEM)
    return pl.pallas_call(
        kernel,
        out_shape=tuple(jax.ShapeDtypeStruct(shape, dtype) for shape, dtype in outs),
        in_specs=[spec] * len(args),
        out_specs=tuple(spec for _ in outs),
        scratch_shapes=scratch,
        compiler_params=pltpu.CompilerParams(collective_id=collective_id, has_side_effects=True),
    )(*args)


def exchange(x, axis, mode, collective_id, out_dtype=None):
    n = lax.axis_size(axis)
    out_dtype = out_dtype or x.dtype
    sems = [pltpu.SemaphoreType.DMA((n,)), pltpu.SemaphoreType.DMA((n,))]
    if mode == "ag":
        out_shape = (n,) + x.shape
        scratch = sems
    elif mode == "rs":
        out_shape = x.shape[1:]
        scratch = [pltpu.VMEM(x.shape, x.dtype)] + sems
    else:
        out_shape = x.shape
        scratch = [pltpu.VMEM(x.shape, x.dtype)] + sems + sems
    return pl.pallas_call(
        functools.partial(exchange_kernel, axis, n, mode),
        out_shape=jax.ShapeDtypeStruct(out_shape, out_dtype),
        in_specs=[pl.BlockSpec(memory_space=pltpu.VMEM)],
        out_specs=pl.BlockSpec(memory_space=pltpu.VMEM),
        scratch_shapes=scratch,
        compiler_params=pltpu.CompilerParams(collective_id=collective_id, has_side_effects=True),
    )(x)


def shift_cols(value, offset):
    if offset == 0:
        return value
    pad = [(0, 0)] * (value.ndim - 1)
    if offset > 0:
        return jnp.pad(value[..., offset:], pad + [(0, offset)])
    return jnp.pad(value[..., :offset], pad + [(-offset, 0)])


def conv_row(weight, row):
    o = weight.shape[0]
    flat = weight.reshape(o, 9, weight.shape[3])
    parts = jnp.einsum("oki,iw->kow", flat, row, preferred_element_type=jnp.float32)
    return [sum(shift_cols(parts[a * 3 + b], b - 1) for b in range(3)) for a in range(3)]


def weight_terms(rows3, full_row):
    cols = []
    for b in range(3):
        moved = shift_cols(rows3, 1 - b)
        cols.append(jnp.einsum("aow,iw->oai", moved, full_row, preferred_element_type=jnp.float32))
    return jnp.stack(cols, axis=2)


def hidden_terms(weight, rows3):
    total = None
    for b in range(3):
        part = jnp.einsum("oai,aow->iw", weight[:, :, b, :], rows3, preferred_element_type=jnp.float32)
        part = shift_cols(part, 1 - b)
        total = part if total is None else total + part
    return total


def per_device(features, first_weight, second_weight, out_grad):
    feat = features[:, 0, :]
    og = out_grad[:, 0, :]
    n_filt = lax.axis_size("filt")
    blk = feat.shape
    f32, bf16 = jnp.float32, jnp.bfloat16
    x_row = exchange(feat, "filt", "ag", 1).reshape(-1, blk[1])
    p0, p1, p2 = conv_row(first_weight, x_row)
    pre_first, h_all = call(
        hidden_kernel,
        (p0, p2, p1),
        [(blk, f32), ((n_filt,) + blk, bf16)],
        [pltpu.VMEM(blk, f32), pltpu.VMEM(blk, f32), pltpu.SemaphoreType.DMA((4,)),
         pltpu.SemaphoreType.DMA((n_filt,)), pltpu.SemaphoreType.DMA((n_filt,))],
        2,
    )
    h_row = h_all.reshape(-1, blk[1])
    q0, q1, q2 = conv_row(second_weight, h_row)
    o, _, _, i_ch = second_weight.shape
    w2t = second_weight.transpose(2, 3, 1, 0).reshape(3, i_ch, 3 * o)
    block_out, grad_second, gs_prev, gs_next, grad_first, gf_prev, gf_next = call(
        backward_kernel,
        (q0, q2, q1, feat, og, w2t, pre_first),
        [(blk, bf16)] * 7,
        [pltpu.VMEM(blk, f32), pltpu.VMEM(blk, f32), pltpu.VMEM((n_filt,) + blk, bf16),
         pltpu.VMEM((n_filt,) + blk, bf16), pltpu.SemaphoreType.DMA((n_filt,)), pltpu.SemaphoreType.DMA((n_filt,)),
         pltpu.SemaphoreType.DMA((4,)), pltpu.SemaphoreType.DMA((4,)), pltpu.SemaphoreType.DMA((4,))],
        3,
    )
    gs3 = jnp.stack([gs_next, grad_second, gs_prev])
    gf3 = jnp.stack([gf_next, grad_first, gf_prev])
    second_local = weight_terms(gs3, h_row)
    first_local = weight_terms(gf3, x_row)
    n_rows = lax.axis_size("rows")
    summed_first, summed_second = row_sum(
        first_local.astype(bf16).reshape(n_rows, -1, 128), second_local.astype(bf16).reshape(n_rows, -1, 128), 0
    )
    first_grad = summed_first.astype(f32).reshape(first_local.shape)
    second_grad = summed_second.astype(f32).reshape(second_local.shape)
    return (block_out[:, None, :], first_grad, second_grad)


def solution(mesh):
    in_specs = (
        P("filt", "rows", None),
        P("filt", None, None, None),
        P("filt", None, None, None),
        P("filt", "rows", None),
    )
    out_specs = (P("filt", "rows", None), P("filt", None, None, None), P("filt", None, None, None))
    return jax.shard_map(
        per_device, mesh=mesh, in_specs=in_specs, out_specs=out_specs, check_vma=False
    )
```

```python
import functools

import jax
import jax.numpy as jnp
from jax import lax
from jax.experimental import pallas as pl
from jax.experimental.pallas import tpu as pltpu
from jax.sharding import PartitionSpec as P

MESH = pl.DeviceIdType.MESH


def peer_id(axis, j):
    if axis == "rows":
        return (j, lax.axis_index("filt"))
    return (lax.axis_index("rows"), j)


def exchange_kernel(axis, n, mode, *refs):
    me = lax.axis_index(axis)

    def each_peer(body):
        def step(k, carry):
            body(lax.rem(me + k, n), lax.rem(me + n - k, n))
            return carry

        lax.fori_loop(1, n, step, 0)

    barrier = pltpu.get_barrier_semaphore()

    def greet(j, s):
        pl.semaphore_signal(barrier, 1, device_id=peer_id(axis, j), device_id_type=MESH)

    each_peer(greet)
    pl.semaphore_wait(barrier, n - 1)

    def gather(src, out_ref, send, recv):
        def copy(j, s):
            return pltpu.make_async_remote_copy(
                src, out_ref.at[me], send.at[j], recv.at[me], device_id=peer_id(axis, j), device_id_type=MESH
            )

        def incoming(j, s):
            return pltpu.make_async_remote_copy(
                src, out_ref.at[s], send.at[s], recv.at[s], device_id=peer_id(axis, s), device_id_type=MESH
            )

        each_peer(lambda j, s: copy(j, s).start())
        return copy, incoming

    def reduce(x_ref, buf, send, recv):
        def copy(j, s):
            return pltpu.make_async_remote_copy(
                x_ref.at[j], buf.at[me], send.at[j], recv.at[me], device_id=peer_id(axis, j), device_id_type=MESH
            )

        def incoming(j, s):
            return pltpu.make_async_remote_copy(
                x_ref.at[s], buf.at[s], send.at[s], recv.at[s], device_id=peer_id(axis, s), device_id_type=MESH
            )

        each_peer(lambda j, s: copy(j, s).start())
        each_peer(lambda j, s: incoming(j, s).wait_recv())
        acc = x_ref[me].astype(jnp.float32)

        def add(k, acc):
            return acc + buf[lax.rem(me + k, n)].astype(jnp.float32)

        acc = lax.fori_loop(1, n, add, acc)
        each_peer(lambda j, s: copy(j, s).wait_send())
        return acc

    if mode == "ag":
        x_ref, out_ref, send, recv = refs
        copy, incoming = gather(x_ref, out_ref, send, recv)
        out_ref[me] = x_ref[...]
        each_peer(lambda j, s: incoming(j, s).wait_recv())
        each_peer(lambda j, s: copy(j, s).wait_send())
    elif mode == "rs":
        x_ref, out_ref, buf, send, recv = refs
        out_ref[...] = reduce(x_ref, buf, send, recv).astype(out_ref.dtype)
    else:
        x_ref, out_ref, buf, send, recv, send2, recv2 = refs
        out_ref[me] = reduce(x_ref, buf, send, recv).astype(out_ref.dtype)
        copy, incoming = gather(out_ref.at[me], out_ref, send2, recv2)
        each_peer(lambda j, s: incoming(j, s).wait_recv())
        each_peer(lambda j, s: copy(j, s).wait_send())


class RowSum:
    def __init__(self, n, x_ref, out_ref, half_buf, half_b, part_buf, sems):
        self.zn = zn = n // 2
        self.me = me = lax.axis_index("rows")
        my_y, self.my_z = me // zn, lax.rem(me, zn)
        self.other = lax.rem(me + zn, n)
        self.mine, self.theirs = my_y * zn, (1 - my_y) * zn
        self.x_ref, self.out_ref, self.half_buf, self.half_b, self.part_buf, self.sems = (
            x_ref, out_ref, half_buf, half_b, part_buf, sems)

    def rcopy(self, src, dst, send, recv, j):
        return pltpu.make_async_remote_copy(
            src, dst, send, recv, device_id=(j, lax.axis_index("filt")), device_id_type=MESH
        )

    def each_z(self, body):
        zn, my_z = self.zn, self.my_z

        def step(k, carry):
            body(lax.rem(my_z + k, zn), lax.rem(my_z + zn - k, zn))
            return carry

        lax.fori_loop(1, zn, step, 0)

    def swap(self):
        return self.rcopy(self.x_ref.at[pl.ds(self.theirs, self.zn)], self.half_buf, self.sems.at[0, 0],
                          self.sems.at[0, 1], self.other)

    def part_out(self, j, s):
        return self.rcopy(self.half_b.at[j], self.part_buf.at[self.my_z], self.sems.at[1, j],
                          self.sems.at[2, self.my_z], self.mine + j)

    def part_in(self, j, s):
        return self.rcopy(self.half_b.at[s], self.part_buf.at[s], self.sems.at[1, s], self.sems.at[2, s],
                          self.mine + s)

    def sum_out(self, j, s):
        me = self.me
        return self.rcopy(self.out_ref.at[me], self.out_ref.at[me], self.sems.at[3, j], self.sems.at[4, self.my_z],
                          self.mine + j)

    def sum_in(self, j, s):
        c = self.mine + s
        return self.rcopy(self.out_ref.at[c], self.out_ref.at[c], self.sems.at[3, s], self.sems.at[4, s], c)

    def back(self):
        half = pl.ds(self.mine, self.zn)
        return self.rcopy(self.out_ref.at[half], self.out_ref.at[half], self.sems.at[5, 0], self.sems.at[5, 1],
                          self.other)

    def s1_start(self):
        self.swap().start()

    def s1_finish(self):
        self.swap().wait_recv()
        x_ref, half_buf, half_b, mine = self.x_ref, self.half_buf, self.half_b, self.mine

        def add_half(t, carry):
            half_b[t] = (x_ref[mine + t].astype(jnp.float32) + half_buf[t].astype(jnp.float32)).astype(half_b.dtype)
            return carry

        lax.fori_loop(0, self.zn, add_half, 0)
        self.swap().wait_send()

    def s2_start(self):
        self.each_z(lambda j, s: self.part_out(j, s).start())

    def s2_finish(self):
        self.each_z(lambda j, s: self.part_in(j, s).wait_recv())
        zn, my_z, part_buf = self.zn, self.my_z, self.part_buf
        acc = self.x_ref[self.me].astype(jnp.float32) + self.half_buf[my_z].astype(jnp.float32)

        def add_part(k, acc):
            return acc + part_buf[lax.rem(my_z + k, zn)].astype(jnp.float32)

        acc = lax.fori_loop(1, zn, add_part, acc)
        self.out_ref[self.me] = acc.astype(self.out_ref.dtype)
        self.each_z(lambda j, s: self.part_out(j, s).wait_send())

    def s3_start(self):
        self.each_z(lambda j, s: self.sum_out(j, s).start())

    def s3_finish(self):
        self.each_z(lambda j, s: self.sum_in(j, s).wait_recv())
        self.each_z(lambda j, s: self.sum_out(j, s).wait_send())

    def s4_start(self):
        self.back().start()

    def s4_finish(self):
        self.back().wait_recv()
        self.back().wait_send()


def row_sum_kernel(n, xa, xb, oa, ob, *scratch):
    zn = n // 2
    me = lax.axis_index("rows")
    my_z = lax.rem(me, zn)
    mine = (me // zn) * zn

    def dev(j):
        return (j, lax.axis_index("filt"))

    barrier = pltpu.get_barrier_semaphore()
    pl.semaphore_signal(barrier, 1, device_id=dev(lax.rem(me + zn, n)), device_id_type=MESH)

    def greet(k, carry):
        pl.semaphore_signal(barrier, 1, device_id=dev(mine + lax.rem(my_z + k, zn)), device_id_type=MESH)
        return carry

    lax.fori_loop(1, zn, greet, 0)
    pl.semaphore_wait(barrier, zn)
    a = RowSum(n, xa, oa, *scratch[:4])
    b = RowSum(n, xb, ob, *scratch[4:])
    a.s1_start()
    a.s1_finish()
    a.s2_start()
    b.s1_start()
    b.s1_finish()
    b.s2_start()
    a.s2_finish()
    a.s3_start()
    b.s2_finish()
    b.s3_start()
    a.s3_finish()
    a.s4_start()
    b.s3_finish()
    b.s4_start()
    a.s4_finish()
    b.s4_finish()


def row_sum(xa, xb, collective_id):
    n = xa.shape[0]
    zn = n // 2
    spec = pl.BlockSpec(memory_space=pltpu.VMEM)
    scratch = []
    for x in (xa, xb):
        blk = (zn,) + x.shape[1:]
        scratch += [pltpu.VMEM(blk, x.dtype), pltpu.VMEM(blk, x.dtype), pltpu.VMEM(blk, x.dtype),
                    pltpu.SemaphoreType.DMA((6, zn))]
    return pl.pallas_call(
        functools.partial(row_sum_kernel, n),
        out_shape=(jax.ShapeDtypeStruct(xa.shape, xa.dtype), jax.ShapeDtypeStruct(xb.shape, xb.dtype)),
        in_specs=[spec, spec],
        out_specs=(spec, spec),
        scratch_shapes=scratch,
        compiler_params=pltpu.CompilerParams(collective_id=collective_id, has_side_effects=True),
    )(xa, xb)


def row_dev(j):
    return (j, lax.axis_index("filt"))


def filt_dev(j):
    return (lax.axis_index("rows"), j)


def rcopy(src, dst, send, recv, dev):
    return pltpu.make_async_remote_copy(src, dst, send, recv, device_id=dev, device_id_type=MESH)


def each_filt_peer(body):
    nf = lax.axis_size("filt")
    me = lax.axis_index("filt")

    def step(k, carry):
        body(lax.rem(me + k, nf), lax.rem(me + nf - k, nf))
        return carry

    lax.fori_loop(1, nf, step, 0)


def enter(with_filt):
    nr = lax.axis_size("rows")
    me = lax.axis_index("rows")
    barrier = pltpu.get_barrier_semaphore()

    @pl.when(me > 0)
    def _():
        pl.semaphore_signal(barrier, 1, device_id=row_dev(me - 1), device_id_type=MESH)

    @pl.when(me < nr - 1)
    def _():
        pl.semaphore_signal(barrier, 1, device_id=row_dev(me + 1), device_id_type=MESH)

    count = (me + nr - 1) // nr + (2 * nr - 2 - me) // nr
    if with_filt:
        each_filt_peer(lambda j, s: pl.semaphore_signal(barrier, 1, device_id=filt_dev(j), device_id_type=MESH))
        count = count + lax.axis_size("filt") - 1
    pl.semaphore_wait(barrier, count)


class Halo:
    def __init__(self, down_src, up_src, from_prev, from_next, sems):
        self.nr = lax.axis_size("rows")
        self.me = lax.axis_index("rows")
        self.down = lambda j: rcopy(down_src, from_prev, sems.at[0], sems.at[1], row_dev(j))
        self.up = lambda j: rcopy(up_src, from_next, sems.at[2], sems.at[3], row_dev(j))
        me, nr = self.me, self.nr

        @pl.when(me < nr - 1)
        def _():
            self.down(me + 1).start()

        @pl.when(me > 0)
        def _():
            self.up(me - 1).start()

        @pl.when(me == 0)
        def _():
            from_prev[...] = jnp.zeros(from_prev.shape, from_prev.dtype)

        @pl.when(me == nr - 1)
        def _():
            from_next[...] = jnp.zeros(from_next.shape, from_next.dtype)

    def arrived(self):
        me, nr = self.me, self.nr

        @pl.when(me > 0)
        def _():
            self.down(me - 1).wait_recv()

        @pl.when(me < nr - 1)
        def _():
            self.up(me + 1).wait_recv()

    def sent(self):
        me, nr = self.me, self.nr

        @pl.when(me > 0)
        def _():
            self.up(me - 1).wait_send()

        @pl.when(me < nr - 1)
        def _():
            self.down(me + 1).wait_send()


def lane_shift(part, offset):
    width = part.shape[1]
    col = lax.broadcasted_iota(jnp.int32, part.shape, 1)
    if offset == 1:
        return jnp.where(col == width - 1, 0.0, pltpu.roll(part, width - 1, 1))
    return jnp.where(col == 0, 0.0, pltpu.roll(part, 1, 1))


def forward_kernel(feat, w1r, x_ref, pre_ref, h_ref, p0s, p2s, from_prev, from_next, hsems, xsend, xrecv, fsend, frecv):
    mf = lax.axis_index("filt")
    blk = feat.shape[0]
    enter(True)

    def xout(j, s):
        return rcopy(feat, x_ref.at[pl.ds(mf * blk, blk)], xsend.at[j], xrecv.at[mf], filt_dev(j))

    def xin(j, s):
        return rcopy(feat, x_ref.at[pl.ds(s * blk, blk)], xsend.at[s], xrecv.at[s], filt_dev(s))

    each_filt_peer(lambda j, s: xout(j, s).start())
    x_ref[pl.ds(mf * blk, blk)] = feat[...]
    each_filt_peer(lambda j, s: xin(j, s).wait_recv())
    x = x_ref[...]
    parts = []
    for a in range(3):
        total = None
        for b in range(3):
            part = jnp.dot(w1r[a * 3 + b], x, preferred_element_type=jnp.float32)
            if b != 1:
                part = lane_shift(part, b - 1)
            total = part if total is None else total + part
        parts.append(total)
    p0s[...] = parts[0]
    p2s[...] = parts[2]
    halo = Halo(p0s, p2s, from_prev, from_next, hsems)
    halo.arrived()
    pre = parts[1] + from_prev[...] + from_next[...]
    pre_ref[...] = pre
    h_ref[mf] = jnp.maximum(pre, 0.0).astype(h_ref.dtype)

    def out(j, s):
        return rcopy(h_ref.at[mf], h_ref.at[mf], fsend.at[j], frecv.at[mf], filt_dev(j))

    def inc(j, s):
        return rcopy(h_ref.at[s], h_ref.at[s], fsend.at[s], frecv.at[s], filt_dev(s))

    each_filt_peer(lambda j, s: out(j, s).start())
    each_filt_peer(lambda j, s: inc(j, s).wait_recv())
    each_filt_peer(lambda j, s: xout(j, s).wait_send())
    each_filt_peer(lambda j, s: out(j, s).wait_send())
    halo.sent()


def backward_kernel(q0, q2, q1, feat, og, w2t, pre_first, out_ref, gs_ref, gprev, gnext, gf_ref, fprev, fnext,
                    from_prev, from_next, tbuf, rbuf, fsend, frecv, sems1, sems2, sems3):
    nf = lax.axis_size("filt")
    mf = lax.axis_index("filt")
    enter(True)
    halo = Halo(q0, q2, from_prev, from_next, sems1)
    halo.arrived()
    pre = q1[...] + from_prev[...] + from_next[...] + feat[...].astype(jnp.float32)
    out_ref[...] = jnp.maximum(pre, 0.0).astype(out_ref.dtype)
    gs_ref[...] = jnp.where(pre > 0, og[...].astype(jnp.float32), 0.0).astype(gs_ref.dtype)
    halo2 = Halo(gs_ref, gs_ref, gprev, gnext, sems2)
    halo2.arrived()
    rows3 = jnp.concatenate([gnext[...], gs_ref[...], gprev[...]], axis=0)
    blk, width = tbuf.shape[1], tbuf.shape[2]
    col = lax.broadcasted_iota(jnp.int32, (blk, width), 1)

    def block(t, carry):
        rows = pl.ds(pl.multiple_of(t * blk, blk), blk)
        total = None
        for b in range(3):
            part = jnp.dot(w2t[b, rows, :], rows3, preferred_element_type=jnp.float32)
            if b == 0:
                part = jnp.where(col == width - 1, 0.0, pltpu.roll(part, width - 1, 1))
            elif b == 2:
                part = jnp.where(col == 0, 0.0, pltpu.roll(part, 1, 1))
            total = part if total is None else total + part
        tbuf[t] = total.astype(tbuf.dtype)
        return carry

    lax.fori_loop(0, nf, block, 0)

    def out(j, s):
        return rcopy(tbuf.at[j], rbuf.at[mf], fsend.at[j], frecv.at[mf], filt_dev(j))

    def inc(j, s):
        return rcopy(tbuf.at[s], rbuf.at[s], fsend.at[s], frecv.at[s], filt_dev(s))

    each_filt_peer(lambda j, s: out(j, s).start())
    each_filt_peer(lambda j, s: inc(j, s).wait_recv())
    acc = tbuf[mf].astype(jnp.float32)

    def add(k, acc):
        return acc + rbuf[lax.rem(mf + k, nf)].astype(jnp.float32)

    acc = lax.fori_loop(1, nf, add, acc)
    gf_ref[...] = jnp.where(pre_first[...] > 0, acc, 0.0).astype(gf_ref.dtype)
    halo3 = Halo(gf_ref, gf_ref, fprev, fnext, sems3)
    halo3.arrived()
    each_filt_peer(lambda j, s: out(j, s).wait_send())
    halo.sent()
    halo2.sent()
    halo3.sent()


def call(kernel, args, outs, scratch, collective_id):
    spec = pl.BlockSpec(memory_space=pltpu.VMEM)
    return pl.pallas_call(
        kernel,
        out_shape=tuple(jax.ShapeDtypeStruct(shape, dtype) for shape, dtype in outs),
        in_specs=[spec] * len(args),
        out_specs=tuple(spec for _ in outs),
        scratch_shapes=scratch,
        compiler_params=pltpu.CompilerParams(collective_id=collective_id, has_side_effects=True),
    )(*args)


def exchange(x, axis, mode, collective_id, out_dtype=None):
    n = lax.axis_size(axis)
    out_dtype = out_dtype or x.dtype
    sems = [pltpu.SemaphoreType.DMA((n,)), pltpu.SemaphoreType.DMA((n,))]
    if mode == "ag":
        out_shape = (n,) + x.shape
        scratch = sems
    elif mode == "rs":
        out_shape = x.shape[1:]
        scratch = [pltpu.VMEM(x.shape, x.dtype)] + sems
    else:
        out_shape = x.shape
        scratch = [pltpu.VMEM(x.shape, x.dtype)] + sems + sems
    return pl.pallas_call(
        functools.partial(exchange_kernel, axis, n, mode),
        out_shape=jax.ShapeDtypeStruct(out_shape, out_dtype),
        in_specs=[pl.BlockSpec(memory_space=pltpu.VMEM)],
        out_specs=pl.BlockSpec(memory_space=pltpu.VMEM),
        scratch_shapes=scratch,
        compiler_params=pltpu.CompilerParams(collective_id=collective_id, has_side_effects=True),
    )(x)


def shift_cols(value, offset):
    if offset == 0:
        return value
    pad = [(0, 0)] * (value.ndim - 1)
    if offset > 0:
        return jnp.pad(value[..., offset:], pad + [(0, offset)])
    return jnp.pad(value[..., :offset], pad + [(-offset, 0)])


def conv_row(weight, row):
    o = weight.shape[0]
    flat = weight.reshape(o, 9, weight.shape[3])
    parts = jnp.einsum("oki,iw->kow", flat, row, preferred_element_type=jnp.float32)
    return [sum(shift_cols(parts[a * 3 + b], b - 1) for b in range(3)) for a in range(3)]


def weight_terms(rows3, full_row):
    cols = []
    for b in range(3):
        moved = shift_cols(rows3, 1 - b)
        cols.append(jnp.einsum("aow,iw->oai", moved, full_row, preferred_element_type=jnp.float32))
    return jnp.stack(cols, axis=2)


def hidden_terms(weight, rows3):
    total = None
    for b in range(3):
        part = jnp.einsum("oai,aow->iw", weight[:, :, b, :], rows3, preferred_element_type=jnp.float32)
        part = shift_cols(part, 1 - b)
        total = part if total is None else total + part
    return total


def per_device(features, first_weight, second_weight, out_grad):
    feat = features[:, 0, :]
    og = out_grad[:, 0, :]
    n_filt = lax.axis_size("filt")
    blk = feat.shape
    f32, bf16 = jnp.float32, jnp.bfloat16
    o, _, _, i_ch = first_weight.shape
    w1r = first_weight.transpose(1, 2, 0, 3).reshape(9, o, i_ch)
    sem = pltpu.SemaphoreType.DMA
    x_row, pre_first, h_all = call(
        forward_kernel,
        (feat, w1r),
        [((n_filt * blk[0], blk[1]), bf16), (blk, f32), ((n_filt,) + blk, bf16)],
        [pltpu.VMEM(blk, f32)] * 4 + [sem((4,)), sem((n_filt,)), sem((n_filt,)), sem((n_filt,)), sem((n_filt,))],
        2,
    )
    h_row = h_all.reshape(-1, blk[1])
    q0, q1, q2 = conv_row(second_weight, h_row)
    w2t = second_weight.transpose(2, 3, 1, 0).reshape(3, i_ch, 3 * o)
    block_out, grad_second, gs_prev, gs_next, grad_first, gf_prev, gf_next = call(
        backward_kernel,
        (q0, q2, q1, feat, og, w2t, pre_first),
        [(blk, bf16)] * 7,
        [pltpu.VMEM(blk, f32), pltpu.VMEM(blk, f32), pltpu.VMEM((n_filt,) + blk, bf16),
         pltpu.VMEM((n_filt,) + blk, bf16), pltpu.SemaphoreType.DMA((n_filt,)), pltpu.SemaphoreType.DMA((n_filt,)),
         pltpu.SemaphoreType.DMA((4,)), pltpu.SemaphoreType.DMA((4,)), pltpu.SemaphoreType.DMA((4,))],
        3,
    )
    gs3 = jnp.stack([gs_next, grad_second, gs_prev])
    gf3 = jnp.stack([gf_next, grad_first, gf_prev])
    second_local = weight_terms(gs3, h_row)
    first_local = weight_terms(gf3, x_row)
    n_rows = lax.axis_size("rows")
    summed_first, summed_second = row_sum(
        first_local.astype(bf16).reshape(n_rows, -1, 128), second_local.astype(bf16).reshape(n_rows, -1, 128), 0
    )
    first_grad = summed_first.astype(f32).reshape(first_local.shape)
    second_grad = summed_second.astype(f32).reshape(second_local.shape)
    return (block_out[:, None, :], first_grad, second_grad)


def solution(mesh):
    in_specs = (
        P("filt", "rows", None),
        P("filt", None, None, None),
        P("filt", None, None, None),
        P("filt", "rows", None),
    )
    out_specs = (P("filt", "rows", None), P("filt", None, None, None), P("filt", None, None, None))
    return jax.shard_map(
        per_device, mesh=mesh, in_specs=in_specs, out_specs=out_specs, check_vma=False
    )
```

```python
import functools

import jax
import jax.numpy as jnp
from jax import lax
from jax.experimental import pallas as pl
from jax.experimental.pallas import tpu as pltpu
from jax.sharding import PartitionSpec as P

MESH = pl.DeviceIdType.MESH


def peer_id(axis, j):
    if axis == "rows":
        return (j, lax.axis_index("filt"))
    return (lax.axis_index("rows"), j)


def exchange_kernel(axis, n, mode, *refs):
    me = lax.axis_index(axis)

    def each_peer(body):
        def step(k, carry):
            body(lax.rem(me + k, n), lax.rem(me + n - k, n))
            return carry

        lax.fori_loop(1, n, step, 0)

    barrier = pltpu.get_barrier_semaphore()

    def greet(j, s):
        pl.semaphore_signal(barrier, 1, device_id=peer_id(axis, j), device_id_type=MESH)

    each_peer(greet)
    pl.semaphore_wait(barrier, n - 1)

    def gather(src, out_ref, send, recv):
        def copy(j, s):
            return pltpu.make_async_remote_copy(
                src, out_ref.at[me], send.at[j], recv.at[me], device_id=peer_id(axis, j), device_id_type=MESH
            )

        def incoming(j, s):
            return pltpu.make_async_remote_copy(
                src, out_ref.at[s], send.at[s], recv.at[s], device_id=peer_id(axis, s), device_id_type=MESH
            )

        each_peer(lambda j, s: copy(j, s).start())
        return copy, incoming

    def reduce(x_ref, buf, send, recv):
        def copy(j, s):
            return pltpu.make_async_remote_copy(
                x_ref.at[j], buf.at[me], send.at[j], recv.at[me], device_id=peer_id(axis, j), device_id_type=MESH
            )

        def incoming(j, s):
            return pltpu.make_async_remote_copy(
                x_ref.at[s], buf.at[s], send.at[s], recv.at[s], device_id=peer_id(axis, s), device_id_type=MESH
            )

        each_peer(lambda j, s: copy(j, s).start())
        each_peer(lambda j, s: incoming(j, s).wait_recv())
        acc = x_ref[me].astype(jnp.float32)

        def add(k, acc):
            return acc + buf[lax.rem(me + k, n)].astype(jnp.float32)

        acc = lax.fori_loop(1, n, add, acc)
        each_peer(lambda j, s: copy(j, s).wait_send())
        return acc

    if mode == "ag":
        x_ref, out_ref, send, recv = refs
        copy, incoming = gather(x_ref, out_ref, send, recv)
        out_ref[me] = x_ref[...]
        each_peer(lambda j, s: incoming(j, s).wait_recv())
        each_peer(lambda j, s: copy(j, s).wait_send())
    elif mode == "rs":
        x_ref, out_ref, buf, send, recv = refs
        out_ref[...] = reduce(x_ref, buf, send, recv).astype(out_ref.dtype)
    else:
        x_ref, out_ref, buf, send, recv, send2, recv2 = refs
        out_ref[me] = reduce(x_ref, buf, send, recv).astype(out_ref.dtype)
        copy, incoming = gather(out_ref.at[me], out_ref, send2, recv2)
        each_peer(lambda j, s: incoming(j, s).wait_recv())
        each_peer(lambda j, s: copy(j, s).wait_send())


class RowSum:
    def __init__(self, n, x_ref, out_ref, half_buf, half_b, part_buf, sems):
        self.zn = zn = n // 2
        self.me = me = lax.axis_index("rows")
        my_y, self.my_z = me // zn, lax.rem(me, zn)
        self.other = lax.rem(me + zn, n)
        self.mine, self.theirs = my_y * zn, (1 - my_y) * zn
        self.x_ref, self.out_ref, self.half_buf, self.half_b, self.part_buf, self.sems = (
            x_ref, out_ref, half_buf, half_b, part_buf, sems)

    def rcopy(self, src, dst, send, recv, j):
        return pltpu.make_async_remote_copy(
            src, dst, send, recv, device_id=(j, lax.axis_index("filt")), device_id_type=MESH
        )

    def each_z(self, body):
        zn, my_z = self.zn, self.my_z

        def step(k, carry):
            body(lax.rem(my_z + k, zn), lax.rem(my_z + zn - k, zn))
            return carry

        lax.fori_loop(1, zn, step, 0)

    def swap(self):
        return self.rcopy(self.x_ref.at[pl.ds(self.theirs, self.zn)], self.half_buf, self.sems.at[0, 0],
                          self.sems.at[0, 1], self.other)

    def part_out(self, j, s):
        return self.rcopy(self.half_b.at[j], self.part_buf.at[self.my_z], self.sems.at[1, j],
                          self.sems.at[2, self.my_z], self.mine + j)

    def part_in(self, j, s):
        return self.rcopy(self.half_b.at[s], self.part_buf.at[s], self.sems.at[1, s], self.sems.at[2, s],
                          self.mine + s)

    def sum_out(self, j, s):
        me = self.me
        return self.rcopy(self.out_ref.at[me], self.out_ref.at[me], self.sems.at[3, j], self.sems.at[4, self.my_z],
                          self.mine + j)

    def sum_in(self, j, s):
        c = self.mine + s
        return self.rcopy(self.out_ref.at[c], self.out_ref.at[c], self.sems.at[3, s], self.sems.at[4, s], c)

    def back(self):
        half = pl.ds(self.mine, self.zn)
        return self.rcopy(self.out_ref.at[half], self.out_ref.at[half], self.sems.at[5, 0], self.sems.at[5, 1],
                          self.other)

    def s1_start(self):
        self.swap().start()

    def s1_finish(self):
        self.swap().wait_recv()
        x_ref, half_buf, half_b, mine = self.x_ref, self.half_buf, self.half_b, self.mine

        def add_half(t, carry):
            half_b[t] = (x_ref[mine + t].astype(jnp.float32) + half_buf[t].astype(jnp.float32)).astype(half_b.dtype)
            return carry

        lax.fori_loop(0, self.zn, add_half, 0)
        self.swap().wait_send()

    def s2_start(self):
        self.each_z(lambda j, s: self.part_out(j, s).start())

    def s2_finish(self):
        self.each_z(lambda j, s: self.part_in(j, s).wait_recv())
        zn, my_z, part_buf = self.zn, self.my_z, self.part_buf
        acc = self.x_ref[self.me].astype(jnp.float32) + self.half_buf[my_z].astype(jnp.float32)

        def add_part(k, acc):
            return acc + part_buf[lax.rem(my_z + k, zn)].astype(jnp.float32)

        acc = lax.fori_loop(1, zn, add_part, acc)
        self.out_ref[self.me] = acc.astype(self.out_ref.dtype)
        self.each_z(lambda j, s: self.part_out(j, s).wait_send())

    def s3_start(self):
        self.each_z(lambda j, s: self.sum_out(j, s).start())

    def s3_finish(self):
        self.each_z(lambda j, s: self.sum_in(j, s).wait_recv())
        self.each_z(lambda j, s: self.sum_out(j, s).wait_send())

    def s4_start(self):
        self.back().start()

    def s4_finish(self):
        self.back().wait_recv()
        self.back().wait_send()


def row_sum_kernel(n, xa, xb, oa, ob, *scratch):
    zn = n // 2
    me = lax.axis_index("rows")
    my_z = lax.rem(me, zn)
    mine = (me // zn) * zn

    def dev(j):
        return (j, lax.axis_index("filt"))

    barrier = pltpu.get_barrier_semaphore()
    pl.semaphore_signal(barrier, 1, device_id=dev(lax.rem(me + zn, n)), device_id_type=MESH)

    def greet(k, carry):
        pl.semaphore_signal(barrier, 1, device_id=dev(mine + lax.rem(my_z + k, zn)), device_id_type=MESH)
        return carry

    lax.fori_loop(1, zn, greet, 0)
    pl.semaphore_wait(barrier, zn)
    a = RowSum(n, xa, oa, *scratch[:4])
    b = RowSum(n, xb, ob, *scratch[4:])
    a.s1_start()
    a.s1_finish()
    a.s2_start()
    b.s1_start()
    b.s1_finish()
    b.s2_start()
    a.s2_finish()
    a.s3_start()
    b.s2_finish()
    b.s3_start()
    a.s3_finish()
    a.s4_start()
    b.s3_finish()
    b.s4_start()
    a.s4_finish()
    b.s4_finish()


def row_sum(xa, xb, collective_id):
    n = xa.shape[0]
    zn = n // 2
    spec = pl.BlockSpec(memory_space=pltpu.VMEM)
    scratch = []
    for x in (xa, xb):
        blk = (zn,) + x.shape[1:]
        scratch += [pltpu.VMEM(blk, x.dtype), pltpu.VMEM(blk, x.dtype), pltpu.VMEM(blk, x.dtype),
                    pltpu.SemaphoreType.DMA((6, zn))]
    return pl.pallas_call(
        functools.partial(row_sum_kernel, n),
        out_shape=(jax.ShapeDtypeStruct(xa.shape, xa.dtype), jax.ShapeDtypeStruct(xb.shape, xb.dtype)),
        in_specs=[spec, spec],
        out_specs=(spec, spec),
        scratch_shapes=scratch,
        compiler_params=pltpu.CompilerParams(collective_id=collective_id, has_side_effects=True),
    )(xa, xb)


def row_dev(j):
    return (j, lax.axis_index("filt"))


def filt_dev(j):
    return (lax.axis_index("rows"), j)


def rcopy(src, dst, send, recv, dev):
    return pltpu.make_async_remote_copy(src, dst, send, recv, device_id=dev, device_id_type=MESH)


def each_filt_peer(body):
    nf = lax.axis_size("filt")
    me = lax.axis_index("filt")

    def step(k, carry):
        body(lax.rem(me + k, nf), lax.rem(me + nf - k, nf))
        return carry

    lax.fori_loop(1, nf, step, 0)


def enter(with_filt):
    nr = lax.axis_size("rows")
    me = lax.axis_index("rows")
    barrier = pltpu.get_barrier_semaphore()

    @pl.when(me > 0)
    def _():
        pl.semaphore_signal(barrier, 1, device_id=row_dev(me - 1), device_id_type=MESH)

    @pl.when(me < nr - 1)
    def _():
        pl.semaphore_signal(barrier, 1, device_id=row_dev(me + 1), device_id_type=MESH)

    count = (me + nr - 1) // nr + (2 * nr - 2 - me) // nr
    if with_filt:
        each_filt_peer(lambda j, s: pl.semaphore_signal(barrier, 1, device_id=filt_dev(j), device_id_type=MESH))
        count = count + lax.axis_size("filt") - 1
    pl.semaphore_wait(barrier, count)


class Halo:
    def __init__(self, down_src, up_src, from_prev, from_next, sems):
        self.nr = lax.axis_size("rows")
        self.me = lax.axis_index("rows")
        self.down = lambda j: rcopy(down_src, from_prev, sems.at[0], sems.at[1], row_dev(j))
        self.up = lambda j: rcopy(up_src, from_next, sems.at[2], sems.at[3], row_dev(j))
        me, nr = self.me, self.nr

        @pl.when(me < nr - 1)
        def _():
            self.down(me + 1).start()

        @pl.when(me > 0)
        def _():
            self.up(me - 1).start()

        @pl.when(me == 0)
        def _():
            from_prev[...] = jnp.zeros(from_prev.shape, from_prev.dtype)

        @pl.when(me == nr - 1)
        def _():
            from_next[...] = jnp.zeros(from_next.shape, from_next.dtype)

    def arrived(self):
        me, nr = self.me, self.nr

        @pl.when(me > 0)
        def _():
            self.down(me - 1).wait_recv()

        @pl.when(me < nr - 1)
        def _():
            self.up(me + 1).wait_recv()

    def sent(self):
        me, nr = self.me, self.nr

        @pl.when(me > 0)
        def _():
            self.up(me - 1).wait_send()

        @pl.when(me < nr - 1)
        def _():
            self.down(me + 1).wait_send()


def lane_shift(part, offset):
    width = part.shape[1]
    col = lax.broadcasted_iota(jnp.int32, part.shape, 1)
    if offset == 1:
        return jnp.where(col == width - 1, 0.0, pltpu.roll(part, width - 1, 1))
    return jnp.where(col == 0, 0.0, pltpu.roll(part, 1, 1))


def conv_parts(w_ref, x):
    parts = []
    for a in range(3):
        total = None
        for b in range(3):
            part = jnp.dot(w_ref[a * 3 + b], x, preferred_element_type=jnp.float32)
            if b != 1:
                part = lane_shift(part, b - 1)
            total = part if total is None else total + part
        parts.append(total)
    return parts


def filt_gather(src, dst, blk, send, recv):
    mf = lax.axis_index("filt")

    def out(j, s):
        return rcopy(src, dst.at[pl.ds(mf * blk, blk)], send.at[j], recv.at[mf], filt_dev(j))

    def inc(j, s):
        return rcopy(src, dst.at[pl.ds(s * blk, blk)], send.at[s], recv.at[s], filt_dev(s))

    each_filt_peer(lambda j, s: out(j, s).start())
    dst[pl.ds(mf * blk, blk)] = src[...]
    return (lambda: each_filt_peer(lambda j, s: inc(j, s).wait_recv()),
            lambda: each_filt_peer(lambda j, s: out(j, s).wait_send()))


def block_kernel(feat, og, w1r, w2r, w2t, x_ref, h_ref, out_ref, gs_ref, gprev, gnext, gf_ref, fprev, fnext,
                 p0s, p2s, from_prev, from_next, q0s, q2s, qprev, qnext, hsrc, pre1, tbuf, rbuf,
                 hsems, xsend, xrecv, fsend, frecv, sems1, sems2, sems3, tsend, trecv):
    nf = lax.axis_size("filt")
    mf = lax.axis_index("filt")
    blk = feat.shape[0]
    enter(True)
    x_arrived, x_sent = filt_gather(feat, x_ref, blk, xsend, xrecv)
    x_arrived()
    parts = conv_parts(w1r, x_ref[...])
    p0s[...] = parts[0]
    p2s[...] = parts[2]
    halo = Halo(p0s, p2s, from_prev, from_next, hsems)
    halo.arrived()
    pre1[...] = parts[1] + from_prev[...] + from_next[...]
    hsrc[...] = jnp.maximum(pre1[...], 0.0).astype(hsrc.dtype)
    h_arrived, h_sent = filt_gather(hsrc, h_ref, blk, fsend, frecv)
    h_arrived()
    qs = conv_parts(w2r, h_ref[...])
    q0s[...] = qs[0]
    q2s[...] = qs[2]
    halo1 = Halo(q0s, q2s, qprev, qnext, sems1)
    halo1.arrived()
    pre = qs[1] + qprev[...] + qnext[...] + feat[...].astype(jnp.float32)
    out_ref[...] = jnp.maximum(pre, 0.0).astype(out_ref.dtype)
    gs_ref[...] = jnp.where(pre > 0, og[...].astype(jnp.float32), 0.0).astype(gs_ref.dtype)
    halo2 = Halo(gs_ref, gs_ref, gprev, gnext, sems2)
    halo2.arrived()
    rows3 = jnp.concatenate([gnext[...], gs_ref[...], gprev[...]], axis=0)

    def block(t, carry):
        rows = pl.ds(pl.multiple_of(t * blk, blk), blk)
        total = None
        for b in range(3):
            part = jnp.dot(w2t[b, rows, :], rows3, preferred_element_type=jnp.float32)
            if b != 1:
                part = lane_shift(part, 1 - b)
            total = part if total is None else total + part
        tbuf[t] = total.astype(tbuf.dtype)
        return carry

    lax.fori_loop(0, nf, block, 0)

    def out(j, s):
        return rcopy(tbuf.at[j], rbuf.at[mf], tsend.at[j], trecv.at[mf], filt_dev(j))

    def inc(j, s):
        return rcopy(tbuf.at[s], rbuf.at[s], tsend.at[s], trecv.at[s], filt_dev(s))

    each_filt_peer(lambda j, s: out(j, s).start())
    each_filt_peer(lambda j, s: inc(j, s).wait_recv())
    acc = tbuf[mf].astype(jnp.float32)

    def add(k, acc):
        return acc + rbuf[lax.rem(mf + k, nf)].astype(jnp.float32)

    acc = lax.fori_loop(1, nf, add, acc)
    gf_ref[...] = jnp.where(pre1[...] > 0, acc, 0.0).astype(gf_ref.dtype)
    halo3 = Halo(gf_ref, gf_ref, fprev, fnext, sems3)
    halo3.arrived()
    x_sent()
    h_sent()
    each_filt_peer(lambda j, s: out(j, s).wait_send())
    halo.sent()
    halo1.sent()
    halo2.sent()
    halo3.sent()


def call(kernel, args, outs, scratch, collective_id):
    spec = pl.BlockSpec(memory_space=pltpu.VMEM)
    return pl.pallas_call(
        kernel,
        out_shape=tuple(jax.ShapeDtypeStruct(shape, dtype) for shape, dtype in outs),
        in_specs=[spec] * len(args),
        out_specs=tuple(spec for _ in outs),
        scratch_shapes=scratch,
        compiler_params=pltpu.CompilerParams(collective_id=collective_id, has_side_effects=True),
    )(*args)


def exchange(x, axis, mode, collective_id, out_dtype=None):
    n = lax.axis_size(axis)
    out_dtype = out_dtype or x.dtype
    sems = [pltpu.SemaphoreType.DMA((n,)), pltpu.SemaphoreType.DMA((n,))]
    if mode == "ag":
        out_shape = (n,) + x.shape
        scratch = sems
    elif mode == "rs":
        out_shape = x.shape[1:]
        scratch = [pltpu.VMEM(x.shape, x.dtype)] + sems
    else:
        out_shape = x.shape
        scratch = [pltpu.VMEM(x.shape, x.dtype)] + sems + sems
    return pl.pallas_call(
        functools.partial(exchange_kernel, axis, n, mode),
        out_shape=jax.ShapeDtypeStruct(out_shape, out_dtype),
        in_specs=[pl.BlockSpec(memory_space=pltpu.VMEM)],
        out_specs=pl.BlockSpec(memory_space=pltpu.VMEM),
        scratch_shapes=scratch,
        compiler_params=pltpu.CompilerParams(collective_id=collective_id, has_side_effects=True),
    )(x)


def shift_cols(value, offset):
    if offset == 0:
        return value
    pad = [(0, 0)] * (value.ndim - 1)
    if offset > 0:
        return jnp.pad(value[..., offset:], pad + [(0, offset)])
    return jnp.pad(value[..., :offset], pad + [(-offset, 0)])


def conv_row(weight, row):
    o = weight.shape[0]
    flat = weight.reshape(o, 9, weight.shape[3])
    parts = jnp.einsum("oki,iw->kow", flat, row, preferred_element_type=jnp.float32)
    return [sum(shift_cols(parts[a * 3 + b], b - 1) for b in range(3)) for a in range(3)]


def weight_terms(rows3, full_row):
    cols = []
    for b in range(3):
        moved = shift_cols(rows3, 1 - b)
        cols.append(jnp.einsum("aow,iw->oai", moved, full_row, preferred_element_type=jnp.float32))
    return jnp.stack(cols, axis=2)


def hidden_terms(weight, rows3):
    total = None
    for b in range(3):
        part = jnp.einsum("oai,aow->iw", weight[:, :, b, :], rows3, preferred_element_type=jnp.float32)
        part = shift_cols(part, 1 - b)
        total = part if total is None else total + part
    return total


def per_device(features, first_weight, second_weight, out_grad):
    feat = features[:, 0, :]
    og = out_grad[:, 0, :]
    n_filt = lax.axis_size("filt")
    blk = feat.shape
    f32, bf16 = jnp.float32, jnp.bfloat16
    o, _, _, i_ch = first_weight.shape
    w1r = first_weight.transpose(1, 2, 0, 3).reshape(9, o, i_ch)
    w2r = second_weight.transpose(1, 2, 0, 3).reshape(9, o, i_ch)
    w2t = second_weight.transpose(2, 3, 1, 0).reshape(3, i_ch, 3 * o)
    sem = pltpu.SemaphoreType.DMA
    full = (n_filt * blk[0], blk[1])
    x_row, h_row, block_out, grad_second, gs_prev, gs_next, grad_first, gf_prev, gf_next = call(
        block_kernel,
        (feat, og, w1r, w2r, w2t),
        [(full, bf16), (full, bf16)] + [(blk, bf16)] * 7,
        [pltpu.VMEM(blk, f32)] * 8 + [pltpu.VMEM(blk, bf16), pltpu.VMEM(blk, f32),
                                      pltpu.VMEM((n_filt,) + blk, bf16), pltpu.VMEM((n_filt,) + blk, bf16)]
        + [sem((4,))] + [sem((n_filt,))] * 4 + [sem((4,))] * 3 + [sem((n_filt,))] * 2,
        2,
    )
    gs3 = jnp.stack([gs_next, grad_second, gs_prev])
    gf3 = jnp.stack([gf_next, grad_first, gf_prev])
    second_local = weight_terms(gs3, h_row)
    first_local = weight_terms(gf3, x_row)
    n_rows = lax.axis_size("rows")
    summed_first, summed_second = row_sum(
        first_local.astype(bf16).reshape(n_rows, -1, 128), second_local.astype(bf16).reshape(n_rows, -1, 128), 0
    )
    first_grad = summed_first.astype(f32).reshape(first_local.shape)
    second_grad = summed_second.astype(f32).reshape(second_local.shape)
    return (block_out[:, None, :], first_grad, second_grad)


def solution(mesh):
    in_specs = (
        P("filt", "rows", None),
        P("filt", None, None, None),
        P("filt", None, None, None),
        P("filt", "rows", None),
    )
    out_specs = (P("filt", "rows", None), P("filt", None, None, None), P("filt", None, None, None))
    return jax.shard_map(
        per_device, mesh=mesh, in_specs=in_specs, out_specs=out_specs, check_vma=False
    )
```

```python
import functools

import jax
import jax.numpy as jnp
from jax import lax
from jax.experimental import pallas as pl
from jax.experimental.pallas import tpu as pltpu
from jax.sharding import PartitionSpec as P

MESH = pl.DeviceIdType.MESH


def peer_id(axis, j):
    if axis == "rows":
        return (j, lax.axis_index("filt"))
    return (lax.axis_index("rows"), j)


def exchange_kernel(axis, n, mode, *refs):
    me = lax.axis_index(axis)

    def each_peer(body):
        def step(k, carry):
            body(lax.rem(me + k, n), lax.rem(me + n - k, n))
            return carry

        lax.fori_loop(1, n, step, 0)

    barrier = pltpu.get_barrier_semaphore()

    def greet(j, s):
        pl.semaphore_signal(barrier, 1, device_id=peer_id(axis, j), device_id_type=MESH)

    each_peer(greet)
    pl.semaphore_wait(barrier, n - 1)

    def gather(src, out_ref, send, recv):
        def copy(j, s):
            return pltpu.make_async_remote_copy(
                src, out_ref.at[me], send.at[j], recv.at[me], device_id=peer_id(axis, j), device_id_type=MESH
            )

        def incoming(j, s):
            return pltpu.make_async_remote_copy(
                src, out_ref.at[s], send.at[s], recv.at[s], device_id=peer_id(axis, s), device_id_type=MESH
            )

        each_peer(lambda j, s: copy(j, s).start())
        return copy, incoming

    def reduce(x_ref, buf, send, recv):
        def copy(j, s):
            return pltpu.make_async_remote_copy(
                x_ref.at[j], buf.at[me], send.at[j], recv.at[me], device_id=peer_id(axis, j), device_id_type=MESH
            )

        def incoming(j, s):
            return pltpu.make_async_remote_copy(
                x_ref.at[s], buf.at[s], send.at[s], recv.at[s], device_id=peer_id(axis, s), device_id_type=MESH
            )

        each_peer(lambda j, s: copy(j, s).start())
        each_peer(lambda j, s: incoming(j, s).wait_recv())
        acc = x_ref[me].astype(jnp.float32)

        def add(k, acc):
            return acc + buf[lax.rem(me + k, n)].astype(jnp.float32)

        acc = lax.fori_loop(1, n, add, acc)
        each_peer(lambda j, s: copy(j, s).wait_send())
        return acc

    if mode == "ag":
        x_ref, out_ref, send, recv = refs
        copy, incoming = gather(x_ref, out_ref, send, recv)
        out_ref[me] = x_ref[...]
        each_peer(lambda j, s: incoming(j, s).wait_recv())
        each_peer(lambda j, s: copy(j, s).wait_send())
    elif mode == "rs":
        x_ref, out_ref, buf, send, recv = refs
        out_ref[...] = reduce(x_ref, buf, send, recv).astype(out_ref.dtype)
    else:
        x_ref, out_ref, buf, send, recv, send2, recv2 = refs
        out_ref[me] = reduce(x_ref, buf, send, recv).astype(out_ref.dtype)
        copy, incoming = gather(out_ref.at[me], out_ref, send2, recv2)
        each_peer(lambda j, s: incoming(j, s).wait_recv())
        each_peer(lambda j, s: copy(j, s).wait_send())


class RowSum:
    def __init__(self, n, x_ref, out_ref, half_buf, half_b, part_buf, sems):
        self.zn = zn = n // 2
        self.me = me = lax.axis_index("rows")
        my_y, self.my_z = me // zn, lax.rem(me, zn)
        self.other = lax.rem(me + zn, n)
        self.mine, self.theirs = my_y * zn, (1 - my_y) * zn
        self.x_ref, self.out_ref, self.half_buf, self.half_b, self.part_buf, self.sems = (
            x_ref, out_ref, half_buf, half_b, part_buf, sems)

    def rcopy(self, src, dst, send, recv, j):
        return pltpu.make_async_remote_copy(
            src, dst, send, recv, device_id=(j, lax.axis_index("filt")), device_id_type=MESH
        )

    def each_z(self, body):
        zn, my_z = self.zn, self.my_z

        def step(k, carry):
            body(lax.rem(my_z + k, zn), lax.rem(my_z + zn - k, zn))
            return carry

        lax.fori_loop(1, zn, step, 0)

    def swap(self):
        return self.rcopy(self.x_ref.at[pl.ds(self.theirs, self.zn)], self.half_buf, self.sems.at[0, 0],
                          self.sems.at[0, 1], self.other)

    def part_out(self, j, s):
        return self.rcopy(self.half_b.at[j], self.part_buf.at[self.my_z], self.sems.at[1, j],
                          self.sems.at[2, self.my_z], self.mine + j)

    def part_in(self, j, s):
        return self.rcopy(self.half_b.at[s], self.part_buf.at[s], self.sems.at[1, s], self.sems.at[2, s],
                          self.mine + s)

    def sum_out(self, j, s):
        me = self.me
        return self.rcopy(self.out_ref.at[me], self.out_ref.at[me], self.sems.at[3, j], self.sems.at[4, self.my_z],
                          self.mine + j)

    def sum_in(self, j, s):
        c = self.mine + s
        return self.rcopy(self.out_ref.at[c], self.out_ref.at[c], self.sems.at[3, s], self.sems.at[4, s], c)

    def back(self):
        half = pl.ds(self.mine, self.zn)
        return self.rcopy(self.out_ref.at[half], self.out_ref.at[half], self.sems.at[5, 0], self.sems.at[5, 1],
                          self.other)

    def s1_start(self):
        self.swap().start()

    def s1_finish(self):
        self.swap().wait_recv()
        x_ref, half_buf, half_b, mine = self.x_ref, self.half_buf, self.half_b, self.mine

        def add_half(t, carry):
            half_b[t] = (x_ref[mine + t].astype(jnp.float32) + half_buf[t].astype(jnp.float32)).astype(half_b.dtype)
            return carry

        lax.fori_loop(0, self.zn, add_half, 0)
        self.swap().wait_send()

    def s2_start(self):
        self.each_z(lambda j, s: self.part_out(j, s).start())

    def s2_finish(self):
        self.each_z(lambda j, s: self.part_in(j, s).wait_recv())
        zn, my_z, part_buf = self.zn, self.my_z, self.part_buf
        acc = self.x_ref[self.me].astype(jnp.float32) + self.half_buf[my_z].astype(jnp.float32)

        def add_part(k, acc):
            return acc + part_buf[lax.rem(my_z + k, zn)].astype(jnp.float32)

        acc = lax.fori_loop(1, zn, add_part, acc)
        self.out_ref[self.me] = acc.astype(self.out_ref.dtype)
        self.each_z(lambda j, s: self.part_out(j, s).wait_send())

    def s3_start(self):
        self.each_z(lambda j, s: self.sum_out(j, s).start())

    def s3_finish(self):
        self.each_z(lambda j, s: self.sum_in(j, s).wait_recv())
        self.each_z(lambda j, s: self.sum_out(j, s).wait_send())

    def s4_start(self):
        self.back().start()

    def s4_finish(self):
        self.back().wait_recv()
        self.back().wait_send()


def row_sum_kernel(n, xa, xb, oa, ob, *scratch):
    zn = n // 2
    me = lax.axis_index("rows")
    my_z = lax.rem(me, zn)
    mine = (me // zn) * zn

    def dev(j):
        return (j, lax.axis_index("filt"))

    barrier = pltpu.get_barrier_semaphore()
    pl.semaphore_signal(barrier, 1, device_id=dev(lax.rem(me + zn, n)), device_id_type=MESH)

    def greet(k, carry):
        pl.semaphore_signal(barrier, 1, device_id=dev(mine + lax.rem(my_z + k, zn)), device_id_type=MESH)
        return carry

    lax.fori_loop(1, zn, greet, 0)
    pl.semaphore_wait(barrier, zn)
    a = RowSum(n, xa, oa, *scratch[:4])
    b = RowSum(n, xb, ob, *scratch[4:])
    a.s1_start()
    a.s1_finish()
    a.s2_start()
    b.s1_start()
    b.s1_finish()
    b.s2_start()
    a.s2_finish()
    a.s3_start()
    b.s2_finish()
    b.s3_start()
    a.s3_finish()
    a.s4_start()
    b.s3_finish()
    b.s4_start()
    a.s4_finish()
    b.s4_finish()


def row_sum(xa, xb, collective_id):
    n = xa.shape[0]
    zn = n // 2
    spec = pl.BlockSpec(memory_space=pltpu.VMEM)
    scratch = []
    for x in (xa, xb):
        blk = (zn,) + x.shape[1:]
        scratch += [pltpu.VMEM(blk, x.dtype), pltpu.VMEM(blk, x.dtype), pltpu.VMEM(blk, x.dtype),
                    pltpu.SemaphoreType.DMA((6, zn))]
    return pl.pallas_call(
        functools.partial(row_sum_kernel, n),
        out_shape=(jax.ShapeDtypeStruct(xa.shape, xa.dtype), jax.ShapeDtypeStruct(xb.shape, xb.dtype)),
        in_specs=[spec, spec],
        out_specs=(spec, spec),
        scratch_shapes=scratch,
        compiler_params=pltpu.CompilerParams(collective_id=collective_id, has_side_effects=True),
    )(xa, xb)


def row_dev(j):
    return (j, lax.axis_index("filt"))


def filt_dev(j):
    return (lax.axis_index("rows"), j)


def rcopy(src, dst, send, recv, dev):
    return pltpu.make_async_remote_copy(src, dst, send, recv, device_id=dev, device_id_type=MESH)


def each_filt_peer(body):
    nf = lax.axis_size("filt")
    half = nf // 2
    me = lax.axis_index("filt")

    def step(k, carry):
        far = (nf - k) // half
        off = k - 1 - (half - 1) * (1 - far)
        j = lax.rem(me // half + far, 2) * half + lax.rem(lax.rem(me, half) + off, half)
        body(j, j)
        return carry

    lax.fori_loop(1, nf, step, 0)


def enter(with_filt):
    nr = lax.axis_size("rows")
    me = lax.axis_index("rows")
    barrier = pltpu.get_barrier_semaphore()

    @pl.when(me > 0)
    def _():
        pl.semaphore_signal(barrier, 1, device_id=row_dev(me - 1), device_id_type=MESH)

    @pl.when(me < nr - 1)
    def _():
        pl.semaphore_signal(barrier, 1, device_id=row_dev(me + 1), device_id_type=MESH)

    count = (me + nr - 1) // nr + (2 * nr - 2 - me) // nr
    if with_filt:
        each_filt_peer(lambda j, s: pl.semaphore_signal(barrier, 1, device_id=filt_dev(j), device_id_type=MESH))
        count = count + lax.axis_size("filt") - 1
    pl.semaphore_wait(barrier, count)


class Halo:
    def __init__(self, down_src, up_src, from_prev, from_next, sems):
        self.nr = lax.axis_size("rows")
        self.me = lax.axis_index("rows")
        self.down = lambda j: rcopy(down_src, from_prev, sems.at[0], sems.at[1], row_dev(j))
        self.up = lambda j: rcopy(up_src, from_next, sems.at[2], sems.at[3], row_dev(j))
        me, nr = self.me, self.nr

        @pl.when(me < nr - 1)
        def _():
            self.down(me + 1).start()

        @pl.when(me > 0)
        def _():
            self.up(me - 1).start()

        @pl.when(me == 0)
        def _():
            from_prev[...] = jnp.zeros(from_prev.shape, from_prev.dtype)

        @pl.when(me == nr - 1)
        def _():
            from_next[...] = jnp.zeros(from_next.shape, from_next.dtype)

    def arrived(self):
        me, nr = self.me, self.nr

        @pl.when(me > 0)
        def _():
            self.down(me - 1).wait_recv()

        @pl.when(me < nr - 1)
        def _():
            self.up(me + 1).wait_recv()

    def sent(self):
        me, nr = self.me, self.nr

        @pl.when(me > 0)
        def _():
            self.up(me - 1).wait_send()

        @pl.when(me < nr - 1)
        def _():
            self.down(me + 1).wait_send()


def lane_shift(part, offset):
    width = part.shape[1]
    col = lax.broadcasted_iota(jnp.int32, part.shape, 1)
    if offset == 1:
        return jnp.where(col == width - 1, 0.0, pltpu.roll(part, width - 1, 1))
    return jnp.where(col == 0, 0.0, pltpu.roll(part, 1, 1))


def conv_parts(w_ref, x):
    parts = []
    for a in range(3):
        total = None
        for b in range(3):
            part = jnp.dot(w_ref[a * 3 + b], x, preferred_element_type=jnp.float32)
            if b != 1:
                part = lane_shift(part, b - 1)
            total = part if total is None else total + part
        parts.append(total)
    return parts


def filt_gather(src, dst, blk, send, recv):
    mf = lax.axis_index("filt")

    def out(j, s):
        return rcopy(src, dst.at[pl.ds(mf * blk, blk)], send.at[j], recv.at[mf], filt_dev(j))

    def inc(j, s):
        return rcopy(src, dst.at[pl.ds(s * blk, blk)], send.at[s], recv.at[s], filt_dev(s))

    each_filt_peer(lambda j, s: out(j, s).start())
    dst[pl.ds(mf * blk, blk)] = src[...]
    return (lambda: each_filt_peer(lambda j, s: inc(j, s).wait_recv()),
            lambda: each_filt_peer(lambda j, s: out(j, s).wait_send()))


def block_kernel(feat, og, w1r, w2r, w2t, x_ref, h_ref, out_ref, gs_ref, gprev, gnext, gf_ref, fprev, fnext,
                 p0s, p2s, from_prev, from_next, q0s, q2s, qprev, qnext, hsrc, pre1, tbuf, rbuf,
                 hsems, xsend, xrecv, fsend, frecv, sems1, sems2, sems3, tsend, trecv):
    nf = lax.axis_size("filt")
    mf = lax.axis_index("filt")
    blk = feat.shape[0]
    enter(True)
    x_arrived, x_sent = filt_gather(feat, x_ref, blk, xsend, xrecv)
    x_arrived()
    parts = conv_parts(w1r, x_ref[...])
    p0s[...] = parts[0]
    p2s[...] = parts[2]
    halo = Halo(p0s, p2s, from_prev, from_next, hsems)
    halo.arrived()
    pre1[...] = parts[1] + from_prev[...] + from_next[...]
    hsrc[...] = jnp.maximum(pre1[...], 0.0).astype(hsrc.dtype)
    h_arrived, h_sent = filt_gather(hsrc, h_ref, blk, fsend, frecv)
    h_arrived()
    qs = conv_parts(w2r, h_ref[...])
    q0s[...] = qs[0]
    q2s[...] = qs[2]
    halo1 = Halo(q0s, q2s, qprev, qnext, sems1)
    halo1.arrived()
    pre = qs[1] + qprev[...] + qnext[...] + feat[...].astype(jnp.float32)
    out_ref[...] = jnp.maximum(pre, 0.0).astype(out_ref.dtype)
    gs_ref[...] = jnp.where(pre > 0, og[...].astype(jnp.float32), 0.0).astype(gs_ref.dtype)
    halo2 = Halo(gs_ref, gs_ref, gprev, gnext, sems2)
    halo2.arrived()
    rows3 = jnp.concatenate([gnext[...], gs_ref[...], gprev[...]], axis=0)

    def block(t, carry):
        rows = pl.ds(pl.multiple_of(t * blk, blk), blk)
        total = None
        for b in range(3):
            part = jnp.dot(w2t[b, rows, :], rows3, preferred_element_type=jnp.float32)
            if b != 1:
                part = lane_shift(part, 1 - b)
            total = part if total is None else total + part
        tbuf[t] = total.astype(tbuf.dtype)
        return carry

    lax.fori_loop(0, nf, block, 0)

    def out(j, s):
        return rcopy(tbuf.at[j], rbuf.at[mf], tsend.at[j], trecv.at[mf], filt_dev(j))

    def inc(j, s):
        return rcopy(tbuf.at[s], rbuf.at[s], tsend.at[s], trecv.at[s], filt_dev(s))

    each_filt_peer(lambda j, s: out(j, s).start())
    each_filt_peer(lambda j, s: inc(j, s).wait_recv())
    acc = tbuf[mf].astype(jnp.float32)

    def add(k, acc):
        return acc + rbuf[lax.rem(mf + k, nf)].astype(jnp.float32)

    acc = lax.fori_loop(1, nf, add, acc)
    gf_ref[...] = jnp.where(pre1[...] > 0, acc, 0.0).astype(gf_ref.dtype)
    halo3 = Halo(gf_ref, gf_ref, fprev, fnext, sems3)
    halo3.arrived()
    x_sent()
    h_sent()
    each_filt_peer(lambda j, s: out(j, s).wait_send())
    halo.sent()
    halo1.sent()
    halo2.sent()
    halo3.sent()


def call(kernel, args, outs, scratch, collective_id):
    spec = pl.BlockSpec(memory_space=pltpu.VMEM)
    return pl.pallas_call(
        kernel,
        out_shape=tuple(jax.ShapeDtypeStruct(shape, dtype) for shape, dtype in outs),
        in_specs=[spec] * len(args),
        out_specs=tuple(spec for _ in outs),
        scratch_shapes=scratch,
        compiler_params=pltpu.CompilerParams(collective_id=collective_id, has_side_effects=True),
    )(*args)


def exchange(x, axis, mode, collective_id, out_dtype=None):
    n = lax.axis_size(axis)
    out_dtype = out_dtype or x.dtype
    sems = [pltpu.SemaphoreType.DMA((n,)), pltpu.SemaphoreType.DMA((n,))]
    if mode == "ag":
        out_shape = (n,) + x.shape
        scratch = sems
    elif mode == "rs":
        out_shape = x.shape[1:]
        scratch = [pltpu.VMEM(x.shape, x.dtype)] + sems
    else:
        out_shape = x.shape
        scratch = [pltpu.VMEM(x.shape, x.dtype)] + sems + sems
    return pl.pallas_call(
        functools.partial(exchange_kernel, axis, n, mode),
        out_shape=jax.ShapeDtypeStruct(out_shape, out_dtype),
        in_specs=[pl.BlockSpec(memory_space=pltpu.VMEM)],
        out_specs=pl.BlockSpec(memory_space=pltpu.VMEM),
        scratch_shapes=scratch,
        compiler_params=pltpu.CompilerParams(collective_id=collective_id, has_side_effects=True),
    )(x)


def shift_cols(value, offset):
    if offset == 0:
        return value
    pad = [(0, 0)] * (value.ndim - 1)
    if offset > 0:
        return jnp.pad(value[..., offset:], pad + [(0, offset)])
    return jnp.pad(value[..., :offset], pad + [(-offset, 0)])


def conv_row(weight, row):
    o = weight.shape[0]
    flat = weight.reshape(o, 9, weight.shape[3])
    parts = jnp.einsum("oki,iw->kow", flat, row, preferred_element_type=jnp.float32)
    return [sum(shift_cols(parts[a * 3 + b], b - 1) for b in range(3)) for a in range(3)]


def weight_terms(rows3, full_row):
    cols = []
    for b in range(3):
        moved = shift_cols(rows3, 1 - b)
        cols.append(jnp.einsum("aow,iw->oai", moved, full_row, preferred_element_type=jnp.float32))
    return jnp.stack(cols, axis=2)


def hidden_terms(weight, rows3):
    total = None
    for b in range(3):
        part = jnp.einsum("oai,aow->iw", weight[:, :, b, :], rows3, preferred_element_type=jnp.float32)
        part = shift_cols(part, 1 - b)
        total = part if total is None else total + part
    return total


def per_device(features, first_weight, second_weight, out_grad):
    feat = features[:, 0, :]
    og = out_grad[:, 0, :]
    n_filt = lax.axis_size("filt")
    blk = feat.shape
    f32, bf16 = jnp.float32, jnp.bfloat16
    o, _, _, i_ch = first_weight.shape
    w1r = first_weight.transpose(1, 2, 0, 3).reshape(9, o, i_ch)
    w2r = second_weight.transpose(1, 2, 0, 3).reshape(9, o, i_ch)
    w2t = second_weight.transpose(2, 3, 1, 0).reshape(3, i_ch, 3 * o)
    sem = pltpu.SemaphoreType.DMA
    full = (n_filt * blk[0], blk[1])
    x_row, h_row, block_out, grad_second, gs_prev, gs_next, grad_first, gf_prev, gf_next = call(
        block_kernel,
        (feat, og, w1r, w2r, w2t),
        [(full, bf16), (full, bf16)] + [(blk, bf16)] * 7,
        [pltpu.VMEM(blk, f32)] * 8 + [pltpu.VMEM(blk, bf16), pltpu.VMEM(blk, f32),
                                      pltpu.VMEM((n_filt,) + blk, bf16), pltpu.VMEM((n_filt,) + blk, bf16)]
        + [sem((4,))] + [sem((n_filt,))] * 4 + [sem((4,))] * 3 + [sem((n_filt,))] * 2,
        2,
    )
    gs3 = jnp.stack([gs_next, grad_second, gs_prev])
    gf3 = jnp.stack([gf_next, grad_first, gf_prev])
    second_local = weight_terms(gs3, h_row)
    first_local = weight_terms(gf3, x_row)
    n_rows = lax.axis_size("rows")
    summed_first, summed_second = row_sum(
        first_local.astype(bf16).reshape(n_rows, -1, 128), second_local.astype(bf16).reshape(n_rows, -1, 128), 0
    )
    first_grad = summed_first.astype(f32).reshape(first_local.shape)
    second_grad = summed_second.astype(f32).reshape(second_local.shape)
    return (block_out[:, None, :], first_grad, second_grad)


def solution(mesh):
    in_specs = (
        P("filt", "rows", None),
        P("filt", None, None, None),
        P("filt", None, None, None),
        P("filt", "rows", None),
    )
    out_specs = (P("filt", "rows", None), P("filt", None, None, None), P("filt", None, None, None))
    return jax.shard_map(
        per_device, mesh=mesh, in_specs=in_specs, out_specs=out_specs, check_vma=False
    )
```

```python
import functools

import jax
import jax.numpy as jnp
from jax import lax
from jax.experimental import pallas as pl
from jax.experimental.pallas import tpu as pltpu
from jax.sharding import PartitionSpec as P

MESH = pl.DeviceIdType.MESH


def peer_id(axis, j):
    if axis == "rows":
        return (j, lax.axis_index("filt"))
    return (lax.axis_index("rows"), j)


def exchange_kernel(axis, n, mode, *refs):
    me = lax.axis_index(axis)

    def each_peer(body):
        def step(k, carry):
            body(lax.rem(me + k, n), lax.rem(me + n - k, n))
            return carry

        lax.fori_loop(1, n, step, 0)

    barrier = pltpu.get_barrier_semaphore()

    def greet(j, s):
        pl.semaphore_signal(barrier, 1, device_id=peer_id(axis, j), device_id_type=MESH)

    each_peer(greet)
    pl.semaphore_wait(barrier, n - 1)

    def gather(src, out_ref, send, recv):
        def copy(j, s):
            return pltpu.make_async_remote_copy(
                src, out_ref.at[me], send.at[j], recv.at[me], device_id=peer_id(axis, j), device_id_type=MESH
            )

        def incoming(j, s):
            return pltpu.make_async_remote_copy(
                src, out_ref.at[s], send.at[s], recv.at[s], device_id=peer_id(axis, s), device_id_type=MESH
            )

        each_peer(lambda j, s: copy(j, s).start())
        return copy, incoming

    def reduce(x_ref, buf, send, recv):
        def copy(j, s):
            return pltpu.make_async_remote_copy(
                x_ref.at[j], buf.at[me], send.at[j], recv.at[me], device_id=peer_id(axis, j), device_id_type=MESH
            )

        def incoming(j, s):
            return pltpu.make_async_remote_copy(
                x_ref.at[s], buf.at[s], send.at[s], recv.at[s], device_id=peer_id(axis, s), device_id_type=MESH
            )

        each_peer(lambda j, s: copy(j, s).start())
        each_peer(lambda j, s: incoming(j, s).wait_recv())
        acc = x_ref[me].astype(jnp.float32)

        def add(k, acc):
            return acc + buf[lax.rem(me + k, n)].astype(jnp.float32)

        acc = lax.fori_loop(1, n, add, acc)
        each_peer(lambda j, s: copy(j, s).wait_send())
        return acc

    if mode == "ag":
        x_ref, out_ref, send, recv = refs
        copy, incoming = gather(x_ref, out_ref, send, recv)
        out_ref[me] = x_ref[...]
        each_peer(lambda j, s: incoming(j, s).wait_recv())
        each_peer(lambda j, s: copy(j, s).wait_send())
    elif mode == "rs":
        x_ref, out_ref, buf, send, recv = refs
        out_ref[...] = reduce(x_ref, buf, send, recv).astype(out_ref.dtype)
    else:
        x_ref, out_ref, buf, send, recv, send2, recv2 = refs
        out_ref[me] = reduce(x_ref, buf, send, recv).astype(out_ref.dtype)
        copy, incoming = gather(out_ref.at[me], out_ref, send2, recv2)
        each_peer(lambda j, s: incoming(j, s).wait_recv())
        each_peer(lambda j, s: copy(j, s).wait_send())


class RowSum:
    def __init__(self, n, x_ref, out_ref, half_buf, half_b, part_buf, sems):
        self.zn = zn = n // 2
        self.me = me = lax.axis_index("rows")
        my_y, self.my_z = me // zn, lax.rem(me, zn)
        self.other = lax.rem(me + zn, n)
        self.mine, self.theirs = my_y * zn, (1 - my_y) * zn
        self.x_ref, self.out_ref, self.half_buf, self.half_b, self.part_buf, self.sems = (
            x_ref, out_ref, half_buf, half_b, part_buf, sems)

    def rcopy(self, src, dst, send, recv, j):
        return pltpu.make_async_remote_copy(
            src, dst, send, recv, device_id=(j, lax.axis_index("filt")), device_id_type=MESH
        )

    def each_z(self, body):
        zn, my_z = self.zn, self.my_z

        def step(t, carry):
            j = lax.rem(my_z + zn // 2 + (t // 2) * (2 * lax.rem(t, 2) - 1), zn)
            body(j, j)
            return carry

        lax.fori_loop(1, zn, step, 0)

    def swap(self):
        return self.rcopy(self.x_ref.at[pl.ds(self.theirs, self.zn)], self.half_buf, self.sems.at[0, 0],
                          self.sems.at[0, 1], self.other)

    def part_out(self, j, s):
        return self.rcopy(self.half_b.at[j], self.part_buf.at[self.my_z], self.sems.at[1, j],
                          self.sems.at[2, self.my_z], self.mine + j)

    def part_in(self, j, s):
        return self.rcopy(self.half_b.at[s], self.part_buf.at[s], self.sems.at[1, s], self.sems.at[2, s],
                          self.mine + s)

    def sum_out(self, j, s):
        me = self.me
        return self.rcopy(self.out_ref.at[me], self.out_ref.at[me], self.sems.at[3, j], self.sems.at[4, self.my_z],
                          self.mine + j)

    def sum_in(self, j, s):
        c = self.mine + s
        return self.rcopy(self.out_ref.at[c], self.out_ref.at[c], self.sems.at[3, s], self.sems.at[4, s], c)

    def back(self):
        half = pl.ds(self.mine, self.zn)
        return self.rcopy(self.out_ref.at[half], self.out_ref.at[half], self.sems.at[5, 0], self.sems.at[5, 1],
                          self.other)

    def s1_start(self):
        self.swap().start()

    def s1_finish(self):
        self.swap().wait_recv()
        x_ref, half_buf, half_b, mine = self.x_ref, self.half_buf, self.half_b, self.mine

        def add_half(t, carry):
            half_b[t] = (x_ref[mine + t].astype(jnp.float32) + half_buf[t].astype(jnp.float32)).astype(half_b.dtype)
            return carry

        lax.fori_loop(0, self.zn, add_half, 0)
        self.swap().wait_send()

    def s2_start(self):
        self.each_z(lambda j, s: self.part_out(j, s).start())

    def s2_finish(self):
        self.each_z(lambda j, s: self.part_in(j, s).wait_recv())
        zn, my_z, part_buf = self.zn, self.my_z, self.part_buf
        acc = self.x_ref[self.me].astype(jnp.float32) + self.half_buf[my_z].astype(jnp.float32)

        def add_part(k, acc):
            return acc + part_buf[lax.rem(my_z + k, zn)].astype(jnp.float32)

        acc = lax.fori_loop(1, zn, add_part, acc)
        self.out_ref[self.me] = acc.astype(self.out_ref.dtype)
        self.each_z(lambda j, s: self.part_out(j, s).wait_send())

    def s3_start(self):
        self.each_z(lambda j, s: self.sum_out(j, s).start())

    def s3_finish(self):
        self.each_z(lambda j, s: self.sum_in(j, s).wait_recv())
        self.each_z(lambda j, s: self.sum_out(j, s).wait_send())

    def s4_start(self):
        self.back().start()

    def s4_finish(self):
        self.back().wait_recv()
        self.back().wait_send()


def row_sum_kernel(n, xa, xb, oa, ob, *scratch):
    zn = n // 2
    me = lax.axis_index("rows")
    my_z = lax.rem(me, zn)
    mine = (me // zn) * zn

    def dev(j):
        return (j, lax.axis_index("filt"))

    barrier = pltpu.get_barrier_semaphore()
    pl.semaphore_signal(barrier, 1, device_id=dev(lax.rem(me + zn, n)), device_id_type=MESH)

    def greet(k, carry):
        pl.semaphore_signal(barrier, 1, device_id=dev(mine + lax.rem(my_z + k, zn)), device_id_type=MESH)
        return carry

    lax.fori_loop(1, zn, greet, 0)
    pl.semaphore_wait(barrier, zn)
    a = RowSum(n, xa, oa, *scratch[:4])
    b = RowSum(n, xb, ob, *scratch[4:])
    a.s1_start()
    a.s1_finish()
    a.s2_start()
    b.s1_start()
    b.s1_finish()
    b.s2_start()
    a.s2_finish()
    a.s3_start()
    b.s2_finish()
    b.s3_start()
    a.s3_finish()
    a.s4_start()
    b.s3_finish()
    b.s4_start()
    a.s4_finish()
    b.s4_finish()


def row_sum(xa, xb, collective_id):
    n = xa.shape[0]
    zn = n // 2
    spec = pl.BlockSpec(memory_space=pltpu.VMEM)
    scratch = []
    for x in (xa, xb):
        blk = (zn,) + x.shape[1:]
        scratch += [pltpu.VMEM(blk, x.dtype), pltpu.VMEM(blk, x.dtype), pltpu.VMEM(blk, x.dtype),
                    pltpu.SemaphoreType.DMA((6, zn))]
    return pl.pallas_call(
        functools.partial(row_sum_kernel, n),
        out_shape=(jax.ShapeDtypeStruct(xa.shape, xa.dtype), jax.ShapeDtypeStruct(xb.shape, xb.dtype)),
        in_specs=[spec, spec],
        out_specs=(spec, spec),
        scratch_shapes=scratch,
        compiler_params=pltpu.CompilerParams(collective_id=collective_id, has_side_effects=True),
    )(xa, xb)


def row_dev(j):
    return (j, lax.axis_index("filt"))


def filt_dev(j):
    return (lax.axis_index("rows"), j)


def rcopy(src, dst, send, recv, dev):
    return pltpu.make_async_remote_copy(src, dst, send, recv, device_id=dev, device_id_type=MESH)


def each_filt_peer(body):
    nf = lax.axis_size("filt")
    half = nf // 2
    me = lax.axis_index("filt")

    def step(k, carry):
        far = (nf - k) // half
        off = k - 1 - (half - 1) * (1 - far)
        j = lax.rem(me // half + far, 2) * half + lax.rem(lax.rem(me, half) + off, half)
        body(j, j)
        return carry

    lax.fori_loop(1, nf, step, 0)


def enter(with_filt):
    nr = lax.axis_size("rows")
    me = lax.axis_index("rows")
    barrier = pltpu.get_barrier_semaphore()

    @pl.when(me > 0)
    def _():
        pl.semaphore_signal(barrier, 1, device_id=row_dev(me - 1), device_id_type=MESH)

    @pl.when(me < nr - 1)
    def _():
        pl.semaphore_signal(barrier, 1, device_id=row_dev(me + 1), device_id_type=MESH)

    count = (me + nr - 1) // nr + (2 * nr - 2 - me) // nr
    if with_filt:
        each_filt_peer(lambda j, s: pl.semaphore_signal(barrier, 1, device_id=filt_dev(j), device_id_type=MESH))
        count = count + lax.axis_size("filt") - 1
    pl.semaphore_wait(barrier, count)


class Halo:
    def __init__(self, down_src, up_src, from_prev, from_next, sems):
        self.nr = lax.axis_size("rows")
        self.me = lax.axis_index("rows")
        self.down = lambda j: rcopy(down_src, from_prev, sems.at[0], sems.at[1], row_dev(j))
        self.up = lambda j: rcopy(up_src, from_next, sems.at[2], sems.at[3], row_dev(j))
        me, nr = self.me, self.nr

        @pl.when(me < nr - 1)
        def _():
            self.down(me + 1).start()

        @pl.when(me > 0)
        def _():
            self.up(me - 1).start()

        @pl.when(me == 0)
        def _():
            from_prev[...] = jnp.zeros(from_prev.shape, from_prev.dtype)

        @pl.when(me == nr - 1)
        def _():
            from_next[...] = jnp.zeros(from_next.shape, from_next.dtype)

    def arrived(self):
        me, nr = self.me, self.nr

        @pl.when(me > 0)
        def _():
            self.down(me - 1).wait_recv()

        @pl.when(me < nr - 1)
        def _():
            self.up(me + 1).wait_recv()

    def sent(self):
        me, nr = self.me, self.nr

        @pl.when(me > 0)
        def _():
            self.up(me - 1).wait_send()

        @pl.when(me < nr - 1)
        def _():
            self.down(me + 1).wait_send()


def lane_shift(part, offset):
    width = part.shape[1]
    col = lax.broadcasted_iota(jnp.int32, part.shape, 1)
    if offset == 1:
        return jnp.where(col == width - 1, 0.0, pltpu.roll(part, width - 1, 1))
    return jnp.where(col == 0, 0.0, pltpu.roll(part, 1, 1))


def conv_parts(w_ref, x):
    parts = []
    for a in range(3):
        total = None
        for b in range(3):
            part = jnp.dot(w_ref[a * 3 + b], x, preferred_element_type=jnp.float32)
            if b != 1:
                part = lane_shift(part, b - 1)
            total = part if total is None else total + part
        parts.append(total)
    return parts


def filt_gather(src, dst, blk, send, recv):
    mf = lax.axis_index("filt")

    def out(j, s):
        return rcopy(src, dst.at[pl.ds(mf * blk, blk)], send.at[j], recv.at[mf], filt_dev(j))

    def inc(j, s):
        return rcopy(src, dst.at[pl.ds(s * blk, blk)], send.at[s], recv.at[s], filt_dev(s))

    each_filt_peer(lambda j, s: out(j, s).start())
    dst[pl.ds(mf * blk, blk)] = src[...]
    return (lambda: each_filt_peer(lambda j, s: inc(j, s).wait_recv()),
            lambda: each_filt_peer(lambda j, s: out(j, s).wait_send()))


def block_kernel(feat, og, w1r, w2r, w2t, x_ref, h_ref, out_ref, gs_ref, gprev, gnext, gf_ref, fprev, fnext,
                 p0s, p2s, from_prev, from_next, q0s, q2s, qprev, qnext, hsrc, pre1, tbuf, rbuf,
                 hsems, xsend, xrecv, fsend, frecv, sems1, sems2, sems3, tsend, trecv):
    nf = lax.axis_size("filt")
    mf = lax.axis_index("filt")
    blk = feat.shape[0]
    enter(True)
    x_arrived, x_sent = filt_gather(feat, x_ref, blk, xsend, xrecv)
    x_arrived()
    parts = conv_parts(w1r, x_ref[...])
    p0s[...] = parts[0]
    p2s[...] = parts[2]
    halo = Halo(p0s, p2s, from_prev, from_next, hsems)
    halo.arrived()
    pre1[...] = parts[1] + from_prev[...] + from_next[...]
    hsrc[...] = jnp.maximum(pre1[...], 0.0).astype(hsrc.dtype)
    h_arrived, h_sent = filt_gather(hsrc, h_ref, blk, fsend, frecv)
    h_arrived()
    qs = conv_parts(w2r, h_ref[...])
    q0s[...] = qs[0]
    q2s[...] = qs[2]
    halo1 = Halo(q0s, q2s, qprev, qnext, sems1)
    halo1.arrived()
    pre = qs[1] + qprev[...] + qnext[...] + feat[...].astype(jnp.float32)
    out_ref[...] = jnp.maximum(pre, 0.0).astype(out_ref.dtype)
    gs_ref[...] = jnp.where(pre > 0, og[...].astype(jnp.float32), 0.0).astype(gs_ref.dtype)
    halo2 = Halo(gs_ref, gs_ref, gprev, gnext, sems2)
    halo2.arrived()
    rows3 = jnp.concatenate([gnext[...], gs_ref[...], gprev[...]], axis=0)

    def block(t, carry):
        rows = pl.ds(pl.multiple_of(t * blk, blk), blk)
        total = None
        for b in range(3):
            part = jnp.dot(w2t[b, rows, :], rows3, preferred_element_type=jnp.float32)
            if b != 1:
                part = lane_shift(part, 1 - b)
            total = part if total is None else total + part
        tbuf[t] = total.astype(tbuf.dtype)
        return carry

    lax.fori_loop(0, nf, block, 0)

    def out(j, s):
        return rcopy(tbuf.at[j], rbuf.at[mf], tsend.at[j], trecv.at[mf], filt_dev(j))

    def inc(j, s):
        return rcopy(tbuf.at[s], rbuf.at[s], tsend.at[s], trecv.at[s], filt_dev(s))

    each_filt_peer(lambda j, s: out(j, s).start())
    each_filt_peer(lambda j, s: inc(j, s).wait_recv())
    acc = tbuf[mf].astype(jnp.float32)

    def add(k, acc):
        return acc + rbuf[lax.rem(mf + k, nf)].astype(jnp.float32)

    acc = lax.fori_loop(1, nf, add, acc)
    gf_ref[...] = jnp.where(pre1[...] > 0, acc, 0.0).astype(gf_ref.dtype)
    halo3 = Halo(gf_ref, gf_ref, fprev, fnext, sems3)
    halo3.arrived()
    x_sent()
    h_sent()
    each_filt_peer(lambda j, s: out(j, s).wait_send())
    halo.sent()
    halo1.sent()
    halo2.sent()
    halo3.sent()


def call(kernel, args, outs, scratch, collective_id):
    spec = pl.BlockSpec(memory_space=pltpu.VMEM)
    return pl.pallas_call(
        kernel,
        out_shape=tuple(jax.ShapeDtypeStruct(shape, dtype) for shape, dtype in outs),
        in_specs=[spec] * len(args),
        out_specs=tuple(spec for _ in outs),
        scratch_shapes=scratch,
        compiler_params=pltpu.CompilerParams(collective_id=collective_id, has_side_effects=True),
    )(*args)


def exchange(x, axis, mode, collective_id, out_dtype=None):
    n = lax.axis_size(axis)
    out_dtype = out_dtype or x.dtype
    sems = [pltpu.SemaphoreType.DMA((n,)), pltpu.SemaphoreType.DMA((n,))]
    if mode == "ag":
        out_shape = (n,) + x.shape
        scratch = sems
    elif mode == "rs":
        out_shape = x.shape[1:]
        scratch = [pltpu.VMEM(x.shape, x.dtype)] + sems
    else:
        out_shape = x.shape
        scratch = [pltpu.VMEM(x.shape, x.dtype)] + sems + sems
    return pl.pallas_call(
        functools.partial(exchange_kernel, axis, n, mode),
        out_shape=jax.ShapeDtypeStruct(out_shape, out_dtype),
        in_specs=[pl.BlockSpec(memory_space=pltpu.VMEM)],
        out_specs=pl.BlockSpec(memory_space=pltpu.VMEM),
        scratch_shapes=scratch,
        compiler_params=pltpu.CompilerParams(collective_id=collective_id, has_side_effects=True),
    )(x)


def shift_cols(value, offset):
    if offset == 0:
        return value
    pad = [(0, 0)] * (value.ndim - 1)
    if offset > 0:
        return jnp.pad(value[..., offset:], pad + [(0, offset)])
    return jnp.pad(value[..., :offset], pad + [(-offset, 0)])


def conv_row(weight, row):
    o = weight.shape[0]
    flat = weight.reshape(o, 9, weight.shape[3])
    parts = jnp.einsum("oki,iw->kow", flat, row, preferred_element_type=jnp.float32)
    return [sum(shift_cols(parts[a * 3 + b], b - 1) for b in range(3)) for a in range(3)]


def weight_terms(rows3, full_row):
    cols = []
    for b in range(3):
        moved = shift_cols(rows3, 1 - b)
        cols.append(jnp.einsum("aow,iw->oai", moved, full_row, preferred_element_type=jnp.float32))
    return jnp.stack(cols, axis=2)


def hidden_terms(weight, rows3):
    total = None
    for b in range(3):
        part = jnp.einsum("oai,aow->iw", weight[:, :, b, :], rows3, preferred_element_type=jnp.float32)
        part = shift_cols(part, 1 - b)
        total = part if total is None else total + part
    return total


def per_device(features, first_weight, second_weight, out_grad):
    feat = features[:, 0, :]
    og = out_grad[:, 0, :]
    n_filt = lax.axis_size("filt")
    blk = feat.shape
    f32, bf16 = jnp.float32, jnp.bfloat16
    o, _, _, i_ch = first_weight.shape
    w1r = first_weight.transpose(1, 2, 0, 3).reshape(9, o, i_ch)
    w2r = second_weight.transpose(1, 2, 0, 3).reshape(9, o, i_ch)
    w2t = second_weight.transpose(2, 3, 1, 0).reshape(3, i_ch, 3 * o)
    sem = pltpu.SemaphoreType.DMA
    full = (n_filt * blk[0], blk[1])
    x_row, h_row, block_out, grad_second, gs_prev, gs_next, grad_first, gf_prev, gf_next = call(
        block_kernel,
        (feat, og, w1r, w2r, w2t),
        [(full, bf16), (full, bf16)] + [(blk, bf16)] * 7,
        [pltpu.VMEM(blk, f32)] * 8 + [pltpu.VMEM(blk, bf16), pltpu.VMEM(blk, f32),
                                      pltpu.VMEM((n_filt,) + blk, bf16), pltpu.VMEM((n_filt,) + blk, bf16)]
        + [sem((4,))] + [sem((n_filt,))] * 4 + [sem((4,))] * 3 + [sem((n_filt,))] * 2,
        2,
    )
    gs3 = jnp.stack([gs_next, grad_second, gs_prev])
    gf3 = jnp.stack([gf_next, grad_first, gf_prev])
    second_local = weight_terms(gs3, h_row)
    first_local = weight_terms(gf3, x_row)
    n_rows = lax.axis_size("rows")
    summed_first, summed_second = row_sum(
        first_local.astype(bf16).reshape(n_rows, -1, 128), second_local.astype(bf16).reshape(n_rows, -1, 128), 0
    )
    first_grad = summed_first.astype(f32).reshape(first_local.shape)
    second_grad = summed_second.astype(f32).reshape(second_local.shape)
    return (block_out[:, None, :], first_grad, second_grad)


def solution(mesh):
    in_specs = (
        P("filt", "rows", None),
        P("filt", None, None, None),
        P("filt", None, None, None),
        P("filt", "rows", None),
    )
    out_specs = (P("filt", "rows", None), P("filt", None, None, None), P("filt", None, None, None))
    return jax.shard_map(
        per_device, mesh=mesh, in_specs=in_specs, out_specs=out_specs, check_vma=False
    )
```

```python
import functools

import jax
import jax.numpy as jnp
from jax import lax
from jax.experimental import pallas as pl
from jax.experimental.pallas import tpu as pltpu
from jax.sharding import PartitionSpec as P

MESH = pl.DeviceIdType.MESH


def peer_id(axis, j):
    if axis == "rows":
        return (j, lax.axis_index("filt"))
    return (lax.axis_index("rows"), j)


def exchange_kernel(axis, n, mode, *refs):
    me = lax.axis_index(axis)

    def each_peer(body):
        def step(k, carry):
            body(lax.rem(me + k, n), lax.rem(me + n - k, n))
            return carry

        lax.fori_loop(1, n, step, 0)

    barrier = pltpu.get_barrier_semaphore()

    def greet(j, s):
        pl.semaphore_signal(barrier, 1, device_id=peer_id(axis, j), device_id_type=MESH)

    each_peer(greet)
    pl.semaphore_wait(barrier, n - 1)

    def gather(src, out_ref, send, recv):
        def copy(j, s):
            return pltpu.make_async_remote_copy(
                src, out_ref.at[me], send.at[j], recv.at[me], device_id=peer_id(axis, j), device_id_type=MESH
            )

        def incoming(j, s):
            return pltpu.make_async_remote_copy(
                src, out_ref.at[s], send.at[s], recv.at[s], device_id=peer_id(axis, s), device_id_type=MESH
            )

        each_peer(lambda j, s: copy(j, s).start())
        return copy, incoming

    def reduce(x_ref, buf, send, recv):
        def copy(j, s):
            return pltpu.make_async_remote_copy(
                x_ref.at[j], buf.at[me], send.at[j], recv.at[me], device_id=peer_id(axis, j), device_id_type=MESH
            )

        def incoming(j, s):
            return pltpu.make_async_remote_copy(
                x_ref.at[s], buf.at[s], send.at[s], recv.at[s], device_id=peer_id(axis, s), device_id_type=MESH
            )

        each_peer(lambda j, s: copy(j, s).start())
        each_peer(lambda j, s: incoming(j, s).wait_recv())
        acc = x_ref[me].astype(jnp.float32)

        def add(k, acc):
            return acc + buf[lax.rem(me + k, n)].astype(jnp.float32)

        acc = lax.fori_loop(1, n, add, acc)
        each_peer(lambda j, s: copy(j, s).wait_send())
        return acc

    if mode == "ag":
        x_ref, out_ref, send, recv = refs
        copy, incoming = gather(x_ref, out_ref, send, recv)
        out_ref[me] = x_ref[...]
        each_peer(lambda j, s: incoming(j, s).wait_recv())
        each_peer(lambda j, s: copy(j, s).wait_send())
    elif mode == "rs":
        x_ref, out_ref, buf, send, recv = refs
        out_ref[...] = reduce(x_ref, buf, send, recv).astype(out_ref.dtype)
    else:
        x_ref, out_ref, buf, send, recv, send2, recv2 = refs
        out_ref[me] = reduce(x_ref, buf, send, recv).astype(out_ref.dtype)
        copy, incoming = gather(out_ref.at[me], out_ref, send2, recv2)
        each_peer(lambda j, s: incoming(j, s).wait_recv())
        each_peer(lambda j, s: copy(j, s).wait_send())


class RowSum:
    def __init__(self, n, x_ref, out_ref, half_buf, half_b, part_buf, sems):
        self.zn = zn = n // 2
        self.me = me = lax.axis_index("rows")
        my_y, self.my_z = me // zn, lax.rem(me, zn)
        self.other = lax.rem(me + zn, n)
        self.mine, self.theirs = my_y * zn, (1 - my_y) * zn
        self.x_ref, self.out_ref, self.half_buf, self.half_b, self.part_buf, self.sems = (
            x_ref, out_ref, half_buf, half_b, part_buf, sems)

    def rcopy(self, src, dst, send, recv, j):
        return pltpu.make_async_remote_copy(
            src, dst, send, recv, device_id=(j, lax.axis_index("filt")), device_id_type=MESH
        )

    def each_z(self, body):
        zn, my_z = self.zn, self.my_z

        def step(t, carry):
            j = lax.rem(my_z + zn // 2 + (t // 2) * (2 * lax.rem(t, 2) - 1), zn)
            body(j, j)
            return carry

        lax.fori_loop(1, zn, step, 0)

    def swap(self):
        return self.rcopy(self.x_ref.at[pl.ds(self.theirs, self.zn)], self.half_buf, self.sems.at[0, 0],
                          self.sems.at[0, 1], self.other)

    def part_out(self, j, s):
        return self.rcopy(self.half_b.at[j], self.part_buf.at[self.my_z], self.sems.at[1, j],
                          self.sems.at[2, self.my_z], self.mine + j)

    def part_in(self, j, s):
        return self.rcopy(self.half_b.at[s], self.part_buf.at[s], self.sems.at[1, s], self.sems.at[2, s],
                          self.mine + s)

    def sum_out(self, j, s):
        me = self.me
        return self.rcopy(self.out_ref.at[me], self.out_ref.at[me], self.sems.at[3, j], self.sems.at[4, self.my_z],
                          self.mine + j)

    def sum_in(self, j, s):
        c = self.mine + s
        return self.rcopy(self.out_ref.at[c], self.out_ref.at[c], self.sems.at[3, s], self.sems.at[4, s], c)

    def back(self):
        half = pl.ds(self.mine, self.zn)
        return self.rcopy(self.out_ref.at[half], self.out_ref.at[half], self.sems.at[5, 0], self.sems.at[5, 1],
                          self.other)

    def s1_start(self):
        self.swap().start()

    def s1_finish(self):
        self.swap().wait_recv()
        x_ref, half_buf, half_b, mine = self.x_ref, self.half_buf, self.half_b, self.mine

        def add_half(t, carry):
            half_b[t] = (x_ref[mine + t].astype(jnp.float32) + half_buf[t].astype(jnp.float32)).astype(half_b.dtype)
            return carry

        lax.fori_loop(0, self.zn, add_half, 0)
        self.swap().wait_send()

    def s2_start(self):
        self.each_z(lambda j, s: self.part_out(j, s).start())

    def s2_finish(self):
        self.each_z(lambda j, s: self.part_in(j, s).wait_recv())
        zn, my_z, part_buf = self.zn, self.my_z, self.part_buf
        acc = self.x_ref[self.me].astype(jnp.float32) + self.half_buf[my_z].astype(jnp.float32)

        def add_part(k, acc):
            return acc + part_buf[lax.rem(my_z + k, zn)].astype(jnp.float32)

        acc = lax.fori_loop(1, zn, add_part, acc)
        self.out_ref[self.me] = acc.astype(self.out_ref.dtype)
        self.each_z(lambda j, s: self.part_out(j, s).wait_send())

    def s3_start(self):
        self.each_z(lambda j, s: self.sum_out(j, s).start())

    def s3_finish(self):
        self.each_z(lambda j, s: self.sum_in(j, s).wait_recv())
        self.each_z(lambda j, s: self.sum_out(j, s).wait_send())

    def s4_start(self):
        self.back().start()

    def s4_finish(self):
        self.back().wait_recv()
        self.back().wait_send()


def row_sum_kernel(n, xa, xb, oa, ob, *scratch):
    zn = n // 2
    me = lax.axis_index("rows")
    my_z = lax.rem(me, zn)
    mine = (me // zn) * zn

    def dev(j):
        return (j, lax.axis_index("filt"))

    barrier = pltpu.get_barrier_semaphore()
    pl.semaphore_signal(barrier, 1, device_id=dev(lax.rem(me + zn, n)), device_id_type=MESH)

    def greet(k, carry):
        pl.semaphore_signal(barrier, 1, device_id=dev(mine + lax.rem(my_z + k, zn)), device_id_type=MESH)
        return carry

    lax.fori_loop(1, zn, greet, 0)
    pl.semaphore_wait(barrier, zn)
    a = RowSum(n, xa, oa, *scratch[:4])
    b = RowSum(n, xb, ob, *scratch[4:])
    a.s1_start()
    a.s1_finish()
    a.s2_start()
    b.s1_start()
    b.s1_finish()
    b.s2_start()
    a.s2_finish()
    a.s3_start()
    b.s2_finish()
    b.s3_start()
    a.s3_finish()
    a.s4_start()
    b.s3_finish()
    b.s4_start()
    a.s4_finish()
    b.s4_finish()


def row_sum(xa, xb, collective_id):
    n = xa.shape[0]
    zn = n // 2
    spec = pl.BlockSpec(memory_space=pltpu.VMEM)
    scratch = []
    for x in (xa, xb):
        blk = (zn,) + x.shape[1:]
        scratch += [pltpu.VMEM(blk, x.dtype), pltpu.VMEM(blk, x.dtype), pltpu.VMEM(blk, x.dtype),
                    pltpu.SemaphoreType.DMA((6, zn))]
    return pl.pallas_call(
        functools.partial(row_sum_kernel, n),
        out_shape=(jax.ShapeDtypeStruct(xa.shape, xa.dtype), jax.ShapeDtypeStruct(xb.shape, xb.dtype)),
        in_specs=[spec, spec],
        out_specs=(spec, spec),
        scratch_shapes=scratch,
        compiler_params=pltpu.CompilerParams(collective_id=collective_id, has_side_effects=True),
    )(xa, xb)


def row_dev(j):
    return (j, lax.axis_index("filt"))


def filt_dev(j):
    return (lax.axis_index("rows"), j)


def rcopy(src, dst, send, recv, dev):
    return pltpu.make_async_remote_copy(src, dst, send, recv, device_id=dev, device_id_type=MESH)


def each_filt_peer(body):
    nf = lax.axis_size("filt")
    half = nf // 2
    me = lax.axis_index("filt")

    def step(k, carry):
        far = (nf - k) // half
        off = k - 1 - (half - 1) * (1 - far)
        j = lax.rem(me // half + far, 2) * half + lax.rem(lax.rem(me, half) + off, half)
        body(j, j)
        return carry

    lax.fori_loop(1, nf, step, 0)


def enter(with_filt):
    nr = lax.axis_size("rows")
    me = lax.axis_index("rows")
    barrier = pltpu.get_barrier_semaphore()

    @pl.when(me > 0)
    def _():
        pl.semaphore_signal(barrier, 1, device_id=row_dev(me - 1), device_id_type=MESH)

    @pl.when(me < nr - 1)
    def _():
        pl.semaphore_signal(barrier, 1, device_id=row_dev(me + 1), device_id_type=MESH)

    count = (me + nr - 1) // nr + (2 * nr - 2 - me) // nr
    if with_filt:
        each_filt_peer(lambda j, s: pl.semaphore_signal(barrier, 1, device_id=filt_dev(j), device_id_type=MESH))
        count = count + lax.axis_size("filt") - 1
    pl.semaphore_wait(barrier, count)


class Halo:
    def __init__(self, down_src, up_src, from_prev, from_next, sems):
        self.nr = lax.axis_size("rows")
        self.me = lax.axis_index("rows")
        self.down = lambda j: rcopy(down_src, from_prev, sems.at[0], sems.at[1], row_dev(j))
        self.up = lambda j: rcopy(up_src, from_next, sems.at[2], sems.at[3], row_dev(j))
        me, nr = self.me, self.nr

        @pl.when(me < nr - 1)
        def _():
            self.down(me + 1).start()

        @pl.when(me > 0)
        def _():
            self.up(me - 1).start()

        @pl.when(me == 0)
        def _():
            from_prev[...] = jnp.zeros(from_prev.shape, from_prev.dtype)

        @pl.when(me == nr - 1)
        def _():
            from_next[...] = jnp.zeros(from_next.shape, from_next.dtype)

    def arrived(self):
        me, nr = self.me, self.nr

        @pl.when(me > 0)
        def _():
            self.down(me - 1).wait_recv()

        @pl.when(me < nr - 1)
        def _():
            self.up(me + 1).wait_recv()

    def sent(self):
        me, nr = self.me, self.nr

        @pl.when(me > 0)
        def _():
            self.up(me - 1).wait_send()

        @pl.when(me < nr - 1)
        def _():
            self.down(me + 1).wait_send()


def lane_shift(part, offset):
    width = part.shape[1]
    col = lax.broadcasted_iota(jnp.int32, part.shape, 1)
    if offset == 1:
        return jnp.where(col == width - 1, 0.0, pltpu.roll(part, width - 1, 1))
    return jnp.where(col == 0, 0.0, pltpu.roll(part, 1, 1))


def conv_parts(w_ref, x):
    parts = []
    for a in range(3):
        total = None
        for b in range(3):
            part = jnp.dot(w_ref[a * 3 + b], x, preferred_element_type=jnp.float32)
            if b != 1:
                part = lane_shift(part, b - 1)
            total = part if total is None else total + part
        parts.append(total)
    return parts


def filt_gather(src, dst, blk, send, recv):
    mf = lax.axis_index("filt")

    def out(j, s):
        return rcopy(src, dst.at[pl.ds(mf * blk, blk)], send.at[j], recv.at[mf], filt_dev(j))

    def inc(j, s):
        return rcopy(src, dst.at[pl.ds(s * blk, blk)], send.at[s], recv.at[s], filt_dev(s))

    each_filt_peer(lambda j, s: out(j, s).start())
    dst[pl.ds(mf * blk, blk)] = src[...]
    return (lambda: each_filt_peer(lambda j, s: inc(j, s).wait_recv()),
            lambda: each_filt_peer(lambda j, s: out(j, s).wait_send()))


def weight_rows(rows3, full, wt_ref):
    for b in range(3):
        moved = rows3
        if b != 1:
            moved = lane_shift(rows3.astype(jnp.float32), 1 - b).astype(rows3.dtype)
        wt_ref[b] = lax.dot_general(moved, full, (((1,), (1,)), ((), ())), preferred_element_type=jnp.float32)


def block_kernel(feat, og, w1r, w2r, w2t, x_ref, h_ref, out_ref, gs_ref, gprev, gnext, gf_ref, fprev, fnext,
                 wt_first, wt_second, p0s, p2s, from_prev, from_next, q0s, q2s, qprev, qnext, hsrc, pre1, tbuf, rbuf,
                 hsems, xsend, xrecv, fsend, frecv, sems1, sems2, sems3, tsend, trecv):
    nf = lax.axis_size("filt")
    mf = lax.axis_index("filt")
    blk = feat.shape[0]
    enter(True)
    x_arrived, x_sent = filt_gather(feat, x_ref, blk, xsend, xrecv)
    x_arrived()
    parts = conv_parts(w1r, x_ref[...])
    p0s[...] = parts[0]
    p2s[...] = parts[2]
    halo = Halo(p0s, p2s, from_prev, from_next, hsems)
    halo.arrived()
    pre1[...] = parts[1] + from_prev[...] + from_next[...]
    hsrc[...] = jnp.maximum(pre1[...], 0.0).astype(hsrc.dtype)
    h_arrived, h_sent = filt_gather(hsrc, h_ref, blk, fsend, frecv)
    h_arrived()
    qs = conv_parts(w2r, h_ref[...])
    q0s[...] = qs[0]
    q2s[...] = qs[2]
    halo1 = Halo(q0s, q2s, qprev, qnext, sems1)
    halo1.arrived()
    pre = qs[1] + qprev[...] + qnext[...] + feat[...].astype(jnp.float32)
    out_ref[...] = jnp.maximum(pre, 0.0).astype(out_ref.dtype)
    gs_ref[...] = jnp.where(pre > 0, og[...].astype(jnp.float32), 0.0).astype(gs_ref.dtype)
    halo2 = Halo(gs_ref, gs_ref, gprev, gnext, sems2)
    halo2.arrived()
    rows3 = jnp.concatenate([gnext[...], gs_ref[...], gprev[...]], axis=0)

    def block(t, carry):
        rows = pl.ds(pl.multiple_of(t * blk, blk), blk)
        total = None
        for b in range(3):
            part = jnp.dot(w2t[b, rows, :], rows3, preferred_element_type=jnp.float32)
            if b != 1:
                part = lane_shift(part, 1 - b)
            total = part if total is None else total + part
        tbuf[t] = total.astype(tbuf.dtype)
        return carry

    lax.fori_loop(0, nf, block, 0)

    def out(j, s):
        return rcopy(tbuf.at[j], rbuf.at[mf], tsend.at[j], trecv.at[mf], filt_dev(j))

    weight_rows(rows3, h_ref[...], wt_second)

    def inc(j, s):
        return rcopy(tbuf.at[s], rbuf.at[s], tsend.at[s], trecv.at[s], filt_dev(s))

    each_filt_peer(lambda j, s: out(j, s).start())
    each_filt_peer(lambda j, s: inc(j, s).wait_recv())
    acc = tbuf[mf].astype(jnp.float32)

    def add(k, acc):
        return acc + rbuf[lax.rem(mf + k, nf)].astype(jnp.float32)

    acc = lax.fori_loop(1, nf, add, acc)
    gf_ref[...] = jnp.where(pre1[...] > 0, acc, 0.0).astype(gf_ref.dtype)
    halo3 = Halo(gf_ref, gf_ref, fprev, fnext, sems3)
    halo3.arrived()
    weight_rows(jnp.concatenate([fnext[...], gf_ref[...], fprev[...]], axis=0), x_ref[...], wt_first)
    x_sent()
    h_sent()
    each_filt_peer(lambda j, s: out(j, s).wait_send())
    halo.sent()
    halo1.sent()
    halo2.sent()
    halo3.sent()


def call(kernel, args, outs, scratch, collective_id):
    spec = pl.BlockSpec(memory_space=pltpu.VMEM)
    return pl.pallas_call(
        kernel,
        out_shape=tuple(jax.ShapeDtypeStruct(shape, dtype) for shape, dtype in outs),
        in_specs=[spec] * len(args),
        out_specs=tuple(spec for _ in outs),
        scratch_shapes=scratch,
        compiler_params=pltpu.CompilerParams(collective_id=collective_id, has_side_effects=True),
    )(*args)


def exchange(x, axis, mode, collective_id, out_dtype=None):
    n = lax.axis_size(axis)
    out_dtype = out_dtype or x.dtype
    sems = [pltpu.SemaphoreType.DMA((n,)), pltpu.SemaphoreType.DMA((n,))]
    if mode == "ag":
        out_shape = (n,) + x.shape
        scratch = sems
    elif mode == "rs":
        out_shape = x.shape[1:]
        scratch = [pltpu.VMEM(x.shape, x.dtype)] + sems
    else:
        out_shape = x.shape
        scratch = [pltpu.VMEM(x.shape, x.dtype)] + sems + sems
    return pl.pallas_call(
        functools.partial(exchange_kernel, axis, n, mode),
        out_shape=jax.ShapeDtypeStruct(out_shape, out_dtype),
        in_specs=[pl.BlockSpec(memory_space=pltpu.VMEM)],
        out_specs=pl.BlockSpec(memory_space=pltpu.VMEM),
        scratch_shapes=scratch,
        compiler_params=pltpu.CompilerParams(collective_id=collective_id, has_side_effects=True),
    )(x)


def shift_cols(value, offset):
    if offset == 0:
        return value
    pad = [(0, 0)] * (value.ndim - 1)
    if offset > 0:
        return jnp.pad(value[..., offset:], pad + [(0, offset)])
    return jnp.pad(value[..., :offset], pad + [(-offset, 0)])


def conv_row(weight, row):
    o = weight.shape[0]
    flat = weight.reshape(o, 9, weight.shape[3])
    parts = jnp.einsum("oki,iw->kow", flat, row, preferred_element_type=jnp.float32)
    return [sum(shift_cols(parts[a * 3 + b], b - 1) for b in range(3)) for a in range(3)]


def weight_terms(rows3, full_row):
    cols = []
    for b in range(3):
        moved = shift_cols(rows3, 1 - b)
        cols.append(jnp.einsum("aow,iw->oai", moved, full_row, preferred_element_type=jnp.float32))
    return jnp.stack(cols, axis=2)


def hidden_terms(weight, rows3):
    total = None
    for b in range(3):
        part = jnp.einsum("oai,aow->iw", weight[:, :, b, :], rows3, preferred_element_type=jnp.float32)
        part = shift_cols(part, 1 - b)
        total = part if total is None else total + part
    return total


def per_device(features, first_weight, second_weight, out_grad):
    feat = features[:, 0, :]
    og = out_grad[:, 0, :]
    n_filt = lax.axis_size("filt")
    blk = feat.shape
    f32, bf16 = jnp.float32, jnp.bfloat16
    o, _, _, i_ch = first_weight.shape
    w1r = first_weight.transpose(1, 2, 0, 3).reshape(9, o, i_ch)
    w2r = second_weight.transpose(1, 2, 0, 3).reshape(9, o, i_ch)
    w2t = second_weight.transpose(2, 3, 1, 0).reshape(3, i_ch, 3 * o)
    sem = pltpu.SemaphoreType.DMA
    full = (n_filt * blk[0], blk[1])
    wt = (3, 3 * o, i_ch)
    _, _, block_out, _, _, _, _, _, _, wt_first, wt_second = call(
        block_kernel,
        (feat, og, w1r, w2r, w2t),
        [(full, bf16), (full, bf16)] + [(blk, bf16)] * 7 + [(wt, f32), (wt, f32)],
        [pltpu.VMEM(blk, f32)] * 8 + [pltpu.VMEM(blk, bf16), pltpu.VMEM(blk, f32),
                                      pltpu.VMEM((n_filt,) + blk, bf16), pltpu.VMEM((n_filt,) + blk, bf16)]
        + [sem((4,))] + [sem((n_filt,))] * 4 + [sem((4,))] * 3 + [sem((n_filt,))] * 2,
        2,
    )
    second_local = wt_second.reshape(3, 3, o, i_ch).transpose(2, 1, 0, 3)
    first_local = wt_first.reshape(3, 3, o, i_ch).transpose(2, 1, 0, 3)
    n_rows = lax.axis_size("rows")
    summed_first, summed_second = row_sum(
        first_local.astype(bf16).reshape(n_rows, -1, 128), second_local.astype(bf16).reshape(n_rows, -1, 128), 0
    )
    first_grad = summed_first.astype(f32).reshape(first_local.shape)
    second_grad = summed_second.astype(f32).reshape(second_local.shape)
    return (block_out[:, None, :], first_grad, second_grad)


def solution(mesh):
    in_specs = (
        P("filt", "rows", None),
        P("filt", None, None, None),
        P("filt", None, None, None),
        P("filt", "rows", None),
    )
    out_specs = (P("filt", "rows", None), P("filt", None, None, None), P("filt", None, None, None))
    return jax.shard_map(
        per_device, mesh=mesh, in_specs=in_specs, out_specs=out_specs, check_vma=False
    )
```

```python
import functools

import jax
import jax.numpy as jnp
from jax import lax
from jax.experimental import pallas as pl
from jax.experimental.pallas import tpu as pltpu
from jax.sharding import PartitionSpec as P

MESH = pl.DeviceIdType.MESH


def peer_id(axis, j):
    if axis == "rows":
        return (j, lax.axis_index("filt"))
    return (lax.axis_index("rows"), j)


def exchange_kernel(axis, n, mode, *refs):
    me = lax.axis_index(axis)

    def each_peer(body):
        def step(k, carry):
            body(lax.rem(me + k, n), lax.rem(me + n - k, n))
            return carry

        lax.fori_loop(1, n, step, 0)

    barrier = pltpu.get_barrier_semaphore()

    def greet(j, s):
        pl.semaphore_signal(barrier, 1, device_id=peer_id(axis, j), device_id_type=MESH)

    each_peer(greet)
    pl.semaphore_wait(barrier, n - 1)

    def gather(src, out_ref, send, recv):
        def copy(j, s):
            return pltpu.make_async_remote_copy(
                src, out_ref.at[me], send.at[j], recv.at[me], device_id=peer_id(axis, j), device_id_type=MESH
            )

        def incoming(j, s):
            return pltpu.make_async_remote_copy(
                src, out_ref.at[s], send.at[s], recv.at[s], device_id=peer_id(axis, s), device_id_type=MESH
            )

        each_peer(lambda j, s: copy(j, s).start())
        return copy, incoming

    def reduce(x_ref, buf, send, recv):
        def copy(j, s):
            return pltpu.make_async_remote_copy(
                x_ref.at[j], buf.at[me], send.at[j], recv.at[me], device_id=peer_id(axis, j), device_id_type=MESH
            )

        def incoming(j, s):
            return pltpu.make_async_remote_copy(
                x_ref.at[s], buf.at[s], send.at[s], recv.at[s], device_id=peer_id(axis, s), device_id_type=MESH
            )

        each_peer(lambda j, s: copy(j, s).start())
        each_peer(lambda j, s: incoming(j, s).wait_recv())
        acc = x_ref[me].astype(jnp.float32)

        def add(k, acc):
            return acc + buf[lax.rem(me + k, n)].astype(jnp.float32)

        acc = lax.fori_loop(1, n, add, acc)
        each_peer(lambda j, s: copy(j, s).wait_send())
        return acc

    if mode == "ag":
        x_ref, out_ref, send, recv = refs
        copy, incoming = gather(x_ref, out_ref, send, recv)
        out_ref[me] = x_ref[...]
        each_peer(lambda j, s: incoming(j, s).wait_recv())
        each_peer(lambda j, s: copy(j, s).wait_send())
    elif mode == "rs":
        x_ref, out_ref, buf, send, recv = refs
        out_ref[...] = reduce(x_ref, buf, send, recv).astype(out_ref.dtype)
    else:
        x_ref, out_ref, buf, send, recv, send2, recv2 = refs
        out_ref[me] = reduce(x_ref, buf, send, recv).astype(out_ref.dtype)
        copy, incoming = gather(out_ref.at[me], out_ref, send2, recv2)
        each_peer(lambda j, s: incoming(j, s).wait_recv())
        each_peer(lambda j, s: copy(j, s).wait_send())


class RowSum:
    def __init__(self, n, x_ref, out_ref, half_buf, half_b, part_buf, sems):
        self.zn = zn = n // 2
        self.me = me = lax.axis_index("rows")
        my_y, self.my_z = me // zn, lax.rem(me, zn)
        self.other = lax.rem(me + zn, n)
        self.mine, self.theirs = my_y * zn, (1 - my_y) * zn
        self.x_ref, self.out_ref, self.half_buf, self.half_b, self.part_buf, self.sems = (
            x_ref, out_ref, half_buf, half_b, part_buf, sems)

    def rcopy(self, src, dst, send, recv, j):
        return pltpu.make_async_remote_copy(
            src, dst, send, recv, device_id=(j, lax.axis_index("filt")), device_id_type=MESH
        )

    def each_z(self, body):
        zn, my_z = self.zn, self.my_z

        def step(t, carry):
            j = lax.rem(my_z + zn // 2 + (t // 2) * (2 * lax.rem(t, 2) - 1), zn)
            body(j, j)
            return carry

        lax.fori_loop(1, zn, step, 0)

    def swap(self):
        return self.rcopy(self.x_ref.at[pl.ds(self.theirs, self.zn)], self.half_buf, self.sems.at[0, 0],
                          self.sems.at[0, 1], self.other)

    def part_out(self, j, s):
        return self.rcopy(self.half_b.at[j], self.part_buf.at[self.my_z], self.sems.at[1, j],
                          self.sems.at[2, self.my_z], self.mine + j)

    def part_in(self, j, s):
        return self.rcopy(self.half_b.at[s], self.part_buf.at[s], self.sems.at[1, s], self.sems.at[2, s],
                          self.mine + s)

    def sum_out(self, j, s):
        me = self.me
        return self.rcopy(self.out_ref.at[me], self.out_ref.at[me], self.sems.at[3, j], self.sems.at[4, self.my_z],
                          self.mine + j)

    def sum_in(self, j, s):
        c = self.mine + s
        return self.rcopy(self.out_ref.at[c], self.out_ref.at[c], self.sems.at[3, s], self.sems.at[4, s], c)

    def back(self):
        half = pl.ds(self.mine, self.zn)
        return self.rcopy(self.out_ref.at[half], self.out_ref.at[half], self.sems.at[5, 0], self.sems.at[5, 1],
                          self.other)

    def s1_start(self):
        self.swap().start()

    def s1_finish(self):
        self.swap().wait_recv()
        x_ref, half_buf, half_b, mine = self.x_ref, self.half_buf, self.half_b, self.mine

        def add_half(t, carry):
            half_b[t] = (x_ref[mine + t].astype(jnp.float32) + half_buf[t].astype(jnp.float32)).astype(half_b.dtype)
            return carry

        lax.fori_loop(0, self.zn, add_half, 0)
        self.swap().wait_send()

    def s2_start(self):
        self.each_z(lambda j, s: self.part_out(j, s).start())

    def s2_finish(self):
        self.each_z(lambda j, s: self.part_in(j, s).wait_recv())
        zn, my_z, part_buf = self.zn, self.my_z, self.part_buf
        acc = self.x_ref[self.me].astype(jnp.float32) + self.half_buf[my_z].astype(jnp.float32)

        def add_part(k, acc):
            return acc + part_buf[lax.rem(my_z + k, zn)].astype(jnp.float32)

        acc = lax.fori_loop(1, zn, add_part, acc)
        self.out_ref[self.me] = acc.astype(self.out_ref.dtype)
        self.each_z(lambda j, s: self.part_out(j, s).wait_send())

    def s3_start(self):
        self.each_z(lambda j, s: self.sum_out(j, s).start())

    def s3_finish(self):
        self.each_z(lambda j, s: self.sum_in(j, s).wait_recv())
        self.each_z(lambda j, s: self.sum_out(j, s).wait_send())

    def s4_start(self):
        self.back().start()

    def s4_finish(self):
        self.back().wait_recv()
        self.back().wait_send()


def row_sum_kernel(n, xa, xb, oa, ob, *scratch):
    zn = n // 2
    me = lax.axis_index("rows")
    my_z = lax.rem(me, zn)
    mine = (me // zn) * zn

    def dev(j):
        return (j, lax.axis_index("filt"))

    barrier = pltpu.get_barrier_semaphore()
    pl.semaphore_signal(barrier, 1, device_id=dev(lax.rem(me + zn, n)), device_id_type=MESH)

    def greet(k, carry):
        pl.semaphore_signal(barrier, 1, device_id=dev(mine + lax.rem(my_z + k, zn)), device_id_type=MESH)
        return carry

    lax.fori_loop(1, zn, greet, 0)
    pl.semaphore_wait(barrier, zn)
    a = RowSum(n, xa, oa, *scratch[:4])
    b = RowSum(n, xb, ob, *scratch[4:])
    a.s1_start()
    a.s1_finish()
    a.s2_start()
    b.s1_start()
    b.s1_finish()
    b.s2_start()
    a.s2_finish()
    a.s3_start()
    b.s2_finish()
    b.s3_start()
    a.s3_finish()
    a.s4_start()
    b.s3_finish()
    b.s4_start()
    a.s4_finish()
    b.s4_finish()


def row_sum(xa, xb, collective_id):
    n = xa.shape[0]
    zn = n // 2
    spec = pl.BlockSpec(memory_space=pltpu.VMEM)
    scratch = []
    for x in (xa, xb):
        blk = (zn,) + x.shape[1:]
        scratch += [pltpu.VMEM(blk, x.dtype), pltpu.VMEM(blk, x.dtype), pltpu.VMEM(blk, x.dtype),
                    pltpu.SemaphoreType.DMA((6, zn))]
    return pl.pallas_call(
        functools.partial(row_sum_kernel, n),
        out_shape=(jax.ShapeDtypeStruct(xa.shape, xa.dtype), jax.ShapeDtypeStruct(xb.shape, xb.dtype)),
        in_specs=[spec, spec],
        out_specs=(spec, spec),
        scratch_shapes=scratch,
        compiler_params=pltpu.CompilerParams(collective_id=collective_id, has_side_effects=True),
    )(xa, xb)


def row_dev(j):
    return (j, lax.axis_index("filt"))


def filt_dev(j):
    return (lax.axis_index("rows"), j)


def rcopy(src, dst, send, recv, dev):
    return pltpu.make_async_remote_copy(src, dst, send, recv, device_id=dev, device_id_type=MESH)


def each_filt_peer(body):
    nf = lax.axis_size("filt")
    half = nf // 2
    me = lax.axis_index("filt")

    def step(k, carry):
        far = (nf - k) // half
        off = k - 1 - (half - 1) * (1 - far)
        j = lax.rem(me // half + far, 2) * half + lax.rem(lax.rem(me, half) + off, half)
        body(j, j)
        return carry

    lax.fori_loop(1, nf, step, 0)


def enter(with_filt):
    nr = lax.axis_size("rows")
    me = lax.axis_index("rows")
    barrier = pltpu.get_barrier_semaphore()

    @pl.when(me > 0)
    def _():
        pl.semaphore_signal(barrier, 1, device_id=row_dev(me - 1), device_id_type=MESH)

    @pl.when(me < nr - 1)
    def _():
        pl.semaphore_signal(barrier, 1, device_id=row_dev(me + 1), device_id_type=MESH)

    count = (me + nr - 1) // nr + (2 * nr - 2 - me) // nr
    if with_filt:
        each_filt_peer(lambda j, s: pl.semaphore_signal(barrier, 1, device_id=filt_dev(j), device_id_type=MESH))
        count = count + lax.axis_size("filt") - 1
    pl.semaphore_wait(barrier, count)


class Halo:
    def __init__(self, down_src, up_src, from_prev, from_next, sems):
        self.nr = lax.axis_size("rows")
        self.me = lax.axis_index("rows")
        self.down = lambda j: rcopy(down_src, from_prev, sems.at[0], sems.at[1], row_dev(j))
        self.up = lambda j: rcopy(up_src, from_next, sems.at[2], sems.at[3], row_dev(j))
        me, nr = self.me, self.nr

        @pl.when(me < nr - 1)
        def _():
            self.down(me + 1).start()

        @pl.when(me > 0)
        def _():
            self.up(me - 1).start()

        @pl.when(me == 0)
        def _():
            from_prev[...] = jnp.zeros(from_prev.shape, from_prev.dtype)

        @pl.when(me == nr - 1)
        def _():
            from_next[...] = jnp.zeros(from_next.shape, from_next.dtype)

    def arrived(self):
        me, nr = self.me, self.nr

        @pl.when(me > 0)
        def _():
            self.down(me - 1).wait_recv()

        @pl.when(me < nr - 1)
        def _():
            self.up(me + 1).wait_recv()

    def sent(self):
        me, nr = self.me, self.nr

        @pl.when(me > 0)
        def _():
            self.up(me - 1).wait_send()

        @pl.when(me < nr - 1)
        def _():
            self.down(me + 1).wait_send()


def lane_shift(part, offset):
    width = part.shape[1]
    col = lax.broadcasted_iota(jnp.int32, part.shape, 1)
    if offset == 1:
        return jnp.where(col == width - 1, 0.0, pltpu.roll(part, width - 1, 1))
    return jnp.where(col == 0, 0.0, pltpu.roll(part, 1, 1))


def conv_parts(w_ref, x):
    parts = []
    for a in range(3):
        total = None
        for b in range(3):
            part = jnp.dot(w_ref[a * 3 + b], x, preferred_element_type=jnp.float32)
            if b != 1:
                part = lane_shift(part, b - 1)
            total = part if total is None else total + part
        parts.append(total)
    return parts


def filt_gather(src, dst, blk, send, recv):
    mf = lax.axis_index("filt")

    def out(j, s):
        return rcopy(src, dst.at[pl.ds(mf * blk, blk)], send.at[j], recv.at[mf], filt_dev(j))

    def inc(j, s):
        return rcopy(src, dst.at[pl.ds(s * blk, blk)], send.at[s], recv.at[s], filt_dev(s))

    each_filt_peer(lambda j, s: out(j, s).start())
    dst[pl.ds(mf * blk, blk)] = src[...]
    return (lambda: each_filt_peer(lambda j, s: inc(j, s).wait_recv()),
            lambda: each_filt_peer(lambda j, s: out(j, s).wait_send()))


def weight_rows(rows3, full, wt_ref):
    for b in range(3):
        moved = rows3
        if b != 1:
            moved = lane_shift(rows3.astype(jnp.float32), 1 - b).astype(rows3.dtype)
        wt_ref[b] = lax.dot_general(
            moved, full, (((1,), (1,)), ((), ())), preferred_element_type=jnp.float32
        ).astype(wt_ref.dtype)


def block_kernel(feat, og, w1r, w2r, w2t, out_ref, gs_ref, gprev, gnext, gf_ref, fprev, fnext,
                 wt_first, wt_second, x_ref, h_ref, p0s, p2s, from_prev, from_next, q0s, q2s, qprev, qnext, hsrc, pre1, tbuf, rbuf,
                 hsems, xsend, xrecv, fsend, frecv, sems1, sems2, sems3, tsend, trecv):
    nf = lax.axis_size("filt")
    mf = lax.axis_index("filt")
    blk = feat.shape[0]
    enter(True)
    x_arrived, x_sent = filt_gather(feat, x_ref, blk, xsend, xrecv)
    x_arrived()
    parts = conv_parts(w1r, x_ref[...])
    p0s[...] = parts[0]
    p2s[...] = parts[2]
    halo = Halo(p0s, p2s, from_prev, from_next, hsems)
    halo.arrived()
    pre1[...] = parts[1] + from_prev[...] + from_next[...]
    hsrc[...] = jnp.maximum(pre1[...], 0.0).astype(hsrc.dtype)
    h_arrived, h_sent = filt_gather(hsrc, h_ref, blk, fsend, frecv)
    h_arrived()
    qs = conv_parts(w2r, h_ref[...])
    q0s[...] = qs[0]
    q2s[...] = qs[2]
    halo1 = Halo(q0s, q2s, qprev, qnext, sems1)
    halo1.arrived()
    pre = qs[1] + qprev[...] + qnext[...] + feat[...].astype(jnp.float32)
    out_ref[...] = jnp.maximum(pre, 0.0).astype(out_ref.dtype)
    gs_ref[...] = jnp.where(pre > 0, og[...].astype(jnp.float32), 0.0).astype(gs_ref.dtype)
    halo2 = Halo(gs_ref, gs_ref, gprev, gnext, sems2)
    halo2.arrived()
    rows3 = jnp.concatenate([gnext[...], gs_ref[...], gprev[...]], axis=0)

    def block(t, carry):
        rows = pl.ds(pl.multiple_of(t * blk, blk), blk)
        total = None
        for b in range(3):
            part = jnp.dot(w2t[b, rows, :], rows3, preferred_element_type=jnp.float32)
            if b != 1:
                part = lane_shift(part, 1 - b)
            total = part if total is None else total + part
        tbuf[t] = total.astype(tbuf.dtype)
        return carry

    lax.fori_loop(0, nf, block, 0)

    def out(j, s):
        return rcopy(tbuf.at[j], rbuf.at[mf], tsend.at[j], trecv.at[mf], filt_dev(j))

    weight_rows(rows3, h_ref[...], wt_second)

    def inc(j, s):
        return rcopy(tbuf.at[s], rbuf.at[s], tsend.at[s], trecv.at[s], filt_dev(s))

    each_filt_peer(lambda j, s: out(j, s).start())
    each_filt_peer(lambda j, s: inc(j, s).wait_recv())
    acc = tbuf[mf].astype(jnp.float32)

    def add(k, acc):
        return acc + rbuf[lax.rem(mf + k, nf)].astype(jnp.float32)

    acc = lax.fori_loop(1, nf, add, acc)
    gf_ref[...] = jnp.where(pre1[...] > 0, acc, 0.0).astype(gf_ref.dtype)
    halo3 = Halo(gf_ref, gf_ref, fprev, fnext, sems3)
    halo3.arrived()
    weight_rows(jnp.concatenate([fnext[...], gf_ref[...], fprev[...]], axis=0), x_ref[...], wt_first)
    x_sent()
    h_sent()
    each_filt_peer(lambda j, s: out(j, s).wait_send())
    halo.sent()
    halo1.sent()
    halo2.sent()
    halo3.sent()


def call(kernel, args, outs, scratch, collective_id):
    spec = pl.BlockSpec(memory_space=pltpu.VMEM)
    return pl.pallas_call(
        kernel,
        out_shape=tuple(jax.ShapeDtypeStruct(shape, dtype) for shape, dtype in outs),
        in_specs=[spec] * len(args),
        out_specs=tuple(spec for _ in outs),
        scratch_shapes=scratch,
        compiler_params=pltpu.CompilerParams(collective_id=collective_id, has_side_effects=True),
    )(*args)


def exchange(x, axis, mode, collective_id, out_dtype=None):
    n = lax.axis_size(axis)
    out_dtype = out_dtype or x.dtype
    sems = [pltpu.SemaphoreType.DMA((n,)), pltpu.SemaphoreType.DMA((n,))]
    if mode == "ag":
        out_shape = (n,) + x.shape
        scratch = sems
    elif mode == "rs":
        out_shape = x.shape[1:]
        scratch = [pltpu.VMEM(x.shape, x.dtype)] + sems
    else:
        out_shape = x.shape
        scratch = [pltpu.VMEM(x.shape, x.dtype)] + sems + sems
    return pl.pallas_call(
        functools.partial(exchange_kernel, axis, n, mode),
        out_shape=jax.ShapeDtypeStruct(out_shape, out_dtype),
        in_specs=[pl.BlockSpec(memory_space=pltpu.VMEM)],
        out_specs=pl.BlockSpec(memory_space=pltpu.VMEM),
        scratch_shapes=scratch,
        compiler_params=pltpu.CompilerParams(collective_id=collective_id, has_side_effects=True),
    )(x)


def shift_cols(value, offset):
    if offset == 0:
        return value
    pad = [(0, 0)] * (value.ndim - 1)
    if offset > 0:
        return jnp.pad(value[..., offset:], pad + [(0, offset)])
    return jnp.pad(value[..., :offset], pad + [(-offset, 0)])


def conv_row(weight, row):
    o = weight.shape[0]
    flat = weight.reshape(o, 9, weight.shape[3])
    parts = jnp.einsum("oki,iw->kow", flat, row, preferred_element_type=jnp.float32)
    return [sum(shift_cols(parts[a * 3 + b], b - 1) for b in range(3)) for a in range(3)]


def weight_terms(rows3, full_row):
    cols = []
    for b in range(3):
        moved = shift_cols(rows3, 1 - b)
        cols.append(jnp.einsum("aow,iw->oai", moved, full_row, preferred_element_type=jnp.float32))
    return jnp.stack(cols, axis=2)


def hidden_terms(weight, rows3):
    total = None
    for b in range(3):
        part = jnp.einsum("oai,aow->iw", weight[:, :, b, :], rows3, preferred_element_type=jnp.float32)
        part = shift_cols(part, 1 - b)
        total = part if total is None else total + part
    return total


def per_device(features, first_weight, second_weight, out_grad):
    feat = features[:, 0, :]
    og = out_grad[:, 0, :]
    n_filt = lax.axis_size("filt")
    blk = feat.shape
    f32, bf16 = jnp.float32, jnp.bfloat16
    o, _, _, i_ch = first_weight.shape
    w1r = first_weight.transpose(1, 2, 0, 3).reshape(9, o, i_ch)
    w2r = second_weight.transpose(1, 2, 0, 3).reshape(9, o, i_ch)
    w2t = second_weight.transpose(2, 3, 1, 0).reshape(3, i_ch, 3 * o)
    sem = pltpu.SemaphoreType.DMA
    full = (n_filt * blk[0], blk[1])
    wt = (3, 3 * o, i_ch)
    block_out, _, _, _, _, _, _, wt_first, wt_second = call(
        block_kernel,
        (feat, og, w1r, w2r, w2t),
        [(blk, bf16)] * 7 + [(wt, bf16), (wt, bf16)],
        [pltpu.VMEM(full, bf16), pltpu.VMEM(full, bf16)] + [pltpu.VMEM(blk, f32)] * 8 + [pltpu.VMEM(blk, bf16), pltpu.VMEM(blk, f32),
                                      pltpu.VMEM((n_filt,) + blk, bf16), pltpu.VMEM((n_filt,) + blk, bf16)]
        + [sem((4,))] + [sem((n_filt,))] * 4 + [sem((4,))] * 3 + [sem((n_filt,))] * 2,
        2,
    )
    second_local = wt_second.reshape(3, 3, o, i_ch).transpose(2, 1, 0, 3)
    first_local = wt_first.reshape(3, 3, o, i_ch).transpose(2, 1, 0, 3)
    n_rows = lax.axis_size("rows")
    summed_first, summed_second = row_sum(
        first_local.reshape(n_rows, -1, 128), second_local.reshape(n_rows, -1, 128), 0
    )
    first_grad = summed_first.astype(f32).reshape(first_local.shape)
    second_grad = summed_second.astype(f32).reshape(second_local.shape)
    return (block_out[:, None, :], first_grad, second_grad)


def solution(mesh):
    in_specs = (
        P("filt", "rows", None),
        P("filt", None, None, None),
        P("filt", None, None, None),
        P("filt", "rows", None),
    )
    out_specs = (P("filt", "rows", None), P("filt", None, None, None), P("filt", None, None, None))
    return jax.shard_map(
        per_device, mesh=mesh, in_specs=in_specs, out_specs=out_specs, check_vma=False
    )
```

```python
import functools

import jax
import jax.numpy as jnp
from jax import lax
from jax.experimental import pallas as pl
from jax.experimental.pallas import tpu as pltpu
from jax.sharding import PartitionSpec as P

MESH = pl.DeviceIdType.MESH


def peer_id(axis, j):
    if axis == "rows":
        return (j, lax.axis_index("filt"))
    return (lax.axis_index("rows"), j)


def exchange_kernel(axis, n, mode, *refs):
    me = lax.axis_index(axis)

    def each_peer(body):
        def step(k, carry):
            body(lax.rem(me + k, n), lax.rem(me + n - k, n))
            return carry

        lax.fori_loop(1, n, step, 0)

    barrier = pltpu.get_barrier_semaphore()

    def greet(j, s):
        pl.semaphore_signal(barrier, 1, device_id=peer_id(axis, j), device_id_type=MESH)

    each_peer(greet)
    pl.semaphore_wait(barrier, n - 1)

    def gather(src, out_ref, send, recv):
        def copy(j, s):
            return pltpu.make_async_remote_copy(
                src, out_ref.at[me], send.at[j], recv.at[me], device_id=peer_id(axis, j), device_id_type=MESH
            )

        def incoming(j, s):
            return pltpu.make_async_remote_copy(
                src, out_ref.at[s], send.at[s], recv.at[s], device_id=peer_id(axis, s), device_id_type=MESH
            )

        each_peer(lambda j, s: copy(j, s).start())
        return copy, incoming

    def reduce(x_ref, buf, send, recv):
        def copy(j, s):
            return pltpu.make_async_remote_copy(
                x_ref.at[j], buf.at[me], send.at[j], recv.at[me], device_id=peer_id(axis, j), device_id_type=MESH
            )

        def incoming(j, s):
            return pltpu.make_async_remote_copy(
                x_ref.at[s], buf.at[s], send.at[s], recv.at[s], device_id=peer_id(axis, s), device_id_type=MESH
            )

        each_peer(lambda j, s: copy(j, s).start())
        each_peer(lambda j, s: incoming(j, s).wait_recv())
        acc = x_ref[me].astype(jnp.float32)

        def add(k, acc):
            return acc + buf[lax.rem(me + k, n)].astype(jnp.float32)

        acc = lax.fori_loop(1, n, add, acc)
        each_peer(lambda j, s: copy(j, s).wait_send())
        return acc

    if mode == "ag":
        x_ref, out_ref, send, recv = refs
        copy, incoming = gather(x_ref, out_ref, send, recv)
        out_ref[me] = x_ref[...]
        each_peer(lambda j, s: incoming(j, s).wait_recv())
        each_peer(lambda j, s: copy(j, s).wait_send())
    elif mode == "rs":
        x_ref, out_ref, buf, send, recv = refs
        out_ref[...] = reduce(x_ref, buf, send, recv).astype(out_ref.dtype)
    else:
        x_ref, out_ref, buf, send, recv, send2, recv2 = refs
        out_ref[me] = reduce(x_ref, buf, send, recv).astype(out_ref.dtype)
        copy, incoming = gather(out_ref.at[me], out_ref, send2, recv2)
        each_peer(lambda j, s: incoming(j, s).wait_recv())
        each_peer(lambda j, s: copy(j, s).wait_send())


class RowSum:
    def __init__(self, n, x_ref, out_ref, half_buf, half_b, part_buf, sems):
        self.zn = zn = n // 2
        self.me = me = lax.axis_index("rows")
        my_y, self.my_z = me // zn, lax.rem(me, zn)
        self.other = lax.rem(me + zn, n)
        self.mine, self.theirs = my_y * zn, (1 - my_y) * zn
        self.x_ref, self.out_ref, self.half_buf, self.half_b, self.part_buf, self.sems = (
            x_ref, out_ref, half_buf, half_b, part_buf, sems)

    def rcopy(self, src, dst, send, recv, j):
        return pltpu.make_async_remote_copy(
            src, dst, send, recv, device_id=(j, lax.axis_index("filt")), device_id_type=MESH
        )

    def each_z(self, body):
        zn, my_z = self.zn, self.my_z

        def step(t, carry):
            j = lax.rem(my_z + zn // 2 + (t // 2) * (2 * lax.rem(t, 2) - 1), zn)
            body(j, j)
            return carry

        lax.fori_loop(1, zn, step, 0)

    def swap(self):
        return self.rcopy(self.x_ref.at[pl.ds(self.theirs, self.zn)], self.half_buf, self.sems.at[0, 0],
                          self.sems.at[0, 1], self.other)

    def part_out(self, j, s):
        return self.rcopy(self.half_b.at[j], self.part_buf.at[self.my_z], self.sems.at[1, j],
                          self.sems.at[2, self.my_z], self.mine + j)

    def part_in(self, j, s):
        return self.rcopy(self.half_b.at[s], self.part_buf.at[s], self.sems.at[1, s], self.sems.at[2, s],
                          self.mine + s)

    def sum_out(self, j, s):
        me = self.me
        return self.rcopy(self.out_ref.at[me], self.out_ref.at[me], self.sems.at[3, j], self.sems.at[4, self.my_z],
                          self.mine + j)

    def sum_in(self, j, s):
        c = self.mine + s
        return self.rcopy(self.out_ref.at[c], self.out_ref.at[c], self.sems.at[3, s], self.sems.at[4, s], c)

    def back(self):
        half = pl.ds(self.mine, self.zn)
        return self.rcopy(self.out_ref.at[half], self.out_ref.at[half], self.sems.at[5, 0], self.sems.at[5, 1],
                          self.other)

    def s1_start(self):
        self.swap().start()

    def s1_finish(self):
        self.swap().wait_recv()
        x_ref, half_buf, half_b, mine = self.x_ref, self.half_buf, self.half_b, self.mine

        def add_half(t, carry):
            half_b[t] = (x_ref[mine + t].astype(jnp.float32) + half_buf[t].astype(jnp.float32)).astype(half_b.dtype)
            return carry

        lax.fori_loop(0, self.zn, add_half, 0)
        self.swap().wait_send()

    def s2_start(self):
        self.each_z(lambda j, s: self.part_out(j, s).start())

    def s2_finish(self):
        self.each_z(lambda j, s: self.part_in(j, s).wait_recv())
        zn, my_z, part_buf = self.zn, self.my_z, self.part_buf
        acc = self.x_ref[self.me].astype(jnp.float32) + self.half_buf[my_z].astype(jnp.float32)

        def add_part(k, acc):
            return acc + part_buf[lax.rem(my_z + k, zn)].astype(jnp.float32)

        acc = lax.fori_loop(1, zn, add_part, acc)
        self.out_ref[self.me] = acc.astype(self.out_ref.dtype)
        self.each_z(lambda j, s: self.part_out(j, s).wait_send())

    def s3_start(self):
        self.each_z(lambda j, s: self.sum_out(j, s).start())

    def s3_finish(self):
        self.each_z(lambda j, s: self.sum_in(j, s).wait_recv())
        self.each_z(lambda j, s: self.sum_out(j, s).wait_send())

    def s4_start(self):
        self.back().start()

    def s4_finish(self):
        self.back().wait_recv()
        self.back().wait_send()


def row_sum_kernel(n, xa, xb, fa, fb, oa, ob, *scratch):
    zn = n // 2
    me = lax.axis_index("rows")
    my_z = lax.rem(me, zn)
    mine = (me // zn) * zn

    def dev(j):
        return (j, lax.axis_index("filt"))

    barrier = pltpu.get_barrier_semaphore()
    pl.semaphore_signal(barrier, 1, device_id=dev(lax.rem(me + zn, n)), device_id_type=MESH)

    def greet(k, carry):
        pl.semaphore_signal(barrier, 1, device_id=dev(mine + lax.rem(my_z + k, zn)), device_id_type=MESH)
        return carry

    lax.fori_loop(1, zn, greet, 0)
    pl.semaphore_wait(barrier, zn)
    a = RowSum(n, xa, oa, *scratch[:4])
    b = RowSum(n, xb, ob, *scratch[4:])
    a.s1_start()
    a.s1_finish()
    a.s2_start()
    b.s1_start()
    b.s1_finish()
    b.s2_start()
    a.s2_finish()
    a.s3_start()
    b.s2_finish()
    b.s3_start()
    a.s3_finish()
    a.s4_start()
    b.s3_finish()
    b.s4_start()
    a.s4_finish()
    b.s4_finish()

    def widen(c, carry):
        fa[c] = oa[c].astype(fa.dtype)
        fb[c] = ob[c].astype(fb.dtype)
        return carry

    lax.fori_loop(0, n, widen, 0)


def row_sum(xa, xb, collective_id):
    n = xa.shape[0]
    zn = n // 2
    spec = pl.BlockSpec(memory_space=pltpu.VMEM)
    scratch = [pltpu.VMEM(xa.shape, xa.dtype), pltpu.VMEM(xb.shape, xb.dtype)]
    for x in (xa, xb):
        blk = (zn,) + x.shape[1:]
        scratch += [pltpu.VMEM(blk, x.dtype), pltpu.VMEM(blk, x.dtype), pltpu.VMEM(blk, x.dtype),
                    pltpu.SemaphoreType.DMA((6, zn))]
    return pl.pallas_call(
        functools.partial(row_sum_kernel, n),
        out_shape=(jax.ShapeDtypeStruct(xa.shape, jnp.float32), jax.ShapeDtypeStruct(xb.shape, jnp.float32)),
        in_specs=[spec, spec],
        out_specs=(spec, spec),
        scratch_shapes=scratch,
        compiler_params=pltpu.CompilerParams(collective_id=collective_id, has_side_effects=True),
    )(xa, xb)


def row_dev(j):
    return (j, lax.axis_index("filt"))


def filt_dev(j):
    return (lax.axis_index("rows"), j)


def rcopy(src, dst, send, recv, dev):
    return pltpu.make_async_remote_copy(src, dst, send, recv, device_id=dev, device_id_type=MESH)


def each_filt_peer(body):
    nf = lax.axis_size("filt")
    half = nf // 2
    me = lax.axis_index("filt")

    def step(k, carry):
        far = (nf - k) // half
        off = k - 1 - (half - 1) * (1 - far)
        j = lax.rem(me // half + far, 2) * half + lax.rem(lax.rem(me, half) + off, half)
        body(j, j)
        return carry

    lax.fori_loop(1, nf, step, 0)


def enter(with_filt):
    nr = lax.axis_size("rows")
    me = lax.axis_index("rows")
    barrier = pltpu.get_barrier_semaphore()

    @pl.when(me > 0)
    def _():
        pl.semaphore_signal(barrier, 1, device_id=row_dev(me - 1), device_id_type=MESH)

    @pl.when(me < nr - 1)
    def _():
        pl.semaphore_signal(barrier, 1, device_id=row_dev(me + 1), device_id_type=MESH)

    count = (me + nr - 1) // nr + (2 * nr - 2 - me) // nr
    if with_filt:
        each_filt_peer(lambda j, s: pl.semaphore_signal(barrier, 1, device_id=filt_dev(j), device_id_type=MESH))
        count = count + lax.axis_size("filt") - 1
    pl.semaphore_wait(barrier, count)


class Halo:
    def __init__(self, down_src, up_src, from_prev, from_next, sems):
        self.nr = lax.axis_size("rows")
        self.me = lax.axis_index("rows")
        self.down = lambda j: rcopy(down_src, from_prev, sems.at[0], sems.at[1], row_dev(j))
        self.up = lambda j: rcopy(up_src, from_next, sems.at[2], sems.at[3], row_dev(j))
        me, nr = self.me, self.nr

        @pl.when(me < nr - 1)
        def _():
            self.down(me + 1).start()

        @pl.when(me > 0)
        def _():
            self.up(me - 1).start()

        @pl.when(me == 0)
        def _():
            from_prev[...] = jnp.zeros(from_prev.shape, from_prev.dtype)

        @pl.when(me == nr - 1)
        def _():
            from_next[...] = jnp.zeros(from_next.shape, from_next.dtype)

    def arrived(self):
        me, nr = self.me, self.nr

        @pl.when(me > 0)
        def _():
            self.down(me - 1).wait_recv()

        @pl.when(me < nr - 1)
        def _():
            self.up(me + 1).wait_recv()

    def sent(self):
        me, nr = self.me, self.nr

        @pl.when(me > 0)
        def _():
            self.up(me - 1).wait_send()

        @pl.when(me < nr - 1)
        def _():
            self.down(me + 1).wait_send()


def lane_shift(part, offset):
    width = part.shape[1]
    col = lax.broadcasted_iota(jnp.int32, part.shape, 1)
    if offset == 1:
        return jnp.where(col == width - 1, 0.0, pltpu.roll(part, width - 1, 1))
    return jnp.where(col == 0, 0.0, pltpu.roll(part, 1, 1))


def conv_parts(w_ref, x):
    parts = []
    for a in range(3):
        total = None
        for b in range(3):
            part = jnp.dot(w_ref[a * 3 + b], x, preferred_element_type=jnp.float32)
            if b != 1:
                part = lane_shift(part, b - 1)
            total = part if total is None else total + part
        parts.append(total)
    return parts


def filt_gather(src, dst, blk, send, recv):
    mf = lax.axis_index("filt")

    def out(j, s):
        return rcopy(src, dst.at[pl.ds(mf * blk, blk)], send.at[j], recv.at[mf], filt_dev(j))

    def inc(j, s):
        return rcopy(src, dst.at[pl.ds(s * blk, blk)], send.at[s], recv.at[s], filt_dev(s))

    each_filt_peer(lambda j, s: out(j, s).start())
    dst[pl.ds(mf * blk, blk)] = src[...]
    return (lambda: each_filt_peer(lambda j, s: inc(j, s).wait_recv()),
            lambda: each_filt_peer(lambda j, s: out(j, s).wait_send()))


def weight_rows(rows3, full, wt_ref):
    for b in range(3):
        moved = rows3
        if b != 1:
            moved = lane_shift(rows3.astype(jnp.float32), 1 - b).astype(rows3.dtype)
        wt_ref[b] = lax.dot_general(
            moved, full, (((1,), (1,)), ((), ())), preferred_element_type=jnp.float32
        ).astype(wt_ref.dtype)


def block_kernel(feat, og, w1r, w2r, w2t, out_ref, gs_ref, gprev, gnext, gf_ref, fprev, fnext,
                 wt_first, wt_second, x_ref, h_ref, p0s, p2s, from_prev, from_next, q0s, q2s, qprev, qnext, hsrc, pre1, tbuf, rbuf,
                 hsems, xsend, xrecv, fsend, frecv, sems1, sems2, sems3, tsend, trecv):
    nf = lax.axis_size("filt")
    mf = lax.axis_index("filt")
    blk = feat.shape[0]
    enter(True)
    x_arrived, x_sent = filt_gather(feat, x_ref, blk, xsend, xrecv)
    x_arrived()
    parts = conv_parts(w1r, x_ref[...])
    p0s[...] = parts[0]
    p2s[...] = parts[2]
    halo = Halo(p0s, p2s, from_prev, from_next, hsems)
    halo.arrived()
    pre1[...] = parts[1] + from_prev[...] + from_next[...]
    hsrc[...] = jnp.maximum(pre1[...], 0.0).astype(hsrc.dtype)
    h_arrived, h_sent = filt_gather(hsrc, h_ref, blk, fsend, frecv)
    h_arrived()
    qs = conv_parts(w2r, h_ref[...])
    q0s[...] = qs[0]
    q2s[...] = qs[2]
    halo1 = Halo(q0s, q2s, qprev, qnext, sems1)
    halo1.arrived()
    pre = qs[1] + qprev[...] + qnext[...] + feat[...].astype(jnp.float32)
    out_ref[...] = jnp.maximum(pre, 0.0).astype(out_ref.dtype)
    gs_ref[...] = jnp.where(pre > 0, og[...].astype(jnp.float32), 0.0).astype(gs_ref.dtype)
    halo2 = Halo(gs_ref, gs_ref, gprev, gnext, sems2)
    halo2.arrived()
    rows3 = jnp.concatenate([gnext[...], gs_ref[...], gprev[...]], axis=0)

    def block(t, carry):
        rows = pl.ds(pl.multiple_of(t * blk, blk), blk)
        total = None
        for b in range(3):
            part = jnp.dot(w2t[b, rows, :], rows3, preferred_element_type=jnp.float32)
            if b != 1:
                part = lane_shift(part, 1 - b)
            total = part if total is None else total + part
        tbuf[t] = total.astype(tbuf.dtype)
        return carry

    lax.fori_loop(0, nf, block, 0)

    def out(j, s):
        return rcopy(tbuf.at[j], rbuf.at[mf], tsend.at[j], trecv.at[mf], filt_dev(j))

    weight_rows(rows3, h_ref[...], wt_second)

    def inc(j, s):
        return rcopy(tbuf.at[s], rbuf.at[s], tsend.at[s], trecv.at[s], filt_dev(s))

    each_filt_peer(lambda j, s: out(j, s).start())
    each_filt_peer(lambda j, s: inc(j, s).wait_recv())
    acc = tbuf[mf].astype(jnp.float32)

    def add(k, acc):
        return acc + rbuf[lax.rem(mf + k, nf)].astype(jnp.float32)

    acc = lax.fori_loop(1, nf, add, acc)
    gf_ref[...] = jnp.where(pre1[...] > 0, acc, 0.0).astype(gf_ref.dtype)
    halo3 = Halo(gf_ref, gf_ref, fprev, fnext, sems3)
    halo3.arrived()
    weight_rows(jnp.concatenate([fnext[...], gf_ref[...], fprev[...]], axis=0), x_ref[...], wt_first)
    x_sent()
    h_sent()
    each_filt_peer(lambda j, s: out(j, s).wait_send())
    halo.sent()
    halo1.sent()
    halo2.sent()
    halo3.sent()


def call(kernel, args, outs, scratch, collective_id):
    spec = pl.BlockSpec(memory_space=pltpu.VMEM)
    return pl.pallas_call(
        kernel,
        out_shape=tuple(jax.ShapeDtypeStruct(shape, dtype) for shape, dtype in outs),
        in_specs=[spec] * len(args),
        out_specs=tuple(spec for _ in outs),
        scratch_shapes=scratch,
        compiler_params=pltpu.CompilerParams(collective_id=collective_id, has_side_effects=True),
    )(*args)


def exchange(x, axis, mode, collective_id, out_dtype=None):
    n = lax.axis_size(axis)
    out_dtype = out_dtype or x.dtype
    sems = [pltpu.SemaphoreType.DMA((n,)), pltpu.SemaphoreType.DMA((n,))]
    if mode == "ag":
        out_shape = (n,) + x.shape
        scratch = sems
    elif mode == "rs":
        out_shape = x.shape[1:]
        scratch = [pltpu.VMEM(x.shape, x.dtype)] + sems
    else:
        out_shape = x.shape
        scratch = [pltpu.VMEM(x.shape, x.dtype)] + sems + sems
    return pl.pallas_call(
        functools.partial(exchange_kernel, axis, n, mode),
        out_shape=jax.ShapeDtypeStruct(out_shape, out_dtype),
        in_specs=[pl.BlockSpec(memory_space=pltpu.VMEM)],
        out_specs=pl.BlockSpec(memory_space=pltpu.VMEM),
        scratch_shapes=scratch,
        compiler_params=pltpu.CompilerParams(collective_id=collective_id, has_side_effects=True),
    )(x)


def shift_cols(value, offset):
    if offset == 0:
        return value
    pad = [(0, 0)] * (value.ndim - 1)
    if offset > 0:
        return jnp.pad(value[..., offset:], pad + [(0, offset)])
    return jnp.pad(value[..., :offset], pad + [(-offset, 0)])


def conv_row(weight, row):
    o = weight.shape[0]
    flat = weight.reshape(o, 9, weight.shape[3])
    parts = jnp.einsum("oki,iw->kow", flat, row, preferred_element_type=jnp.float32)
    return [sum(shift_cols(parts[a * 3 + b], b - 1) for b in range(3)) for a in range(3)]


def weight_terms(rows3, full_row):
    cols = []
    for b in range(3):
        moved = shift_cols(rows3, 1 - b)
        cols.append(jnp.einsum("aow,iw->oai", moved, full_row, preferred_element_type=jnp.float32))
    return jnp.stack(cols, axis=2)


def hidden_terms(weight, rows3):
    total = None
    for b in range(3):
        part = jnp.einsum("oai,aow->iw", weight[:, :, b, :], rows3, preferred_element_type=jnp.float32)
        part = shift_cols(part, 1 - b)
        total = part if total is None else total + part
    return total


def per_device(features, first_weight, second_weight, out_grad):
    feat = features[:, 0, :]
    og = out_grad[:, 0, :]
    n_filt = lax.axis_size("filt")
    blk = feat.shape
    f32, bf16 = jnp.float32, jnp.bfloat16
    o, _, _, i_ch = first_weight.shape
    w1r = first_weight.transpose(1, 2, 0, 3).reshape(9, o, i_ch)
    w2r = second_weight.transpose(1, 2, 0, 3).reshape(9, o, i_ch)
    w2t = second_weight.transpose(2, 3, 1, 0).reshape(3, i_ch, 3 * o)
    sem = pltpu.SemaphoreType.DMA
    full = (n_filt * blk[0], blk[1])
    wt = (3, 3 * o, i_ch)
    block_out, _, _, _, _, _, _, wt_first, wt_second = call(
        block_kernel,
        (feat, og, w1r, w2r, w2t),
        [(blk, bf16)] * 7 + [(wt, bf16), (wt, bf16)],
        [pltpu.VMEM(full, bf16), pltpu.VMEM(full, bf16)] + [pltpu.VMEM(blk, f32)] * 8 + [pltpu.VMEM(blk, bf16), pltpu.VMEM(blk, f32),
                                      pltpu.VMEM((n_filt,) + blk, bf16), pltpu.VMEM((n_filt,) + blk, bf16)]
        + [sem((4,))] + [sem((n_filt,))] * 4 + [sem((4,))] * 3 + [sem((n_filt,))] * 2,
        2,
    )
    second_local = wt_second.reshape(3, 3, o, i_ch).transpose(2, 1, 0, 3)
    first_local = wt_first.reshape(3, 3, o, i_ch).transpose(2, 1, 0, 3)
    n_rows = lax.axis_size("rows")
    summed_first, summed_second = row_sum(
        first_local.reshape(n_rows, -1, 128), second_local.reshape(n_rows, -1, 128), 0
    )
    first_grad = summed_first.reshape(first_local.shape)
    second_grad = summed_second.reshape(second_local.shape)
    return (block_out[:, None, :], first_grad, second_grad)


def solution(mesh):
    in_specs = (
        P("filt", "rows", None),
        P("filt", None, None, None),
        P("filt", None, None, None),
        P("filt", "rows", None),
    )
    out_specs = (P("filt", "rows", None), P("filt", None, None, None), P("filt", None, None, None))
    return jax.shard_map(
        per_device, mesh=mesh, in_specs=in_specs, out_specs=out_specs, check_vma=False
    )
```

```python
import functools

import jax
import jax.numpy as jnp
from jax import lax
from jax.experimental import pallas as pl
from jax.experimental.pallas import tpu as pltpu
from jax.sharding import PartitionSpec as P

MESH = pl.DeviceIdType.MESH


def peer_id(axis, j):
    if axis == "rows":
        return (j, lax.axis_index("filt"))
    return (lax.axis_index("rows"), j)


def exchange_kernel(axis, n, mode, *refs):
    me = lax.axis_index(axis)

    def each_peer(body):
        def step(k, carry):
            body(lax.rem(me + k, n), lax.rem(me + n - k, n))
            return carry

        lax.fori_loop(1, n, step, 0)

    barrier = pltpu.get_barrier_semaphore()

    def greet(j, s):
        pl.semaphore_signal(barrier, 1, device_id=peer_id(axis, j), device_id_type=MESH)

    each_peer(greet)
    pl.semaphore_wait(barrier, n - 1)

    def gather(src, out_ref, send, recv):
        def copy(j, s):
            return pltpu.make_async_remote_copy(
                src, out_ref.at[me], send.at[j], recv.at[me], device_id=peer_id(axis, j), device_id_type=MESH
            )

        def incoming(j, s):
            return pltpu.make_async_remote_copy(
                src, out_ref.at[s], send.at[s], recv.at[s], device_id=peer_id(axis, s), device_id_type=MESH
            )

        each_peer(lambda j, s: copy(j, s).start())
        return copy, incoming

    def reduce(x_ref, buf, send, recv):
        def copy(j, s):
            return pltpu.make_async_remote_copy(
                x_ref.at[j], buf.at[me], send.at[j], recv.at[me], device_id=peer_id(axis, j), device_id_type=MESH
            )

        def incoming(j, s):
            return pltpu.make_async_remote_copy(
                x_ref.at[s], buf.at[s], send.at[s], recv.at[s], device_id=peer_id(axis, s), device_id_type=MESH
            )

        each_peer(lambda j, s: copy(j, s).start())
        each_peer(lambda j, s: incoming(j, s).wait_recv())
        acc = x_ref[me].astype(jnp.float32)

        def add(k, acc):
            return acc + buf[lax.rem(me + k, n)].astype(jnp.float32)

        acc = lax.fori_loop(1, n, add, acc)
        each_peer(lambda j, s: copy(j, s).wait_send())
        return acc

    if mode == "ag":
        x_ref, out_ref, send, recv = refs
        copy, incoming = gather(x_ref, out_ref, send, recv)
        out_ref[me] = x_ref[...]
        each_peer(lambda j, s: incoming(j, s).wait_recv())
        each_peer(lambda j, s: copy(j, s).wait_send())
    elif mode == "rs":
        x_ref, out_ref, buf, send, recv = refs
        out_ref[...] = reduce(x_ref, buf, send, recv).astype(out_ref.dtype)
    else:
        x_ref, out_ref, buf, send, recv, send2, recv2 = refs
        out_ref[me] = reduce(x_ref, buf, send, recv).astype(out_ref.dtype)
        copy, incoming = gather(out_ref.at[me], out_ref, send2, recv2)
        each_peer(lambda j, s: incoming(j, s).wait_recv())
        each_peer(lambda j, s: copy(j, s).wait_send())


class RowSum:
    def __init__(self, n, x_ref, out_ref, half_buf, half_b, part_buf, sems):
        self.zn = zn = n // 2
        self.me = me = lax.axis_index("rows")
        my_y, self.my_z = me // zn, lax.rem(me, zn)
        self.other = lax.rem(me + zn, n)
        self.mine, self.theirs = my_y * zn, (1 - my_y) * zn
        self.x_ref, self.out_ref, self.half_buf, self.half_b, self.part_buf, self.sems = (
            x_ref, out_ref, half_buf, half_b, part_buf, sems)

    def rcopy(self, src, dst, send, recv, j):
        return pltpu.make_async_remote_copy(
            src, dst, send, recv, device_id=(j, lax.axis_index("filt")), device_id_type=MESH
        )

    def each_z(self, body):
        zn, my_z = self.zn, self.my_z

        def step(t, carry):
            j = lax.rem(my_z + zn // 2 + (t // 2) * (2 * lax.rem(t, 2) - 1), zn)
            body(j, j)
            return carry

        lax.fori_loop(1, zn, step, 0)

    def swap(self):
        return self.rcopy(self.x_ref.at[pl.ds(self.theirs, self.zn)], self.half_buf, self.sems.at[0, 0],
                          self.sems.at[0, 1], self.other)

    def part_out(self, j, s):
        return self.rcopy(self.half_b.at[j], self.part_buf.at[self.my_z], self.sems.at[1, j],
                          self.sems.at[2, self.my_z], self.mine + j)

    def part_in(self, j, s):
        return self.rcopy(self.half_b.at[s], self.part_buf.at[s], self.sems.at[1, s], self.sems.at[2, s],
                          self.mine + s)

    def sum_out(self, j, s):
        me = self.me
        return self.rcopy(self.out_ref.at[me], self.out_ref.at[me], self.sems.at[3, j], self.sems.at[4, self.my_z],
                          self.mine + j)

    def sum_in(self, j, s):
        c = self.mine + s
        return self.rcopy(self.out_ref.at[c], self.out_ref.at[c], self.sems.at[3, s], self.sems.at[4, s], c)

    def back(self):
        half = pl.ds(self.mine, self.zn)
        return self.rcopy(self.out_ref.at[half], self.out_ref.at[half], self.sems.at[5, 0], self.sems.at[5, 1],
                          self.other)

    def s1_start(self):
        self.swap().start()

    def s1_finish(self):
        self.swap().wait_recv()
        x_ref, half_buf, half_b, mine = self.x_ref, self.half_buf, self.half_b, self.mine

        def add_half(t, carry):
            half_b[t] = (x_ref[mine + t].astype(jnp.float32) + half_buf[t].astype(jnp.float32)).astype(half_b.dtype)
            return carry

        lax.fori_loop(0, self.zn, add_half, 0)
        self.swap().wait_send()

    def s2_start(self):
        self.each_z(lambda j, s: self.part_out(j, s).start())

    def s2_finish(self):
        self.each_z(lambda j, s: self.part_in(j, s).wait_recv())
        zn, my_z, part_buf = self.zn, self.my_z, self.part_buf
        acc = self.x_ref[self.me].astype(jnp.float32) + self.half_buf[my_z].astype(jnp.float32)

        def add_part(k, acc):
            return acc + part_buf[lax.rem(my_z + k, zn)].astype(jnp.float32)

        acc = lax.fori_loop(1, zn, add_part, acc)
        self.out_ref[self.me] = acc.astype(self.out_ref.dtype)
        self.each_z(lambda j, s: self.part_out(j, s).wait_send())

    def s3_start(self):
        self.each_z(lambda j, s: self.sum_out(j, s).start())

    def s3_finish(self):
        self.each_z(lambda j, s: self.sum_in(j, s).wait_recv())
        self.each_z(lambda j, s: self.sum_out(j, s).wait_send())

    def s4_start(self):
        self.back().start()

    def s4_finish(self):
        self.back().wait_recv()
        self.back().wait_send()


def row_sum_kernel(n, xa, xb, oa, ob, *scratch):
    zn = n // 2
    me = lax.axis_index("rows")
    my_z = lax.rem(me, zn)
    mine = (me // zn) * zn

    def dev(j):
        return (j, lax.axis_index("filt"))

    barrier = pltpu.get_barrier_semaphore()
    pl.semaphore_signal(barrier, 1, device_id=dev(lax.rem(me + zn, n)), device_id_type=MESH)

    def greet(k, carry):
        pl.semaphore_signal(barrier, 1, device_id=dev(mine + lax.rem(my_z + k, zn)), device_id_type=MESH)
        return carry

    lax.fori_loop(1, zn, greet, 0)
    pl.semaphore_wait(barrier, zn)
    a = RowSum(n, xa, oa, *scratch[:4])
    b = RowSum(n, xb, ob, *scratch[4:])
    a.s1_start()
    a.s1_finish()
    a.s2_start()
    b.s1_start()
    b.s1_finish()
    b.s2_start()
    a.s2_finish()
    a.s3_start()
    b.s2_finish()
    b.s3_start()
    a.s3_finish()
    a.s4_start()
    b.s3_finish()
    b.s4_start()
    a.s4_finish()
    b.s4_finish()


def row_sum(xa, xb, collective_id):
    n = xa.shape[0]
    zn = n // 2
    spec = pl.BlockSpec(memory_space=pltpu.VMEM)
    scratch = []
    for x in (xa, xb):
        blk = (zn,) + x.shape[1:]
        scratch += [pltpu.VMEM(blk, x.dtype), pltpu.VMEM(blk, x.dtype), pltpu.VMEM(blk, x.dtype),
                    pltpu.SemaphoreType.DMA((6, zn))]
    return pl.pallas_call(
        functools.partial(row_sum_kernel, n),
        out_shape=(jax.ShapeDtypeStruct(xa.shape, xa.dtype), jax.ShapeDtypeStruct(xb.shape, xb.dtype)),
        in_specs=[spec, spec],
        out_specs=(spec, spec),
        scratch_shapes=scratch,
        compiler_params=pltpu.CompilerParams(collective_id=collective_id, has_side_effects=True),
    )(xa, xb)


def row_dev(j):
    return (j, lax.axis_index("filt"))


def filt_dev(j):
    return (lax.axis_index("rows"), j)


def rcopy(src, dst, send, recv, dev):
    return pltpu.make_async_remote_copy(src, dst, send, recv, device_id=dev, device_id_type=MESH)


def each_filt_peer(body):
    nf = lax.axis_size("filt")
    half = nf // 2
    me = lax.axis_index("filt")

    def step(k, carry):
        far = (nf - k) // half
        off = k - 1 - (half - 1) * (1 - far)
        j = lax.rem(me // half + far, 2) * half + lax.rem(lax.rem(me, half) + off, half)
        body(j, j)
        return carry

    lax.fori_loop(1, nf, step, 0)


def enter(with_filt):
    nr = lax.axis_size("rows")
    me = lax.axis_index("rows")
    barrier = pltpu.get_barrier_semaphore()

    @pl.when(me > 0)
    def _():
        pl.semaphore_signal(barrier, 1, device_id=row_dev(me - 1), device_id_type=MESH)

    @pl.when(me < nr - 1)
    def _():
        pl.semaphore_signal(barrier, 1, device_id=row_dev(me + 1), device_id_type=MESH)

    count = (me + nr - 1) // nr + (2 * nr - 2 - me) // nr
    if with_filt:
        each_filt_peer(lambda j, s: pl.semaphore_signal(barrier, 1, device_id=filt_dev(j), device_id_type=MESH))
        count = count + lax.axis_size("filt") - 1
    pl.semaphore_wait(barrier, count)


class Halo:
    def __init__(self, down_src, up_src, from_prev, from_next, sems):
        self.nr = lax.axis_size("rows")
        self.me = lax.axis_index("rows")
        self.down = lambda j: rcopy(down_src, from_prev, sems.at[0], sems.at[1], row_dev(j))
        self.up = lambda j: rcopy(up_src, from_next, sems.at[2], sems.at[3], row_dev(j))
        me, nr = self.me, self.nr

        @pl.when(me < nr - 1)
        def _():
            self.down(me + 1).start()

        @pl.when(me > 0)
        def _():
            self.up(me - 1).start()

        @pl.when(me == 0)
        def _():
            from_prev[...] = jnp.zeros(from_prev.shape, from_prev.dtype)

        @pl.when(me == nr - 1)
        def _():
            from_next[...] = jnp.zeros(from_next.shape, from_next.dtype)

    def arrived(self):
        me, nr = self.me, self.nr

        @pl.when(me > 0)
        def _():
            self.down(me - 1).wait_recv()

        @pl.when(me < nr - 1)
        def _():
            self.up(me + 1).wait_recv()

    def sent(self):
        me, nr = self.me, self.nr

        @pl.when(me > 0)
        def _():
            self.up(me - 1).wait_send()

        @pl.when(me < nr - 1)
        def _():
            self.down(me + 1).wait_send()


def lane_shift(part, offset):
    width = part.shape[1]
    col = lax.broadcasted_iota(jnp.int32, part.shape, 1)
    if offset == 1:
        return jnp.where(col == width - 1, 0.0, pltpu.roll(part, width - 1, 1))
    return jnp.where(col == 0, 0.0, pltpu.roll(part, 1, 1))


def conv_parts(w_ref, x):
    parts = []
    for a in range(3):
        total = None
        for b in range(3):
            part = jnp.dot(w_ref[a * 3 + b], x, preferred_element_type=jnp.float32)
            if b != 1:
                part = lane_shift(part, b - 1)
            total = part if total is None else total + part
        parts.append(total)
    return parts


def filt_gather(src, dst, blk, send, recv):
    mf = lax.axis_index("filt")

    def out(j, s):
        return rcopy(src, dst.at[pl.ds(mf * blk, blk)], send.at[j], recv.at[mf], filt_dev(j))

    def inc(j, s):
        return rcopy(src, dst.at[pl.ds(s * blk, blk)], send.at[s], recv.at[s], filt_dev(s))

    each_filt_peer(lambda j, s: out(j, s).start())
    dst[pl.ds(mf * blk, blk)] = src[...]
    return (lambda: each_filt_peer(lambda j, s: inc(j, s).wait_recv()),
            lambda: each_filt_peer(lambda j, s: out(j, s).wait_send()))


def weight_rows(rows3, full, wt_ref):
    for b in range(3):
        moved = rows3
        if b != 1:
            moved = lane_shift(rows3.astype(jnp.float32), 1 - b).astype(rows3.dtype)
        wt_ref[b] = lax.dot_general(
            moved, full, (((1,), (1,)), ((), ())), preferred_element_type=jnp.float32
        ).astype(wt_ref.dtype)


def block_kernel(feat, og, w1r, w2r, w2t, out_ref, gs_ref, gprev, gnext, gf_ref, fprev, fnext,
                 wt_first, wt_second, x_ref, h_ref, p0s, p2s, from_prev, from_next, q0s, q2s, qprev, qnext, hsrc, pre1, tbuf, rbuf,
                 hsems, xsend, xrecv, fsend, frecv, sems1, sems2, sems3, tsend, trecv):
    nf = lax.axis_size("filt")
    mf = lax.axis_index("filt")
    blk = feat.shape[0]
    enter(True)
    x_arrived, x_sent = filt_gather(feat, x_ref, blk, xsend, xrecv)
    x_arrived()
    parts = conv_parts(w1r, x_ref[...])
    p0s[...] = parts[0]
    p2s[...] = parts[2]
    halo = Halo(p0s, p2s, from_prev, from_next, hsems)
    halo.arrived()
    pre1[...] = parts[1] + from_prev[...] + from_next[...]
    hsrc[...] = jnp.maximum(pre1[...], 0.0).astype(hsrc.dtype)
    h_arrived, h_sent = filt_gather(hsrc, h_ref, blk, fsend, frecv)
    h_arrived()
    qs = conv_parts(w2r, h_ref[...])
    q0s[...] = qs[0]
    q2s[...] = qs[2]
    halo1 = Halo(q0s, q2s, qprev, qnext, sems1)
    halo1.arrived()
    pre = qs[1] + qprev[...] + qnext[...] + feat[...].astype(jnp.float32)
    out_ref[...] = jnp.maximum(pre, 0.0).astype(out_ref.dtype)
    gs_ref[...] = jnp.where(pre > 0, og[...].astype(jnp.float32), 0.0).astype(gs_ref.dtype)
    halo2 = Halo(gs_ref, gs_ref, gprev, gnext, sems2)
    halo2.arrived()
    rows3 = jnp.concatenate([gnext[...], gs_ref[...], gprev[...]], axis=0)

    def block(t, carry):
        rows = pl.ds(pl.multiple_of(t * blk, blk), blk)
        total = None
        for b in range(3):
            part = jnp.dot(w2t[b, rows, :], rows3, preferred_element_type=jnp.float32)
            if b != 1:
                part = lane_shift(part, 1 - b)
            total = part if total is None else total + part
        tbuf[t] = total.astype(tbuf.dtype)
        return carry

    lax.fori_loop(0, nf, block, 0)

    def out(j, s):
        return rcopy(tbuf.at[j], rbuf.at[mf], tsend.at[j], trecv.at[mf], filt_dev(j))

    weight_rows(rows3, h_ref[...], wt_second)

    def inc(j, s):
        return rcopy(tbuf.at[s], rbuf.at[s], tsend.at[s], trecv.at[s], filt_dev(s))

    each_filt_peer(lambda j, s: out(j, s).start())
    each_filt_peer(lambda j, s: inc(j, s).wait_recv())
    acc = tbuf[mf].astype(jnp.float32)

    def add(k, acc):
        return acc + rbuf[lax.rem(mf + k, nf)].astype(jnp.float32)

    acc = lax.fori_loop(1, nf, add, acc)
    gf_ref[...] = jnp.where(pre1[...] > 0, acc, 0.0).astype(gf_ref.dtype)
    halo3 = Halo(gf_ref, gf_ref, fprev, fnext, sems3)
    halo3.arrived()
    weight_rows(jnp.concatenate([fnext[...], gf_ref[...], fprev[...]], axis=0), x_ref[...], wt_first)
    x_sent()
    h_sent()
    each_filt_peer(lambda j, s: out(j, s).wait_send())
    halo.sent()
    halo1.sent()
    halo2.sent()
    halo3.sent()


def call(kernel, args, outs, scratch, collective_id):
    spec = pl.BlockSpec(memory_space=pltpu.VMEM)
    return pl.pallas_call(
        kernel,
        out_shape=tuple(jax.ShapeDtypeStruct(shape, dtype) for shape, dtype in outs),
        in_specs=[spec] * len(args),
        out_specs=tuple(spec for _ in outs),
        scratch_shapes=scratch,
        compiler_params=pltpu.CompilerParams(collective_id=collective_id, has_side_effects=True),
    )(*args)


def exchange(x, axis, mode, collective_id, out_dtype=None):
    n = lax.axis_size(axis)
    out_dtype = out_dtype or x.dtype
    sems = [pltpu.SemaphoreType.DMA((n,)), pltpu.SemaphoreType.DMA((n,))]
    if mode == "ag":
        out_shape = (n,) + x.shape
        scratch = sems
    elif mode == "rs":
        out_shape = x.shape[1:]
        scratch = [pltpu.VMEM(x.shape, x.dtype)] + sems
    else:
        out_shape = x.shape
        scratch = [pltpu.VMEM(x.shape, x.dtype)] + sems + sems
    return pl.pallas_call(
        functools.partial(exchange_kernel, axis, n, mode),
        out_shape=jax.ShapeDtypeStruct(out_shape, out_dtype),
        in_specs=[pl.BlockSpec(memory_space=pltpu.VMEM)],
        out_specs=pl.BlockSpec(memory_space=pltpu.VMEM),
        scratch_shapes=scratch,
        compiler_params=pltpu.CompilerParams(collective_id=collective_id, has_side_effects=True),
    )(x)


def shift_cols(value, offset):
    if offset == 0:
        return value
    pad = [(0, 0)] * (value.ndim - 1)
    if offset > 0:
        return jnp.pad(value[..., offset:], pad + [(0, offset)])
    return jnp.pad(value[..., :offset], pad + [(-offset, 0)])


def conv_row(weight, row):
    o = weight.shape[0]
    flat = weight.reshape(o, 9, weight.shape[3])
    parts = jnp.einsum("oki,iw->kow", flat, row, preferred_element_type=jnp.float32)
    return [sum(shift_cols(parts[a * 3 + b], b - 1) for b in range(3)) for a in range(3)]


def weight_terms(rows3, full_row):
    cols = []
    for b in range(3):
        moved = shift_cols(rows3, 1 - b)
        cols.append(jnp.einsum("aow,iw->oai", moved, full_row, preferred_element_type=jnp.float32))
    return jnp.stack(cols, axis=2)


def hidden_terms(weight, rows3):
    total = None
    for b in range(3):
        part = jnp.einsum("oai,aow->iw", weight[:, :, b, :], rows3, preferred_element_type=jnp.float32)
        part = shift_cols(part, 1 - b)
        total = part if total is None else total + part
    return total


def per_device(features, first_weight, second_weight, out_grad):
    feat = features[:, 0, :]
    og = out_grad[:, 0, :]
    n_filt = lax.axis_size("filt")
    blk = feat.shape
    f32, bf16 = jnp.float32, jnp.bfloat16
    o, _, _, i_ch = first_weight.shape
    w1r = first_weight.transpose(1, 2, 0, 3).reshape(9, o, i_ch)
    w2r = second_weight.transpose(1, 2, 0, 3).reshape(9, o, i_ch)
    w2t = second_weight.transpose(2, 3, 1, 0).reshape(3, i_ch, 3 * o)
    sem = pltpu.SemaphoreType.DMA
    full = (n_filt * blk[0], blk[1])
    wt = (3, 3 * o, i_ch)
    block_out, _, _, _, _, _, _, wt_first, wt_second = call(
        block_kernel,
        (feat, og, w1r, w2r, w2t),
        [(blk, bf16)] * 7 + [(wt, bf16), (wt, bf16)],
        [pltpu.VMEM(full, bf16), pltpu.VMEM(full, bf16)] + [pltpu.VMEM(blk, f32)] * 8 + [pltpu.VMEM(blk, bf16), pltpu.VMEM(blk, f32),
                                      pltpu.VMEM((n_filt,) + blk, bf16), pltpu.VMEM((n_filt,) + blk, bf16)]
        + [sem((4,))] + [sem((n_filt,))] * 4 + [sem((4,))] * 3 + [sem((n_filt,))] * 2,
        2,
    )
    n_rows = lax.axis_size("rows")
    summed_first, summed_second = row_sum(
        wt_first.reshape(n_rows, -1, 128), wt_second.reshape(n_rows, -1, 128), 0
    )
    first_grad = summed_first.astype(f32).reshape(3, 3, o, i_ch).transpose(2, 1, 0, 3)
    second_grad = summed_second.astype(f32).reshape(3, 3, o, i_ch).transpose(2, 1, 0, 3)
    return (block_out[:, None, :], first_grad, second_grad)


def solution(mesh):
    in_specs = (
        P("filt", "rows", None),
        P("filt", None, None, None),
        P("filt", None, None, None),
        P("filt", "rows", None),
    )
    out_specs = (P("filt", "rows", None), P("filt", None, None, None), P("filt", None, None, None))
    return jax.shard_map(
        per_device, mesh=mesh, in_specs=in_specs, out_specs=out_specs, check_vma=False
    )
```

```python
import functools

import jax
import jax.numpy as jnp
from jax import lax
from jax.experimental import pallas as pl
from jax.experimental.pallas import tpu as pltpu
from jax.sharding import PartitionSpec as P

MESH = pl.DeviceIdType.MESH


def peer_id(axis, j):
    if axis == "rows":
        return (j, lax.axis_index("filt"))
    return (lax.axis_index("rows"), j)


def exchange_kernel(axis, n, mode, *refs):
    me = lax.axis_index(axis)

    def each_peer(body):
        def step(k, carry):
            body(lax.rem(me + k, n), lax.rem(me + n - k, n))
            return carry

        lax.fori_loop(1, n, step, 0)

    barrier = pltpu.get_barrier_semaphore()

    def greet(j, s):
        pl.semaphore_signal(barrier, 1, device_id=peer_id(axis, j), device_id_type=MESH)

    each_peer(greet)
    pl.semaphore_wait(barrier, n - 1)

    def gather(src, out_ref, send, recv):
        def copy(j, s):
            return pltpu.make_async_remote_copy(
                src, out_ref.at[me], send.at[j], recv.at[me], device_id=peer_id(axis, j), device_id_type=MESH
            )

        def incoming(j, s):
            return pltpu.make_async_remote_copy(
                src, out_ref.at[s], send.at[s], recv.at[s], device_id=peer_id(axis, s), device_id_type=MESH
            )

        each_peer(lambda j, s: copy(j, s).start())
        return copy, incoming

    def reduce(x_ref, buf, send, recv):
        def copy(j, s):
            return pltpu.make_async_remote_copy(
                x_ref.at[j], buf.at[me], send.at[j], recv.at[me], device_id=peer_id(axis, j), device_id_type=MESH
            )

        def incoming(j, s):
            return pltpu.make_async_remote_copy(
                x_ref.at[s], buf.at[s], send.at[s], recv.at[s], device_id=peer_id(axis, s), device_id_type=MESH
            )

        each_peer(lambda j, s: copy(j, s).start())
        each_peer(lambda j, s: incoming(j, s).wait_recv())
        acc = x_ref[me].astype(jnp.float32)

        def add(k, acc):
            return acc + buf[lax.rem(me + k, n)].astype(jnp.float32)

        acc = lax.fori_loop(1, n, add, acc)
        each_peer(lambda j, s: copy(j, s).wait_send())
        return acc

    if mode == "ag":
        x_ref, out_ref, send, recv = refs
        copy, incoming = gather(x_ref, out_ref, send, recv)
        out_ref[me] = x_ref[...]
        each_peer(lambda j, s: incoming(j, s).wait_recv())
        each_peer(lambda j, s: copy(j, s).wait_send())
    elif mode == "rs":
        x_ref, out_ref, buf, send, recv = refs
        out_ref[...] = reduce(x_ref, buf, send, recv).astype(out_ref.dtype)
    else:
        x_ref, out_ref, buf, send, recv, send2, recv2 = refs
        out_ref[me] = reduce(x_ref, buf, send, recv).astype(out_ref.dtype)
        copy, incoming = gather(out_ref.at[me], out_ref, send2, recv2)
        each_peer(lambda j, s: incoming(j, s).wait_recv())
        each_peer(lambda j, s: copy(j, s).wait_send())


class RowSum:
    def __init__(self, n, x_ref, out_ref, half_buf, half_b, part_buf, sems):
        self.zn = zn = n // 2
        self.me = me = lax.axis_index("rows")
        my_y, self.my_z = me // zn, lax.rem(me, zn)
        self.other = lax.rem(me + zn, n)
        self.mine, self.theirs = my_y * zn, (1 - my_y) * zn
        self.x_ref, self.out_ref, self.half_buf, self.half_b, self.part_buf, self.sems = (
            x_ref, out_ref, half_buf, half_b, part_buf, sems)

    def rcopy(self, src, dst, send, recv, j):
        return pltpu.make_async_remote_copy(
            src, dst, send, recv, device_id=(j, lax.axis_index("filt")), device_id_type=MESH
        )

    def each_z(self, body):
        zn, my_z = self.zn, self.my_z

        def step(t, carry):
            j = lax.rem(my_z + zn // 2 + (t // 2) * (2 * lax.rem(t, 2) - 1), zn)
            body(j, j)
            return carry

        lax.fori_loop(1, zn, step, 0)

    def swap(self):
        return self.rcopy(self.x_ref.at[pl.ds(self.theirs, self.zn)], self.half_buf, self.sems.at[0, 0],
                          self.sems.at[0, 1], self.other)

    def part_out(self, j, s):
        return self.rcopy(self.half_b.at[j], self.part_buf.at[self.my_z], self.sems.at[1, j],
                          self.sems.at[2, self.my_z], self.mine + j)

    def part_in(self, j, s):
        return self.rcopy(self.half_b.at[s], self.part_buf.at[s], self.sems.at[1, s], self.sems.at[2, s],
                          self.mine + s)

    def sum_out(self, j, s):
        me = self.me
        return self.rcopy(self.out_ref.at[me], self.out_ref.at[me], self.sems.at[3, j], self.sems.at[4, self.my_z],
                          self.mine + j)

    def sum_in(self, j, s):
        c = self.mine + s
        return self.rcopy(self.out_ref.at[c], self.out_ref.at[c], self.sems.at[3, s], self.sems.at[4, s], c)

    def back(self):
        half = pl.ds(self.mine, self.zn)
        return self.rcopy(self.out_ref.at[half], self.out_ref.at[half], self.sems.at[5, 0], self.sems.at[5, 1],
                          self.other)

    def s1_start(self):
        self.swap().start()

    def s1_finish(self):
        self.swap().wait_recv()
        x_ref, half_buf, half_b, mine = self.x_ref, self.half_buf, self.half_b, self.mine

        def add_half(t, carry):
            half_b[t] = (x_ref[mine + t].astype(jnp.float32) + half_buf[t].astype(jnp.float32)).astype(half_b.dtype)
            return carry

        lax.fori_loop(0, self.zn, add_half, 0)
        self.swap().wait_send()

    def s2_start(self):
        self.each_z(lambda j, s: self.part_out(j, s).start())

    def s2_finish(self):
        self.each_z(lambda j, s: self.part_in(j, s).wait_recv())
        zn, my_z, part_buf = self.zn, self.my_z, self.part_buf
        acc = self.x_ref[self.me].astype(jnp.float32) + self.half_buf[my_z].astype(jnp.float32)

        def add_part(k, acc):
            return acc + part_buf[lax.rem(my_z + k, zn)].astype(jnp.float32)

        acc = lax.fori_loop(1, zn, add_part, acc)
        self.out_ref[self.me] = acc.astype(self.out_ref.dtype)
        self.each_z(lambda j, s: self.part_out(j, s).wait_send())

    def s3_start(self):
        self.each_z(lambda j, s: self.sum_out(j, s).start())

    def s3_finish(self):
        self.each_z(lambda j, s: self.sum_in(j, s).wait_recv())
        self.each_z(lambda j, s: self.sum_out(j, s).wait_send())

    def s4_start(self):
        self.back().start()

    def s4_finish(self):
        self.back().wait_recv()
        self.back().wait_send()


def row_sum_kernel(n, split, x32, f32_out, xa, xb, oa, ob, *scratch):
    zn = n // 2
    me = lax.axis_index("rows")
    my_z = lax.rem(me, zn)
    mine = (me // zn) * zn

    def dev(j):
        return (j, lax.axis_index("filt"))

    def narrow(c, carry):
        xa[c] = x32[c, pl.ds(0, split), :].astype(xa.dtype)
        xb[c] = x32[c, pl.ds(split, x32.shape[1] - split), :].astype(xb.dtype)
        return carry

    lax.fori_loop(0, n, narrow, 0)
    barrier = pltpu.get_barrier_semaphore()
    pl.semaphore_signal(barrier, 1, device_id=dev(lax.rem(me + zn, n)), device_id_type=MESH)

    def greet(k, carry):
        pl.semaphore_signal(barrier, 1, device_id=dev(mine + lax.rem(my_z + k, zn)), device_id_type=MESH)
        return carry

    lax.fori_loop(1, zn, greet, 0)
    pl.semaphore_wait(barrier, zn)
    a = RowSum(n, xa, oa, *scratch[:4])
    b = RowSum(n, xb, ob, *scratch[4:])
    a.s1_start()
    a.s1_finish()
    a.s2_start()
    b.s1_start()
    b.s1_finish()
    b.s2_start()
    a.s2_finish()
    a.s3_start()
    b.s2_finish()
    b.s3_start()
    a.s3_finish()
    a.s4_start()
    b.s3_finish()
    b.s4_start()
    a.s4_finish()
    b.s4_finish()

    def widen(c, carry):
        f32_out[c, pl.ds(0, split), :] = oa[c].astype(f32_out.dtype)
        f32_out[c, pl.ds(split, x32.shape[1] - split), :] = ob[c].astype(f32_out.dtype)
        return carry

    lax.fori_loop(0, n, widen, 0)


def row_sum(x, collective_id):
    n, k, _ = x.shape
    zn = n // 2
    split = 8 * (k // 16)
    spec = pl.BlockSpec(memory_space=pltpu.VMEM)
    halves = [(n, split, 128), (n, k - split, 128)]
    scratch = [pltpu.VMEM(h, jnp.bfloat16) for h in halves] * 2
    for h in halves:
        blk = (zn,) + h[1:]
        scratch += [pltpu.VMEM(blk, jnp.bfloat16)] * 3 + [pltpu.SemaphoreType.DMA((6, zn))]
    return pl.pallas_call(
        functools.partial(row_sum_kernel, n, split),
        out_shape=jax.ShapeDtypeStruct(x.shape, jnp.float32),
        in_specs=[spec],
        out_specs=spec,
        scratch_shapes=scratch,
        compiler_params=pltpu.CompilerParams(collective_id=collective_id, has_side_effects=True),
    )(x)


def row_dev(j):
    return (j, lax.axis_index("filt"))


def filt_dev(j):
    return (lax.axis_index("rows"), j)


def rcopy(src, dst, send, recv, dev):
    return pltpu.make_async_remote_copy(src, dst, send, recv, device_id=dev, device_id_type=MESH)


def each_filt_peer(body):
    nf = lax.axis_size("filt")
    half = nf // 2
    me = lax.axis_index("filt")

    def step(k, carry):
        far = (nf - k) // half
        off = k - 1 - (half - 1) * (1 - far)
        j = lax.rem(me // half + far, 2) * half + lax.rem(lax.rem(me, half) + off, half)
        body(j, j)
        return carry

    lax.fori_loop(1, nf, step, 0)


def enter(with_filt):
    nr = lax.axis_size("rows")
    me = lax.axis_index("rows")
    barrier = pltpu.get_barrier_semaphore()

    @pl.when(me > 0)
    def _():
        pl.semaphore_signal(barrier, 1, device_id=row_dev(me - 1), device_id_type=MESH)

    @pl.when(me < nr - 1)
    def _():
        pl.semaphore_signal(barrier, 1, device_id=row_dev(me + 1), device_id_type=MESH)

    count = (me + nr - 1) // nr + (2 * nr - 2 - me) // nr
    if with_filt:
        each_filt_peer(lambda j, s: pl.semaphore_signal(barrier, 1, device_id=filt_dev(j), device_id_type=MESH))
        count = count + lax.axis_size("filt") - 1
    pl.semaphore_wait(barrier, count)


class Halo:
    def __init__(self, down_src, up_src, from_prev, from_next, sems):
        self.nr = lax.axis_size("rows")
        self.me = lax.axis_index("rows")
        self.down = lambda j: rcopy(down_src, from_prev, sems.at[0], sems.at[1], row_dev(j))
        self.up = lambda j: rcopy(up_src, from_next, sems.at[2], sems.at[3], row_dev(j))
        me, nr = self.me, self.nr

        @pl.when(me < nr - 1)
        def _():
            self.down(me + 1).start()

        @pl.when(me > 0)
        def _():
            self.up(me - 1).start()

        @pl.when(me == 0)
        def _():
            from_prev[...] = jnp.zeros(from_prev.shape, from_prev.dtype)

        @pl.when(me == nr - 1)
        def _():
            from_next[...] = jnp.zeros(from_next.shape, from_next.dtype)

    def arrived(self):
        me, nr = self.me, self.nr

        @pl.when(me > 0)
        def _():
            self.down(me - 1).wait_recv()

        @pl.when(me < nr - 1)
        def _():
            self.up(me + 1).wait_recv()

    def sent(self):
        me, nr = self.me, self.nr

        @pl.when(me > 0)
        def _():
            self.up(me - 1).wait_send()

        @pl.when(me < nr - 1)
        def _():
            self.down(me + 1).wait_send()


def lane_shift(part, offset):
    width = part.shape[1]
    col = lax.broadcasted_iota(jnp.int32, part.shape, 1)
    if offset == 1:
        return jnp.where(col == width - 1, 0.0, pltpu.roll(part, width - 1, 1))
    return jnp.where(col == 0, 0.0, pltpu.roll(part, 1, 1))


def conv_parts(w_ref, x):
    parts = []
    for a in range(3):
        total = None
        for b in range(3):
            part = jnp.dot(w_ref[a * 3 + b], x, preferred_element_type=jnp.float32)
            if b != 1:
                part = lane_shift(part, b - 1)
            total = part if total is None else total + part
        parts.append(total)
    return parts


def filt_gather(src, dst, blk, send, recv):
    mf = lax.axis_index("filt")

    def out(j, s):
        return rcopy(src, dst.at[pl.ds(mf * blk, blk)], send.at[j], recv.at[mf], filt_dev(j))

    def inc(j, s):
        return rcopy(src, dst.at[pl.ds(s * blk, blk)], send.at[s], recv.at[s], filt_dev(s))

    each_filt_peer(lambda j, s: out(j, s).start())
    dst[pl.ds(mf * blk, blk)] = src[...]
    return (lambda: each_filt_peer(lambda j, s: inc(j, s).wait_recv()),
            lambda: each_filt_peer(lambda j, s: out(j, s).wait_send()))


def weight_rows(rows3, full, wt_ref, base):
    nq = full.shape[0] // 128
    ao = rows3.shape[0]
    for b in range(3):
        moved = rows3
        if b != 1:
            moved = lane_shift(rows3.astype(jnp.float32), 1 - b).astype(rows3.dtype)
        part = lax.dot_general(moved, full, (((1,), (1,)), ((), ())), preferred_element_type=jnp.float32)
        for q in range(nq):
            wt_ref[pl.ds(base + (b * nq + q) * ao, ao), :] = part[:, q * 128:(q + 1) * 128]


def block_kernel(feat, og, w1r, w2r, w2t, out_ref, gs_ref, gprev, gnext, gf_ref, fprev, fnext,
                 wt_all, x_ref, h_ref, p0s, p2s, from_prev, from_next, q0s, q2s, qprev, qnext, hsrc, pre1, tbuf, rbuf,
                 hsems, xsend, xrecv, fsend, frecv, sems1, sems2, sems3, tsend, trecv):
    nf = lax.axis_size("filt")
    mf = lax.axis_index("filt")
    blk = feat.shape[0]
    enter(True)
    x_arrived, x_sent = filt_gather(feat, x_ref, blk, xsend, xrecv)
    x_arrived()
    parts = conv_parts(w1r, x_ref[...])
    p0s[...] = parts[0]
    p2s[...] = parts[2]
    halo = Halo(p0s, p2s, from_prev, from_next, hsems)
    halo.arrived()
    pre1[...] = parts[1] + from_prev[...] + from_next[...]
    hsrc[...] = jnp.maximum(pre1[...], 0.0).astype(hsrc.dtype)
    h_arrived, h_sent = filt_gather(hsrc, h_ref, blk, fsend, frecv)
    h_arrived()
    qs = conv_parts(w2r, h_ref[...])
    q0s[...] = qs[0]
    q2s[...] = qs[2]
    halo1 = Halo(q0s, q2s, qprev, qnext, sems1)
    halo1.arrived()
    pre = qs[1] + qprev[...] + qnext[...] + feat[...].astype(jnp.float32)
    out_ref[...] = jnp.maximum(pre, 0.0).astype(out_ref.dtype)
    gs_ref[...] = jnp.where(pre > 0, og[...].astype(jnp.float32), 0.0).astype(gs_ref.dtype)
    halo2 = Halo(gs_ref, gs_ref, gprev, gnext, sems2)
    halo2.arrived()
    rows3 = jnp.concatenate([gnext[...], gs_ref[...], gprev[...]], axis=0)

    def block(t, carry):
        rows = pl.ds(pl.multiple_of(t * blk, blk), blk)
        total = None
        for b in range(3):
            part = jnp.dot(w2t[b, rows, :], rows3, preferred_element_type=jnp.float32)
            if b != 1:
                part = lane_shift(part, 1 - b)
            total = part if total is None else total + part
        tbuf[t] = total.astype(tbuf.dtype)
        return carry

    lax.fori_loop(0, nf, block, 0)

    def out(j, s):
        return rcopy(tbuf.at[j], rbuf.at[mf], tsend.at[j], trecv.at[mf], filt_dev(j))

    weight_rows(rows3, h_ref[...], wt_all, wt_all.shape[0] // 2)

    def inc(j, s):
        return rcopy(tbuf.at[s], rbuf.at[s], tsend.at[s], trecv.at[s], filt_dev(s))

    each_filt_peer(lambda j, s: out(j, s).start())
    each_filt_peer(lambda j, s: inc(j, s).wait_recv())
    acc = tbuf[mf].astype(jnp.float32)

    def add(k, acc):
        return acc + rbuf[lax.rem(mf + k, nf)].astype(jnp.float32)

    acc = lax.fori_loop(1, nf, add, acc)
    gf_ref[...] = jnp.where(pre1[...] > 0, acc, 0.0).astype(gf_ref.dtype)
    halo3 = Halo(gf_ref, gf_ref, fprev, fnext, sems3)
    halo3.arrived()
    weight_rows(jnp.concatenate([fnext[...], gf_ref[...], fprev[...]], axis=0), x_ref[...], wt_all, 0)
    x_sent()
    h_sent()
    each_filt_peer(lambda j, s: out(j, s).wait_send())
    halo.sent()
    halo1.sent()
    halo2.sent()
    halo3.sent()


def call(kernel, args, outs, scratch, collective_id):
    spec = pl.BlockSpec(memory_space=pltpu.VMEM)
    return pl.pallas_call(
        kernel,
        out_shape=tuple(jax.ShapeDtypeStruct(shape, dtype) for shape, dtype in outs),
        in_specs=[spec] * len(args),
        out_specs=tuple(spec for _ in outs),
        scratch_shapes=scratch,
        compiler_params=pltpu.CompilerParams(collective_id=collective_id, has_side_effects=True),
    )(*args)


def exchange(x, axis, mode, collective_id, out_dtype=None):
    n = lax.axis_size(axis)
    out_dtype = out_dtype or x.dtype
    sems = [pltpu.SemaphoreType.DMA((n,)), pltpu.SemaphoreType.DMA((n,))]
    if mode == "ag":
        out_shape = (n,) + x.shape
        scratch = sems
    elif mode == "rs":
        out_shape = x.shape[1:]
        scratch = [pltpu.VMEM(x.shape, x.dtype)] + sems
    else:
        out_shape = x.shape
        scratch = [pltpu.VMEM(x.shape, x.dtype)] + sems + sems
    return pl.pallas_call(
        functools.partial(exchange_kernel, axis, n, mode),
        out_shape=jax.ShapeDtypeStruct(out_shape, out_dtype),
        in_specs=[pl.BlockSpec(memory_space=pltpu.VMEM)],
        out_specs=pl.BlockSpec(memory_space=pltpu.VMEM),
        scratch_shapes=scratch,
        compiler_params=pltpu.CompilerParams(collective_id=collective_id, has_side_effects=True),
    )(x)


def shift_cols(value, offset):
    if offset == 0:
        return value
    pad = [(0, 0)] * (value.ndim - 1)
    if offset > 0:
        return jnp.pad(value[..., offset:], pad + [(0, offset)])
    return jnp.pad(value[..., :offset], pad + [(-offset, 0)])


def conv_row(weight, row):
    o = weight.shape[0]
    flat = weight.reshape(o, 9, weight.shape[3])
    parts = jnp.einsum("oki,iw->kow", flat, row, preferred_element_type=jnp.float32)
    return [sum(shift_cols(parts[a * 3 + b], b - 1) for b in range(3)) for a in range(3)]


def weight_terms(rows3, full_row):
    cols = []
    for b in range(3):
        moved = shift_cols(rows3, 1 - b)
        cols.append(jnp.einsum("aow,iw->oai", moved, full_row, preferred_element_type=jnp.float32))
    return jnp.stack(cols, axis=2)


def hidden_terms(weight, rows3):
    total = None
    for b in range(3):
        part = jnp.einsum("oai,aow->iw", weight[:, :, b, :], rows3, preferred_element_type=jnp.float32)
        part = shift_cols(part, 1 - b)
        total = part if total is None else total + part
    return total


def per_device(features, first_weight, second_weight, out_grad):
    feat = features[:, 0, :]
    og = out_grad[:, 0, :]
    n_filt = lax.axis_size("filt")
    blk = feat.shape
    f32, bf16 = jnp.float32, jnp.bfloat16
    o, _, _, i_ch = first_weight.shape
    w1r = first_weight.transpose(1, 2, 0, 3).reshape(9, o, i_ch)
    w2r = second_weight.transpose(1, 2, 0, 3).reshape(9, o, i_ch)
    w2t = second_weight.transpose(2, 3, 1, 0).reshape(3, i_ch, 3 * o)
    sem = pltpu.SemaphoreType.DMA
    full = (n_filt * blk[0], blk[1])
    nq = i_ch // 128
    wt = (2 * 3 * nq * 3 * o, 128)
    block_out, _, _, _, _, _, _, wt_all = call(
        block_kernel,
        (feat, og, w1r, w2r, w2t),
        [(blk, bf16)] * 7 + [(wt, f32)],
        [pltpu.VMEM(full, bf16), pltpu.VMEM(full, bf16)] + [pltpu.VMEM(blk, f32)] * 8 + [pltpu.VMEM(blk, bf16), pltpu.VMEM(blk, f32),
                                      pltpu.VMEM((n_filt,) + blk, bf16), pltpu.VMEM((n_filt,) + blk, bf16)]
        + [sem((4,))] + [sem((n_filt,))] * 4 + [sem((4,))] * 3 + [sem((n_filt,))] * 2,
        2,
    )
    n_rows = lax.axis_size("rows")
    summed = row_sum(wt_all.reshape(n_rows, -1, 128), 0)
    grads = summed.reshape(2, 3, nq, 3, o, 128).transpose(0, 4, 3, 1, 2, 5).reshape(2, o, 3, 3, i_ch)
    first_grad, second_grad = grads[0], grads[1]
    return (block_out[:, None, :], first_grad, second_grad)


def solution(mesh):
    in_specs = (
        P("filt", "rows", None),
        P("filt", None, None, None),
        P("filt", None, None, None),
        P("filt", "rows", None),
    )
    out_specs = (P("filt", "rows", None), P("filt", None, None, None), P("filt", None, None, None))
    return jax.shard_map(
        per_device, mesh=mesh, in_specs=in_specs, out_specs=out_specs, check_vma=False
    )
```

```python
import functools

import jax
import jax.numpy as jnp
from jax import lax
from jax.experimental import pallas as pl
from jax.experimental.pallas import tpu as pltpu
from jax.sharding import PartitionSpec as P

MESH = pl.DeviceIdType.MESH


def peer_id(axis, j):
    if axis == "rows":
        return (j, lax.axis_index("filt"))
    return (lax.axis_index("rows"), j)


def exchange_kernel(axis, n, mode, *refs):
    me = lax.axis_index(axis)

    def each_peer(body):
        def step(k, carry):
            body(lax.rem(me + k, n), lax.rem(me + n - k, n))
            return carry

        lax.fori_loop(1, n, step, 0)

    barrier = pltpu.get_barrier_semaphore()

    def greet(j, s):
        pl.semaphore_signal(barrier, 1, device_id=peer_id(axis, j), device_id_type=MESH)

    each_peer(greet)
    pl.semaphore_wait(barrier, n - 1)

    def gather(src, out_ref, send, recv):
        def copy(j, s):
            return pltpu.make_async_remote_copy(
                src, out_ref.at[me], send.at[j], recv.at[me], device_id=peer_id(axis, j), device_id_type=MESH
            )

        def incoming(j, s):
            return pltpu.make_async_remote_copy(
                src, out_ref.at[s], send.at[s], recv.at[s], device_id=peer_id(axis, s), device_id_type=MESH
            )

        each_peer(lambda j, s: copy(j, s).start())
        return copy, incoming

    def reduce(x_ref, buf, send, recv):
        def copy(j, s):
            return pltpu.make_async_remote_copy(
                x_ref.at[j], buf.at[me], send.at[j], recv.at[me], device_id=peer_id(axis, j), device_id_type=MESH
            )

        def incoming(j, s):
            return pltpu.make_async_remote_copy(
                x_ref.at[s], buf.at[s], send.at[s], recv.at[s], device_id=peer_id(axis, s), device_id_type=MESH
            )

        each_peer(lambda j, s: copy(j, s).start())
        each_peer(lambda j, s: incoming(j, s).wait_recv())
        acc = x_ref[me].astype(jnp.float32)

        def add(k, acc):
            return acc + buf[lax.rem(me + k, n)].astype(jnp.float32)

        acc = lax.fori_loop(1, n, add, acc)
        each_peer(lambda j, s: copy(j, s).wait_send())
        return acc

    if mode == "ag":
        x_ref, out_ref, send, recv = refs
        copy, incoming = gather(x_ref, out_ref, send, recv)
        out_ref[me] = x_ref[...]
        each_peer(lambda j, s: incoming(j, s).wait_recv())
        each_peer(lambda j, s: copy(j, s).wait_send())
    elif mode == "rs":
        x_ref, out_ref, buf, send, recv = refs
        out_ref[...] = reduce(x_ref, buf, send, recv).astype(out_ref.dtype)
    else:
        x_ref, out_ref, buf, send, recv, send2, recv2 = refs
        out_ref[me] = reduce(x_ref, buf, send, recv).astype(out_ref.dtype)
        copy, incoming = gather(out_ref.at[me], out_ref, send2, recv2)
        each_peer(lambda j, s: incoming(j, s).wait_recv())
        each_peer(lambda j, s: copy(j, s).wait_send())


class RowSum:
    def __init__(self, n, x_ref, out_ref, half_buf, half_b, part_buf, sems):
        self.zn = zn = n // 2
        self.me = me = lax.axis_index("rows")
        my_y, self.my_z = me // zn, lax.rem(me, zn)
        self.other = lax.rem(me + zn, n)
        self.mine, self.theirs = my_y * zn, (1 - my_y) * zn
        self.x_ref, self.out_ref, self.half_buf, self.half_b, self.part_buf, self.sems = (
            x_ref, out_ref, half_buf, half_b, part_buf, sems)

    def rcopy(self, src, dst, send, recv, j):
        return pltpu.make_async_remote_copy(
            src, dst, send, recv, device_id=(j, lax.axis_index("filt")), device_id_type=MESH
        )

    def each_z(self, body):
        zn, my_z = self.zn, self.my_z

        def step(t, carry):
            j = lax.rem(my_z + zn // 2 + (t // 2) * (2 * lax.rem(t, 2) - 1), zn)
            body(j, j)
            return carry

        lax.fori_loop(1, zn, step, 0)

    def swap(self):
        return self.rcopy(self.x_ref.at[pl.ds(self.theirs, self.zn)], self.half_buf, self.sems.at[0, 0],
                          self.sems.at[0, 1], self.other)

    def part_out(self, j, s):
        return self.rcopy(self.half_b.at[j], self.part_buf.at[self.my_z], self.sems.at[1, j],
                          self.sems.at[2, self.my_z], self.mine + j)

    def part_in(self, j, s):
        return self.rcopy(self.half_b.at[s], self.part_buf.at[s], self.sems.at[1, s], self.sems.at[2, s],
                          self.mine + s)

    def sum_out(self, j, s):
        me = self.me
        return self.rcopy(self.out_ref.at[me], self.out_ref.at[me], self.sems.at[3, j], self.sems.at[4, self.my_z],
                          self.mine + j)

    def sum_in(self, j, s):
        c = self.mine + s
        return self.rcopy(self.out_ref.at[c], self.out_ref.at[c], self.sems.at[3, s], self.sems.at[4, s], c)

    def back(self):
        half = pl.ds(self.mine, self.zn)
        return self.rcopy(self.out_ref.at[half], self.out_ref.at[half], self.sems.at[5, 0], self.sems.at[5, 1],
                          self.other)

    def s1_start(self):
        self.swap().start()

    def s1_finish(self):
        self.swap().wait_recv()
        x_ref, half_buf, half_b, mine = self.x_ref, self.half_buf, self.half_b, self.mine

        def add_half(t, carry):
            half_b[t] = (x_ref[mine + t].astype(jnp.float32) + half_buf[t].astype(jnp.float32)).astype(half_b.dtype)
            return carry

        lax.fori_loop(0, self.zn, add_half, 0)
        self.swap().wait_send()

    def s2_start(self):
        self.each_z(lambda j, s: self.part_out(j, s).start())

    def s2_finish(self):
        self.each_z(lambda j, s: self.part_in(j, s).wait_recv())
        zn, my_z, part_buf = self.zn, self.my_z, self.part_buf
        acc = self.x_ref[self.me].astype(jnp.float32) + self.half_buf[my_z].astype(jnp.float32)

        def add_part(k, acc):
            return acc + part_buf[lax.rem(my_z + k, zn)].astype(jnp.float32)

        acc = lax.fori_loop(1, zn, add_part, acc)
        self.out_ref[self.me] = acc.astype(self.out_ref.dtype)
        self.each_z(lambda j, s: self.part_out(j, s).wait_send())

    def s3_start(self):
        self.each_z(lambda j, s: self.sum_out(j, s).start())

    def s3_finish(self):
        self.each_z(lambda j, s: self.sum_in(j, s).wait_recv())
        self.each_z(lambda j, s: self.sum_out(j, s).wait_send())

    def s4_start(self):
        self.back().start()

    def s4_finish(self):
        self.back().wait_recv()
        self.back().wait_send()


def row_sum_kernel(n, split, x32, f32_out, xa, xb, oa, ob, *scratch):
    zn = n // 2
    me = lax.axis_index("rows")
    my_z = lax.rem(me, zn)
    mine = (me // zn) * zn

    def dev(j):
        return (j, lax.axis_index("filt"))

    def narrow(c, carry):
        xa[c] = x32[c, pl.ds(0, split), :].astype(xa.dtype)
        xb[c] = x32[c, pl.ds(split, x32.shape[1] - split), :].astype(xb.dtype)
        return carry

    lax.fori_loop(0, n, narrow, 0)
    barrier = pltpu.get_barrier_semaphore()
    pl.semaphore_signal(barrier, 1, device_id=dev(lax.rem(me + zn, n)), device_id_type=MESH)

    def greet(k, carry):
        pl.semaphore_signal(barrier, 1, device_id=dev(mine + lax.rem(my_z + k, zn)), device_id_type=MESH)
        return carry

    lax.fori_loop(1, zn, greet, 0)
    pl.semaphore_wait(barrier, zn)
    a = RowSum(n, xa, oa, *scratch[:4])
    b = RowSum(n, xb, ob, *scratch[4:])
    a.s1_start()
    a.s1_finish()
    a.s2_start()
    b.s1_start()
    b.s1_finish()
    b.s2_start()
    a.s2_finish()
    a.s3_start()
    b.s2_finish()
    b.s3_start()
    a.s3_finish()
    a.s4_start()
    b.s3_finish()
    b.s4_start()
    a.s4_finish()
    b.s4_finish()

    def widen(c, carry):
        f32_out[c, pl.ds(0, split), :] = oa[c].astype(f32_out.dtype)
        f32_out[c, pl.ds(split, x32.shape[1] - split), :] = ob[c].astype(f32_out.dtype)
        return carry

    lax.fori_loop(0, n, widen, 0)


def row_sum(x, collective_id):
    n, k, _ = x.shape
    zn = n // 2
    split = 8 * (k // 16)
    spec = pl.BlockSpec(memory_space=pltpu.VMEM)
    halves = [(n, split, 128), (n, k - split, 128)]
    scratch = [pltpu.VMEM(h, jnp.bfloat16) for h in halves] * 2
    for h in halves:
        blk = (zn,) + h[1:]
        scratch += [pltpu.VMEM(blk, jnp.bfloat16)] * 3 + [pltpu.SemaphoreType.DMA((6, zn))]
    return pl.pallas_call(
        functools.partial(row_sum_kernel, n, split),
        out_shape=jax.ShapeDtypeStruct(x.shape, jnp.float32),
        in_specs=[spec],
        out_specs=spec,
        scratch_shapes=scratch,
        compiler_params=pltpu.CompilerParams(collective_id=collective_id, has_side_effects=True),
    )(x)


def row_dev(j):
    return (j, lax.axis_index("filt"))


def filt_dev(j):
    return (lax.axis_index("rows"), j)


def rcopy(src, dst, send, recv, dev):
    return pltpu.make_async_remote_copy(src, dst, send, recv, device_id=dev, device_id_type=MESH)


def each_filt_peer(body):
    nf = lax.axis_size("filt")
    half = nf // 2
    me = lax.axis_index("filt")

    def step(k, carry):
        far = (nf - k) // half
        off = k - 1 - (half - 1) * (1 - far)
        j = lax.rem(me // half + far, 2) * half + lax.rem(lax.rem(me, half) + off, half)
        body(j, j)
        return carry

    lax.fori_loop(1, nf, step, 0)


def enter(with_filt):
    nr = lax.axis_size("rows")
    me = lax.axis_index("rows")
    barrier = pltpu.get_barrier_semaphore()

    @pl.when(me > 0)
    def _():
        pl.semaphore_signal(barrier, 1, device_id=row_dev(me - 1), device_id_type=MESH)

    @pl.when(me < nr - 1)
    def _():
        pl.semaphore_signal(barrier, 1, device_id=row_dev(me + 1), device_id_type=MESH)

    count = (me + nr - 1) // nr + (2 * nr - 2 - me) // nr
    if with_filt:
        each_filt_peer(lambda j, s: pl.semaphore_signal(barrier, 1, device_id=filt_dev(j), device_id_type=MESH))
        count = count + lax.axis_size("filt") - 1
    pl.semaphore_wait(barrier, count)


class Halo:
    def __init__(self, down_src, up_src, from_prev, from_next, sems):
        self.nr = lax.axis_size("rows")
        self.me = lax.axis_index("rows")
        self.down = lambda j: rcopy(down_src, from_prev, sems.at[0], sems.at[1], row_dev(j))
        self.up = lambda j: rcopy(up_src, from_next, sems.at[2], sems.at[3], row_dev(j))
        me, nr = self.me, self.nr

        @pl.when(me < nr - 1)
        def _():
            self.down(me + 1).start()

        @pl.when(me > 0)
        def _():
            self.up(me - 1).start()

        @pl.when(me == 0)
        def _():
            from_prev[...] = jnp.zeros(from_prev.shape, from_prev.dtype)

        @pl.when(me == nr - 1)
        def _():
            from_next[...] = jnp.zeros(from_next.shape, from_next.dtype)

    def arrived(self):
        me, nr = self.me, self.nr

        @pl.when(me > 0)
        def _():
            self.down(me - 1).wait_recv()

        @pl.when(me < nr - 1)
        def _():
            self.up(me + 1).wait_recv()

    def sent(self):
        me, nr = self.me, self.nr

        @pl.when(me > 0)
        def _():
            self.up(me - 1).wait_send()

        @pl.when(me < nr - 1)
        def _():
            self.down(me + 1).wait_send()


def lane_shift(part, offset):
    width = part.shape[1]
    col = lax.broadcasted_iota(jnp.int32, part.shape, 1)
    if offset == 1:
        return jnp.where(col == width - 1, 0.0, pltpu.roll(part, width - 1, 1))
    return jnp.where(col == 0, 0.0, pltpu.roll(part, 1, 1))


def conv_parts(w_ref, x):
    parts = []
    for a in range(3):
        total = None
        for b in range(3):
            part = jnp.dot(w_ref[a * 3 + b], x, preferred_element_type=jnp.float32)
            if b != 1:
                part = lane_shift(part, b - 1)
            total = part if total is None else total + part
        parts.append(total)
    return parts


def filt_gather(src, dst, blk, send, recv):
    mf = lax.axis_index("filt")

    def out(j, s):
        return rcopy(src, dst.at[pl.ds(mf * blk, blk)], send.at[j], recv.at[mf], filt_dev(j))

    def inc(j, s):
        return rcopy(src, dst.at[pl.ds(s * blk, blk)], send.at[s], recv.at[s], filt_dev(s))

    each_filt_peer(lambda j, s: out(j, s).start())
    dst[pl.ds(mf * blk, blk)] = src[...]
    return (lambda: each_filt_peer(lambda j, s: inc(j, s).wait_recv()),
            lambda: each_filt_peer(lambda j, s: out(j, s).wait_send()))


def weight_rows(rows3, full, wt_ref, base):
    nq = full.shape[0] // 128
    ao = rows3.shape[0]
    for b in range(3):
        moved = rows3
        if b != 1:
            moved = lane_shift(rows3.astype(jnp.float32), 1 - b).astype(rows3.dtype)
        part = lax.dot_general(moved, full, (((1,), (1,)), ((), ())), preferred_element_type=jnp.float32)
        for q in range(nq):
            wt_ref[pl.ds(base + (b * nq + q) * ao, ao), :] = part[:, q * 128:(q + 1) * 128]


def block_kernel(feat, og, w1r, w2r, w2t, out_ref, gs_ref, gprev, gnext, gf_ref, fprev, fnext,
                 wt_all, x_ref, h_ref, p0s, p2s, from_prev, from_next, q0s, q2s, qprev, qnext, hsrc, pre1, tbuf, rbuf,
                 hsems, xsend, xrecv, fsend, frecv, sems1, sems2, sems3, tsend, trecv):
    nf = lax.axis_size("filt")
    mf = lax.axis_index("filt")
    blk = feat.shape[0]
    enter(True)
    x_arrived, x_sent = filt_gather(feat, x_ref, blk, xsend, xrecv)
    x_arrived()
    parts = conv_parts(w1r, x_ref[...])
    p0s[...] = parts[0]
    p2s[...] = parts[2]
    halo = Halo(p0s, p2s, from_prev, from_next, hsems)
    halo.arrived()
    pre1[...] = parts[1] + from_prev[...] + from_next[...]
    hsrc[...] = jnp.maximum(pre1[...], 0.0).astype(hsrc.dtype)
    h_arrived, h_sent = filt_gather(hsrc, h_ref, blk, fsend, frecv)
    h_arrived()
    qs = conv_parts(w2r, h_ref[...])
    q0s[...] = qs[0]
    q2s[...] = qs[2]
    halo1 = Halo(q0s, q2s, qprev, qnext, sems1)
    halo1.arrived()
    pre = qs[1] + qprev[...] + qnext[...] + feat[...].astype(jnp.float32)
    out_ref[...] = jnp.maximum(pre, 0.0).astype(out_ref.dtype)
    gs_ref[...] = jnp.where(pre > 0, og[...].astype(jnp.float32), 0.0).astype(gs_ref.dtype)
    halo2 = Halo(gs_ref, gs_ref, gprev, gnext, sems2)
    halo2.arrived()
    rows3 = jnp.concatenate([gnext[...], gs_ref[...], gprev[...]], axis=0)

    def block(t, carry):
        rows = pl.ds(pl.multiple_of(t * blk, blk), blk)
        total = None
        for b in range(3):
            part = jnp.dot(w2t[b, rows, :], rows3, preferred_element_type=jnp.float32)
            if b != 1:
                part = lane_shift(part, 1 - b)
            total = part if total is None else total + part
        tbuf[t] = total.astype(tbuf.dtype)
        return carry

    lax.fori_loop(0, nf, block, 0)

    def out(j, s):
        return rcopy(tbuf.at[j], rbuf.at[mf], tsend.at[j], trecv.at[mf], filt_dev(j))

    weight_rows(rows3, h_ref[...], wt_all, wt_all.shape[0] // 2)

    def inc(j, s):
        return rcopy(tbuf.at[s], rbuf.at[s], tsend.at[s], trecv.at[s], filt_dev(s))

    each_filt_peer(lambda j, s: out(j, s).start())
    each_filt_peer(lambda j, s: inc(j, s).wait_recv())
    acc = tbuf[mf].astype(jnp.float32)

    def add(k, acc):
        return acc + rbuf[lax.rem(mf + k, nf)].astype(jnp.float32)

    acc = lax.fori_loop(1, nf, add, acc)
    gf_ref[...] = jnp.where(pre1[...] > 0, acc, 0.0).astype(gf_ref.dtype)
    halo3 = Halo(gf_ref, gf_ref, fprev, fnext, sems3)
    halo3.arrived()
    weight_rows(jnp.concatenate([fnext[...], gf_ref[...], fprev[...]], axis=0), x_ref[...], wt_all, 0)
    x_sent()
    h_sent()
    each_filt_peer(lambda j, s: out(j, s).wait_send())
    halo.sent()
    halo1.sent()
    halo2.sent()
    halo3.sent()


def call(kernel, args, outs, scratch, collective_id):
    spec = pl.BlockSpec(memory_space=pltpu.VMEM)
    return pl.pallas_call(
        kernel,
        out_shape=tuple(jax.ShapeDtypeStruct(shape, dtype) for shape, dtype in outs),
        in_specs=[spec] * len(args),
        out_specs=tuple(spec for _ in outs),
        scratch_shapes=scratch,
        compiler_params=pltpu.CompilerParams(collective_id=collective_id, has_side_effects=True),
    )(*args)


def exchange(x, axis, mode, collective_id, out_dtype=None):
    n = lax.axis_size(axis)
    out_dtype = out_dtype or x.dtype
    sems = [pltpu.SemaphoreType.DMA((n,)), pltpu.SemaphoreType.DMA((n,))]
    if mode == "ag":
        out_shape = (n,) + x.shape
        scratch = sems
    elif mode == "rs":
        out_shape = x.shape[1:]
        scratch = [pltpu.VMEM(x.shape, x.dtype)] + sems
    else:
        out_shape = x.shape
        scratch = [pltpu.VMEM(x.shape, x.dtype)] + sems + sems
    return pl.pallas_call(
        functools.partial(exchange_kernel, axis, n, mode),
        out_shape=jax.ShapeDtypeStruct(out_shape, out_dtype),
        in_specs=[pl.BlockSpec(memory_space=pltpu.VMEM)],
        out_specs=pl.BlockSpec(memory_space=pltpu.VMEM),
        scratch_shapes=scratch,
        compiler_params=pltpu.CompilerParams(collective_id=collective_id, has_side_effects=True),
    )(x)


def shift_cols(value, offset):
    if offset == 0:
        return value
    pad = [(0, 0)] * (value.ndim - 1)
    if offset > 0:
        return jnp.pad(value[..., offset:], pad + [(0, offset)])
    return jnp.pad(value[..., :offset], pad + [(-offset, 0)])


def conv_row(weight, row):
    o = weight.shape[0]
    flat = weight.reshape(o, 9, weight.shape[3])
    parts = jnp.einsum("oki,iw->kow", flat, row, preferred_element_type=jnp.float32)
    return [sum(shift_cols(parts[a * 3 + b], b - 1) for b in range(3)) for a in range(3)]


def weight_terms(rows3, full_row):
    cols = []
    for b in range(3):
        moved = shift_cols(rows3, 1 - b)
        cols.append(jnp.einsum("aow,iw->oai", moved, full_row, preferred_element_type=jnp.float32))
    return jnp.stack(cols, axis=2)


def hidden_terms(weight, rows3):
    total = None
    for b in range(3):
        part = jnp.einsum("oai,aow->iw", weight[:, :, b, :], rows3, preferred_element_type=jnp.float32)
        part = shift_cols(part, 1 - b)
        total = part if total is None else total + part
    return total


def per_device(features, first_weight, second_weight, out_grad):
    feat = features[:, 0, :]
    og = out_grad[:, 0, :]
    n_filt = lax.axis_size("filt")
    blk = feat.shape
    f32, bf16 = jnp.float32, jnp.bfloat16
    o, _, _, i_ch = first_weight.shape
    w1r = first_weight.transpose(1, 2, 0, 3).reshape(9, o, i_ch)
    w2r = second_weight.transpose(1, 2, 0, 3).reshape(9, o, i_ch)
    w2t = second_weight.transpose(2, 3, 1, 0).reshape(3, i_ch, 3 * o)
    sem = pltpu.SemaphoreType.DMA
    full = (n_filt * blk[0], blk[1])
    nq = i_ch // 128
    wt = (2 * 3 * nq * 3 * o, 128)
    block_out, _, _, _, _, _, _, wt_all = call(
        block_kernel,
        (feat, og, w1r, w2r, w2t),
        [(blk, bf16)] * 7 + [(wt, f32)],
        [pltpu.VMEM(full, bf16), pltpu.VMEM(full, bf16)] + [pltpu.VMEM(blk, f32)] * 8 + [pltpu.VMEM(blk, bf16), pltpu.VMEM(blk, f32),
                                      pltpu.VMEM((n_filt,) + blk, bf16), pltpu.VMEM((n_filt,) + blk, bf16)]
        + [sem((4,))] + [sem((n_filt,))] * 4 + [sem((4,))] * 3 + [sem((n_filt,))] * 2,
        2,
    )
    n_rows = lax.axis_size("rows")
    summed = row_sum(wt_all.reshape(n_rows, -1, 128), 0)
    first_grad, second_grad = (
        half.reshape(3, nq, 3, o, 128).transpose(3, 2, 0, 1, 4).reshape(o, 3, 3, i_ch)
        for half in (summed[: n_rows // 2], summed[n_rows // 2:])
    )
    return (block_out[:, None, :], first_grad, second_grad)


def solution(mesh):
    in_specs = (
        P("filt", "rows", None),
        P("filt", None, None, None),
        P("filt", None, None, None),
        P("filt", "rows", None),
    )
    out_specs = (P("filt", "rows", None), P("filt", None, None, None), P("filt", None, None, None))
    return jax.shard_map(
        per_device, mesh=mesh, in_specs=in_specs, out_specs=out_specs, check_vma=False
    )
```

```python
import functools

import jax
import jax.numpy as jnp
from jax import lax
from jax.experimental import pallas as pl
from jax.experimental.pallas import tpu as pltpu
from jax.sharding import PartitionSpec as P

MESH = pl.DeviceIdType.MESH


def peer_id(axis, j):
    if axis == "rows":
        return (j, lax.axis_index("filt"))
    return (lax.axis_index("rows"), j)


def exchange_kernel(axis, n, mode, *refs):
    me = lax.axis_index(axis)

    def each_peer(body):
        def step(k, carry):
            body(lax.rem(me + k, n), lax.rem(me + n - k, n))
            return carry

        lax.fori_loop(1, n, step, 0)

    barrier = pltpu.get_barrier_semaphore()

    def greet(j, s):
        pl.semaphore_signal(barrier, 1, device_id=peer_id(axis, j), device_id_type=MESH)

    each_peer(greet)
    pl.semaphore_wait(barrier, n - 1)

    def gather(src, out_ref, send, recv):
        def copy(j, s):
            return pltpu.make_async_remote_copy(
                src, out_ref.at[me], send.at[j], recv.at[me], device_id=peer_id(axis, j), device_id_type=MESH
            )

        def incoming(j, s):
            return pltpu.make_async_remote_copy(
                src, out_ref.at[s], send.at[s], recv.at[s], device_id=peer_id(axis, s), device_id_type=MESH
            )

        each_peer(lambda j, s: copy(j, s).start())
        return copy, incoming

    def reduce(x_ref, buf, send, recv):
        def copy(j, s):
            return pltpu.make_async_remote_copy(
                x_ref.at[j], buf.at[me], send.at[j], recv.at[me], device_id=peer_id(axis, j), device_id_type=MESH
            )

        def incoming(j, s):
            return pltpu.make_async_remote_copy(
                x_ref.at[s], buf.at[s], send.at[s], recv.at[s], device_id=peer_id(axis, s), device_id_type=MESH
            )

        each_peer(lambda j, s: copy(j, s).start())
        each_peer(lambda j, s: incoming(j, s).wait_recv())
        acc = x_ref[me].astype(jnp.float32)

        def add(k, acc):
            return acc + buf[lax.rem(me + k, n)].astype(jnp.float32)

        acc = lax.fori_loop(1, n, add, acc)
        each_peer(lambda j, s: copy(j, s).wait_send())
        return acc

    if mode == "ag":
        x_ref, out_ref, send, recv = refs
        copy, incoming = gather(x_ref, out_ref, send, recv)
        out_ref[me] = x_ref[...]
        each_peer(lambda j, s: incoming(j, s).wait_recv())
        each_peer(lambda j, s: copy(j, s).wait_send())
    elif mode == "rs":
        x_ref, out_ref, buf, send, recv = refs
        out_ref[...] = reduce(x_ref, buf, send, recv).astype(out_ref.dtype)
    else:
        x_ref, out_ref, buf, send, recv, send2, recv2 = refs
        out_ref[me] = reduce(x_ref, buf, send, recv).astype(out_ref.dtype)
        copy, incoming = gather(out_ref.at[me], out_ref, send2, recv2)
        each_peer(lambda j, s: incoming(j, s).wait_recv())
        each_peer(lambda j, s: copy(j, s).wait_send())


class RowSum:
    def __init__(self, n, x_ref, out_ref, half_buf, half_b, part_buf, sems):
        self.zn = zn = n // 2
        self.me = me = lax.axis_index("rows")
        my_y, self.my_z = me // zn, lax.rem(me, zn)
        self.other = lax.rem(me + zn, n)
        self.mine, self.theirs = my_y * zn, (1 - my_y) * zn
        self.x_ref, self.out_ref, self.half_buf, self.half_b, self.part_buf, self.sems = (
            x_ref, out_ref, half_buf, half_b, part_buf, sems)

    def rcopy(self, src, dst, send, recv, j):
        return pltpu.make_async_remote_copy(
            src, dst, send, recv, device_id=(j, lax.axis_index("filt")), device_id_type=MESH
        )

    def each_z(self, body):
        zn, my_z = self.zn, self.my_z

        def step(t, carry):
            j = lax.rem(my_z + zn // 2 + (t // 2) * (2 * lax.rem(t, 2) - 1), zn)
            body(j, j)
            return carry

        lax.fori_loop(1, zn, step, 0)

    def swap(self):
        return self.rcopy(self.x_ref.at[pl.ds(self.theirs, self.zn)], self.half_buf, self.sems.at[0, 0],
                          self.sems.at[0, 1], self.other)

    def part_out(self, j, s):
        return self.rcopy(self.half_b.at[j], self.part_buf.at[self.my_z], self.sems.at[1, j],
                          self.sems.at[2, self.my_z], self.mine + j)

    def part_in(self, j, s):
        return self.rcopy(self.half_b.at[s], self.part_buf.at[s], self.sems.at[1, s], self.sems.at[2, s],
                          self.mine + s)

    def sum_out(self, j, s):
        me = self.me
        return self.rcopy(self.out_ref.at[me], self.out_ref.at[me], self.sems.at[3, j], self.sems.at[4, self.my_z],
                          self.mine + j)

    def sum_in(self, j, s):
        c = self.mine + s
        return self.rcopy(self.out_ref.at[c], self.out_ref.at[c], self.sems.at[3, s], self.sems.at[4, s], c)

    def back(self):
        half = pl.ds(self.mine, self.zn)
        return self.rcopy(self.out_ref.at[half], self.out_ref.at[half], self.sems.at[5, 0], self.sems.at[5, 1],
                          self.other)

    def s1_start(self):
        self.swap().start()

    def s1_finish(self):
        self.swap().wait_recv()
        x_ref, half_buf, half_b, mine = self.x_ref, self.half_buf, self.half_b, self.mine

        def add_half(t, carry):
            half_b[t] = (x_ref[mine + t].astype(jnp.float32) + half_buf[t].astype(jnp.float32)).astype(half_b.dtype)
            return carry

        lax.fori_loop(0, self.zn, add_half, 0)
        self.swap().wait_send()

    def s2_start(self):
        self.each_z(lambda j, s: self.part_out(j, s).start())

    def s2_finish(self):
        self.each_z(lambda j, s: self.part_in(j, s).wait_recv())
        zn, my_z, part_buf = self.zn, self.my_z, self.part_buf
        acc = self.x_ref[self.me].astype(jnp.float32) + self.half_buf[my_z].astype(jnp.float32)

        def add_part(k, acc):
            return acc + part_buf[lax.rem(my_z + k, zn)].astype(jnp.float32)

        acc = lax.fori_loop(1, zn, add_part, acc)
        self.out_ref[self.me] = acc.astype(self.out_ref.dtype)
        self.each_z(lambda j, s: self.part_out(j, s).wait_send())

    def s3_start(self):
        self.each_z(lambda j, s: self.sum_out(j, s).start())

    def s3_finish(self):
        self.each_z(lambda j, s: self.sum_in(j, s).wait_recv())
        self.each_z(lambda j, s: self.sum_out(j, s).wait_send())

    def s4_start(self):
        self.back().start()

    def s4_finish(self):
        self.back().wait_recv()
        self.back().wait_send()


def row_sum_kernel(n, split, x32, f32_out, xa, xb, oa, ob, *scratch):
    zn = n // 2
    me = lax.axis_index("rows")
    my_z = lax.rem(me, zn)
    mine = (me // zn) * zn

    def dev(j):
        return (j, lax.axis_index("filt"))

    def narrow(c, carry):
        xa[c] = x32[c, pl.ds(0, split), :].astype(xa.dtype)
        xb[c] = x32[c, pl.ds(split, x32.shape[1] - split), :].astype(xb.dtype)
        return carry

    lax.fori_loop(0, n, narrow, 0)
    barrier = pltpu.get_barrier_semaphore()
    pl.semaphore_signal(barrier, 1, device_id=dev(lax.rem(me + zn, n)), device_id_type=MESH)

    def greet(k, carry):
        pl.semaphore_signal(barrier, 1, device_id=dev(mine + lax.rem(my_z + k, zn)), device_id_type=MESH)
        return carry

    lax.fori_loop(1, zn, greet, 0)
    pl.semaphore_wait(barrier, zn)
    a = RowSum(n, xa, oa, *scratch[:4])
    b = RowSum(n, xb, ob, *scratch[4:])
    a.s1_start()
    a.s1_finish()
    a.s2_start()
    b.s1_start()
    b.s1_finish()
    b.s2_start()
    a.s2_finish()
    a.s3_start()
    b.s2_finish()
    b.s3_start()
    a.s3_finish()
    a.s4_start()
    b.s3_finish()
    b.s4_start()
    a.s4_finish()
    b.s4_finish()

    def widen(c, carry):
        f32_out[c, pl.ds(0, split), :] = oa[c].astype(f32_out.dtype)
        f32_out[c, pl.ds(split, x32.shape[1] - split), :] = ob[c].astype(f32_out.dtype)
        return carry

    lax.fori_loop(0, n, widen, 0)


def row_sum(x, collective_id):
    n, k, _ = x.shape
    zn = n // 2
    split = 8 * (k // 16)
    spec = pl.BlockSpec(memory_space=pltpu.VMEM)
    halves = [(n, split, 128), (n, k - split, 128)]
    scratch = [pltpu.VMEM(h, jnp.bfloat16) for h in halves] * 2
    for h in halves:
        blk = (zn,) + h[1:]
        scratch += [pltpu.VMEM(blk, jnp.bfloat16)] * 3 + [pltpu.SemaphoreType.DMA((6, zn))]
    return pl.pallas_call(
        functools.partial(row_sum_kernel, n, split),
        out_shape=jax.ShapeDtypeStruct(x.shape, jnp.float32),
        in_specs=[spec],
        out_specs=spec,
        scratch_shapes=scratch,
        compiler_params=pltpu.CompilerParams(collective_id=collective_id, has_side_effects=True),
    )(x)


def row_dev(j):
    return (j, lax.axis_index("filt"))


def filt_dev(j):
    return (lax.axis_index("rows"), j)


def rcopy(src, dst, send, recv, dev):
    return pltpu.make_async_remote_copy(src, dst, send, recv, device_id=dev, device_id_type=MESH)


def each_filt_peer(body):
    nf = lax.axis_size("filt")
    half = nf // 2
    me = lax.axis_index("filt")

    def step(k, carry):
        far = (nf - k) // half
        off = k - 1 - (half - 1) * (1 - far)
        j = lax.rem(me // half + far, 2) * half + lax.rem(lax.rem(me, half) + off, half)
        body(j, j)
        return carry

    lax.fori_loop(1, nf, step, 0)


def enter(with_filt):
    nr = lax.axis_size("rows")
    me = lax.axis_index("rows")
    barrier = pltpu.get_barrier_semaphore()

    @pl.when(me > 0)
    def _():
        pl.semaphore_signal(barrier, 1, device_id=row_dev(me - 1), device_id_type=MESH)

    @pl.when(me < nr - 1)
    def _():
        pl.semaphore_signal(barrier, 1, device_id=row_dev(me + 1), device_id_type=MESH)

    count = (me + nr - 1) // nr + (2 * nr - 2 - me) // nr
    if with_filt:
        each_filt_peer(lambda j, s: pl.semaphore_signal(barrier, 1, device_id=filt_dev(j), device_id_type=MESH))
        count = count + lax.axis_size("filt") - 1
    pl.semaphore_wait(barrier, count)


class Halo:
    def __init__(self, down_src, up_src, from_prev, from_next, sems):
        self.nr = lax.axis_size("rows")
        self.me = lax.axis_index("rows")
        self.down = lambda j: rcopy(down_src, from_prev, sems.at[0], sems.at[1], row_dev(j))
        self.up = lambda j: rcopy(up_src, from_next, sems.at[2], sems.at[3], row_dev(j))
        me, nr = self.me, self.nr

        @pl.when(me < nr - 1)
        def _():
            self.down(me + 1).start()

        @pl.when(me > 0)
        def _():
            self.up(me - 1).start()

        @pl.when(me == 0)
        def _():
            from_prev[...] = jnp.zeros(from_prev.shape, from_prev.dtype)

        @pl.when(me == nr - 1)
        def _():
            from_next[...] = jnp.zeros(from_next.shape, from_next.dtype)

    def arrived(self):
        me, nr = self.me, self.nr

        @pl.when(me > 0)
        def _():
            self.down(me - 1).wait_recv()

        @pl.when(me < nr - 1)
        def _():
            self.up(me + 1).wait_recv()

    def sent(self):
        me, nr = self.me, self.nr

        @pl.when(me > 0)
        def _():
            self.up(me - 1).wait_send()

        @pl.when(me < nr - 1)
        def _():
            self.down(me + 1).wait_send()


def lane_shift(part, offset):
    width = part.shape[1]
    col = lax.broadcasted_iota(jnp.int32, part.shape, 1)
    if offset == 1:
        return jnp.where(col == width - 1, 0.0, pltpu.roll(part, width - 1, 1))
    return jnp.where(col == 0, 0.0, pltpu.roll(part, 1, 1))


def conv_parts(w_ref, x):
    parts = []
    for a in range(3):
        total = None
        for b in range(3):
            part = jnp.dot(w_ref[a * 3 + b], x, preferred_element_type=jnp.float32)
            if b != 1:
                part = lane_shift(part, b - 1)
            total = part if total is None else total + part
        parts.append(total)
    return parts


def filt_gather(src, dst, blk, send, recv):
    mf = lax.axis_index("filt")

    def out(j, s):
        return rcopy(src, dst.at[pl.ds(mf * blk, blk)], send.at[j], recv.at[mf], filt_dev(j))

    def inc(j, s):
        return rcopy(src, dst.at[pl.ds(s * blk, blk)], send.at[s], recv.at[s], filt_dev(s))

    each_filt_peer(lambda j, s: out(j, s).start())
    dst[pl.ds(mf * blk, blk)] = src[...]
    return (lambda: each_filt_peer(lambda j, s: inc(j, s).wait_recv()),
            lambda: each_filt_peer(lambda j, s: out(j, s).wait_send()))


def weight_rows(rows3, full, wt_ref, base):
    nq = full.shape[0] // 128
    ao = rows3.shape[0]
    for b in range(3):
        moved = rows3
        if b != 1:
            moved = lane_shift(rows3.astype(jnp.float32), 1 - b).astype(rows3.dtype)
        part = lax.dot_general(moved, full, (((1,), (1,)), ((), ())), preferred_element_type=jnp.float32)
        for q in range(nq):
            wt_ref[pl.ds(base + (b * nq + q) * ao, ao), :] = part[:, q * 128:(q + 1) * 128]


def block_kernel(feat, og, w1r, w2r, out_ref, gs_ref, gprev, gnext, gf_ref, fprev, fnext,
                 wt_all, x_ref, h_ref, p0s, p2s, from_prev, from_next, q0s, q2s, qprev, qnext, hsrc, pre1, tbuf, rbuf,
                 hsems, xsend, xrecv, fsend, frecv, sems1, sems2, sems3, tsend, trecv):
    nf = lax.axis_size("filt")
    mf = lax.axis_index("filt")
    blk = feat.shape[0]
    enter(True)
    x_arrived, x_sent = filt_gather(feat, x_ref, blk, xsend, xrecv)
    x_arrived()
    parts = conv_parts(w1r, x_ref[...])
    p0s[...] = parts[0]
    p2s[...] = parts[2]
    halo = Halo(p0s, p2s, from_prev, from_next, hsems)
    halo.arrived()
    pre1[...] = parts[1] + from_prev[...] + from_next[...]
    hsrc[...] = jnp.maximum(pre1[...], 0.0).astype(hsrc.dtype)
    h_arrived, h_sent = filt_gather(hsrc, h_ref, blk, fsend, frecv)
    h_arrived()
    qs = conv_parts(w2r, h_ref[...])
    q0s[...] = qs[0]
    q2s[...] = qs[2]
    halo1 = Halo(q0s, q2s, qprev, qnext, sems1)
    halo1.arrived()
    pre = qs[1] + qprev[...] + qnext[...] + feat[...].astype(jnp.float32)
    out_ref[...] = jnp.maximum(pre, 0.0).astype(out_ref.dtype)
    gs_ref[...] = jnp.where(pre > 0, og[...].astype(jnp.float32), 0.0).astype(gs_ref.dtype)
    halo2 = Halo(gs_ref, gs_ref, gprev, gnext, sems2)
    halo2.arrived()
    rows3 = jnp.concatenate([gnext[...], gs_ref[...], gprev[...]], axis=0)
    per = 128 // blk
    for q in range(w2r.shape[2] // 128):
        total = None
        for b in range(3):
            lhs = jnp.concatenate([w2r[a * 3 + b, :, q * 128:(q + 1) * 128] for a in range(3)], axis=0)
            part = lax.dot_general(lhs, rows3, (((0,), (0,)), ((), ())), preferred_element_type=jnp.float32)
            if b != 1:
                part = lane_shift(part, 1 - b)
            total = part if total is None else total + part
        for u in range(per):
            tbuf[q * per + u] = total[u * blk:(u + 1) * blk].astype(tbuf.dtype)

    def out(j, s):
        return rcopy(tbuf.at[j], rbuf.at[mf], tsend.at[j], trecv.at[mf], filt_dev(j))

    weight_rows(rows3, h_ref[...], wt_all, wt_all.shape[0] // 2)

    def inc(j, s):
        return rcopy(tbuf.at[s], rbuf.at[s], tsend.at[s], trecv.at[s], filt_dev(s))

    each_filt_peer(lambda j, s: out(j, s).start())
    each_filt_peer(lambda j, s: inc(j, s).wait_recv())
    acc = tbuf[mf].astype(jnp.float32)

    def add(k, acc):
        return acc + rbuf[lax.rem(mf + k, nf)].astype(jnp.float32)

    acc = lax.fori_loop(1, nf, add, acc)
    gf_ref[...] = jnp.where(pre1[...] > 0, acc, 0.0).astype(gf_ref.dtype)
    halo3 = Halo(gf_ref, gf_ref, fprev, fnext, sems3)
    halo3.arrived()
    weight_rows(jnp.concatenate([fnext[...], gf_ref[...], fprev[...]], axis=0), x_ref[...], wt_all, 0)
    x_sent()
    h_sent()
    each_filt_peer(lambda j, s: out(j, s).wait_send())
    halo.sent()
    halo1.sent()
    halo2.sent()
    halo3.sent()


def call(kernel, args, outs, scratch, collective_id):
    spec = pl.BlockSpec(memory_space=pltpu.VMEM)
    return pl.pallas_call(
        kernel,
        out_shape=tuple(jax.ShapeDtypeStruct(shape, dtype) for shape, dtype in outs),
        in_specs=[spec] * len(args),
        out_specs=tuple(spec for _ in outs),
        scratch_shapes=scratch,
        compiler_params=pltpu.CompilerParams(collective_id=collective_id, has_side_effects=True),
    )(*args)


def exchange(x, axis, mode, collective_id, out_dtype=None):
    n = lax.axis_size(axis)
    out_dtype = out_dtype or x.dtype
    sems = [pltpu.SemaphoreType.DMA((n,)), pltpu.SemaphoreType.DMA((n,))]
    if mode == "ag":
        out_shape = (n,) + x.shape
        scratch = sems
    elif mode == "rs":
        out_shape = x.shape[1:]
        scratch = [pltpu.VMEM(x.shape, x.dtype)] + sems
    else:
        out_shape = x.shape
        scratch = [pltpu.VMEM(x.shape, x.dtype)] + sems + sems
    return pl.pallas_call(
        functools.partial(exchange_kernel, axis, n, mode),
        out_shape=jax.ShapeDtypeStruct(out_shape, out_dtype),
        in_specs=[pl.BlockSpec(memory_space=pltpu.VMEM)],
        out_specs=pl.BlockSpec(memory_space=pltpu.VMEM),
        scratch_shapes=scratch,
        compiler_params=pltpu.CompilerParams(collective_id=collective_id, has_side_effects=True),
    )(x)


def shift_cols(value, offset):
    if offset == 0:
        return value
    pad = [(0, 0)] * (value.ndim - 1)
    if offset > 0:
        return jnp.pad(value[..., offset:], pad + [(0, offset)])
    return jnp.pad(value[..., :offset], pad + [(-offset, 0)])


def conv_row(weight, row):
    o = weight.shape[0]
    flat = weight.reshape(o, 9, weight.shape[3])
    parts = jnp.einsum("oki,iw->kow", flat, row, preferred_element_type=jnp.float32)
    return [sum(shift_cols(parts[a * 3 + b], b - 1) for b in range(3)) for a in range(3)]


def weight_terms(rows3, full_row):
    cols = []
    for b in range(3):
        moved = shift_cols(rows3, 1 - b)
        cols.append(jnp.einsum("aow,iw->oai", moved, full_row, preferred_element_type=jnp.float32))
    return jnp.stack(cols, axis=2)


def hidden_terms(weight, rows3):
    total = None
    for b in range(3):
        part = jnp.einsum("oai,aow->iw", weight[:, :, b, :], rows3, preferred_element_type=jnp.float32)
        part = shift_cols(part, 1 - b)
        total = part if total is None else total + part
    return total


def per_device(features, first_weight, second_weight, out_grad):
    feat = features[:, 0, :]
    og = out_grad[:, 0, :]
    n_filt = lax.axis_size("filt")
    blk = feat.shape
    f32, bf16 = jnp.float32, jnp.bfloat16
    o, _, _, i_ch = first_weight.shape
    w1r = first_weight.transpose(1, 2, 0, 3).reshape(9, o, i_ch)
    w2r = second_weight.transpose(1, 2, 0, 3).reshape(9, o, i_ch)
    sem = pltpu.SemaphoreType.DMA
    full = (n_filt * blk[0], blk[1])
    nq = i_ch // 128
    wt = (2 * 3 * nq * 3 * o, 128)
    block_out, _, _, _, _, _, _, wt_all = call(
        block_kernel,
        (feat, og, w1r, w2r),
        [(blk, bf16)] * 7 + [(wt, f32)],
        [pltpu.VMEM(full, bf16), pltpu.VMEM(full, bf16)] + [pltpu.VMEM(blk, f32)] * 8 + [pltpu.VMEM(blk, bf16), pltpu.VMEM(blk, f32),
                                      pltpu.VMEM((n_filt,) + blk, bf16), pltpu.VMEM((n_filt,) + blk, bf16)]
        + [sem((4,))] + [sem((n_filt,))] * 4 + [sem((4,))] * 3 + [sem((n_filt,))] * 2,
        2,
    )
    n_rows = lax.axis_size("rows")
    summed = row_sum(wt_all.reshape(n_rows, -1, 128), 0)
    first_grad, second_grad = (
        half.reshape(3, nq, 3, o, 128).transpose(3, 2, 0, 1, 4).reshape(o, 3, 3, i_ch)
        for half in (summed[: n_rows // 2], summed[n_rows // 2:])
    )
    return (block_out[:, None, :], first_grad, second_grad)


def solution(mesh):
    in_specs = (
        P("filt", "rows", None),
        P("filt", None, None, None),
        P("filt", None, None, None),
        P("filt", "rows", None),
    )
    out_specs = (P("filt", "rows", None), P("filt", None, None, None), P("filt", None, None, None))
    return jax.shard_map(
        per_device, mesh=mesh, in_specs=in_specs, out_specs=out_specs, check_vma=False
    )
```

```python
import functools

import jax
import jax.numpy as jnp
from jax import lax
from jax.experimental import pallas as pl
from jax.experimental.pallas import tpu as pltpu
from jax.sharding import PartitionSpec as P

MESH = pl.DeviceIdType.MESH


def peer_id(axis, j):
    if axis == "rows":
        return (j, lax.axis_index("filt"))
    return (lax.axis_index("rows"), j)


def exchange_kernel(axis, n, mode, *refs):
    me = lax.axis_index(axis)

    def each_peer(body):
        def step(k, carry):
            body(lax.rem(me + k, n), lax.rem(me + n - k, n))
            return carry

        lax.fori_loop(1, n, step, 0)

    barrier = pltpu.get_barrier_semaphore()

    def greet(j, s):
        pl.semaphore_signal(barrier, 1, device_id=peer_id(axis, j), device_id_type=MESH)

    each_peer(greet)
    pl.semaphore_wait(barrier, n - 1)

    def gather(src, out_ref, send, recv):
        def copy(j, s):
            return pltpu.make_async_remote_copy(
                src, out_ref.at[me], send.at[j], recv.at[me], device_id=peer_id(axis, j), device_id_type=MESH
            )

        def incoming(j, s):
            return pltpu.make_async_remote_copy(
                src, out_ref.at[s], send.at[s], recv.at[s], device_id=peer_id(axis, s), device_id_type=MESH
            )

        each_peer(lambda j, s: copy(j, s).start())
        return copy, incoming

    def reduce(x_ref, buf, send, recv):
        def copy(j, s):
            return pltpu.make_async_remote_copy(
                x_ref.at[j], buf.at[me], send.at[j], recv.at[me], device_id=peer_id(axis, j), device_id_type=MESH
            )

        def incoming(j, s):
            return pltpu.make_async_remote_copy(
                x_ref.at[s], buf.at[s], send.at[s], recv.at[s], device_id=peer_id(axis, s), device_id_type=MESH
            )

        each_peer(lambda j, s: copy(j, s).start())
        each_peer(lambda j, s: incoming(j, s).wait_recv())
        acc = x_ref[me].astype(jnp.float32)

        def add(k, acc):
            return acc + buf[lax.rem(me + k, n)].astype(jnp.float32)

        acc = lax.fori_loop(1, n, add, acc)
        each_peer(lambda j, s: copy(j, s).wait_send())
        return acc

    if mode == "ag":
        x_ref, out_ref, send, recv = refs
        copy, incoming = gather(x_ref, out_ref, send, recv)
        out_ref[me] = x_ref[...]
        each_peer(lambda j, s: incoming(j, s).wait_recv())
        each_peer(lambda j, s: copy(j, s).wait_send())
    elif mode == "rs":
        x_ref, out_ref, buf, send, recv = refs
        out_ref[...] = reduce(x_ref, buf, send, recv).astype(out_ref.dtype)
    else:
        x_ref, out_ref, buf, send, recv, send2, recv2 = refs
        out_ref[me] = reduce(x_ref, buf, send, recv).astype(out_ref.dtype)
        copy, incoming = gather(out_ref.at[me], out_ref, send2, recv2)
        each_peer(lambda j, s: incoming(j, s).wait_recv())
        each_peer(lambda j, s: copy(j, s).wait_send())


class RowSum:
    def __init__(self, n, x_ref, out_ref, half_buf, half_b, part_buf, sems):
        self.zn = zn = n // 2
        self.me = me = lax.axis_index("rows")
        my_y, self.my_z = me // zn, lax.rem(me, zn)
        self.other = lax.rem(me + zn, n)
        self.mine, self.theirs = my_y * zn, (1 - my_y) * zn
        self.x_ref, self.out_ref, self.half_buf, self.half_b, self.part_buf, self.sems = (
            x_ref, out_ref, half_buf, half_b, part_buf, sems)

    def rcopy(self, src, dst, send, recv, j):
        return pltpu.make_async_remote_copy(
            src, dst, send, recv, device_id=(j, lax.axis_index("filt")), device_id_type=MESH
        )

    def each_z(self, body):
        zn, my_z = self.zn, self.my_z

        def step(t, carry):
            j = lax.rem(my_z + zn // 2 + (t // 2) * (2 * lax.rem(t, 2) - 1), zn)
            body(j, j)
            return carry

        lax.fori_loop(1, zn, step, 0)

    def swap(self):
        return self.rcopy(self.x_ref.at[pl.ds(self.theirs, self.zn)], self.half_buf, self.sems.at[0, 0],
                          self.sems.at[0, 1], self.other)

    def part_out(self, j, s):
        return self.rcopy(self.half_b.at[j], self.part_buf.at[self.my_z], self.sems.at[1, j],
                          self.sems.at[2, self.my_z], self.mine + j)

    def part_in(self, j, s):
        return self.rcopy(self.half_b.at[s], self.part_buf.at[s], self.sems.at[1, s], self.sems.at[2, s],
                          self.mine + s)

    def sum_out(self, j, s):
        me = self.me
        return self.rcopy(self.out_ref.at[me], self.out_ref.at[me], self.sems.at[3, j], self.sems.at[4, self.my_z],
                          self.mine + j)

    def sum_in(self, j, s):
        c = self.mine + s
        return self.rcopy(self.out_ref.at[c], self.out_ref.at[c], self.sems.at[3, s], self.sems.at[4, s], c)

    def back(self):
        half = pl.ds(self.mine, self.zn)
        return self.rcopy(self.out_ref.at[half], self.out_ref.at[half], self.sems.at[5, 0], self.sems.at[5, 1],
                          self.other)

    def s1_start(self):
        self.swap().start()

    def s1_finish(self):
        self.swap().wait_recv()
        x_ref, half_buf, half_b, mine = self.x_ref, self.half_buf, self.half_b, self.mine

        def add_half(t, carry):
            half_b[t] = (x_ref[mine + t].astype(jnp.float32) + half_buf[t].astype(jnp.float32)).astype(half_b.dtype)
            return carry

        lax.fori_loop(0, self.zn, add_half, 0)
        self.swap().wait_send()

    def s2_start(self):
        self.each_z(lambda j, s: self.part_out(j, s).start())

    def s2_finish(self):
        self.each_z(lambda j, s: self.part_in(j, s).wait_recv())
        zn, my_z, part_buf = self.zn, self.my_z, self.part_buf
        acc = self.x_ref[self.me].astype(jnp.float32) + self.half_buf[my_z].astype(jnp.float32)

        def add_part(k, acc):
            return acc + part_buf[lax.rem(my_z + k, zn)].astype(jnp.float32)

        acc = lax.fori_loop(1, zn, add_part, acc)
        self.out_ref[self.me] = acc.astype(self.out_ref.dtype)
        self.each_z(lambda j, s: self.part_out(j, s).wait_send())

    def s3_start(self):
        self.each_z(lambda j, s: self.sum_out(j, s).start())

    def s3_finish(self):
        self.each_z(lambda j, s: self.sum_in(j, s).wait_recv())
        self.each_z(lambda j, s: self.sum_out(j, s).wait_send())

    def s4_start(self):
        self.back().start()

    def s4_finish(self):
        self.back().wait_recv()
        self.back().wait_send()


def row_sum_kernel(n, split, x32, f32_out, xa, xb, oa, ob, *scratch):
    zn = n // 2
    me = lax.axis_index("rows")
    my_z = lax.rem(me, zn)
    mine = (me // zn) * zn

    def dev(j):
        return (j, lax.axis_index("filt"))

    def narrow(c, carry):
        xa[c] = x32[c, pl.ds(0, split), :].astype(xa.dtype)
        xb[c] = x32[c, pl.ds(split, x32.shape[1] - split), :].astype(xb.dtype)
        return carry

    lax.fori_loop(0, n, narrow, 0)
    barrier = pltpu.get_barrier_semaphore()
    pl.semaphore_signal(barrier, 1, device_id=dev(lax.rem(me + zn, n)), device_id_type=MESH)

    def greet(k, carry):
        pl.semaphore_signal(barrier, 1, device_id=dev(mine + lax.rem(my_z + k, zn)), device_id_type=MESH)
        return carry

    lax.fori_loop(1, zn, greet, 0)
    pl.semaphore_wait(barrier, zn)
    a = RowSum(n, xa, oa, *scratch[:4])
    b = RowSum(n, xb, ob, *scratch[4:])
    a.s1_start()
    a.s1_finish()
    a.s2_start()
    b.s1_start()
    b.s1_finish()
    b.s2_start()
    a.s2_finish()
    a.s3_start()
    b.s2_finish()
    b.s3_start()
    a.s3_finish()
    a.s4_start()
    b.s3_finish()
    b.s4_start()
    a.s4_finish()
    b.s4_finish()

    def widen(c, carry):
        f32_out[c, pl.ds(0, split), :] = oa[c].astype(f32_out.dtype)
        f32_out[c, pl.ds(split, x32.shape[1] - split), :] = ob[c].astype(f32_out.dtype)
        return carry

    lax.fori_loop(0, n, widen, 0)


def row_sum(x, collective_id):
    n, k, _ = x.shape
    zn = n // 2
    split = 8 * (k // 16)
    spec = pl.BlockSpec(memory_space=pltpu.VMEM)
    halves = [(n, split, 128), (n, k - split, 128)]
    scratch = [pltpu.VMEM(h, jnp.bfloat16) for h in halves] * 2
    for h in halves:
        blk = (zn,) + h[1:]
        scratch += [pltpu.VMEM(blk, jnp.bfloat16)] * 3 + [pltpu.SemaphoreType.DMA((6, zn))]
    return pl.pallas_call(
        functools.partial(row_sum_kernel, n, split),
        out_shape=jax.ShapeDtypeStruct(x.shape, jnp.float32),
        in_specs=[spec],
        out_specs=spec,
        scratch_shapes=scratch,
        compiler_params=pltpu.CompilerParams(collective_id=collective_id, has_side_effects=True),
    )(x)


def row_dev(j):
    return (j, lax.axis_index("filt"))


def filt_dev(j):
    return (lax.axis_index("rows"), j)


def rcopy(src, dst, send, recv, dev):
    return pltpu.make_async_remote_copy(src, dst, send, recv, device_id=dev, device_id_type=MESH)


def each_filt_peer(body):
    nf = lax.axis_size("filt")
    half = nf // 2
    me = lax.axis_index("filt")

    def step(k, carry):
        far = (nf - k) // half
        off = k - 1 - (half - 1) * (1 - far)
        j = lax.rem(me // half + far, 2) * half + lax.rem(lax.rem(me, half) + off, half)
        body(j, j)
        return carry

    lax.fori_loop(1, nf, step, 0)


def enter(with_filt):
    nr = lax.axis_size("rows")
    me = lax.axis_index("rows")
    barrier = pltpu.get_barrier_semaphore()

    @pl.when(me > 0)
    def _():
        pl.semaphore_signal(barrier, 1, device_id=row_dev(me - 1), device_id_type=MESH)

    @pl.when(me < nr - 1)
    def _():
        pl.semaphore_signal(barrier, 1, device_id=row_dev(me + 1), device_id_type=MESH)

    count = (me + nr - 1) // nr + (2 * nr - 2 - me) // nr
    if with_filt:
        each_filt_peer(lambda j, s: pl.semaphore_signal(barrier, 1, device_id=filt_dev(j), device_id_type=MESH))
        count = count + lax.axis_size("filt") - 1
    pl.semaphore_wait(barrier, count)


class Halo:
    def __init__(self, down_src, up_src, from_prev, from_next, sems):
        self.nr = lax.axis_size("rows")
        self.me = lax.axis_index("rows")
        self.down = lambda j: rcopy(down_src, from_prev, sems.at[0], sems.at[1], row_dev(j))
        self.up = lambda j: rcopy(up_src, from_next, sems.at[2], sems.at[3], row_dev(j))
        me, nr = self.me, self.nr

        @pl.when(me < nr - 1)
        def _():
            self.down(me + 1).start()

        @pl.when(me > 0)
        def _():
            self.up(me - 1).start()

        @pl.when(me == 0)
        def _():
            from_prev[...] = jnp.zeros(from_prev.shape, from_prev.dtype)

        @pl.when(me == nr - 1)
        def _():
            from_next[...] = jnp.zeros(from_next.shape, from_next.dtype)

    def arrived(self):
        me, nr = self.me, self.nr

        @pl.when(me > 0)
        def _():
            self.down(me - 1).wait_recv()

        @pl.when(me < nr - 1)
        def _():
            self.up(me + 1).wait_recv()

    def sent(self):
        me, nr = self.me, self.nr

        @pl.when(me > 0)
        def _():
            self.up(me - 1).wait_send()

        @pl.when(me < nr - 1)
        def _():
            self.down(me + 1).wait_send()


def lane_shift(part, offset):
    width = part.shape[1]
    col = lax.broadcasted_iota(jnp.int32, part.shape, 1)
    if offset == 1:
        return jnp.where(col == width - 1, 0.0, pltpu.roll(part, width - 1, 1))
    return jnp.where(col == 0, 0.0, pltpu.roll(part, 1, 1))


def conv_parts(w_ref, x):
    nk, o, i_ch = w_ref.shape
    every = jnp.dot(w_ref[...].reshape(nk * o, i_ch), x, preferred_element_type=jnp.float32)
    parts = []
    for a in range(3):
        total = None
        for b in range(3):
            k = a * 3 + b
            part = every[k * o:(k + 1) * o]
            if b != 1:
                part = lane_shift(part, b - 1)
            total = part if total is None else total + part
        parts.append(total)
    return parts


def filt_gather(src, dst, blk, send, recv):
    mf = lax.axis_index("filt")

    def out(j, s):
        return rcopy(src, dst.at[pl.ds(mf * blk, blk)], send.at[j], recv.at[mf], filt_dev(j))

    def inc(j, s):
        return rcopy(src, dst.at[pl.ds(s * blk, blk)], send.at[s], recv.at[s], filt_dev(s))

    each_filt_peer(lambda j, s: out(j, s).start())
    dst[pl.ds(mf * blk, blk)] = src[...]
    return (lambda: each_filt_peer(lambda j, s: inc(j, s).wait_recv()),
            lambda: each_filt_peer(lambda j, s: out(j, s).wait_send()))


def weight_rows(rows3, full, wt_ref, base):
    nq = full.shape[0] // 128
    ao = rows3.shape[0]
    shifted = []
    for b in range(3):
        moved = rows3
        if b != 1:
            moved = lane_shift(rows3.astype(jnp.float32), 1 - b).astype(rows3.dtype)
        shifted.append(moved)
    every = lax.dot_general(
        jnp.concatenate(shifted, axis=0), full, (((1,), (1,)), ((), ())), preferred_element_type=jnp.float32
    )
    for b in range(3):
        part = every[b * ao:(b + 1) * ao]
        for q in range(nq):
            wt_ref[pl.ds(base + (b * nq + q) * ao, ao), :] = part[:, q * 128:(q + 1) * 128]


def block_kernel(feat, og, w1r, w2r, out_ref, gs_ref, gprev, gnext, gf_ref, fprev, fnext,
                 wt_all, x_ref, h_ref, p0s, p2s, from_prev, from_next, q0s, q2s, qprev, qnext, hsrc, pre1, tbuf, rbuf,
                 hsems, xsend, xrecv, fsend, frecv, sems1, sems2, sems3, tsend, trecv):
    nf = lax.axis_size("filt")
    mf = lax.axis_index("filt")
    blk = feat.shape[0]
    enter(True)
    x_arrived, x_sent = filt_gather(feat, x_ref, blk, xsend, xrecv)
    x_arrived()
    parts = conv_parts(w1r, x_ref[...])
    p0s[...] = parts[0]
    p2s[...] = parts[2]
    halo = Halo(p0s, p2s, from_prev, from_next, hsems)
    halo.arrived()
    pre1[...] = parts[1] + from_prev[...] + from_next[...]
    hsrc[...] = jnp.maximum(pre1[...], 0.0).astype(hsrc.dtype)
    h_arrived, h_sent = filt_gather(hsrc, h_ref, blk, fsend, frecv)
    h_arrived()
    qs = conv_parts(w2r, h_ref[...])
    q0s[...] = qs[0]
    q2s[...] = qs[2]
    halo1 = Halo(q0s, q2s, qprev, qnext, sems1)
    halo1.arrived()
    pre = qs[1] + qprev[...] + qnext[...] + feat[...].astype(jnp.float32)
    out_ref[...] = jnp.maximum(pre, 0.0).astype(out_ref.dtype)
    gs_ref[...] = jnp.where(pre > 0, og[...].astype(jnp.float32), 0.0).astype(gs_ref.dtype)
    halo2 = Halo(gs_ref, gs_ref, gprev, gnext, sems2)
    halo2.arrived()
    rows3 = jnp.concatenate([gnext[...], gs_ref[...], gprev[...]], axis=0)
    per = 128 // blk
    for q in range(w2r.shape[2] // 128):
        total = None
        for b in range(3):
            lhs = jnp.concatenate([w2r[a * 3 + b, :, q * 128:(q + 1) * 128] for a in range(3)], axis=0)
            part = lax.dot_general(lhs, rows3, (((0,), (0,)), ((), ())), preferred_element_type=jnp.float32)
            if b != 1:
                part = lane_shift(part, 1 - b)
            total = part if total is None else total + part
        for u in range(per):
            tbuf[q * per + u] = total[u * blk:(u + 1) * blk].astype(tbuf.dtype)

    def out(j, s):
        return rcopy(tbuf.at[j], rbuf.at[mf], tsend.at[j], trecv.at[mf], filt_dev(j))

    weight_rows(rows3, h_ref[...], wt_all, wt_all.shape[0] // 2)

    def inc(j, s):
        return rcopy(tbuf.at[s], rbuf.at[s], tsend.at[s], trecv.at[s], filt_dev(s))

    each_filt_peer(lambda j, s: out(j, s).start())
    each_filt_peer(lambda j, s: inc(j, s).wait_recv())
    acc = tbuf[mf].astype(jnp.float32)

    def add(k, acc):
        return acc + rbuf[lax.rem(mf + k, nf)].astype(jnp.float32)

    acc = lax.fori_loop(1, nf, add, acc)
    gf_ref[...] = jnp.where(pre1[...] > 0, acc, 0.0).astype(gf_ref.dtype)
    halo3 = Halo(gf_ref, gf_ref, fprev, fnext, sems3)
    halo3.arrived()
    weight_rows(jnp.concatenate([fnext[...], gf_ref[...], fprev[...]], axis=0), x_ref[...], wt_all, 0)
    x_sent()
    h_sent()
    each_filt_peer(lambda j, s: out(j, s).wait_send())
    halo.sent()
    halo1.sent()
    halo2.sent()
    halo3.sent()


def call(kernel, args, outs, scratch, collective_id):
    spec = pl.BlockSpec(memory_space=pltpu.VMEM)
    return pl.pallas_call(
        kernel,
        out_shape=tuple(jax.ShapeDtypeStruct(shape, dtype) for shape, dtype in outs),
        in_specs=[spec] * len(args),
        out_specs=tuple(spec for _ in outs),
        scratch_shapes=scratch,
        compiler_params=pltpu.CompilerParams(collective_id=collective_id, has_side_effects=True),
    )(*args)


def exchange(x, axis, mode, collective_id, out_dtype=None):
    n = lax.axis_size(axis)
    out_dtype = out_dtype or x.dtype
    sems = [pltpu.SemaphoreType.DMA((n,)), pltpu.SemaphoreType.DMA((n,))]
    if mode == "ag":
        out_shape = (n,) + x.shape
        scratch = sems
    elif mode == "rs":
        out_shape = x.shape[1:]
        scratch = [pltpu.VMEM(x.shape, x.dtype)] + sems
    else:
        out_shape = x.shape
        scratch = [pltpu.VMEM(x.shape, x.dtype)] + sems + sems
    return pl.pallas_call(
        functools.partial(exchange_kernel, axis, n, mode),
        out_shape=jax.ShapeDtypeStruct(out_shape, out_dtype),
        in_specs=[pl.BlockSpec(memory_space=pltpu.VMEM)],
        out_specs=pl.BlockSpec(memory_space=pltpu.VMEM),
        scratch_shapes=scratch,
        compiler_params=pltpu.CompilerParams(collective_id=collective_id, has_side_effects=True),
    )(x)


def shift_cols(value, offset):
    if offset == 0:
        return value
    pad = [(0, 0)] * (value.ndim - 1)
    if offset > 0:
        return jnp.pad(value[..., offset:], pad + [(0, offset)])
    return jnp.pad(value[..., :offset], pad + [(-offset, 0)])


def conv_row(weight, row):
    o = weight.shape[0]
    flat = weight.reshape(o, 9, weight.shape[3])
    parts = jnp.einsum("oki,iw->kow", flat, row, preferred_element_type=jnp.float32)
    return [sum(shift_cols(parts[a * 3 + b], b - 1) for b in range(3)) for a in range(3)]


def weight_terms(rows3, full_row):
    cols = []
    for b in range(3):
        moved = shift_cols(rows3, 1 - b)
        cols.append(jnp.einsum("aow,iw->oai", moved, full_row, preferred_element_type=jnp.float32))
    return jnp.stack(cols, axis=2)


def hidden_terms(weight, rows3):
    total = None
    for b in range(3):
        part = jnp.einsum("oai,aow->iw", weight[:, :, b, :], rows3, preferred_element_type=jnp.float32)
        part = shift_cols(part, 1 - b)
        total = part if total is None else total + part
    return total


def per_device(features, first_weight, second_weight, out_grad):
    feat = features[:, 0, :]
    og = out_grad[:, 0, :]
    n_filt = lax.axis_size("filt")
    blk = feat.shape
    f32, bf16 = jnp.float32, jnp.bfloat16
    o, _, _, i_ch = first_weight.shape
    w1r = first_weight.transpose(1, 2, 0, 3).reshape(9, o, i_ch)
    w2r = second_weight.transpose(1, 2, 0, 3).reshape(9, o, i_ch)
    sem = pltpu.SemaphoreType.DMA
    full = (n_filt * blk[0], blk[1])
    nq = i_ch // 128
    wt = (2 * 3 * nq * 3 * o, 128)
    block_out, _, _, _, _, _, _, wt_all = call(
        block_kernel,
        (feat, og, w1r, w2r),
        [(blk, bf16)] * 7 + [(wt, f32)],
        [pltpu.VMEM(full, bf16), pltpu.VMEM(full, bf16)] + [pltpu.VMEM(blk, f32)] * 8 + [pltpu.VMEM(blk, bf16), pltpu.VMEM(blk, f32),
                                      pltpu.VMEM((n_filt,) + blk, bf16), pltpu.VMEM((n_filt,) + blk, bf16)]
        + [sem((4,))] + [sem((n_filt,))] * 4 + [sem((4,))] * 3 + [sem((n_filt,))] * 2,
        2,
    )
    n_rows = lax.axis_size("rows")
    summed = row_sum(wt_all.reshape(n_rows, -1, 128), 0)
    first_grad, second_grad = (
        half.reshape(3, nq, 3, o, 128).transpose(3, 2, 0, 1, 4).reshape(o, 3, 3, i_ch)
        for half in (summed[: n_rows // 2], summed[n_rows // 2:])
    )
    return (block_out[:, None, :], first_grad, second_grad)


def solution(mesh):
    in_specs = (
        P("filt", "rows", None),
        P("filt", None, None, None),
        P("filt", None, None, None),
        P("filt", "rows", None),
    )
    out_specs = (P("filt", "rows", None), P("filt", None, None, None), P("filt", None, None, None))
    return jax.shard_map(
        per_device, mesh=mesh, in_specs=in_specs, out_specs=out_specs, check_vma=False
    )
```

```python
import functools

import jax
import jax.numpy as jnp
from jax import lax
from jax.experimental import pallas as pl
from jax.experimental.pallas import tpu as pltpu
from jax.sharding import PartitionSpec as P

MESH = pl.DeviceIdType.MESH


def peer_id(axis, j):
    if axis == "rows":
        return (j, lax.axis_index("filt"))
    return (lax.axis_index("rows"), j)


def exchange_kernel(axis, n, mode, *refs):
    me = lax.axis_index(axis)

    def each_peer(body):
        def step(k, carry):
            body(lax.rem(me + k, n), lax.rem(me + n - k, n))
            return carry

        lax.fori_loop(1, n, step, 0)

    barrier = pltpu.get_barrier_semaphore()

    def greet(j, s):
        pl.semaphore_signal(barrier, 1, device_id=peer_id(axis, j), device_id_type=MESH)

    each_peer(greet)
    pl.semaphore_wait(barrier, n - 1)

    def gather(src, out_ref, send, recv):
        def copy(j, s):
            return pltpu.make_async_remote_copy(
                src, out_ref.at[me], send.at[j], recv.at[me], device_id=peer_id(axis, j), device_id_type=MESH
            )

        def incoming(j, s):
            return pltpu.make_async_remote_copy(
                src, out_ref.at[s], send.at[s], recv.at[s], device_id=peer_id(axis, s), device_id_type=MESH
            )

        each_peer(lambda j, s: copy(j, s).start())
        return copy, incoming

    def reduce(x_ref, buf, send, recv):
        def copy(j, s):
            return pltpu.make_async_remote_copy(
                x_ref.at[j], buf.at[me], send.at[j], recv.at[me], device_id=peer_id(axis, j), device_id_type=MESH
            )

        def incoming(j, s):
            return pltpu.make_async_remote_copy(
                x_ref.at[s], buf.at[s], send.at[s], recv.at[s], device_id=peer_id(axis, s), device_id_type=MESH
            )

        each_peer(lambda j, s: copy(j, s).start())
        each_peer(lambda j, s: incoming(j, s).wait_recv())
        acc = x_ref[me].astype(jnp.float32)

        def add(k, acc):
            return acc + buf[lax.rem(me + k, n)].astype(jnp.float32)

        acc = lax.fori_loop(1, n, add, acc)
        each_peer(lambda j, s: copy(j, s).wait_send())
        return acc

    if mode == "ag":
        x_ref, out_ref, send, recv = refs
        copy, incoming = gather(x_ref, out_ref, send, recv)
        out_ref[me] = x_ref[...]
        each_peer(lambda j, s: incoming(j, s).wait_recv())
        each_peer(lambda j, s: copy(j, s).wait_send())
    elif mode == "rs":
        x_ref, out_ref, buf, send, recv = refs
        out_ref[...] = reduce(x_ref, buf, send, recv).astype(out_ref.dtype)
    else:
        x_ref, out_ref, buf, send, recv, send2, recv2 = refs
        out_ref[me] = reduce(x_ref, buf, send, recv).astype(out_ref.dtype)
        copy, incoming = gather(out_ref.at[me], out_ref, send2, recv2)
        each_peer(lambda j, s: incoming(j, s).wait_recv())
        each_peer(lambda j, s: copy(j, s).wait_send())


class RowSum:
    def __init__(self, n, x_ref, out_ref, half_buf, half_b, part_buf, sems):
        self.zn = zn = n // 2
        self.me = me = lax.axis_index("rows")
        my_y, self.my_z = me // zn, lax.rem(me, zn)
        self.other = lax.rem(me + zn, n)
        self.mine, self.theirs = my_y * zn, (1 - my_y) * zn
        self.x_ref, self.out_ref, self.half_buf, self.half_b, self.part_buf, self.sems = (
            x_ref, out_ref, half_buf, half_b, part_buf, sems)

    def rcopy(self, src, dst, send, recv, j):
        return pltpu.make_async_remote_copy(
            src, dst, send, recv, device_id=(j, lax.axis_index("filt")), device_id_type=MESH
        )

    def each_z(self, body):
        zn, my_z = self.zn, self.my_z

        def step(t, carry):
            j = lax.rem(my_z + zn // 2 + (t // 2) * (2 * lax.rem(t, 2) - 1), zn)
            body(j, j)
            return carry

        lax.fori_loop(1, zn, step, 0)

    def swap(self):
        return self.rcopy(self.x_ref.at[pl.ds(self.theirs, self.zn)], self.half_buf, self.sems.at[0, 0],
                          self.sems.at[0, 1], self.other)

    def part_out(self, j, s):
        return self.rcopy(self.half_b.at[j], self.part_buf.at[self.my_z], self.sems.at[1, j],
                          self.sems.at[2, self.my_z], self.mine + j)

    def part_in(self, j, s):
        return self.rcopy(self.half_b.at[s], self.part_buf.at[s], self.sems.at[1, s], self.sems.at[2, s],
                          self.mine + s)

    def sum_out(self, j, s):
        me = self.me
        return self.rcopy(self.out_ref.at[me], self.out_ref.at[me], self.sems.at[3, j], self.sems.at[4, self.my_z],
                          self.mine + j)

    def sum_in(self, j, s):
        c = self.mine + s
        return self.rcopy(self.out_ref.at[c], self.out_ref.at[c], self.sems.at[3, s], self.sems.at[4, s], c)

    def back(self):
        half = pl.ds(self.mine, self.zn)
        return self.rcopy(self.out_ref.at[half], self.out_ref.at[half], self.sems.at[5, 0], self.sems.at[5, 1],
                          self.other)

    def s1_start(self):
        self.swap().start()

    def s1_finish(self):
        self.swap().wait_recv()
        x_ref, half_buf, half_b, mine = self.x_ref, self.half_buf, self.half_b, self.mine

        def add_half(t, carry):
            half_b[t] = (x_ref[mine + t].astype(jnp.float32) + half_buf[t].astype(jnp.float32)).astype(half_b.dtype)
            return carry

        lax.fori_loop(0, self.zn, add_half, 0)
        self.swap().wait_send()

    def s2_start(self):
        self.each_z(lambda j, s: self.part_out(j, s).start())

    def s2_finish(self):
        self.each_z(lambda j, s: self.part_in(j, s).wait_recv())
        zn, my_z, part_buf = self.zn, self.my_z, self.part_buf
        acc = self.x_ref[self.me].astype(jnp.float32) + self.half_buf[my_z].astype(jnp.float32)

        def add_part(k, acc):
            return acc + part_buf[lax.rem(my_z + k, zn)].astype(jnp.float32)

        acc = lax.fori_loop(1, zn, add_part, acc)
        self.out_ref[self.me] = acc.astype(self.out_ref.dtype)
        self.each_z(lambda j, s: self.part_out(j, s).wait_send())

    def s3_start(self):
        self.each_z(lambda j, s: self.sum_out(j, s).start())

    def s3_finish(self):
        self.each_z(lambda j, s: self.sum_in(j, s).wait_recv())
        self.each_z(lambda j, s: self.sum_out(j, s).wait_send())

    def s4_start(self):
        self.back().start()

    def s4_finish(self):
        self.back().wait_recv()
        self.back().wait_send()


def row_sum_kernel(n, split, x32, f32_out, xa, xb, oa, ob, *scratch):
    zn = n // 2
    me = lax.axis_index("rows")
    my_z = lax.rem(me, zn)
    mine = (me // zn) * zn

    def dev(j):
        return (j, lax.axis_index("filt"))

    def narrow(c, carry):
        xa[c] = x32[c, pl.ds(0, split), :].astype(xa.dtype)
        xb[c] = x32[c, pl.ds(split, x32.shape[1] - split), :].astype(xb.dtype)
        return carry

    lax.fori_loop(0, n, narrow, 0)
    barrier = pltpu.get_barrier_semaphore()
    pl.semaphore_signal(barrier, 1, device_id=dev(lax.rem(me + zn, n)), device_id_type=MESH)

    def greet(k, carry):
        pl.semaphore_signal(barrier, 1, device_id=dev(mine + lax.rem(my_z + k, zn)), device_id_type=MESH)
        return carry

    lax.fori_loop(1, zn, greet, 0)
    pl.semaphore_wait(barrier, zn)
    a = RowSum(n, xa, oa, *scratch[:4])
    b = RowSum(n, xb, ob, *scratch[4:])
    a.s1_start()
    a.s1_finish()
    a.s2_start()
    b.s1_start()
    b.s1_finish()
    b.s2_start()
    a.s2_finish()
    a.s3_start()
    b.s2_finish()
    b.s3_start()
    a.s3_finish()
    a.s4_start()
    b.s3_finish()
    b.s4_start()
    a.s4_finish()
    b.s4_finish()

    def widen(c, carry):
        f32_out[c, pl.ds(0, split), :] = oa[c].astype(f32_out.dtype)
        f32_out[c, pl.ds(split, x32.shape[1] - split), :] = ob[c].astype(f32_out.dtype)
        return carry

    lax.fori_loop(0, n, widen, 0)


def row_sum(x, collective_id):
    n, k, _ = x.shape
    zn = n // 2
    split = 8 * (k // 16)
    spec = pl.BlockSpec(memory_space=pltpu.VMEM)
    halves = [(n, split, 128), (n, k - split, 128)]
    scratch = [pltpu.VMEM(h, jnp.bfloat16) for h in halves] * 2
    for h in halves:
        blk = (zn,) + h[1:]
        scratch += [pltpu.VMEM(blk, jnp.bfloat16)] * 3 + [pltpu.SemaphoreType.DMA((6, zn))]
    return pl.pallas_call(
        functools.partial(row_sum_kernel, n, split),
        out_shape=jax.ShapeDtypeStruct(x.shape, jnp.float32),
        in_specs=[spec],
        out_specs=spec,
        scratch_shapes=scratch,
        compiler_params=pltpu.CompilerParams(collective_id=collective_id, has_side_effects=True),
    )(x)


def row_dev(j):
    return (j, lax.axis_index("filt"))


def filt_dev(j):
    return (lax.axis_index("rows"), j)


def rcopy(src, dst, send, recv, dev):
    return pltpu.make_async_remote_copy(src, dst, send, recv, device_id=dev, device_id_type=MESH)


def each_filt_peer(body):
    nf = lax.axis_size("filt")
    half = nf // 2
    me = lax.axis_index("filt")

    def step(k, carry):
        far = (nf - k) // half
        off = k - 1 - (half - 1) * (1 - far)
        j = lax.rem(me // half + far, 2) * half + lax.rem(lax.rem(me, half) + off, half)
        body(j, j)
        return carry

    lax.fori_loop(1, nf, step, 0)


def enter(with_filt):
    nr = lax.axis_size("rows")
    me = lax.axis_index("rows")
    barrier = pltpu.get_barrier_semaphore()

    @pl.when(me > 0)
    def _():
        pl.semaphore_signal(barrier, 1, device_id=row_dev(me - 1), device_id_type=MESH)

    @pl.when(me < nr - 1)
    def _():
        pl.semaphore_signal(barrier, 1, device_id=row_dev(me + 1), device_id_type=MESH)

    count = (me + nr - 1) // nr + (2 * nr - 2 - me) // nr
    if with_filt:
        each_filt_peer(lambda j, s: pl.semaphore_signal(barrier, 1, device_id=filt_dev(j), device_id_type=MESH))
        count = count + lax.axis_size("filt") - 1
    pl.semaphore_wait(barrier, count)


class Halo:
    def __init__(self, down_src, up_src, from_prev, from_next, sems):
        self.nr = lax.axis_size("rows")
        self.me = lax.axis_index("rows")
        self.down = lambda j: rcopy(down_src, from_prev, sems.at[0], sems.at[1], row_dev(j))
        self.up = lambda j: rcopy(up_src, from_next, sems.at[2], sems.at[3], row_dev(j))
        me, nr = self.me, self.nr

        @pl.when(me < nr - 1)
        def _():
            self.down(me + 1).start()

        @pl.when(me > 0)
        def _():
            self.up(me - 1).start()

        @pl.when(me == 0)
        def _():
            from_prev[...] = jnp.zeros(from_prev.shape, from_prev.dtype)

        @pl.when(me == nr - 1)
        def _():
            from_next[...] = jnp.zeros(from_next.shape, from_next.dtype)

    def arrived(self):
        me, nr = self.me, self.nr

        @pl.when(me > 0)
        def _():
            self.down(me - 1).wait_recv()

        @pl.when(me < nr - 1)
        def _():
            self.up(me + 1).wait_recv()

    def sent(self):
        me, nr = self.me, self.nr

        @pl.when(me > 0)
        def _():
            self.up(me - 1).wait_send()

        @pl.when(me < nr - 1)
        def _():
            self.down(me + 1).wait_send()


def lane_shift(part, offset):
    width = part.shape[1]
    col = lax.broadcasted_iota(jnp.int32, part.shape, 1)
    if offset == 1:
        return jnp.where(col == width - 1, 0.0, pltpu.roll(part, width - 1, 1))
    return jnp.where(col == 0, 0.0, pltpu.roll(part, 1, 1))


def conv_parts(w_ref, x):
    nk, o, i_ch = w_ref.shape
    every = jnp.dot(w_ref[...].reshape(nk * o, i_ch), x, preferred_element_type=jnp.float32)
    parts = []
    for a in range(3):
        total = None
        for b in range(3):
            k = a * 3 + b
            part = every[k * o:(k + 1) * o]
            if b != 1:
                part = lane_shift(part, b - 1)
            total = part if total is None else total + part
        parts.append(total)
    return parts


def filt_gather(src, dst, blk, send, recv):
    mf = lax.axis_index("filt")

    def out(j, s):
        return rcopy(src, dst.at[pl.ds(mf * blk, blk)], send.at[j], recv.at[mf], filt_dev(j))

    def inc(j, s):
        return rcopy(src, dst.at[pl.ds(s * blk, blk)], send.at[s], recv.at[s], filt_dev(s))

    each_filt_peer(lambda j, s: out(j, s).start())
    dst[pl.ds(mf * blk, blk)] = src[...]
    return (lambda: each_filt_peer(lambda j, s: inc(j, s).wait_recv()),
            lambda: each_filt_peer(lambda j, s: out(j, s).wait_send()))


def weight_rows(rows3, full, wt_ref, base):
    nq = full.shape[0] // 128
    ao = rows3.shape[0]
    shifted = []
    for b in range(3):
        moved = rows3
        if b != 1:
            moved = lane_shift(rows3.astype(jnp.float32), 1 - b).astype(rows3.dtype)
        shifted.append(moved)
    every = lax.dot_general(
        jnp.concatenate(shifted, axis=0), full, (((1,), (1,)), ((), ())), preferred_element_type=jnp.float32
    )
    for b in range(3):
        part = every[b * ao:(b + 1) * ao]
        for q in range(nq):
            wt_ref[pl.ds(base + (b * nq + q) * ao, ao), :] = part[:, q * 128:(q + 1) * 128]


def block_kernel(feat, og, w1r, w2r, out_ref, gs_ref, gprev, gnext, gf_ref, fprev, fnext,
                 wt_all, x_ref, h_ref, p0s, p2s, from_prev, from_next, q0s, q2s, qprev, qnext, hsrc, pre1, tbuf, rbuf,
                 hsems, xsend, xrecv, fsend, frecv, sems1, sems2, sems3, tsend, trecv):
    nf = lax.axis_size("filt")
    mf = lax.axis_index("filt")
    blk = feat.shape[0]
    enter(True)
    x_arrived, x_sent = filt_gather(feat, x_ref, blk, xsend, xrecv)
    x_arrived()
    parts = conv_parts(w1r, x_ref[...])
    p0s[...] = parts[0]
    p2s[...] = parts[2]
    halo = Halo(p0s, p2s, from_prev, from_next, hsems)
    halo.arrived()
    pre1[...] = parts[1] + from_prev[...] + from_next[...]
    hsrc[...] = jnp.maximum(pre1[...], 0.0).astype(hsrc.dtype)
    h_arrived, h_sent = filt_gather(hsrc, h_ref, blk, fsend, frecv)
    h_arrived()
    qs = conv_parts(w2r, h_ref[...])
    q0s[...] = qs[0]
    q2s[...] = qs[2]
    halo1 = Halo(q0s, q2s, qprev, qnext, sems1)
    halo1.arrived()
    pre = qs[1] + qprev[...] + qnext[...] + feat[...].astype(jnp.float32)
    out_ref[...] = jnp.maximum(pre, 0.0).astype(out_ref.dtype)
    gs_ref[...] = jnp.where(pre > 0, og[...].astype(jnp.float32), 0.0).astype(gs_ref.dtype)
    halo2 = Halo(gs_ref, gs_ref, gprev, gnext, sems2)
    halo2.arrived()
    rows3 = jnp.concatenate([gnext[...], gs_ref[...], gprev[...]], axis=0)
    per = 128 // blk
    for q in range(w2r.shape[2] // 128):
        total = None
        lhs = jnp.concatenate(
            [jnp.concatenate([w2r[a * 3 + b, :, q * 128:(q + 1) * 128] for a in range(3)], axis=0) for b in range(3)],
            axis=1,
        )
        every = lax.dot_general(lhs, rows3, (((0,), (0,)), ((), ())), preferred_element_type=jnp.float32)
        for b in range(3):
            part = every[b * 128:(b + 1) * 128]
            if b != 1:
                part = lane_shift(part, 1 - b)
            total = part if total is None else total + part
        for u in range(per):
            tbuf[q * per + u] = total[u * blk:(u + 1) * blk].astype(tbuf.dtype)

    def out(j, s):
        return rcopy(tbuf.at[j], rbuf.at[mf], tsend.at[j], trecv.at[mf], filt_dev(j))

    weight_rows(rows3, h_ref[...], wt_all, wt_all.shape[0] // 2)

    def inc(j, s):
        return rcopy(tbuf.at[s], rbuf.at[s], tsend.at[s], trecv.at[s], filt_dev(s))

    each_filt_peer(lambda j, s: out(j, s).start())
    each_filt_peer(lambda j, s: inc(j, s).wait_recv())
    acc = tbuf[mf].astype(jnp.float32)

    def add(k, acc):
        return acc + rbuf[lax.rem(mf + k, nf)].astype(jnp.float32)

    acc = lax.fori_loop(1, nf, add, acc)
    gf_ref[...] = jnp.where(pre1[...] > 0, acc, 0.0).astype(gf_ref.dtype)
    halo3 = Halo(gf_ref, gf_ref, fprev, fnext, sems3)
    halo3.arrived()
    weight_rows(jnp.concatenate([fnext[...], gf_ref[...], fprev[...]], axis=0), x_ref[...], wt_all, 0)
    x_sent()
    h_sent()
    each_filt_peer(lambda j, s: out(j, s).wait_send())
    halo.sent()
    halo1.sent()
    halo2.sent()
    halo3.sent()


def call(kernel, args, outs, scratch, collective_id):
    spec = pl.BlockSpec(memory_space=pltpu.VMEM)
    return pl.pallas_call(
        kernel,
        out_shape=tuple(jax.ShapeDtypeStruct(shape, dtype) for shape, dtype in outs),
        in_specs=[spec] * len(args),
        out_specs=tuple(spec for _ in outs),
        scratch_shapes=scratch,
        compiler_params=pltpu.CompilerParams(collective_id=collective_id, has_side_effects=True),
    )(*args)


def exchange(x, axis, mode, collective_id, out_dtype=None):
    n = lax.axis_size(axis)
    out_dtype = out_dtype or x.dtype
    sems = [pltpu.SemaphoreType.DMA((n,)), pltpu.SemaphoreType.DMA((n,))]
    if mode == "ag":
        out_shape = (n,) + x.shape
        scratch = sems
    elif mode == "rs":
        out_shape = x.shape[1:]
        scratch = [pltpu.VMEM(x.shape, x.dtype)] + sems
    else:
        out_shape = x.shape
        scratch = [pltpu.VMEM(x.shape, x.dtype)] + sems + sems
    return pl.pallas_call(
        functools.partial(exchange_kernel, axis, n, mode),
        out_shape=jax.ShapeDtypeStruct(out_shape, out_dtype),
        in_specs=[pl.BlockSpec(memory_space=pltpu.VMEM)],
        out_specs=pl.BlockSpec(memory_space=pltpu.VMEM),
        scratch_shapes=scratch,
        compiler_params=pltpu.CompilerParams(collective_id=collective_id, has_side_effects=True),
    )(x)


def shift_cols(value, offset):
    if offset == 0:
        return value
    pad = [(0, 0)] * (value.ndim - 1)
    if offset > 0:
        return jnp.pad(value[..., offset:], pad + [(0, offset)])
    return jnp.pad(value[..., :offset], pad + [(-offset, 0)])


def conv_row(weight, row):
    o = weight.shape[0]
    flat = weight.reshape(o, 9, weight.shape[3])
    parts = jnp.einsum("oki,iw->kow", flat, row, preferred_element_type=jnp.float32)
    return [sum(shift_cols(parts[a * 3 + b], b - 1) for b in range(3)) for a in range(3)]


def weight_terms(rows3, full_row):
    cols = []
    for b in range(3):
        moved = shift_cols(rows3, 1 - b)
        cols.append(jnp.einsum("aow,iw->oai", moved, full_row, preferred_element_type=jnp.float32))
    return jnp.stack(cols, axis=2)


def hidden_terms(weight, rows3):
    total = None
    for b in range(3):
        part = jnp.einsum("oai,aow->iw", weight[:, :, b, :], rows3, preferred_element_type=jnp.float32)
        part = shift_cols(part, 1 - b)
        total = part if total is None else total + part
    return total


def per_device(features, first_weight, second_weight, out_grad):
    feat = features[:, 0, :]
    og = out_grad[:, 0, :]
    n_filt = lax.axis_size("filt")
    blk = feat.shape
    f32, bf16 = jnp.float32, jnp.bfloat16
    o, _, _, i_ch = first_weight.shape
    w1r = first_weight.transpose(1, 2, 0, 3).reshape(9, o, i_ch)
    w2r = second_weight.transpose(1, 2, 0, 3).reshape(9, o, i_ch)
    sem = pltpu.SemaphoreType.DMA
    full = (n_filt * blk[0], blk[1])
    nq = i_ch // 128
    wt = (2 * 3 * nq * 3 * o, 128)
    block_out, _, _, _, _, _, _, wt_all = call(
        block_kernel,
        (feat, og, w1r, w2r),
        [(blk, bf16)] * 7 + [(wt, f32)],
        [pltpu.VMEM(full, bf16), pltpu.VMEM(full, bf16)] + [pltpu.VMEM(blk, f32)] * 8 + [pltpu.VMEM(blk, bf16), pltpu.VMEM(blk, f32),
                                      pltpu.VMEM((n_filt,) + blk, bf16), pltpu.VMEM((n_filt,) + blk, bf16)]
        + [sem((4,))] + [sem((n_filt,))] * 4 + [sem((4,))] * 3 + [sem((n_filt,))] * 2,
        2,
    )
    n_rows = lax.axis_size("rows")
    summed = row_sum(wt_all.reshape(n_rows, -1, 128), 0)
    first_grad, second_grad = (
        half.reshape(3, nq, 3, o, 128).transpose(3, 2, 0, 1, 4).reshape(o, 3, 3, i_ch)
        for half in (summed[: n_rows // 2], summed[n_rows // 2:])
    )
    return (block_out[:, None, :], first_grad, second_grad)


def solution(mesh):
    in_specs = (
        P("filt", "rows", None),
        P("filt", None, None, None),
        P("filt", None, None, None),
        P("filt", "rows", None),
    )
    out_specs = (P("filt", "rows", None), P("filt", None, None, None), P("filt", None, None, None))
    return jax.shard_map(
        per_device, mesh=mesh, in_specs=in_specs, out_specs=out_specs, check_vma=False
    )
```

```python
import functools

import jax
import jax.numpy as jnp
from jax import lax
from jax.experimental import pallas as pl
from jax.experimental.pallas import tpu as pltpu
from jax.sharding import PartitionSpec as P

MESH = pl.DeviceIdType.MESH


def peer_id(axis, j):
    if axis == "rows":
        return (j, lax.axis_index("filt"))
    return (lax.axis_index("rows"), j)


def exchange_kernel(axis, n, mode, *refs):
    me = lax.axis_index(axis)

    def each_peer(body):
        def step(k, carry):
            body(lax.rem(me + k, n), lax.rem(me + n - k, n))
            return carry

        lax.fori_loop(1, n, step, 0)

    barrier = pltpu.get_barrier_semaphore()

    def greet(j, s):
        pl.semaphore_signal(barrier, 1, device_id=peer_id(axis, j), device_id_type=MESH)

    each_peer(greet)
    pl.semaphore_wait(barrier, n - 1)

    def gather(src, out_ref, send, recv):
        def copy(j, s):
            return pltpu.make_async_remote_copy(
                src, out_ref.at[me], send.at[j], recv.at[me], device_id=peer_id(axis, j), device_id_type=MESH
            )

        def incoming(j, s):
            return pltpu.make_async_remote_copy(
                src, out_ref.at[s], send.at[s], recv.at[s], device_id=peer_id(axis, s), device_id_type=MESH
            )

        each_peer(lambda j, s: copy(j, s).start())
        return copy, incoming

    def reduce(x_ref, buf, send, recv):
        def copy(j, s):
            return pltpu.make_async_remote_copy(
                x_ref.at[j], buf.at[me], send.at[j], recv.at[me], device_id=peer_id(axis, j), device_id_type=MESH
            )

        def incoming(j, s):
            return pltpu.make_async_remote_copy(
                x_ref.at[s], buf.at[s], send.at[s], recv.at[s], device_id=peer_id(axis, s), device_id_type=MESH
            )

        each_peer(lambda j, s: copy(j, s).start())
        each_peer(lambda j, s: incoming(j, s).wait_recv())
        acc = x_ref[me].astype(jnp.float32)

        def add(k, acc):
            return acc + buf[lax.rem(me + k, n)].astype(jnp.float32)

        acc = lax.fori_loop(1, n, add, acc)
        each_peer(lambda j, s: copy(j, s).wait_send())
        return acc

    if mode == "ag":
        x_ref, out_ref, send, recv = refs
        copy, incoming = gather(x_ref, out_ref, send, recv)
        out_ref[me] = x_ref[...]
        each_peer(lambda j, s: incoming(j, s).wait_recv())
        each_peer(lambda j, s: copy(j, s).wait_send())
    elif mode == "rs":
        x_ref, out_ref, buf, send, recv = refs
        out_ref[...] = reduce(x_ref, buf, send, recv).astype(out_ref.dtype)
    else:
        x_ref, out_ref, buf, send, recv, send2, recv2 = refs
        out_ref[me] = reduce(x_ref, buf, send, recv).astype(out_ref.dtype)
        copy, incoming = gather(out_ref.at[me], out_ref, send2, recv2)
        each_peer(lambda j, s: incoming(j, s).wait_recv())
        each_peer(lambda j, s: copy(j, s).wait_send())


class RowSum:
    def __init__(self, n, x_ref, out_ref, half_buf, half_b, part_buf, sems):
        self.zn = zn = n // 2
        self.me = me = lax.axis_index("rows")
        my_y, self.my_z = me // zn, lax.rem(me, zn)
        self.other = lax.rem(me + zn, n)
        self.mine, self.theirs = my_y * zn, (1 - my_y) * zn
        self.x_ref, self.out_ref, self.half_buf, self.half_b, self.part_buf, self.sems = (
            x_ref, out_ref, half_buf, half_b, part_buf, sems)

    def rcopy(self, src, dst, send, recv, j):
        return pltpu.make_async_remote_copy(
            src, dst, send, recv, device_id=(j, lax.axis_index("filt")), device_id_type=MESH
        )

    def each_z(self, body):
        zn, my_z = self.zn, self.my_z

        def step(t, carry):
            j = lax.rem(my_z + zn // 2 + (t // 2) * (2 * lax.rem(t, 2) - 1), zn)
            body(j, j)
            return carry

        lax.fori_loop(1, zn, step, 0)

    def swap(self):
        return self.rcopy(self.x_ref.at[pl.ds(self.theirs, self.zn)], self.half_buf, self.sems.at[0, 0],
                          self.sems.at[0, 1], self.other)

    def part_out(self, j, s):
        return self.rcopy(self.half_b.at[j], self.part_buf.at[self.my_z], self.sems.at[1, j],
                          self.sems.at[2, self.my_z], self.mine + j)

    def part_in(self, j, s):
        return self.rcopy(self.half_b.at[s], self.part_buf.at[s], self.sems.at[1, s], self.sems.at[2, s],
                          self.mine + s)

    def sum_out(self, j, s):
        me = self.me
        return self.rcopy(self.out_ref.at[me], self.out_ref.at[me], self.sems.at[3, j], self.sems.at[4, self.my_z],
                          self.mine + j)

    def sum_in(self, j, s):
        c = self.mine + s
        return self.rcopy(self.out_ref.at[c], self.out_ref.at[c], self.sems.at[3, s], self.sems.at[4, s], c)

    def back(self):
        half = pl.ds(self.mine, self.zn)
        return self.rcopy(self.out_ref.at[half], self.out_ref.at[half], self.sems.at[5, 0], self.sems.at[5, 1],
                          self.other)

    def s1_start(self):
        self.swap().start()

    def s1_finish(self):
        self.swap().wait_recv()
        x_ref, half_buf, half_b, mine = self.x_ref, self.half_buf, self.half_b, self.mine

        def add_half(t, carry):
            half_b[t] = (x_ref[mine + t].astype(jnp.float32) + half_buf[t].astype(jnp.float32)).astype(half_b.dtype)
            return carry

        lax.fori_loop(0, self.zn, add_half, 0)
        self.swap().wait_send()

    def s2_start(self):
        self.each_z(lambda j, s: self.part_out(j, s).start())

    def s2_finish(self):
        self.each_z(lambda j, s: self.part_in(j, s).wait_recv())
        zn, my_z, part_buf = self.zn, self.my_z, self.part_buf
        acc = self.x_ref[self.me].astype(jnp.float32) + self.half_buf[my_z].astype(jnp.float32)

        def add_part(k, acc):
            return acc + part_buf[lax.rem(my_z + k, zn)].astype(jnp.float32)

        acc = lax.fori_loop(1, zn, add_part, acc)
        self.out_ref[self.me] = acc.astype(self.out_ref.dtype)
        self.each_z(lambda j, s: self.part_out(j, s).wait_send())

    def s3_start(self):
        self.each_z(lambda j, s: self.sum_out(j, s).start())

    def s3_finish(self):
        self.each_z(lambda j, s: self.sum_in(j, s).wait_recv())
        self.each_z(lambda j, s: self.sum_out(j, s).wait_send())

    def s4_start(self):
        self.back().start()

    def s4_finish(self):
        self.back().wait_recv()
        self.back().wait_send()


def row_sum_kernel(n, split, x32, f_lo, f_hi, xa, xb, oa, ob, *scratch):
    zn = n // 2
    me = lax.axis_index("rows")
    my_z = lax.rem(me, zn)
    mine = (me // zn) * zn

    def dev(j):
        return (j, lax.axis_index("filt"))

    def narrow(c, carry):
        xa[c] = x32[c, pl.ds(0, split), :].astype(xa.dtype)
        xb[c] = x32[c, pl.ds(split, x32.shape[1] - split), :].astype(xb.dtype)
        return carry

    lax.fori_loop(0, n, narrow, 0)
    barrier = pltpu.get_barrier_semaphore()
    pl.semaphore_signal(barrier, 1, device_id=dev(lax.rem(me + zn, n)), device_id_type=MESH)

    def greet(k, carry):
        pl.semaphore_signal(barrier, 1, device_id=dev(mine + lax.rem(my_z + k, zn)), device_id_type=MESH)
        return carry

    lax.fori_loop(1, zn, greet, 0)
    pl.semaphore_wait(barrier, zn)
    a = RowSum(n, xa, oa, *scratch[:4])
    b = RowSum(n, xb, ob, *scratch[4:])
    a.s1_start()
    a.s1_finish()
    a.s2_start()
    b.s1_start()
    b.s1_finish()
    b.s2_start()
    a.s2_finish()
    a.s3_start()
    b.s2_finish()
    b.s3_start()
    a.s3_finish()
    a.s4_start()
    b.s3_finish()
    b.s4_start()
    a.s4_finish()
    b.s4_finish()

    def widen(f_ref, base):
        def body(c, carry):
            f_ref[c, pl.ds(0, split), :] = oa[base + c].astype(f_ref.dtype)
            f_ref[c, pl.ds(split, x32.shape[1] - split), :] = ob[base + c].astype(f_ref.dtype)
            return carry

        lax.fori_loop(0, f_ref.shape[0], body, 0)

    widen(f_lo, 0)
    widen(f_hi, f_lo.shape[0])


def row_sum(x, collective_id):
    n, k, _ = x.shape
    zn = n // 2
    split = 8 * (k // 16)
    spec = pl.BlockSpec(memory_space=pltpu.VMEM)
    halves = [(n, split, 128), (n, k - split, 128)]
    scratch = [pltpu.VMEM(h, jnp.bfloat16) for h in halves] * 2
    for h in halves:
        blk = (zn,) + h[1:]
        scratch += [pltpu.VMEM(blk, jnp.bfloat16)] * 3 + [pltpu.SemaphoreType.DMA((6, zn))]
    return pl.pallas_call(
        functools.partial(row_sum_kernel, n, split),
        out_shape=(jax.ShapeDtypeStruct((zn,) + x.shape[1:], jnp.float32),) * 2,
        in_specs=[spec],
        out_specs=(spec, spec),
        scratch_shapes=scratch,
        compiler_params=pltpu.CompilerParams(collective_id=collective_id, has_side_effects=True),
    )(x)


def row_dev(j):
    return (j, lax.axis_index("filt"))


def filt_dev(j):
    return (lax.axis_index("rows"), j)


def rcopy(src, dst, send, recv, dev):
    return pltpu.make_async_remote_copy(src, dst, send, recv, device_id=dev, device_id_type=MESH)


def each_filt_peer(body):
    nf = lax.axis_size("filt")
    half = nf // 2
    me = lax.axis_index("filt")

    def step(k, carry):
        far = (nf - k) // half
        off = k - 1 - (half - 1) * (1 - far)
        j = lax.rem(me // half + far, 2) * half + lax.rem(lax.rem(me, half) + off, half)
        body(j, j)
        return carry

    lax.fori_loop(1, nf, step, 0)


def enter(with_filt):
    nr = lax.axis_size("rows")
    me = lax.axis_index("rows")
    barrier = pltpu.get_barrier_semaphore()

    @pl.when(me > 0)
    def _():
        pl.semaphore_signal(barrier, 1, device_id=row_dev(me - 1), device_id_type=MESH)

    @pl.when(me < nr - 1)
    def _():
        pl.semaphore_signal(barrier, 1, device_id=row_dev(me + 1), device_id_type=MESH)

    count = (me + nr - 1) // nr + (2 * nr - 2 - me) // nr
    if with_filt:
        each_filt_peer(lambda j, s: pl.semaphore_signal(barrier, 1, device_id=filt_dev(j), device_id_type=MESH))
        count = count + lax.axis_size("filt") - 1
    pl.semaphore_wait(barrier, count)


class Halo:
    def __init__(self, down_src, up_src, from_prev, from_next, sems):
        self.nr = lax.axis_size("rows")
        self.me = lax.axis_index("rows")
        self.down = lambda j: rcopy(down_src, from_prev, sems.at[0], sems.at[1], row_dev(j))
        self.up = lambda j: rcopy(up_src, from_next, sems.at[2], sems.at[3], row_dev(j))
        me, nr = self.me, self.nr

        @pl.when(me < nr - 1)
        def _():
            self.down(me + 1).start()

        @pl.when(me > 0)
        def _():
            self.up(me - 1).start()

        @pl.when(me == 0)
        def _():
            from_prev[...] = jnp.zeros(from_prev.shape, from_prev.dtype)

        @pl.when(me == nr - 1)
        def _():
            from_next[...] = jnp.zeros(from_next.shape, from_next.dtype)

    def arrived(self):
        me, nr = self.me, self.nr

        @pl.when(me > 0)
        def _():
            self.down(me - 1).wait_recv()

        @pl.when(me < nr - 1)
        def _():
            self.up(me + 1).wait_recv()

    def sent(self):
        me, nr = self.me, self.nr

        @pl.when(me > 0)
        def _():
            self.up(me - 1).wait_send()

        @pl.when(me < nr - 1)
        def _():
            self.down(me + 1).wait_send()


def lane_shift(part, offset):
    width = part.shape[1]
    col = lax.broadcasted_iota(jnp.int32, part.shape, 1)
    if offset == 1:
        return jnp.where(col == width - 1, 0.0, pltpu.roll(part, width - 1, 1))
    return jnp.where(col == 0, 0.0, pltpu.roll(part, 1, 1))


def conv_parts(w_ref, x):
    nk, o, i_ch = w_ref.shape
    every = jnp.dot(w_ref[...].reshape(nk * o, i_ch), x, preferred_element_type=jnp.float32)
    parts = []
    for a in range(3):
        total = None
        for b in range(3):
            k = a * 3 + b
            part = every[k * o:(k + 1) * o]
            if b != 1:
                part = lane_shift(part, b - 1)
            total = part if total is None else total + part
        parts.append(total)
    return parts


def filt_gather(src, dst, blk, send, recv):
    mf = lax.axis_index("filt")

    def out(j, s):
        return rcopy(src, dst.at[pl.ds(mf * blk, blk)], send.at[j], recv.at[mf], filt_dev(j))

    def inc(j, s):
        return rcopy(src, dst.at[pl.ds(s * blk, blk)], send.at[s], recv.at[s], filt_dev(s))

    each_filt_peer(lambda j, s: out(j, s).start())
    dst[pl.ds(mf * blk, blk)] = src[...]
    return (lambda: each_filt_peer(lambda j, s: inc(j, s).wait_recv()),
            lambda: each_filt_peer(lambda j, s: out(j, s).wait_send()))


def weight_rows(rows3, full, wt_ref, base):
    nq = full.shape[0] // 128
    ao = rows3.shape[0]
    shifted = []
    for b in range(3):
        moved = rows3
        if b != 1:
            moved = lane_shift(rows3.astype(jnp.float32), 1 - b).astype(rows3.dtype)
        shifted.append(moved)
    every = lax.dot_general(
        jnp.concatenate(shifted, axis=0), full, (((1,), (1,)), ((), ())), preferred_element_type=jnp.float32
    )
    for b in range(3):
        part = every[b * ao:(b + 1) * ao]
        for q in range(nq):
            wt_ref[pl.ds(base + (b * nq + q) * ao, ao), :] = part[:, q * 128:(q + 1) * 128]


def block_kernel(feat, og, w1r, w2r, out_ref, gs_ref, gprev, gnext, gf_ref, fprev, fnext,
                 wt_all, x_ref, h_ref, p0s, p2s, from_prev, from_next, q0s, q2s, qprev, qnext, hsrc, pre1, tbuf, rbuf,
                 hsems, xsend, xrecv, fsend, frecv, sems1, sems2, sems3, tsend, trecv):
    nf = lax.axis_size("filt")
    mf = lax.axis_index("filt")
    blk = feat.shape[0]
    enter(True)
    x_arrived, x_sent = filt_gather(feat, x_ref, blk, xsend, xrecv)
    x_arrived()
    parts = conv_parts(w1r, x_ref[...])
    p0s[...] = parts[0]
    p2s[...] = parts[2]
    halo = Halo(p0s, p2s, from_prev, from_next, hsems)
    halo.arrived()
    pre1[...] = parts[1] + from_prev[...] + from_next[...]
    hsrc[...] = jnp.maximum(pre1[...], 0.0).astype(hsrc.dtype)
    h_arrived, h_sent = filt_gather(hsrc, h_ref, blk, fsend, frecv)
    h_arrived()
    qs = conv_parts(w2r, h_ref[...])
    q0s[...] = qs[0]
    q2s[...] = qs[2]
    halo1 = Halo(q0s, q2s, qprev, qnext, sems1)
    halo1.arrived()
    pre = qs[1] + qprev[...] + qnext[...] + feat[...].astype(jnp.float32)
    out_ref[...] = jnp.maximum(pre, 0.0).astype(out_ref.dtype)
    gs_ref[...] = jnp.where(pre > 0, og[...].astype(jnp.float32), 0.0).astype(gs_ref.dtype)
    halo2 = Halo(gs_ref, gs_ref, gprev, gnext, sems2)
    halo2.arrived()
    rows3 = jnp.concatenate([gnext[...], gs_ref[...], gprev[...]], axis=0)
    per = 128 // blk
    for q in range(w2r.shape[2] // 128):
        total = None
        for b in range(3):
            lhs = jnp.concatenate([w2r[a * 3 + b, :, q * 128:(q + 1) * 128] for a in range(3)], axis=0)
            part = lax.dot_general(lhs, rows3, (((0,), (0,)), ((), ())), preferred_element_type=jnp.float32)
            if b != 1:
                part = lane_shift(part, 1 - b)
            total = part if total is None else total + part
        for u in range(per):
            tbuf[q * per + u] = total[u * blk:(u + 1) * blk].astype(tbuf.dtype)

    def out(j, s):
        return rcopy(tbuf.at[j], rbuf.at[mf], tsend.at[j], trecv.at[mf], filt_dev(j))

    weight_rows(rows3, h_ref[...], wt_all, wt_all.shape[0] // 2)

    def inc(j, s):
        return rcopy(tbuf.at[s], rbuf.at[s], tsend.at[s], trecv.at[s], filt_dev(s))

    each_filt_peer(lambda j, s: out(j, s).start())
    each_filt_peer(lambda j, s: inc(j, s).wait_recv())
    acc = tbuf[mf].astype(jnp.float32)

    def add(k, acc):
        return acc + rbuf[lax.rem(mf + k, nf)].astype(jnp.float32)

    acc = lax.fori_loop(1, nf, add, acc)
    gf_ref[...] = jnp.where(pre1[...] > 0, acc, 0.0).astype(gf_ref.dtype)
    halo3 = Halo(gf_ref, gf_ref, fprev, fnext, sems3)
    halo3.arrived()
    weight_rows(jnp.concatenate([fnext[...], gf_ref[...], fprev[...]], axis=0), x_ref[...], wt_all, 0)
    x_sent()
    h_sent()
    each_filt_peer(lambda j, s: out(j, s).wait_send())
    halo.sent()
    halo1.sent()
    halo2.sent()
    halo3.sent()


def call(kernel, args, outs, scratch, collective_id):
    spec = pl.BlockSpec(memory_space=pltpu.VMEM)
    return pl.pallas_call(
        kernel,
        out_shape=tuple(jax.ShapeDtypeStruct(shape, dtype) for shape, dtype in outs),
        in_specs=[spec] * len(args),
        out_specs=tuple(spec for _ in outs),
        scratch_shapes=scratch,
        compiler_params=pltpu.CompilerParams(collective_id=collective_id, has_side_effects=True),
    )(*args)


def exchange(x, axis, mode, collective_id, out_dtype=None):
    n = lax.axis_size(axis)
    out_dtype = out_dtype or x.dtype
    sems = [pltpu.SemaphoreType.DMA((n,)), pltpu.SemaphoreType.DMA((n,))]
    if mode == "ag":
        out_shape = (n,) + x.shape
        scratch = sems
    elif mode == "rs":
        out_shape = x.shape[1:]
        scratch = [pltpu.VMEM(x.shape, x.dtype)] + sems
    else:
        out_shape = x.shape
        scratch = [pltpu.VMEM(x.shape, x.dtype)] + sems + sems
    return pl.pallas_call(
        functools.partial(exchange_kernel, axis, n, mode),
        out_shape=jax.ShapeDtypeStruct(out_shape, out_dtype),
        in_specs=[pl.BlockSpec(memory_space=pltpu.VMEM)],
        out_specs=pl.BlockSpec(memory_space=pltpu.VMEM),
        scratch_shapes=scratch,
        compiler_params=pltpu.CompilerParams(collective_id=collective_id, has_side_effects=True),
    )(x)


def shift_cols(value, offset):
    if offset == 0:
        return value
    pad = [(0, 0)] * (value.ndim - 1)
    if offset > 0:
        return jnp.pad(value[..., offset:], pad + [(0, offset)])
    return jnp.pad(value[..., :offset], pad + [(-offset, 0)])


def conv_row(weight, row):
    o = weight.shape[0]
    flat = weight.reshape(o, 9, weight.shape[3])
    parts = jnp.einsum("oki,iw->kow", flat, row, preferred_element_type=jnp.float32)
    return [sum(shift_cols(parts[a * 3 + b], b - 1) for b in range(3)) for a in range(3)]


def weight_terms(rows3, full_row):
    cols = []
    for b in range(3):
        moved = shift_cols(rows3, 1 - b)
        cols.append(jnp.einsum("aow,iw->oai", moved, full_row, preferred_element_type=jnp.float32))
    return jnp.stack(cols, axis=2)


def hidden_terms(weight, rows3):
    total = None
    for b in range(3):
        part = jnp.einsum("oai,aow->iw", weight[:, :, b, :], rows3, preferred_element_type=jnp.float32)
        part = shift_cols(part, 1 - b)
        total = part if total is None else total + part
    return total


def per_device(features, first_weight, second_weight, out_grad):
    feat = features[:, 0, :]
    og = out_grad[:, 0, :]
    n_filt = lax.axis_size("filt")
    blk = feat.shape
    f32, bf16 = jnp.float32, jnp.bfloat16
    o, _, _, i_ch = first_weight.shape
    w1r = first_weight.transpose(1, 2, 0, 3).reshape(9, o, i_ch)
    w2r = second_weight.transpose(1, 2, 0, 3).reshape(9, o, i_ch)
    sem = pltpu.SemaphoreType.DMA
    full = (n_filt * blk[0], blk[1])
    nq = i_ch // 128
    wt = (2 * 3 * nq * 3 * o, 128)
    block_out, _, _, _, _, _, _, wt_all = call(
        block_kernel,
        (feat, og, w1r, w2r),
        [(blk, bf16)] * 7 + [(wt, f32)],
        [pltpu.VMEM(full, bf16), pltpu.VMEM(full, bf16)] + [pltpu.VMEM(blk, f32)] * 8 + [pltpu.VMEM(blk, bf16), pltpu.VMEM(blk, f32),
                                      pltpu.VMEM((n_filt,) + blk, bf16), pltpu.VMEM((n_filt,) + blk, bf16)]
        + [sem((4,))] + [sem((n_filt,))] * 4 + [sem((4,))] * 3 + [sem((n_filt,))] * 2,
        2,
    )
    n_rows = lax.axis_size("rows")
    summed = row_sum(wt_all.reshape(n_rows, -1, 128), 0)
    first_grad, second_grad = (
        half.reshape(3, nq, 3, o, 128).transpose(3, 2, 0, 1, 4).reshape(o, 3, 3, i_ch)
        for half in summed
    )
    return (block_out[:, None, :], first_grad, second_grad)


def solution(mesh):
    in_specs = (
        P("filt", "rows", None),
        P("filt", None, None, None),
        P("filt", None, None, None),
        P("filt", "rows", None),
    )
    out_specs = (P("filt", "rows", None), P("filt", None, None, None), P("filt", None, None, None))
    return jax.shard_map(
        per_device, mesh=mesh, in_specs=in_specs, out_specs=out_specs, check_vma=False
    )
```

```python
import functools

import jax
import jax.numpy as jnp
from jax import lax
from jax.experimental import pallas as pl
from jax.experimental.pallas import tpu as pltpu
from jax.sharding import PartitionSpec as P

MESH = pl.DeviceIdType.MESH


def peer_id(axis, j):
    if axis == "rows":
        return (j, lax.axis_index("filt"))
    return (lax.axis_index("rows"), j)


def exchange_kernel(axis, n, mode, *refs):
    me = lax.axis_index(axis)

    def each_peer(body):
        def step(k, carry):
            body(lax.rem(me + k, n), lax.rem(me + n - k, n))
            return carry

        lax.fori_loop(1, n, step, 0)

    barrier = pltpu.get_barrier_semaphore()

    def greet(j, s):
        pl.semaphore_signal(barrier, 1, device_id=peer_id(axis, j), device_id_type=MESH)

    each_peer(greet)
    pl.semaphore_wait(barrier, n - 1)

    def gather(src, out_ref, send, recv):
        def copy(j, s):
            return pltpu.make_async_remote_copy(
                src, out_ref.at[me], send.at[j], recv.at[me], device_id=peer_id(axis, j), device_id_type=MESH
            )

        def incoming(j, s):
            return pltpu.make_async_remote_copy(
                src, out_ref.at[s], send.at[s], recv.at[s], device_id=peer_id(axis, s), device_id_type=MESH
            )

        each_peer(lambda j, s: copy(j, s).start())
        return copy, incoming

    def reduce(x_ref, buf, send, recv):
        def copy(j, s):
            return pltpu.make_async_remote_copy(
                x_ref.at[j], buf.at[me], send.at[j], recv.at[me], device_id=peer_id(axis, j), device_id_type=MESH
            )

        def incoming(j, s):
            return pltpu.make_async_remote_copy(
                x_ref.at[s], buf.at[s], send.at[s], recv.at[s], device_id=peer_id(axis, s), device_id_type=MESH
            )

        each_peer(lambda j, s: copy(j, s).start())
        each_peer(lambda j, s: incoming(j, s).wait_recv())
        acc = x_ref[me].astype(jnp.float32)

        def add(k, acc):
            return acc + buf[lax.rem(me + k, n)].astype(jnp.float32)

        acc = lax.fori_loop(1, n, add, acc)
        each_peer(lambda j, s: copy(j, s).wait_send())
        return acc

    if mode == "ag":
        x_ref, out_ref, send, recv = refs
        copy, incoming = gather(x_ref, out_ref, send, recv)
        out_ref[me] = x_ref[...]
        each_peer(lambda j, s: incoming(j, s).wait_recv())
        each_peer(lambda j, s: copy(j, s).wait_send())
    elif mode == "rs":
        x_ref, out_ref, buf, send, recv = refs
        out_ref[...] = reduce(x_ref, buf, send, recv).astype(out_ref.dtype)
    else:
        x_ref, out_ref, buf, send, recv, send2, recv2 = refs
        out_ref[me] = reduce(x_ref, buf, send, recv).astype(out_ref.dtype)
        copy, incoming = gather(out_ref.at[me], out_ref, send2, recv2)
        each_peer(lambda j, s: incoming(j, s).wait_recv())
        each_peer(lambda j, s: copy(j, s).wait_send())


class RowSum:
    def __init__(self, n, x_ref, out_ref, half_buf, half_b, part_buf, sems):
        self.zn = zn = n // 2
        self.me = me = lax.axis_index("rows")
        my_y, self.my_z = me // zn, lax.rem(me, zn)
        self.other = lax.rem(me + zn, n)
        self.mine, self.theirs = my_y * zn, (1 - my_y) * zn
        self.x_ref, self.out_ref, self.half_buf, self.half_b, self.part_buf, self.sems = (
            x_ref, out_ref, half_buf, half_b, part_buf, sems)

    def rcopy(self, src, dst, send, recv, j):
        return pltpu.make_async_remote_copy(
            src, dst, send, recv, device_id=(j, lax.axis_index("filt")), device_id_type=MESH
        )

    def each_z(self, body):
        zn, my_z = self.zn, self.my_z

        def step(t, carry):
            j = lax.rem(my_z + zn // 2 + (t // 2) * (2 * lax.rem(t, 2) - 1), zn)
            body(j, j)
            return carry

        lax.fori_loop(1, zn, step, 0)

    def swap(self):
        return self.rcopy(self.x_ref.at[pl.ds(self.theirs, self.zn)], self.half_buf, self.sems.at[0, 0],
                          self.sems.at[0, 1], self.other)

    def part_out(self, j, s):
        return self.rcopy(self.half_b.at[j], self.part_buf.at[self.my_z], self.sems.at[1, j],
                          self.sems.at[2, self.my_z], self.mine + j)

    def part_in(self, j, s):
        return self.rcopy(self.half_b.at[s], self.part_buf.at[s], self.sems.at[1, s], self.sems.at[2, s],
                          self.mine + s)

    def sum_out(self, j, s):
        me = self.me
        return self.rcopy(self.out_ref.at[me], self.out_ref.at[me], self.sems.at[3, j], self.sems.at[4, self.my_z],
                          self.mine + j)

    def sum_in(self, j, s):
        c = self.mine + s
        return self.rcopy(self.out_ref.at[c], self.out_ref.at[c], self.sems.at[3, s], self.sems.at[4, s], c)

    def back(self):
        half = pl.ds(self.mine, self.zn)
        return self.rcopy(self.out_ref.at[half], self.out_ref.at[half], self.sems.at[5, 0], self.sems.at[5, 1],
                          self.other)

    def s1_start(self):
        self.swap().start()

    def s1_finish(self):
        self.swap().wait_recv()
        x_ref, half_buf, half_b, mine = self.x_ref, self.half_buf, self.half_b, self.mine

        def add_half(t, carry):
            half_b[t] = (x_ref[mine + t].astype(jnp.float32) + half_buf[t].astype(jnp.float32)).astype(half_b.dtype)
            return carry

        lax.fori_loop(0, self.zn, add_half, 0)
        self.swap().wait_send()

    def s2_start(self):
        self.each_z(lambda j, s: self.part_out(j, s).start())

    def s2_finish(self):
        self.each_z(lambda j, s: self.part_in(j, s).wait_recv())
        zn, my_z, part_buf = self.zn, self.my_z, self.part_buf
        acc = self.x_ref[self.me].astype(jnp.float32) + self.half_buf[my_z].astype(jnp.float32)

        def add_part(k, acc):
            return acc + part_buf[lax.rem(my_z + k, zn)].astype(jnp.float32)

        acc = lax.fori_loop(1, zn, add_part, acc)
        self.out_ref[self.me] = acc.astype(self.out_ref.dtype)
        self.each_z(lambda j, s: self.part_out(j, s).wait_send())

    def s3_start(self):
        self.each_z(lambda j, s: self.sum_out(j, s).start())

    def s3_finish(self):
        self.each_z(lambda j, s: self.sum_in(j, s).wait_recv())
        self.each_z(lambda j, s: self.sum_out(j, s).wait_send())

    def s4_start(self):
        self.back().start()

    def s4_finish(self):
        self.back().wait_recv()
        self.back().wait_send()


def row_sum_kernel(n, split, x32, f32_out, xa, xb, oa, ob, *scratch):
    zn = n // 2
    me = lax.axis_index("rows")
    my_z = lax.rem(me, zn)
    mine = (me // zn) * zn

    def dev(j):
        return (j, lax.axis_index("filt"))

    def narrow(c, carry):
        xa[c] = x32[c, pl.ds(0, split), :].astype(xa.dtype)
        xb[c] = x32[c, pl.ds(split, x32.shape[1] - split), :].astype(xb.dtype)
        return carry

    barrier = pltpu.get_barrier_semaphore()
    pl.semaphore_signal(barrier, 1, device_id=dev(lax.rem(me + zn, n)), device_id_type=MESH)

    def greet(k, carry):
        pl.semaphore_signal(barrier, 1, device_id=dev(mine + lax.rem(my_z + k, zn)), device_id_type=MESH)
        return carry

    lax.fori_loop(1, zn, greet, 0)
    lax.fori_loop(0, n, narrow, 0)
    pl.semaphore_wait(barrier, zn)
    a = RowSum(n, xa, oa, *scratch[:4])
    b = RowSum(n, xb, ob, *scratch[4:])
    a.s1_start()
    a.s1_finish()
    a.s2_start()
    b.s1_start()
    b.s1_finish()
    b.s2_start()
    a.s2_finish()
    a.s3_start()
    b.s2_finish()
    b.s3_start()
    a.s3_finish()
    a.s4_start()
    b.s3_finish()
    b.s4_start()
    a.s4_finish()
    b.s4_finish()

    def widen(c, carry):
        f32_out[c, pl.ds(0, split), :] = oa[c].astype(f32_out.dtype)
        f32_out[c, pl.ds(split, x32.shape[1] - split), :] = ob[c].astype(f32_out.dtype)
        return carry

    lax.fori_loop(0, n, widen, 0)


def row_sum(x, collective_id):
    n, k, _ = x.shape
    zn = n // 2
    split = 8 * (k // 16)
    spec = pl.BlockSpec(memory_space=pltpu.VMEM)
    halves = [(n, split, 128), (n, k - split, 128)]
    scratch = [pltpu.VMEM(h, jnp.bfloat16) for h in halves] * 2
    for h in halves:
        blk = (zn,) + h[1:]
        scratch += [pltpu.VMEM(blk, jnp.bfloat16)] * 3 + [pltpu.SemaphoreType.DMA((6, zn))]
    return pl.pallas_call(
        functools.partial(row_sum_kernel, n, split),
        out_shape=jax.ShapeDtypeStruct(x.shape, jnp.float32),
        in_specs=[spec],
        out_specs=spec,
        scratch_shapes=scratch,
        compiler_params=pltpu.CompilerParams(collective_id=collective_id, has_side_effects=True),
    )(x)


def row_dev(j):
    return (j, lax.axis_index("filt"))


def filt_dev(j):
    return (lax.axis_index("rows"), j)


def rcopy(src, dst, send, recv, dev):
    return pltpu.make_async_remote_copy(src, dst, send, recv, device_id=dev, device_id_type=MESH)


def each_filt_peer(body):
    nf = lax.axis_size("filt")
    half = nf // 2
    me = lax.axis_index("filt")

    def step(k, carry):
        far = (nf - k) // half
        off = k - 1 - (half - 1) * (1 - far)
        j = lax.rem(me // half + far, 2) * half + lax.rem(lax.rem(me, half) + off, half)
        body(j, j)
        return carry

    lax.fori_loop(1, nf, step, 0)


def enter(with_filt):
    nr = lax.axis_size("rows")
    me = lax.axis_index("rows")
    barrier = pltpu.get_barrier_semaphore()

    @pl.when(me > 0)
    def _():
        pl.semaphore_signal(barrier, 1, device_id=row_dev(me - 1), device_id_type=MESH)

    @pl.when(me < nr - 1)
    def _():
        pl.semaphore_signal(barrier, 1, device_id=row_dev(me + 1), device_id_type=MESH)

    count = (me + nr - 1) // nr + (2 * nr - 2 - me) // nr
    if with_filt:
        each_filt_peer(lambda j, s: pl.semaphore_signal(barrier, 1, device_id=filt_dev(j), device_id_type=MESH))
        count = count + lax.axis_size("filt") - 1
    pl.semaphore_wait(barrier, count)


class Halo:
    def __init__(self, down_src, up_src, from_prev, from_next, sems):
        self.nr = lax.axis_size("rows")
        self.me = lax.axis_index("rows")
        self.down = lambda j: rcopy(down_src, from_prev, sems.at[0], sems.at[1], row_dev(j))
        self.up = lambda j: rcopy(up_src, from_next, sems.at[2], sems.at[3], row_dev(j))
        me, nr = self.me, self.nr

        @pl.when(me < nr - 1)
        def _():
            self.down(me + 1).start()

        @pl.when(me > 0)
        def _():
            self.up(me - 1).start()

        @pl.when(me == 0)
        def _():
            from_prev[...] = jnp.zeros(from_prev.shape, from_prev.dtype)

        @pl.when(me == nr - 1)
        def _():
            from_next[...] = jnp.zeros(from_next.shape, from_next.dtype)

    def arrived(self):
        me, nr = self.me, self.nr

        @pl.when(me > 0)
        def _():
            self.down(me - 1).wait_recv()

        @pl.when(me < nr - 1)
        def _():
            self.up(me + 1).wait_recv()

    def sent(self):
        me, nr = self.me, self.nr

        @pl.when(me > 0)
        def _():
            self.up(me - 1).wait_send()

        @pl.when(me < nr - 1)
        def _():
            self.down(me + 1).wait_send()


def lane_shift(part, offset):
    width = part.shape[1]
    col = lax.broadcasted_iota(jnp.int32, part.shape, 1)
    if offset == 1:
        return jnp.where(col == width - 1, 0.0, pltpu.roll(part, width - 1, 1))
    return jnp.where(col == 0, 0.0, pltpu.roll(part, 1, 1))


def conv_parts(w_ref, x):
    nk, o, i_ch = w_ref.shape
    every = jnp.dot(w_ref[...].reshape(nk * o, i_ch), x, preferred_element_type=jnp.float32)
    parts = []
    for a in range(3):
        total = None
        for b in range(3):
            k = a * 3 + b
            part = every[k * o:(k + 1) * o]
            if b != 1:
                part = lane_shift(part, b - 1)
            total = part if total is None else total + part
        parts.append(total)
    return parts


def filt_gather(src, dst, blk, send, recv):
    mf = lax.axis_index("filt")

    def out(j, s):
        return rcopy(src, dst.at[pl.ds(mf * blk, blk)], send.at[j], recv.at[mf], filt_dev(j))

    def inc(j, s):
        return rcopy(src, dst.at[pl.ds(s * blk, blk)], send.at[s], recv.at[s], filt_dev(s))

    each_filt_peer(lambda j, s: out(j, s).start())
    dst[pl.ds(mf * blk, blk)] = src[...]
    return (lambda: each_filt_peer(lambda j, s: inc(j, s).wait_recv()),
            lambda: each_filt_peer(lambda j, s: out(j, s).wait_send()))


def weight_rows(rows3, full, wt_ref, base):
    nq = full.shape[0] // 128
    ao = rows3.shape[0]
    shifted = []
    for b in range(3):
        moved = rows3
        if b != 1:
            moved = lane_shift(rows3.astype(jnp.float32), 1 - b).astype(rows3.dtype)
        shifted.append(moved)
    every = lax.dot_general(
        jnp.concatenate(shifted, axis=0), full, (((1,), (1,)), ((), ())), preferred_element_type=jnp.float32
    )
    for b in range(3):
        part = every[b * ao:(b + 1) * ao]
        for q in range(nq):
            wt_ref[pl.ds(base + (b * nq + q) * ao, ao), :] = part[:, q * 128:(q + 1) * 128]


def block_kernel(feat, og, w1r, w2r, out_ref, gs_ref, gprev, gnext, gf_ref, fprev, fnext,
                 wt_all, x_ref, h_ref, p0s, p2s, from_prev, from_next, q0s, q2s, qprev, qnext, hsrc, pre1, tbuf, rbuf,
                 hsems, xsend, xrecv, fsend, frecv, sems1, sems2, sems3, tsend, trecv):
    nf = lax.axis_size("filt")
    mf = lax.axis_index("filt")
    blk = feat.shape[0]
    enter(True)
    x_arrived, x_sent = filt_gather(feat, x_ref, blk, xsend, xrecv)
    x_arrived()
    parts = conv_parts(w1r, x_ref[...])
    p0s[...] = parts[0]
    p2s[...] = parts[2]
    halo = Halo(p0s, p2s, from_prev, from_next, hsems)
    halo.arrived()
    pre1[...] = parts[1] + from_prev[...] + from_next[...]
    hsrc[...] = jnp.maximum(pre1[...], 0.0).astype(hsrc.dtype)
    h_arrived, h_sent = filt_gather(hsrc, h_ref, blk, fsend, frecv)
    h_arrived()
    qs = conv_parts(w2r, h_ref[...])
    q0s[...] = qs[0]
    q2s[...] = qs[2]
    halo1 = Halo(q0s, q2s, qprev, qnext, sems1)
    halo1.arrived()
    pre = qs[1] + qprev[...] + qnext[...] + feat[...].astype(jnp.float32)
    out_ref[...] = jnp.maximum(pre, 0.0).astype(out_ref.dtype)
    gs_ref[...] = jnp.where(pre > 0, og[...].astype(jnp.float32), 0.0).astype(gs_ref.dtype)
    halo2 = Halo(gs_ref, gs_ref, gprev, gnext, sems2)
    halo2.arrived()
    rows3 = jnp.concatenate([gnext[...], gs_ref[...], gprev[...]], axis=0)
    per = 128 // blk
    for q in range(w2r.shape[2] // 128):
        total = None
        for b in range(3):
            lhs = jnp.concatenate([w2r[a * 3 + b, :, q * 128:(q + 1) * 128] for a in range(3)], axis=0)
            part = lax.dot_general(lhs, rows3, (((0,), (0,)), ((), ())), preferred_element_type=jnp.float32)
            if b != 1:
                part = lane_shift(part, 1 - b)
            total = part if total is None else total + part
        for u in range(per):
            tbuf[q * per + u] = total[u * blk:(u + 1) * blk].astype(tbuf.dtype)

    def out(j, s):
        return rcopy(tbuf.at[j], rbuf.at[mf], tsend.at[j], trecv.at[mf], filt_dev(j))

    weight_rows(rows3, h_ref[...], wt_all, wt_all.shape[0] // 2)

    def inc(j, s):
        return rcopy(tbuf.at[s], rbuf.at[s], tsend.at[s], trecv.at[s], filt_dev(s))

    each_filt_peer(lambda j, s: out(j, s).start())
    each_filt_peer(lambda j, s: inc(j, s).wait_recv())
    acc = tbuf[mf].astype(jnp.float32)

    def add(k, acc):
        return acc + rbuf[lax.rem(mf + k, nf)].astype(jnp.float32)

    acc = lax.fori_loop(1, nf, add, acc)
    gf_ref[...] = jnp.where(pre1[...] > 0, acc, 0.0).astype(gf_ref.dtype)
    halo3 = Halo(gf_ref, gf_ref, fprev, fnext, sems3)
    halo3.arrived()
    weight_rows(jnp.concatenate([fnext[...], gf_ref[...], fprev[...]], axis=0), x_ref[...], wt_all, 0)
    x_sent()
    h_sent()
    each_filt_peer(lambda j, s: out(j, s).wait_send())
    halo.sent()
    halo1.sent()
    halo2.sent()
    halo3.sent()


def call(kernel, args, outs, scratch, collective_id):
    spec = pl.BlockSpec(memory_space=pltpu.VMEM)
    return pl.pallas_call(
        kernel,
        out_shape=tuple(jax.ShapeDtypeStruct(shape, dtype) for shape, dtype in outs),
        in_specs=[spec] * len(args),
        out_specs=tuple(spec for _ in outs),
        scratch_shapes=scratch,
        compiler_params=pltpu.CompilerParams(collective_id=collective_id, has_side_effects=True),
    )(*args)


def exchange(x, axis, mode, collective_id, out_dtype=None):
    n = lax.axis_size(axis)
    out_dtype = out_dtype or x.dtype
    sems = [pltpu.SemaphoreType.DMA((n,)), pltpu.SemaphoreType.DMA((n,))]
    if mode == "ag":
        out_shape = (n,) + x.shape
        scratch = sems
    elif mode == "rs":
        out_shape = x.shape[1:]
        scratch = [pltpu.VMEM(x.shape, x.dtype)] + sems
    else:
        out_shape = x.shape
        scratch = [pltpu.VMEM(x.shape, x.dtype)] + sems + sems
    return pl.pallas_call(
        functools.partial(exchange_kernel, axis, n, mode),
        out_shape=jax.ShapeDtypeStruct(out_shape, out_dtype),
        in_specs=[pl.BlockSpec(memory_space=pltpu.VMEM)],
        out_specs=pl.BlockSpec(memory_space=pltpu.VMEM),
        scratch_shapes=scratch,
        compiler_params=pltpu.CompilerParams(collective_id=collective_id, has_side_effects=True),
    )(x)


def shift_cols(value, offset):
    if offset == 0:
        return value
    pad = [(0, 0)] * (value.ndim - 1)
    if offset > 0:
        return jnp.pad(value[..., offset:], pad + [(0, offset)])
    return jnp.pad(value[..., :offset], pad + [(-offset, 0)])


def conv_row(weight, row):
    o = weight.shape[0]
    flat = weight.reshape(o, 9, weight.shape[3])
    parts = jnp.einsum("oki,iw->kow", flat, row, preferred_element_type=jnp.float32)
    return [sum(shift_cols(parts[a * 3 + b], b - 1) for b in range(3)) for a in range(3)]


def weight_terms(rows3, full_row):
    cols = []
    for b in range(3):
        moved = shift_cols(rows3, 1 - b)
        cols.append(jnp.einsum("aow,iw->oai", moved, full_row, preferred_element_type=jnp.float32))
    return jnp.stack(cols, axis=2)


def hidden_terms(weight, rows3):
    total = None
    for b in range(3):
        part = jnp.einsum("oai,aow->iw", weight[:, :, b, :], rows3, preferred_element_type=jnp.float32)
        part = shift_cols(part, 1 - b)
        total = part if total is None else total + part
    return total


def per_device(features, first_weight, second_weight, out_grad):
    feat = features[:, 0, :]
    og = out_grad[:, 0, :]
    n_filt = lax.axis_size("filt")
    blk = feat.shape
    f32, bf16 = jnp.float32, jnp.bfloat16
    o, _, _, i_ch = first_weight.shape
    w1r = first_weight.transpose(1, 2, 0, 3).reshape(9, o, i_ch)
    w2r = second_weight.transpose(1, 2, 0, 3).reshape(9, o, i_ch)
    sem = pltpu.SemaphoreType.DMA
    full = (n_filt * blk[0], blk[1])
    nq = i_ch // 128
    wt = (2 * 3 * nq * 3 * o, 128)
    block_out, _, _, _, _, _, _, wt_all = call(
        block_kernel,
        (feat, og, w1r, w2r),
        [(blk, bf16)] * 7 + [(wt, f32)],
        [pltpu.VMEM(full, bf16), pltpu.VMEM(full, bf16)] + [pltpu.VMEM(blk, f32)] * 8 + [pltpu.VMEM(blk, bf16), pltpu.VMEM(blk, f32),
                                      pltpu.VMEM((n_filt,) + blk, bf16), pltpu.VMEM((n_filt,) + blk, bf16)]
        + [sem((4,))] + [sem((n_filt,))] * 4 + [sem((4,))] * 3 + [sem((n_filt,))] * 2,
        2,
    )
    n_rows = lax.axis_size("rows")
    summed = row_sum(wt_all.reshape(n_rows, -1, 128), 0)
    first_grad, second_grad = (
        half.reshape(3, nq, 3, o, 128).transpose(3, 2, 0, 1, 4).reshape(o, 3, 3, i_ch)
        for half in (summed[: n_rows // 2], summed[n_rows // 2:])
    )
    return (block_out[:, None, :], first_grad, second_grad)


def solution(mesh):
    in_specs = (
        P("filt", "rows", None),
        P("filt", None, None, None),
        P("filt", None, None, None),
        P("filt", "rows", None),
    )
    out_specs = (P("filt", "rows", None), P("filt", None, None, None), P("filt", None, None, None))
    return jax.shard_map(
        per_device, mesh=mesh, in_specs=in_specs, out_specs=out_specs, check_vma=False
    )
```
